32 devices in a mesh: orb: 8 (over y, x, core), grid: 4 (over z).
Axes of the slice: x: 2, y: 2, z: 4, core: 2. Of those that a mesh axis runs over, the one named last changes fastest.
Arguments:
- orbitals: float32 [128, 32, 4096], P('orb', 'grid'), may hold values from -6 to 6
- rotation: float32 [128, 128], replicated, may hold values from -0.5 to 0.5
- tile_list: int32 [4, 2], replicated, may hold values from 0 to 31, as said below
- pair_mask: int32 [128, 128], replicated, may hold values from 0 to 1, as said below
Outputs:
- exchange_term: float32 [128, 32, 4096], P('orb', 'grid')
The draws below stay inside these ranges and needn't reach their ends.
Inputs may be any that keep to these rules, and one draw needn't show every extreme that they name: `tile_list`: row t names one tile: its target block and its source block of 4 orbitals each; no tile is named twice. `pair_mask`: among the 64 orbital pairs that lie in listed tiles, exactly 32 are 1.
All inputs are finite; a program needn't handle non-finite values.
Results may differ from the reference program's by a relative error of at most 0.0003.
Values sent between devices are 32-bit elements; how exact they have to be, the bound alone decides.
No kernel may reach another device: no remote copies, remote signals or barrier semaphores. Data moves between devices by JAX's collectives and lax.ppermute only.
A program may use at most 64 MiB of HBM per device.

```python
import jax
import jax.numpy as jnp
from jax import lax

NORB = 128
BLK = 4
NX = 32
NY = 64
NZ = 64
NB = 32
NPAIR = 64
TILES = 4
LIVE = 32
N_ORB = 8


def tile_draw(key):
    shuffled = jax.random.permutation(jax.random.fold_in(key, 11), NB * NB)
    chosen = shuffled[:TILES].astype(jnp.int32)
    return jnp.stack([chosen // NB, chosen % NB], axis=1).astype(jnp.int32)


def draw_tile_list(key, part):
    return tile_draw(key)


def draw_pair_mask(key, part):
    tiles = tile_draw(key)
    within = jnp.arange(BLK * BLK, dtype=jnp.int32)
    targets = (BLK * tiles[:, 0:1] + within[None, :] // BLK).reshape(-1)
    sources = (BLK * tiles[:, 1:2] + within[None, :] % BLK).reshape(-1)
    background = jax.random.randint(jax.random.fold_in(key, 12), (NORB, NORB), 0, 2).astype(jnp.int32)
    shuffled = jax.random.permutation(jax.random.fold_in(key, 13), NPAIR)
    live_flags = jnp.zeros((NPAIR,), jnp.int32).at[shuffled[:LIVE]].set(1)
    return background.at[targets, sources].set(live_flags).astype(jnp.int32)


def steps_of(own_key, dims, pieces, low, top_value):
    level, own = 1.0, jax.random.fold_in(own_key, 6)
    for axis_at, parts in pieces:
        heights = jnp.exp(jax.random.uniform(jax.random.fold_in(own, axis_at), (parts,), jnp.float32, low / len(pieces), top_value / len(pieces)))
        level = level * jnp.repeat(heights, dims[axis_at] // parts).reshape([-1 if axis == axis_at else 1 for axis in range(len(dims))])
    return level


def scatter_about(rng, extent, spread, bound, split=(), kind=jnp.bfloat16):
    factor_of = steps_of(rng, extent, split, -0.22, 0.18) if split else 1.0
    entries = jax.random.normal(rng, extent, jnp.float32) * spread * factor_of
    return jnp.minimum(jnp.maximum(entries, -bound), bound).astype(kind)


def setup_inputs(seed: int = 0) -> dict:
    key_list = jax.random.split(jax.random.key(seed), 5)
    orbitals = scatter_about(key_list[0], (NORB, NX, NY * NZ), 1.0, 6.0, ((0, 8), (1, 4)), jnp.float32)
    rotation = scatter_about(key_list[1], (NORB, NORB), NORB ** -0.5, 0.5, (), jnp.float32)
    tile_list = draw_tile_list(jax.random.fold_in(key_list[4], 71), 0)
    pair_mask = draw_pair_mask(jax.random.fold_in(key_list[4], 71), 0)
    return dict(orbitals=orbitals, rotation=rotation, tile_list=tile_list, pair_mask=pair_mask)


precise = lax.Precision.HIGHEST
coupling = 0.25
screening = 0.1

def sine_table(length):
    wave_index = jnp.arange(length, dtype=jnp.float32) + 1.0
    return jnp.sqrt(2.0 / (length + 1.0)) * jnp.sin(jnp.pi * wave_index[:, None] * wave_index[None, :] / (length + 1.0))

def eigen_values(length):
    wave_index = jnp.arange(length, dtype=jnp.float32) + 1.0
    return 2.0 - 2.0 * jnp.cos(jnp.pi * wave_index / (length + 1.0))

def green_kernel(size_x, size_y, size_z):
    summed = eigen_values(size_x)[:, None, None] + eigen_values(size_y)[None, :, None] + eigen_values(size_z)[None, None, :]
    return coupling / (summed + screening)

def pair_lists(tile_list, pair_mask):
    within = jnp.arange(BLK * BLK, dtype=jnp.int32)
    targets = (BLK * tile_list[:, 0:1] + within[None, :] // BLK).reshape(-1).astype(jnp.int32)
    sources = (BLK * tile_list[:, 1:2] + within[None, :] % BLK).reshape(-1).astype(jnp.int32)
    return (targets, sources, pair_mask[targets, sources])

def compact(targets, sources, live_flags, number):
    ranking = (jnp.cumsum(live_flags) - 1).astype(jnp.int32)
    places = jnp.where(live_flags == 1, ranking, number).astype(jnp.int32)
    picked = jnp.zeros((number,), jnp.int32).at[places].set(jnp.arange(live_flags.shape[0], dtype=jnp.int32), mode='drop')
    return (targets[picked], sources[picked])

def transform_all(values, matrix_x, matrix_y, matrix_z):
    values = jnp.einsum('gxyz,zk->gxyk', values, matrix_z, precision=precise)
    values = jnp.einsum('gxyz,yk->gxkz', values, matrix_y, precision=precise)
    return jnp.einsum('gxyz,xk->gkyz', values, matrix_x, precision=precise)

def reference(orbitals, rotation, tile_list, pair_mask):
    rotated = jnp.einsum('ij,ixc->jxc', rotation, orbitals, precision=precise).reshape(NORB, NX, NY, NZ)
    targets, sources, live_flags = pair_lists(tile_list, pair_mask)
    targets, sources = compact(targets, sources, live_flags, LIVE)
    targets = targets.reshape(N_ORB, -1)
    sources = sources.reshape(N_ORB, -1)
    matrix_x = sine_table(NX)
    matrix_y = sine_table(NY)
    matrix_z = sine_table(NZ)
    kernel = green_kernel(NX, NY, NZ)

    def accumulate(carry, pair_group):
        group_targets, group_sources = pair_group
        density = rotated[group_targets] * rotated[group_sources]
        spectrum = transform_all(density, matrix_x, matrix_y, matrix_z) * kernel
        potential = transform_all(spectrum, matrix_x, matrix_y, matrix_z)
        products = potential * rotated[group_sources]
        selector = (group_targets[:, None] == jnp.arange(NORB, dtype=jnp.int32)[None, :]).astype(jnp.float32)
        return (carry - jnp.einsum('gi,gxyz->ixyz', selector, products, precision=precise), None)
    start = jnp.zeros((NORB, NX, NY, NZ), jnp.float32)
    summed, ignored = lax.scan(accumulate, start, (targets, sources))
    return summed.reshape(NORB, NX, NY * NZ)
```

```python
import functools

import jax
import jax.numpy as jnp
import numpy as np
from jax import lax
from jax.experimental import pallas as pl
from jax.experimental.pallas import tpu as pltpu
from jax.sharding import PartitionSpec as P

BLK = 4
NY = 64
NZ = 64
LANES = 128
SUB = 8
COUPLING = 0.25
SCREENING = 0.1

precise = lax.Precision.HIGHEST
f32 = jnp.float32
bf16 = jnp.bfloat16


def sine_np(n):
    k = np.arange(1, n + 1, dtype=np.float64)
    return np.sqrt(2.0 / (n + 1)) * np.sin(np.pi * k[:, None] * k[None, :] / (n + 1))


def eigen_np(n):
    k = np.arange(1, n + 1, dtype=np.float64)
    return 2.0 - 2.0 * np.cos(np.pi * k / (n + 1))


def halves_np(table):
    high = np.asarray(table, np.float32).astype(jnp.bfloat16)
    low = (np.asarray(table, np.float64) - high.astype(np.float64)).astype(jnp.bfloat16)
    return jnp.asarray(high), jnp.asarray(low)


def y_order():
    rows = LANES // NZ
    return np.arange(NY).reshape(NY // rows, rows).T.reshape(-1)


def y_table():
    order = y_order()
    return np.kron(sine_np(NY)[order][:, order], np.eye(SUB))


def z_table():
    half = LANES // NZ
    sine = sine_np(NZ)
    table = np.zeros((2, half, NZ, half, 2, NZ))
    for pair in range(2):
        for h in range(half):
            table[pair, h, :, h, pair, :] = sine
    return table.reshape(2 * half * NZ, half * 2 * NZ)


def decay_np():
    c = eigen_np(NY)[y_order()][:, None] + eigen_np(NZ)[None, :] + SCREENING
    r = 2.0 / (2.0 + c + np.sqrt(c * (c + 4.0)))
    return np.concatenate([r, r], axis=1)


def dot(a, b):
    return jnp.dot(a, b, preferred_element_type=f32)


def split(x):
    high = x.astype(bf16)
    return high, (x - high.astype(f32)).astype(bf16)


def dot3(a, b):
    return dot(a[0], b[0]) + dot(a[0], b[1]) + dot(a[1], b[0])


def rotate_kernel(own, sib, mine, theirs, send, keep):
    rows, width = send.shape[0] * SUB, send.shape[2]
    depth = mine.shape[0] * SUB
    a = split(mine[...].reshape(depth, width))
    b = split(theirs[...].reshape(depth, width))
    for out, at in ((send, 0), (keep, rows)):
        part = pl.ds(at, rows)
        total = dot3(split(own[part, :]), a) + dot3(split(sib[part, :]), b)
        out[...] = total.reshape(out.shape)


def forward_kernel(u, where, own, other, y_hi, y_lo, z_hi, z_lo, decay, left, right, k_left, k_right,
                   local, a_out, b_out, dens, work, fwd, bwd):
    tiles = own.shape[2] // LANES
    core = where[0]
    for side, ref, source, target in ((0, own, BLK // 2, BLK // 2 + BLK + u), (1, other, 2, u)):
        offset = jnp.where(core == side, 0, tiles * SUB) if side == 0 else jnp.where(core == 0, tiles * SUB, 0)
        for t in range(tiles):
            lanes = pl.ds(t * LANES, LANES)
            value = ref[target, :, lanes]
            rows = pl.ds(pl.multiple_of(offset + t * SUB, SUB), SUB)
            for w in range(BLK):
                dens[rows, w * LANES:(w + 1) * LANES] = value * ref[source + w, :, lanes]
    z = (z_hi[...], z_lo[...])
    half = dens.shape[0]
    for q in range(BLK // 2):
        out = dot3(split(dens[:, q * 2 * LANES:(q + 1) * 2 * LANES]), z)
        work[:half, q * LANES:(q + 1) * LANES] = out[:, :LANES]
        work[half:, q * LANES:(q + 1) * LANES] = out[:, LANES:]
    work[...] = dot3((y_hi[...], y_lo[...]), split(work[...]))
    plane = lax.broadcasted_iota(jnp.int32, (SUB, LANES), 0)

    def solve(k, carry):
        rows = pl.ds(pl.multiple_of(k * SUB, SUB), SUB)
        r = decay[rows, :]
        steps = []
        power = r
        for s in (1, 2, 4):
            steps.append((s, jnp.where(plane >= s, power, 0.0), jnp.where(plane < SUB - s, power, 0.0)))
            power = power * power
        lf, rt, kl, kr = left[rows, :], right[rows, :], k_left[rows, :], k_right[rows, :]
        for q in range(BLK // 2):
            lanes = slice(q * LANES, (q + 1) * LANES)
            rho = work[rows, lanes]
            f = lf * rho
            own_term = rt * rho
            h = own_term
            for s, down, up in steps:
                f = f + down * pltpu.roll(f, s, 0)
                h = h + up * pltpu.roll(h, SUB - s, 0)
            fwd[q, rows, :] = f
            bwd[q, rows, :] = h
            local[rows, lanes] = kl * f + kr * (h - own_term)
        return carry

    lax.fori_loop(0, NY, solve, 0, unroll=4)
    for q in range(BLK // 2):
        lanes = slice(q * LANES, (q + 1) * LANES)
        a_out[:, lanes] = fwd[q, pl.ds(SUB - 1, NY, stride=SUB), :]
        b_out[:, lanes] = bwd[q, pl.ds(0, NY, stride=SUB), :]


def backward_kernel(u, where, flags, own, other, y_hi, y_lo, z_hi, z_lo, local, from_left, from_right,
                    in_left, in_right, out, work, pot):
    tiles = own.shape[2] // LANES
    core = where[0]

    def add(group, carry):
        lines = pl.ds(pl.multiple_of(group * SUB, SUB), SUB)
        for q in range(BLK // 2):
            lanes = slice(q * LANES, (q + 1) * LANES)
            lp, rp = from_left[lines, lanes], from_right[lines, lanes]
            for k in range(SUB):
                rows = pl.ds(pl.multiple_of((group * SUB + k) * SUB, SUB), SUB)
                here = in_left[rows, :] * lp[k:k + 1] + in_right[rows, :] * rp[k:k + 1]
                work[rows, lanes] = local[rows, lanes] + here
        return carry

    lax.fori_loop(0, NY // SUB, add, 0)
    work[...] = dot3((y_hi[...], y_lo[...]), split(work[...]))
    z = (z_hi[...], z_lo[...])
    half = pot.shape[0]
    for q in range(BLK // 2):
        lanes = slice(q * LANES, (q + 1) * LANES)
        rows = jnp.concatenate([work[:half, lanes], work[half:, lanes]], axis=1)
        pot[:, q * 2 * LANES:(q + 1) * 2 * LANES] = dot3(split(rows), z)
    for side, ref, source in ((0, own, BLK // 2), (1, other, 2)):
        offset = jnp.where(core == 0, 0, tiles) if side == 0 else jnp.where(core == 0, tiles, 0)
        for t in range(tiles):
            lanes = pl.ds(t * LANES, LANES)
            rows = pl.ds(pl.multiple_of((offset + t) * SUB, SUB), SUB)
            total = None
            for w in range(BLK):
                term = flags[u * BLK + w] * (pot[rows, w * LANES:(w + 1) * LANES] * ref[source + w, :, lanes])
                total = term if total is None else total + term
            out[:, pl.ds(pl.multiple_of((offset + t) * LANES, LANES), LANES)] = -total


def place_kernel(match, *refs):
    parts, out = refs[:-1], refs[-1]
    blocks = out.shape[0] // BLK
    count = len(parts) // 2
    for b in range(blocks):
        for own_core in range(2):
            for u in range(BLK // 2):
                total = None
                for n in range(count):
                    ref = parts[own_core * count + n]
                    term = match[(b * 2 + own_core) * count + n] * ref[u]
                    total = term if total is None else total + term
                row = match_row(out, b, u, own_core)
                out[row] = total


def match_row(out, b, u, own_core):
    core = lax.rem(lax.axis_index("orb"), 2)
    which = core if own_core == 0 else 1 - core
    return b * BLK + which * (BLK // 2) + u


VM = pl.BlockSpec(memory_space=pltpu.VMEM)
SM = pl.BlockSpec(memory_space=pltpu.SMEM)


def tile_device(orbitals, rotation, tile_list, pair_mask):
    per_device, planes, width = orbitals.shape
    n_orb, n_grid = lax.axis_size("orb"), lax.axis_size("grid")
    size_x = planes * n_grid
    half = width // 2
    axes = ("orb", "grid")
    o, g = lax.axis_index("orb"), lax.axis_index("grid")
    core, chip = o % 2, o // 2

    def swap(x, even, odd):
        moves = []
        for a in range(n_orb):
            flip = even if a % 2 == 0 else odd
            moves += [(a * n_grid + b, (a ^ flip) * n_grid + b) for b in range(n_grid)]
        return lax.ppermute(x, axes, moves)

    def shift(x, step):
        moves = [(a * n_grid + b, a * n_grid + b + step) for a in range(n_orb)
                 for b in range(n_grid) if 0 <= b + step < n_grid]
        return lax.ppermute(x, axes, moves)

    low, high = orbitals[:, :, :half], orbitals[:, :, half:]
    mine = jnp.where(core == 0, low, high)
    theirs = swap(jnp.where(core == 0, high, low), 1, 1)

    bit_1 = jnp.where(core == 0, 1, 2)
    bit_2 = 3 - bit_1
    order = jnp.stack([chip ^ 3, chip ^ bit_1, chip ^ bit_2, chip])
    blocks = tile_list[order]
    pick = jnp.arange(BLK // 2)
    wanted = jnp.concatenate(
        [
            BLK * blocks[:, 0:1] + (BLK // 2) * (1 - core) + pick,
            BLK * blocks[:, 1:2] + jnp.arange(BLK),
            BLK * blocks[:, 0:1] + (BLK // 2) * core + pick,
        ],
        axis=1,
    ).reshape(-1)
    chosen = (jnp.repeat(wanted, SUB)[:, None] == jnp.arange(rotation.shape[1])[None, :]).astype(f32)
    rows = jnp.einsum("rj,ij->ri", chosen, rotation, precision=precise)
    same_plane = jnp.arange(chosen.shape[0])[:, None] % SUB == jnp.arange(per_device * SUB)[None, :] % SUB

    def spread(who):
        source = who * per_device + jnp.arange(per_device * SUB) // SUB
        columns = (jnp.arange(rotation.shape[0])[:, None] == source[None, :]).astype(f32)
        table = jnp.einsum("ri,ic->rc", rows, columns, precision=precise)
        return jnp.where(same_plane, table, 0.0)

    slots = wanted.shape[0]
    part = jax.ShapeDtypeStruct((slots // 2, planes, half), f32)
    send, keep = pl.pallas_call(
        rotate_kernel, out_shape=(part, part), in_specs=[VM] * 4, out_specs=(VM, VM), name="rotate",
    )(spread(o), spread(o ^ 1), mine, theirs)
    keep = keep + swap(send, 2, 4)
    cut = slots // 4
    own = keep[cut:] + swap(keep[:cut], 4, 2)
    other = swap(own[: cut - BLK // 2], 1, 1)

    decay = decay_np()
    log_r = jnp.asarray(np.log(decay), f32)[:, None, :]
    p = jnp.arange(planes, dtype=f32)[None, :, None]
    place = planes * g.astype(f32) + p + 1.0
    left = 1.0 - jnp.exp(2.0 * place * log_r)
    right = 1.0 - jnp.exp(2.0 * (size_x + 1.0 - place) * log_r)
    scale = jnp.asarray(COUPLING * decay / ((1 - decay**2) * (1 - decay ** (2 * size_x + 2))), f32)[:, None, :]
    k_left, k_right = scale * right, scale * left
    in_left = (k_left * jnp.exp((p + 1.0) * log_r)).reshape(-1, LANES)
    in_right = (k_right * jnp.exp((planes - p) * log_r)).reshape(-1, LANES)
    left, right, k_left, k_right = (v.reshape(-1, LANES) for v in (left, right, k_left, k_right))
    spread_decay = jnp.asarray(np.repeat(decay, SUB, axis=0), f32)
    slab = np.concatenate([decay, decay], axis=1) ** planes

    y_hi, y_lo = halves_np(y_table())
    z_hi, z_lo = halves_np(z_table())
    zt_hi, zt_lo = halves_np(z_table().T)
    where = jnp.stack([core, g]).astype(jnp.int32)
    tile = tile_list[chip]
    flags = lax.dynamic_slice(
        pair_mask, (BLK * tile[0] + (BLK // 2) * core, BLK * tile[1]), (BLK // 2, BLK)
    ).astype(f32).reshape(-1)

    solved = []
    for u in range(BLK // 2):
        lines = jax.ShapeDtypeStruct((NY, 2 * LANES), f32)
        cube = (NY * SUB, 2 * LANES)
        local, a, b = pl.pallas_call(
            functools.partial(forward_kernel, u),
            out_shape=(jax.ShapeDtypeStruct(cube, f32), lines, lines),
            in_specs=[SM] + [VM] * 11,
            out_specs=(VM, VM, VM),
            scratch_shapes=[pltpu.VMEM((width // LANES * SUB, BLK * LANES), f32), pltpu.VMEM(cube, f32)]
            + [pltpu.VMEM((BLK // 2, NY * SUB, LANES), f32)] * 2,
            name=f"forward_{u}",
        )(where, own, other, y_hi, y_lo, z_hi, z_lo, spread_decay, left, right, k_left, k_right)
        from_left = from_right = None
        step = 1
        while step < n_grid:
            got_a, got_b = shift(a, step), shift(b, -step)
            if from_left is None:
                from_left, from_right = got_a, got_b
            else:
                factor = jnp.asarray(slab ** (step - 1), f32)
                from_left, from_right = from_left + factor * got_a, from_right + factor * got_b
            factor = jnp.asarray(slab**step, f32)
            a, b = a + factor * got_a, b + factor * got_b
            step *= 2
        solved.append((local, from_left, from_right))

    terms = []
    for u, (local, from_left, from_right) in enumerate(solved):
        terms.append(pl.pallas_call(
            functools.partial(backward_kernel, u),
            out_shape=jax.ShapeDtypeStruct((planes, width), f32),
            in_specs=[SM, SM] + [VM] * 11,
            out_specs=VM,
            scratch_shapes=[pltpu.VMEM(cube, f32), pltpu.VMEM((width // LANES * SUB, BLK * LANES), f32)],
            name=f"backward_{u}",
        )(where, flags, own, other, y_hi, y_lo, zt_hi, zt_lo, local, from_left, from_right, in_left, in_right))

    term = jnp.stack(terms)
    near_1 = swap(term, 2, 4)
    near_2 = swap(term, 4, 2)
    far = swap(near_1, 4, 2)
    own_parts = [term, near_1, near_2, far]
    sib_parts = [swap(v, 1, 1) for v in own_parts]
    own_tiles = jnp.stack([chip, chip ^ bit_1, chip ^ bit_2, chip ^ 3])
    sib_tiles = jnp.stack([chip, chip ^ bit_2, chip ^ bit_1, chip ^ 3])
    home = tile_list[:, 0][jnp.stack([own_tiles, sib_tiles])]
    base = o * (per_device // BLK) + jnp.arange(per_device // BLK)
    match = (base[:, None, None] == home[None]).astype(f32).reshape(-1)
    chunk = width // 4
    spec = pl.BlockSpec((BLK // 2, planes, chunk), lambda i: (0, 0, i))
    return pl.pallas_call(
        place_kernel,
        out_shape=jax.ShapeDtypeStruct(orbitals.shape, f32),
        grid=(width // chunk,),
        in_specs=[SM] + [spec] * 8,
        out_specs=pl.BlockSpec((per_device, planes, chunk), lambda i: (0, 0, i)),
        name="place",
    )(match, *own_parts, *sib_parts)


def sine_table(length):
    wave_index = jnp.arange(length, dtype=f32) + 1.0
    return jnp.sqrt(2.0 / (length + 1.0)) * jnp.sin(
        jnp.pi * wave_index[:, None] * wave_index[None, :] / (length + 1.0)
    )


def eigen_values(length):
    wave_index = jnp.arange(length, dtype=f32) + 1.0
    return 2.0 - 2.0 * jnp.cos(jnp.pi * wave_index / (length + 1.0))


def green_kernel(size_x, size_y, size_z):
    summed = (
        eigen_values(size_x)[:, None, None]
        + eigen_values(size_y)[None, :, None]
        + eigen_values(size_z)[None, None, :]
    )
    return COUPLING / (summed + SCREENING)


def pair_lists(tile_list, pair_mask):
    within = jnp.arange(BLK * BLK, dtype=jnp.int32)
    targets = (BLK * tile_list[:, 0:1] + within[None, :] // BLK).reshape(-1)
    sources = (BLK * tile_list[:, 1:2] + within[None, :] % BLK).reshape(-1)
    return (targets, sources, pair_mask[targets, sources])


def compact(targets, sources, live_flags, number):
    ranking = jnp.cumsum(live_flags) - 1
    places = jnp.where(live_flags == 1, ranking, number)
    picked = (
        jnp.zeros((number,), jnp.int32)
        .at[places]
        .set(jnp.arange(live_flags.shape[0], dtype=jnp.int32), mode="drop")
    )
    return (targets[picked], sources[picked])


def along_z(values, matrix):
    number, planes, width_yz = values.shape
    size_z = matrix.shape[0]
    shaped = values.reshape(number, planes, width_yz // size_z, size_z)
    return jnp.einsum("pxrz,zk->pxrk", shaped, matrix, precision=precise).reshape(number, planes, width_yz)


def along_y(values, matrix):
    number, planes, width_yz = values.shape
    size_y = matrix.shape[0]
    shaped = values.reshape(number, planes, size_y, width_yz // size_y)
    return jnp.einsum("pxyz,yk->pxkz", shaped, matrix, precision=precise).reshape(number, planes, width_yz)


def along_x(values, matrix):
    return jnp.einsum("pxc,xk->pkc", values, matrix, precision=precise)


def any_device(orbitals, rotation, tile_list, pair_mask):
    n_orb, n_grid = lax.axis_size("orb"), lax.axis_size("grid")
    number_orbitals, size_x = rotation.shape[0], orbitals.shape[1] * n_grid
    rotated = jnp.einsum(
        "ij,ixc->jxc",
        rotation,
        lax.all_to_all(orbitals, "orb", split_axis=2, concat_axis=0, tiled=True),
        precision=precise,
    )
    planes, width_yz = rotated.shape[1:]
    targets, sources, live_flags = pair_lists(tile_list, pair_mask)
    matrix_x, matrix_y, matrix_z = sine_table(size_x), sine_table(NY), sine_table(NZ)
    kernel = green_kernel(size_x, NY, NZ).reshape(size_x, NY * NZ)
    orbital_ids = jnp.arange(number_orbitals, dtype=jnp.int32)
    targets, sources = compact(targets, sources, live_flags, targets.shape[0] // 2)
    density = rotated[targets] * rotated[sources]
    number = density.shape[0]
    spectrum = along_z(density, matrix_z)
    spectrum = lax.all_to_all(spectrum, "orb", split_axis=0, concat_axis=2, tiled=True)
    spectrum = along_y(spectrum, matrix_y)
    spectrum = lax.all_to_all(spectrum, "grid", split_axis=0, concat_axis=1, tiled=True)
    spectrum = along_x(along_x(spectrum, matrix_x) * kernel, matrix_x)
    spectrum = lax.all_to_all(spectrum, "grid", split_axis=1, concat_axis=0, tiled=True)
    spectrum = along_y(spectrum, matrix_y)
    spectrum = lax.all_to_all(spectrum, "orb", split_axis=2, concat_axis=0, tiled=True)
    potential = along_z(spectrum, matrix_z)
    products = potential * rotated[sources]
    selector = (targets[None, :] == orbital_ids[:, None]).astype(f32)
    partial_value = -jnp.dot(selector, products.reshape(number, planes * width_yz), precision=precise)
    partial_value = partial_value.reshape(number_orbitals, planes, width_yz)
    return lax.all_to_all(partial_value, "orb", split_axis=0, concat_axis=2, tiled=True)


def solution(mesh):
    n_orb, n_grid = mesh.shape["orb"], mesh.shape["grid"]

    def on_device(orbitals, rotation, tile_list, pair_mask):
        per_device, planes, width = orbitals.shape
        fits = n_orb == 8 and 2 * tile_list.shape[0] == n_orb and planes == SUB and per_device % BLK == 0
        fits = fits and width == NY * NZ and 2 * NZ == LANES
        body = tile_device if fits else any_device
        return body(orbitals, rotation, tile_list, pair_mask)

    in_specs = (P("orb", "grid", None), P(), P(), P())
    out_specs = P("orb", "grid", None)
    return jax.shard_map(on_device, mesh=mesh, in_specs=in_specs, out_specs=out_specs, check_vma=False)
```

```python
import functools

import jax
import jax.numpy as jnp
import numpy as np
from jax import lax
from jax.experimental import pallas as pl
from jax.experimental.pallas import tpu as pltpu
from jax.sharding import PartitionSpec as P

BLK = 4
NY = 64
NZ = 64
LANES = 128
SUB = 8
COUPLING = 0.25
SCREENING = 0.1

precise = lax.Precision.HIGHEST
f32 = jnp.float32
bf16 = jnp.bfloat16


def sine_np(n):
    k = np.arange(1, n + 1, dtype=np.float64)
    return np.sqrt(2.0 / (n + 1)) * np.sin(np.pi * k[:, None] * k[None, :] / (n + 1))


def eigen_np(n):
    k = np.arange(1, n + 1, dtype=np.float64)
    return 2.0 - 2.0 * np.cos(np.pi * k / (n + 1))


def halves_np(table):
    high = np.asarray(table, np.float32).astype(jnp.bfloat16)
    low = (np.asarray(table, np.float64) - high.astype(np.float64)).astype(jnp.bfloat16)
    return jnp.asarray(high), jnp.asarray(low)


def y_order():
    rows = LANES // NZ
    return np.arange(NY).reshape(NY // rows, rows).T.reshape(-1)


def y_table():
    order = y_order()
    return np.kron(sine_np(NY)[order][:, order], np.eye(SUB))


def z_table():
    half = LANES // NZ
    sine = sine_np(NZ)
    table = np.zeros((2, half, NZ, half, 2, NZ))
    for pair in range(2):
        for h in range(half):
            table[pair, h, :, h, pair, :] = sine
    return table.reshape(2 * half * NZ, half * 2 * NZ)


def decay_np():
    c = eigen_np(NY)[y_order()][:, None] + eigen_np(NZ)[None, :] + SCREENING
    r = 2.0 / (2.0 + c + np.sqrt(c * (c + 4.0)))
    return np.concatenate([r, r], axis=1)


def dot(a, b):
    return jnp.dot(a, b, preferred_element_type=f32)


def split(x):
    high = x.astype(bf16)
    return high, (x - high.astype(f32)).astype(bf16)


def dot3(a, b):
    return dot(a[0], b[0]) + dot(a[0], b[1]) + dot(a[1], b[0])


def rotate_kernel(own, sib, mine, theirs, send, keep):
    rows, width = send.shape[0] * SUB, send.shape[2]
    depth = mine.shape[0] * SUB
    a = split(mine[...].reshape(depth, width))
    b = split(theirs[...].reshape(depth, width))
    for out, at in ((send, 0), (keep, rows)):
        part = pl.ds(at, rows)
        total = dot3(split(own[part, :]), a) + dot3(split(sib[part, :]), b)
        out[...] = total.reshape(out.shape)


def forward_kernel(u, where, own, other, y_hi, y_lo, z_hi, z_lo, decay, left, right, k_left, k_right,
                   local, *rest):
    messages, (dens, work, fwd, bwd) = rest[:-4], rest[-4:]
    tiles = own.shape[2] // LANES
    core = where[0]
    for side, ref, source, target in ((0, own, BLK // 2, BLK // 2 + BLK + u), (1, other, 2, u)):
        offset = jnp.where(core == side, 0, tiles * SUB) if side == 0 else jnp.where(core == 0, tiles * SUB, 0)
        for t in range(tiles):
            lanes = pl.ds(t * LANES, LANES)
            value = ref[target, :, lanes]
            rows = pl.ds(pl.multiple_of(offset + t * SUB, SUB), SUB)
            for w in range(BLK):
                dens[rows, w * LANES:(w + 1) * LANES] = value * ref[source + w, :, lanes]
    z = (z_hi[...], z_lo[...])
    half = dens.shape[0]
    for q in range(BLK // 2):
        out = dot3(split(dens[:, q * 2 * LANES:(q + 1) * 2 * LANES]), z)
        work[:half, q * LANES:(q + 1) * LANES] = out[:, :LANES]
        work[half:, q * LANES:(q + 1) * LANES] = out[:, LANES:]
    work[...] = dot3((y_hi[...], y_lo[...]), split(work[...]))
    plane = lax.broadcasted_iota(jnp.int32, (SUB, LANES), 0)

    def solve(k, carry):
        rows = pl.ds(pl.multiple_of(k * SUB, SUB), SUB)
        r = decay[rows, :]
        steps = []
        power = r
        for s in (1, 2, 4):
            steps.append((s, jnp.where(plane >= s, power, 0.0), jnp.where(plane < SUB - s, power, 0.0)))
            power = power * power
        lf, rt, kl, kr = left[rows, :], right[rows, :], k_left[rows, :], k_right[rows, :]
        for q in range(BLK // 2):
            lanes = slice(q * LANES, (q + 1) * LANES)
            rho = work[rows, lanes]
            f = lf * rho
            own_term = rt * rho
            h = own_term
            for s, down, up in steps:
                f = f + down * pltpu.roll(f, s, 0)
                h = h + up * pltpu.roll(h, SUB - s, 0)
            fwd[q, rows, :] = f
            bwd[q, rows, :] = h
            local[rows, lanes] = kl * f + kr * (h - own_term)
        return carry

    lax.fori_loop(0, NY, solve, 0, unroll=4)
    g = where[1]
    for q in range(BLK // 2):
        lanes = slice(q * LANES, (q + 1) * LANES)
        rightward = fwd[q, pl.ds(SUB - 1, NY, stride=SUB), :]
        leftward = bwd[q, pl.ds(0, NY, stride=SUB), :]
        for k, out in enumerate(messages, 1):
            out[:, lanes] = jnp.where((g ^ k) > g, rightward, leftward)


def backward_kernel(u, where, flags, own, other, y_hi, y_lo, z_hi, z_lo, local, in_left, in_right, slab, *rest):
    received, (out, work, pot) = rest[:-3], rest[-3:]
    g = where[1]
    tiles = own.shape[2] // LANES
    core = where[0]

    def add(group, carry):
        lines = pl.ds(pl.multiple_of(group * SUB, SUB), SUB)
        for q in range(BLK // 2):
            lanes = slice(q * LANES, (q + 1) * LANES)
            lp = rp = jnp.zeros((SUB, LANES), f32)
            powers = [jnp.ones((SUB, LANES), f32), slab[lines, :]]
            while len(powers) < len(received):
                powers.append(powers[-1] * powers[1])
            for n, ref in enumerate(received, 1):
                peer = g ^ n
                distance = jnp.abs(peer - g)
                value = ref[lines, lanes]
                factor = powers[n - 1]
                for d in range(1, n):
                    factor = jnp.where(distance == d, powers[d - 1], factor)
                value = factor * value
                lp = lp + jnp.where(peer < g, value, 0.0)
                rp = rp + jnp.where(peer < g, 0.0, value)
            for k in range(SUB):
                rows = pl.ds(pl.multiple_of((group * SUB + k) * SUB, SUB), SUB)
                here = in_left[rows, :] * lp[k:k + 1] + in_right[rows, :] * rp[k:k + 1]
                work[rows, lanes] = local[rows, lanes] + here
        return carry

    lax.fori_loop(0, NY // SUB, add, 0)
    work[...] = dot3((y_hi[...], y_lo[...]), split(work[...]))
    z = (z_hi[...], z_lo[...])
    half = pot.shape[0]
    for q in range(BLK // 2):
        lanes = slice(q * LANES, (q + 1) * LANES)
        rows = jnp.concatenate([work[:half, lanes], work[half:, lanes]], axis=1)
        pot[:, q * 2 * LANES:(q + 1) * 2 * LANES] = dot3(split(rows), z)
    for side, ref, source in ((0, own, BLK // 2), (1, other, 2)):
        offset = jnp.where(core == 0, 0, tiles) if side == 0 else jnp.where(core == 0, tiles, 0)
        for t in range(tiles):
            lanes = pl.ds(t * LANES, LANES)
            rows = pl.ds(pl.multiple_of((offset + t) * SUB, SUB), SUB)
            total = None
            for w in range(BLK):
                term = flags[u * BLK + w] * (pot[rows, w * LANES:(w + 1) * LANES] * ref[source + w, :, lanes])
                total = term if total is None else total + term
            out[:, pl.ds(pl.multiple_of((offset + t) * LANES, LANES), LANES)] = -total


def place_kernel(match, *refs):
    parts, out = refs[:-1], refs[-1]
    blocks = out.shape[0] // BLK
    count = len(parts) // 2
    for b in range(blocks):
        for own_core in range(2):
            for u in range(BLK // 2):
                total = None
                for n in range(count):
                    ref = parts[own_core * count + n]
                    term = match[(b * 2 + own_core) * count + n] * ref[u]
                    total = term if total is None else total + term
                row = match_row(out, b, u, own_core)
                out[row] = total


def match_row(out, b, u, own_core):
    core = lax.rem(lax.axis_index("orb"), 2)
    which = core if own_core == 0 else 1 - core
    return b * BLK + which * (BLK // 2) + u


VM = pl.BlockSpec(memory_space=pltpu.VMEM)
SM = pl.BlockSpec(memory_space=pltpu.SMEM)


def tile_device(orbitals, rotation, tile_list, pair_mask):
    per_device, planes, width = orbitals.shape
    n_orb, n_grid = lax.axis_size("orb"), lax.axis_size("grid")
    size_x = planes * n_grid
    half = width // 2
    axes = ("orb", "grid")
    o, g = lax.axis_index("orb"), lax.axis_index("grid")
    core, chip = o % 2, o // 2

    def swap(x, even, odd):
        moves = []
        for a in range(n_orb):
            flip = even if a % 2 == 0 else odd
            moves += [(a * n_grid + b, (a ^ flip) * n_grid + b) for b in range(n_grid)]
        return lax.ppermute(x, axes, moves)

    def cross(x, k):
        moves = [(a * n_grid + b, a * n_grid + (b ^ k)) for a in range(n_orb) for b in range(n_grid)]
        return lax.ppermute(x, axes, moves)

    low, high = orbitals[:, :, :half], orbitals[:, :, half:]
    mine = jnp.where(core == 0, low, high)
    theirs = swap(jnp.where(core == 0, high, low), 1, 1)

    bit_1 = jnp.where(core == 0, 1, 2)
    bit_2 = 3 - bit_1
    order = jnp.stack([chip ^ 3, chip ^ bit_1, chip ^ bit_2, chip])
    blocks = tile_list[order]
    pick = jnp.arange(BLK // 2)
    wanted = jnp.concatenate(
        [
            BLK * blocks[:, 0:1] + (BLK // 2) * (1 - core) + pick,
            BLK * blocks[:, 1:2] + jnp.arange(BLK),
            BLK * blocks[:, 0:1] + (BLK // 2) * core + pick,
        ],
        axis=1,
    ).reshape(-1)
    chosen = (jnp.repeat(wanted, SUB)[:, None] == jnp.arange(rotation.shape[1])[None, :]).astype(f32)
    rows = jnp.einsum("rj,ij->ri", chosen, rotation, precision=precise)
    same_plane = jnp.arange(chosen.shape[0])[:, None] % SUB == jnp.arange(per_device * SUB)[None, :] % SUB

    def spread(who):
        source = who * per_device + jnp.arange(per_device * SUB) // SUB
        columns = (jnp.arange(rotation.shape[0])[:, None] == source[None, :]).astype(f32)
        table = jnp.einsum("ri,ic->rc", rows, columns, precision=precise)
        return jnp.where(same_plane, table, 0.0)

    slots = wanted.shape[0]
    part = jax.ShapeDtypeStruct((slots // 2, planes, half), f32)
    send, keep = pl.pallas_call(
        rotate_kernel, out_shape=(part, part), in_specs=[VM] * 4, out_specs=(VM, VM), name="rotate",
    )(spread(o), spread(o ^ 1), mine, theirs)
    keep = keep + swap(send, 2, 4)
    cut = slots // 4
    own = keep[cut:] + swap(keep[:cut], 4, 2)
    other = swap(own[: cut - BLK // 2], 1, 1)

    decay = decay_np()
    log_r = jnp.asarray(np.log(decay), f32)[:, None, :]
    p = jnp.arange(planes, dtype=f32)[None, :, None]
    place = planes * g.astype(f32) + p + 1.0
    left = 1.0 - jnp.exp(2.0 * place * log_r)
    right = 1.0 - jnp.exp(2.0 * (size_x + 1.0 - place) * log_r)
    scale = jnp.asarray(COUPLING * decay / ((1 - decay**2) * (1 - decay ** (2 * size_x + 2))), f32)[:, None, :]
    k_left, k_right = scale * right, scale * left
    in_left = (k_left * jnp.exp((p + 1.0) * log_r)).reshape(-1, LANES)
    in_right = (k_right * jnp.exp((planes - p) * log_r)).reshape(-1, LANES)
    left, right, k_left, k_right = (v.reshape(-1, LANES) for v in (left, right, k_left, k_right))
    spread_decay = jnp.asarray(np.repeat(decay, SUB, axis=0), f32)
    slab = jnp.asarray(decay**planes, f32)

    y_hi, y_lo = halves_np(y_table())
    z_hi, z_lo = halves_np(z_table())
    zt_hi, zt_lo = halves_np(z_table().T)
    where = jnp.stack([core, g]).astype(jnp.int32)
    tile = tile_list[chip]
    flags = lax.dynamic_slice(
        pair_mask, (BLK * tile[0] + (BLK // 2) * core, BLK * tile[1]), (BLK // 2, BLK)
    ).astype(f32).reshape(-1)

    solved = []
    for u in range(BLK // 2):
        lines = jax.ShapeDtypeStruct((NY, 2 * LANES), f32)
        cube = (NY * SUB, 2 * LANES)
        local, *messages = pl.pallas_call(
            functools.partial(forward_kernel, u),
            out_shape=[jax.ShapeDtypeStruct(cube, f32)] + [lines] * (n_grid - 1),
            in_specs=[SM] + [VM] * 11,
            out_specs=[VM] * n_grid,
            scratch_shapes=[pltpu.VMEM((width // LANES * SUB, BLK * LANES), f32), pltpu.VMEM(cube, f32)]
            + [pltpu.VMEM((BLK // 2, NY * SUB, LANES), f32)] * 2,
            name=f"forward_{u}",
        )(where, own, other, y_hi, y_lo, z_hi, z_lo, spread_decay, left, right, k_left, k_right)
        solved.append((local, [cross(m, k) for k, m in enumerate(messages, 1)]))

    terms = []
    for u, (local, received) in enumerate(solved):
        terms.append(pl.pallas_call(
            functools.partial(backward_kernel, u),
            out_shape=jax.ShapeDtypeStruct((planes, width), f32),
            in_specs=[SM, SM] + [VM] * (9 + n_grid),
            out_specs=VM,
            scratch_shapes=[pltpu.VMEM(cube, f32), pltpu.VMEM((width // LANES * SUB, BLK * LANES), f32)],
            name=f"backward_{u}",
        )(where, flags, own, other, y_hi, y_lo, zt_hi, zt_lo, local, in_left, in_right, slab, *received))

    term = jnp.stack(terms)
    near_1 = swap(term, 2, 4)
    near_2 = swap(term, 4, 2)
    far = swap(near_1, 4, 2)
    own_parts = [term, near_1, near_2, far]
    sib_parts = [swap(v, 1, 1) for v in own_parts]
    own_tiles = jnp.stack([chip, chip ^ bit_1, chip ^ bit_2, chip ^ 3])
    sib_tiles = jnp.stack([chip, chip ^ bit_2, chip ^ bit_1, chip ^ 3])
    home = tile_list[:, 0][jnp.stack([own_tiles, sib_tiles])]
    base = o * (per_device // BLK) + jnp.arange(per_device // BLK)
    match = (base[:, None, None] == home[None]).astype(f32).reshape(-1)
    chunk = width // 4
    spec = pl.BlockSpec((BLK // 2, planes, chunk), lambda i: (0, 0, i))
    return pl.pallas_call(
        place_kernel,
        out_shape=jax.ShapeDtypeStruct(orbitals.shape, f32),
        grid=(width // chunk,),
        in_specs=[SM] + [spec] * 8,
        out_specs=pl.BlockSpec((per_device, planes, chunk), lambda i: (0, 0, i)),
        name="place",
    )(match, *own_parts, *sib_parts)


def sine_table(length):
    wave_index = jnp.arange(length, dtype=f32) + 1.0
    return jnp.sqrt(2.0 / (length + 1.0)) * jnp.sin(
        jnp.pi * wave_index[:, None] * wave_index[None, :] / (length + 1.0)
    )


def eigen_values(length):
    wave_index = jnp.arange(length, dtype=f32) + 1.0
    return 2.0 - 2.0 * jnp.cos(jnp.pi * wave_index / (length + 1.0))


def green_kernel(size_x, size_y, size_z):
    summed = (
        eigen_values(size_x)[:, None, None]
        + eigen_values(size_y)[None, :, None]
        + eigen_values(size_z)[None, None, :]
    )
    return COUPLING / (summed + SCREENING)


def pair_lists(tile_list, pair_mask):
    within = jnp.arange(BLK * BLK, dtype=jnp.int32)
    targets = (BLK * tile_list[:, 0:1] + within[None, :] // BLK).reshape(-1)
    sources = (BLK * tile_list[:, 1:2] + within[None, :] % BLK).reshape(-1)
    return (targets, sources, pair_mask[targets, sources])


def compact(targets, sources, live_flags, number):
    ranking = jnp.cumsum(live_flags) - 1
    places = jnp.where(live_flags == 1, ranking, number)
    picked = (
        jnp.zeros((number,), jnp.int32)
        .at[places]
        .set(jnp.arange(live_flags.shape[0], dtype=jnp.int32), mode="drop")
    )
    return (targets[picked], sources[picked])


def along_z(values, matrix):
    number, planes, width_yz = values.shape
    size_z = matrix.shape[0]
    shaped = values.reshape(number, planes, width_yz // size_z, size_z)
    return jnp.einsum("pxrz,zk->pxrk", shaped, matrix, precision=precise).reshape(number, planes, width_yz)


def along_y(values, matrix):
    number, planes, width_yz = values.shape
    size_y = matrix.shape[0]
    shaped = values.reshape(number, planes, size_y, width_yz // size_y)
    return jnp.einsum("pxyz,yk->pxkz", shaped, matrix, precision=precise).reshape(number, planes, width_yz)


def along_x(values, matrix):
    return jnp.einsum("pxc,xk->pkc", values, matrix, precision=precise)


def any_device(orbitals, rotation, tile_list, pair_mask):
    n_orb, n_grid = lax.axis_size("orb"), lax.axis_size("grid")
    number_orbitals, size_x = rotation.shape[0], orbitals.shape[1] * n_grid
    rotated = jnp.einsum(
        "ij,ixc->jxc",
        rotation,
        lax.all_to_all(orbitals, "orb", split_axis=2, concat_axis=0, tiled=True),
        precision=precise,
    )
    planes, width_yz = rotated.shape[1:]
    targets, sources, live_flags = pair_lists(tile_list, pair_mask)
    matrix_x, matrix_y, matrix_z = sine_table(size_x), sine_table(NY), sine_table(NZ)
    kernel = green_kernel(size_x, NY, NZ).reshape(size_x, NY * NZ)
    orbital_ids = jnp.arange(number_orbitals, dtype=jnp.int32)
    targets, sources = compact(targets, sources, live_flags, targets.shape[0] // 2)
    density = rotated[targets] * rotated[sources]
    number = density.shape[0]
    spectrum = along_z(density, matrix_z)
    spectrum = lax.all_to_all(spectrum, "orb", split_axis=0, concat_axis=2, tiled=True)
    spectrum = along_y(spectrum, matrix_y)
    spectrum = lax.all_to_all(spectrum, "grid", split_axis=0, concat_axis=1, tiled=True)
    spectrum = along_x(along_x(spectrum, matrix_x) * kernel, matrix_x)
    spectrum = lax.all_to_all(spectrum, "grid", split_axis=1, concat_axis=0, tiled=True)
    spectrum = along_y(spectrum, matrix_y)
    spectrum = lax.all_to_all(spectrum, "orb", split_axis=2, concat_axis=0, tiled=True)
    potential = along_z(spectrum, matrix_z)
    products = potential * rotated[sources]
    selector = (targets[None, :] == orbital_ids[:, None]).astype(f32)
    partial_value = -jnp.dot(selector, products.reshape(number, planes * width_yz), precision=precise)
    partial_value = partial_value.reshape(number_orbitals, planes, width_yz)
    return lax.all_to_all(partial_value, "orb", split_axis=0, concat_axis=2, tiled=True)


def solution(mesh):
    n_orb, n_grid = mesh.shape["orb"], mesh.shape["grid"]

    def on_device(orbitals, rotation, tile_list, pair_mask):
        per_device, planes, width = orbitals.shape
        fits = n_orb == 8 and 2 * tile_list.shape[0] == n_orb and planes == SUB and per_device % BLK == 0
        fits = fits and width == NY * NZ and 2 * NZ == LANES and n_grid in (2, 4, 8)
        body = tile_device if fits else any_device
        return body(orbitals, rotation, tile_list, pair_mask)

    in_specs = (P("orb", "grid", None), P(), P(), P())
    out_specs = P("orb", "grid", None)
    return jax.shard_map(on_device, mesh=mesh, in_specs=in_specs, out_specs=out_specs, check_vma=False)
```

```python
import functools
import itertools

import jax
import jax.numpy as jnp
import numpy as np
from jax import lax
from jax.experimental import pallas as pl
from jax.experimental.pallas import tpu as pltpu
from jax.sharding import PartitionSpec as P

BLK = 4
NY = 64
NZ = 64
LANES = 128
SUB = 8
CHUNKS = 2
COUPLING = 0.25
SCREENING = 0.1

precise = lax.Precision.HIGHEST
f32 = jnp.float32
bf16 = jnp.bfloat16

VM = pl.BlockSpec(memory_space=pltpu.VMEM)
SM = pl.BlockSpec(memory_space=pltpu.SMEM)
ANY = pl.BlockSpec(memory_space=pl.ANY)
DMA = pltpu.SemaphoreType.DMA


def grant(mib):
    return pltpu.CompilerParams(vmem_limit_bytes=mib << 20)


def sine_np(n):
    k = np.arange(1, n + 1, dtype=np.float64)
    return np.sqrt(2.0 / (n + 1)) * np.sin(np.pi * k[:, None] * k[None, :] / (n + 1))


def eigen_np(n):
    k = np.arange(1, n + 1, dtype=np.float64)
    return 2.0 - 2.0 * np.cos(np.pi * k / (n + 1))


def halves_np(table):
    high = np.asarray(table, np.float32).astype(jnp.bfloat16)
    low = (np.asarray(table, np.float64) - high.astype(np.float64)).astype(jnp.bfloat16)
    return jnp.asarray(high), jnp.asarray(low)


def y_order():
    rows = LANES // NZ
    return np.arange(NY).reshape(NY // rows, rows).T.reshape(-1)


def y_table():
    order = y_order()
    return np.kron(sine_np(NY)[order][:, order], sine_np(SUB))


def z_table():
    half = LANES // NZ
    sine = sine_np(NZ)
    table = np.zeros((2, half, NZ, half, 2, NZ))
    for pair in range(2):
        for h in range(half):
            table[pair, h, :, h, pair, :] = sine
    return table.reshape(2 * half * NZ, half * 2 * NZ)


def line_np():
    c = eigen_np(NY)[y_order()][:, None] + eigen_np(NZ)[None, :] + SCREENING
    c = np.concatenate([c, c], axis=1)
    return c, 2.0 / (2.0 + c + np.sqrt(c * (c + 4.0)))


def host_np(chips):
    table = np.zeros((chips**chips, chips), np.int32)
    for owners in itertools.product(range(chips), repeat=chips):
        best = None
        for tiles in itertools.permutations(range(chips)):
            hops = [bin(chip ^ owners[tile]).count("1") for chip, tile in enumerate(tiles)]
            cost = (max(hops), sum(hops))
            if best is None or cost < best[0]:
                best = (cost, tiles)
        table[sum(own * chips**t for t, own in enumerate(owners))] = best[1]
    return table


def dot(a, b):
    return jnp.dot(a, b, preferred_element_type=f32)


def split(x):
    high = x.astype(bf16)
    return high, (x - high.astype(f32)).astype(bf16)


def dot3(a, b):
    return dot(a[0], b[0]) + dot(a[0], b[1]) + dot(a[1], b[0])


def my_core():
    return lax.rem(lax.axis_index("orb"), 2)


def take_kernel(flip, start, source, out, sem):
    core = my_core()
    side = 1 - core if flip else core
    at = pl.multiple_of(side * (source.shape[2] // 2) + start, LANES)
    copy = pltpu.make_async_copy(source.at[:, :, pl.ds(at, out.shape[2])], out, sem)
    copy.start()
    copy.wait()


def rotate_kernel(table, mine, theirs, send, keep):
    rows, width = send.shape[0] * SUB, send.shape[2]
    high, low = split(table[...])
    step = 2 * LANES
    for at in range(0, width, step):
        lanes = slice(at, at + step)
        depth = mine.shape[0] * SUB
        cells = jnp.concatenate([mine[:, :, lanes].reshape(depth, step), theirs[:, :, lanes].reshape(depth, step)])
        total = dot3((high, low), split(cells))
        send[:, :, lanes] = total[:rows].reshape(send.shape[0], SUB, step)
        keep[:, :, lanes] = total[rows:].reshape(keep.shape[0], SUB, step)


def sub_sums(values):
    row = lax.broadcasted_iota(jnp.int32, values[0].shape, 0)
    for s in (4, 2):
        low = (row & s) == 0
        paired = []
        for n in range(s):
            a, b = values[n], values[n + s]
            paired.append(jnp.where(low, a, pltpu.roll(b, s, 0)) + jnp.where(low, pltpu.roll(a, SUB - s, 0), b))
        values = paired
    even = (row & 1) == 0
    a, b = values
    return jnp.where(even, a, pltpu.roll(b, 1, 0)), jnp.where(even, pltpu.roll(a, SUB - 1, 0), b)


def forward_kernel(u, *refs):
    own, other = refs[:CHUNKS], refs[CHUNKS:2 * CHUNKS]
    y_hi, y_lo, z_hi, z_lo, ends, powers, spectrum, a_out, b_out = refs[2 * CHUNKS:2 * CHUNKS + 9]
    messages, (dens,) = refs[2 * CHUNKS + 9:-1], refs[-1:]
    core, g = my_core(), lax.axis_index("grid")
    tiles = own[0].shape[2] // LANES
    for side, group, source, target in ((0, own, BLK // 2, BLK // 2 + BLK + u), (1, other, 2, u)):
        half = (core if side == 0 else 1 - core) * (CHUNKS * tiles * SUB)
        for n, ref in enumerate(group):
            for t in range(tiles):
                lanes = pl.ds(t * LANES, LANES)
                value = ref[target, :, lanes]
                rows = pl.ds(pl.multiple_of(half + (n * tiles + t) * SUB, SUB), SUB)
                for w in range(BLK):
                    dens[rows, w * LANES:(w + 1) * LANES] = value * ref[source + w, :, lanes]
    z = (z_hi[...], z_lo[...])
    half = dens.shape[0]
    for q in range(BLK // 2):
        out = dot3(split(dens[:, q * 2 * LANES:(q + 1) * 2 * LANES]), z)
        spectrum[:half, q * LANES:(q + 1) * LANES] = out[:, :LANES]
        spectrum[half:, q * LANES:(q + 1) * LANES] = out[:, LANES:]
    spectrum[...] = dot3((y_hi[...], y_lo[...]), split(spectrum[...]))

    def reduce(group, carry):
        lines = pl.ds(pl.multiple_of(group * SUB, SUB), SUB)
        near, far = powers[0, lines, :], powers[1, lines, :]
        for q in range(BLK // 2):
            lanes = slice(q * LANES, (q + 1) * LANES)
            values = []
            for k in range(SUB):
                rows = pl.ds(pl.multiple_of((group * SUB + k) * SUB, SUB), SUB)
                values.append(ends[rows, :] * spectrum[rows, lanes])
            even, odd = sub_sums(values)
            rightward = (even + odd) - near * (even - odd)
            leftward = (even - odd) - far * (even + odd)
            a_out[lines, lanes] = rightward
            b_out[lines, lanes] = leftward
            for k, out in enumerate(messages, 1):
                out[lines, lanes] = jnp.where((g ^ k) > g, rightward, leftward)
        return carry

    lax.fori_loop(0, NY // SUB, reduce, 0)


def backward_kernel(u, flags, *refs):
    own, other = refs[:CHUNKS], refs[CHUNKS:2 * CHUNKS]
    (y_hi, y_lo, z_hi, z_lo, inverse, basis, powers, steady, spectrum, a_in, b_in) = refs[2 * CHUNKS:2 * CHUNKS + 11]
    received, (out, work, pot) = refs[2 * CHUNKS + 11:-3], refs[-3:]
    core, g = my_core(), lax.axis_index("grid")
    tiles = own[0].shape[2] // LANES
    first, last = basis[0], basis[1]

    def ends(group, carry):
        lines = pl.ds(pl.multiple_of(group * SUB, SUB), SUB)
        scale, r, slab = steady[0, lines, :], steady[1, lines, :], steady[2, lines, :]
        decays = [None, jnp.ones((SUB, LANES), f32), slab]
        while len(decays) <= len(received):
            decays.append(decays[-1] * slab)
        for q in range(BLK // 2):
            lanes = slice(q * LANES, (q + 1) * LANES)
            from_left = from_right = jnp.zeros((SUB, LANES), f32)
            for n, ref in enumerate(received, 1):
                distance = jnp.abs((g ^ n) - g)
                factor = decays[n]
                for d in range(1, n):
                    factor = jnp.where(distance == d, decays[d], factor)
                value = factor * ref[lines, lanes]
                is_left = (g ^ n) < g
                from_left = from_left + jnp.where(is_left, value, 0.0)
                from_right = from_right + jnp.where(is_left, 0.0, value)
            before = scale * (powers[2, lines, :] * from_left
                              + r * powers[3, lines, :] * (b_in[lines, lanes] + slab * from_right))
            after = scale * (powers[4, lines, :] * from_right
                             + r * powers[5, lines, :] * (a_in[lines, lanes] + slab * from_left))
            for k in range(SUB):
                rows = pl.ds(pl.multiple_of((group * SUB + k) * SUB, SUB), SUB)
                edge = first * before[k:k + 1] + last * after[k:k + 1]
                work[rows, lanes] = inverse[rows, :] * (spectrum[rows, lanes] + edge)
        return carry

    lax.fori_loop(0, NY // SUB, ends, 0)
    work[...] = dot3((y_hi[...], y_lo[...]), split(work[...]))
    z = (z_hi[...], z_lo[...])
    half = pot.shape[0]
    for q in range(BLK // 2):
        lanes = slice(q * LANES, (q + 1) * LANES)
        rows = jnp.concatenate([work[:half, lanes], work[half:, lanes]], axis=1)
        pot[:, q * 2 * LANES:(q + 1) * 2 * LANES] = dot3(split(rows), z)
    for side, group, source in ((0, own, BLK // 2), (1, other, 2)):
        half = (core if side == 0 else 1 - core) * (CHUNKS * tiles)
        for n, ref in enumerate(group):
            for t in range(tiles):
                lanes = pl.ds(t * LANES, LANES)
                at = half + n * tiles + t
                rows = pl.ds(pl.multiple_of(at * SUB, SUB), SUB)
                total = None
                for w in range(BLK):
                    term = flags[u * BLK + w] * (pot[rows, w * LANES:(w + 1) * LANES] * ref[source + w, :, lanes])
                    total = term if total is None else total + term
                out[:, pl.ds(pl.multiple_of(at * LANES, LANES), LANES)] = -total


def place_kernel(match, *refs):
    parts, (out, rows, sem) = refs[:-4], refs[-3:]
    blocks, count = out.shape[0] // BLK, len(parts)
    pair = BLK // 2
    core = my_core()

    def found(b, side):
        total = 0
        for n in range(side * count // 2, (side + 1) * count // 2):
            total = total + match[b * count + n]
        return total > 0

    def move(b, side):
        which = core if side == 0 else 1 - core
        at = b * BLK + which * pair
        return pltpu.make_async_copy(rows.at[b, side], out.at[pl.ds(at, pair)], sem.at[b, side])

    for b in range(blocks):
        for side in range(2):

            @pl.when(found(b, side))
            def _():
                rows[b, side] = jnp.zeros(rows.shape[2:], f32)
                for n in range(side * count // 2, (side + 1) * count // 2):

                    @pl.when(match[b * count + n] > 0)
                    def _():
                        rows[b, side] += parts[n][...].reshape(rows.shape[2:])

                move(b, side).start()

    for b in range(blocks):
        for side in range(2):

            @pl.when(found(b, side))
            def _():
                move(b, side).wait()


def tile_device(orbitals, rotation, tile_list, pair_mask):
    per_device, planes, width = orbitals.shape
    n_orb, n_grid = lax.axis_size("orb"), lax.axis_size("grid")
    size_x = planes * n_grid
    half = width // 2
    chips = n_orb // 2
    axes = ("orb", "grid")
    o, g = lax.axis_index("orb"), lax.axis_index("grid")
    core, chip = o % 2, o // 2

    def swap(x, even, odd):
        moves = []
        for a in range(n_orb):
            flip = even if a % 2 == 0 else odd
            moves += [(a * n_grid + b, (a ^ flip) * n_grid + b) for b in range(n_grid)]
        return lax.ppermute(x, axes, moves)

    def cross(x, k):
        moves = [(a * n_grid + b, a * n_grid + (b ^ k)) for a in range(n_orb) for b in range(n_grid)]
        return lax.ppermute(x, axes, moves)

    chunk = half // CHUNKS

    def take(flip, start, lanes):
        return pl.pallas_call(
            functools.partial(take_kernel, flip, start),
            out_shape=jax.ShapeDtypeStruct((per_device, planes, lanes), f32),
            in_specs=[ANY], out_specs=VM, scratch_shapes=[DMA], name=f"take_{flip}_{start}",
            compiler_params=grant(8),
        )(orbitals)

    theirs = [swap(take(True, n * chunk, chunk), 1, 1) for n in range(CHUNKS)]
    mine = [take(False, n * chunk, chunk) for n in range(CHUNKS)]

    owner = tile_list[:, 0] * BLK // (2 * per_device)
    key = jnp.sum(owner * (chips ** jnp.arange(chips)))
    hosted = lax.dynamic_index_in_dim(jnp.asarray(host_np(chips)), key, 0, keepdims=False)

    bit_1 = jnp.where(core == 0, 1, 2)
    bit_2 = 3 - bit_1
    order = jnp.stack([chip ^ 3, chip ^ bit_1, chip ^ bit_2, chip])
    blocks = tile_list[hosted[order]]
    pick = jnp.arange(BLK // 2)
    wanted = jnp.concatenate(
        [
            BLK * blocks[:, 0:1] + (BLK // 2) * (1 - core) + pick,
            BLK * blocks[:, 1:2] + jnp.arange(BLK),
            BLK * blocks[:, 0:1] + (BLK // 2) * core + pick,
        ],
        axis=1,
    ).reshape(-1)
    chosen = (jnp.repeat(wanted, SUB)[:, None] == jnp.arange(rotation.shape[1])[None, :]).astype(f32)
    picked = jnp.einsum("rj,ij->ri", chosen, rotation, precision=precise)
    column = jnp.arange(2 * per_device * SUB)
    source = (o ^ (column // (per_device * SUB))) * per_device + column // SUB % per_device
    columns = (jnp.arange(rotation.shape[0])[:, None] == source[None, :]).astype(f32)
    same_plane = jnp.arange(chosen.shape[0])[:, None] % SUB == column[None, :] % SUB
    table = jnp.where(same_plane, jnp.einsum("ri,ic->rc", picked, columns, precision=precise), 0.0)

    slots = wanted.shape[0]
    cut = slots // 4
    part = jax.ShapeDtypeStruct((slots // 2, planes, chunk), f32)
    own, other = [], []
    sums = []
    for n in range(CHUNKS):
        send, keep = pl.pallas_call(
            rotate_kernel, out_shape=(part, part), in_specs=[VM] * 3, out_specs=(VM, VM), name=f"rotate_{n}",
            compiler_params=grant(16),
        )(table, mine[n], theirs[n])
        sums.append((keep, swap(send, 2, 4)))
    for keep, got in sums:
        passed = swap(keep[:cut] + got[:cut], 4, 2)
        own.append(keep[cut:] + got[cut:] + passed)
        other.append(swap(own[-1][: cut - BLK // 2], 1, 1))

    c, r = line_np()
    sine_x, eigen_x = sine_np(planes), eigen_np(planes)
    ends = jnp.asarray(np.einsum("jp,pkl->kjl", sine_x, r[None] ** np.arange(planes - 1, -1, -1)[:, None, None])
                       .reshape(-1, LANES), f32)
    inverse = jnp.asarray((COUPLING / (eigen_x[None, :, None] + c[:, None, :])).reshape(-1, LANES), f32)
    basis = jnp.asarray(np.broadcast_to(sine_x[:, [0, -1]].T[:, :, None], (2, planes, LANES)), f32)
    steady = jnp.asarray(np.stack([r / ((1 - r**2) * (1 - r ** (2 * size_x + 2))), r, r**planes]), f32)
    at = planes * g
    exponents = jnp.stack([
        2 * at + planes + 1,
        2 * size_x + 1 - planes - 2 * at,
        2 * size_x + 2 - 2 * at,
        2 * at,
        2 * at + 2 * planes + 2,
        2 * size_x - 2 * planes - 2 * at,
    ]).astype(f32)
    powers = jnp.exp(exponents[:, None, None] * jnp.asarray(np.log(r), f32)[None])
    powers = jnp.where(jnp.arange(6)[:, None, None] < 2, powers, 1.0 - powers)

    y_hi, y_lo = halves_np(y_table())
    z_hi, z_lo = halves_np(z_table())
    zt_hi, zt_lo = halves_np(z_table().T)
    tile = tile_list[hosted[chip]]
    flags = lax.dynamic_slice(
        pair_mask, (BLK * tile[0] + (BLK // 2) * core, BLK * tile[1]), (BLK // 2, BLK)
    ).astype(f32).reshape(-1)

    solved = []
    lines = jax.ShapeDtypeStruct((NY, 2 * LANES), f32)
    cube = (NY * SUB, 2 * LANES)
    wide = pltpu.VMEM((width // LANES * SUB, BLK * LANES), f32)
    for u in range(BLK // 2):
        spectrum, a, b, *messages = pl.pallas_call(
            functools.partial(forward_kernel, u),
            out_shape=[jax.ShapeDtypeStruct(cube, f32)] + [lines] * (n_grid + 1),
            in_specs=[VM] * (2 * CHUNKS + 6),
            out_specs=[VM] * (n_grid + 2),
            scratch_shapes=[wide],
            name=f"forward_{u}",
            compiler_params=grant(24),
        )(*own, *other, y_hi, y_lo, z_hi, z_lo, ends, powers)
        solved.append((spectrum, a, b, *(cross(m, k) for k, m in enumerate(messages, 1))))

    terms = []
    for u, fields in enumerate(solved):
        terms.append(pl.pallas_call(
            functools.partial(backward_kernel, u),
            out_shape=jax.ShapeDtypeStruct((planes, width), f32),
            in_specs=[SM] + [VM] * (2 * CHUNKS + 8 + len(fields)),
            out_specs=VM,
            scratch_shapes=[pltpu.VMEM(cube, f32), wide],
            name=f"backward_{u}",
            compiler_params=grant(24),
        )(flags, *own, *other, y_hi, y_lo, zt_hi, zt_lo, inverse, basis, powers, steady, *fields))

    term = jnp.stack(terms)
    near_1 = swap(term, 2, 4)
    near_2 = swap(term, 4, 2)

    def distant(x):
        far = swap(x, 4, 2)
        return far, swap(far, 1, 1)

    def nothing(x):
        return jnp.zeros_like(x), jnp.zeros_like(x)

    all_one = jnp.all(owner == owner[0])
    far, far_sib = lax.cond(all_one, distant, nothing, near_1)
    own_parts = [term, near_1, near_2, far]
    sib_parts = [swap(v, 1, 1) for v in own_parts[:3]] + [far_sib]
    own_chips = jnp.stack([chip, chip ^ bit_1, chip ^ bit_2, chip ^ 3])
    sib_chips = jnp.stack([chip, chip ^ bit_2, chip ^ bit_1, chip ^ 3])
    home = tile_list[:, 0][hosted[jnp.concatenate([own_chips, sib_chips])]]
    base = o * (per_device // BLK) + jnp.arange(per_device // BLK)
    match = (base[:, None] == home[None]).astype(jnp.int32)
    distant_parts = jnp.arange(8) % 4 == 3
    match = jnp.where(distant_parts[None] & ~all_one, 0, match).reshape(-1)
    empty = jnp.zeros(orbitals.shape, f32)
    return pl.pallas_call(
        place_kernel,
        out_shape=jax.ShapeDtypeStruct(orbitals.shape, f32),
        in_specs=[SM] + [VM] * 8 + [ANY],
        out_specs=ANY,
        input_output_aliases={9: 0},
        scratch_shapes=[pltpu.VMEM((per_device // BLK, 2, BLK // 2, planes, width), f32), DMA((per_device // BLK, 2))],
        name="place",
        compiler_params=grant(16),
    )(match, *own_parts, *sib_parts, empty)


def sine_table(length):
    wave_index = jnp.arange(length, dtype=f32) + 1.0
    return jnp.sqrt(2.0 / (length + 1.0)) * jnp.sin(
        jnp.pi * wave_index[:, None] * wave_index[None, :] / (length + 1.0)
    )


def eigen_values(length):
    wave_index = jnp.arange(length, dtype=f32) + 1.0
    return 2.0 - 2.0 * jnp.cos(jnp.pi * wave_index / (length + 1.0))


def green_kernel(size_x, size_y, size_z):
    summed = (
        eigen_values(size_x)[:, None, None]
        + eigen_values(size_y)[None, :, None]
        + eigen_values(size_z)[None, None, :]
    )
    return COUPLING / (summed + SCREENING)


def pair_lists(tile_list, pair_mask):
    within = jnp.arange(BLK * BLK, dtype=jnp.int32)
    targets = (BLK * tile_list[:, 0:1] + within[None, :] // BLK).reshape(-1)
    sources = (BLK * tile_list[:, 1:2] + within[None, :] % BLK).reshape(-1)
    return (targets, sources, pair_mask[targets, sources])


def compact(targets, sources, live_flags, number):
    ranking = jnp.cumsum(live_flags) - 1
    places = jnp.where(live_flags == 1, ranking, number)
    picked = (
        jnp.zeros((number,), jnp.int32)
        .at[places]
        .set(jnp.arange(live_flags.shape[0], dtype=jnp.int32), mode="drop")
    )
    return (targets[picked], sources[picked])


def along_z(values, matrix):
    number, planes, width_yz = values.shape
    size_z = matrix.shape[0]
    shaped = values.reshape(number, planes, width_yz // size_z, size_z)
    return jnp.einsum("pxrz,zk->pxrk", shaped, matrix, precision=precise).reshape(number, planes, width_yz)


def along_y(values, matrix):
    number, planes, width_yz = values.shape
    size_y = matrix.shape[0]
    shaped = values.reshape(number, planes, size_y, width_yz // size_y)
    return jnp.einsum("pxyz,yk->pxkz", shaped, matrix, precision=precise).reshape(number, planes, width_yz)


def along_x(values, matrix):
    return jnp.einsum("pxc,xk->pkc", values, matrix, precision=precise)


def any_device(orbitals, rotation, tile_list, pair_mask):
    n_orb, n_grid = lax.axis_size("orb"), lax.axis_size("grid")
    number_orbitals, size_x = rotation.shape[0], orbitals.shape[1] * n_grid
    rotated = jnp.einsum(
        "ij,ixc->jxc",
        rotation,
        lax.all_to_all(orbitals, "orb", split_axis=2, concat_axis=0, tiled=True),
        precision=precise,
    )
    planes, width_yz = rotated.shape[1:]
    targets, sources, live_flags = pair_lists(tile_list, pair_mask)
    matrix_x, matrix_y, matrix_z = sine_table(size_x), sine_table(NY), sine_table(NZ)
    kernel = green_kernel(size_x, NY, NZ).reshape(size_x, NY * NZ)
    orbital_ids = jnp.arange(number_orbitals, dtype=jnp.int32)
    targets, sources = compact(targets, sources, live_flags, targets.shape[0] // 2)
    density = rotated[targets] * rotated[sources]
    number = density.shape[0]
    spectrum = along_z(density, matrix_z)
    spectrum = lax.all_to_all(spectrum, "orb", split_axis=0, concat_axis=2, tiled=True)
    spectrum = along_y(spectrum, matrix_y)
    spectrum = lax.all_to_all(spectrum, "grid", split_axis=0, concat_axis=1, tiled=True)
    spectrum = along_x(along_x(spectrum, matrix_x) * kernel, matrix_x)
    spectrum = lax.all_to_all(spectrum, "grid", split_axis=1, concat_axis=0, tiled=True)
    spectrum = along_y(spectrum, matrix_y)
    spectrum = lax.all_to_all(spectrum, "orb", split_axis=2, concat_axis=0, tiled=True)
    potential = along_z(spectrum, matrix_z)
    products = potential * rotated[sources]
    selector = (targets[None, :] == orbital_ids[:, None]).astype(f32)
    partial_value = -jnp.dot(selector, products.reshape(number, planes * width_yz), precision=precise)
    partial_value = partial_value.reshape(number_orbitals, planes, width_yz)
    return lax.all_to_all(partial_value, "orb", split_axis=0, concat_axis=2, tiled=True)


def solution(mesh):
    n_orb, n_grid = mesh.shape["orb"], mesh.shape["grid"]

    def on_device(orbitals, rotation, tile_list, pair_mask):
        per_device, planes, width = orbitals.shape
        fits = n_orb == 8 and 2 * tile_list.shape[0] == n_orb and planes == SUB and per_device % BLK == 0
        fits = fits and width == NY * NZ and 2 * NZ == LANES and n_grid in (2, 4, 8)
        body = tile_device if fits else any_device
        return body(orbitals, rotation, tile_list, pair_mask)

    in_specs = (P("orb", "grid", None), P(), P(), P())
    out_specs = P("orb", "grid", None)
    return jax.shard_map(on_device, mesh=mesh, in_specs=in_specs, out_specs=out_specs, check_vma=False)
```

```python
import functools
import itertools

import jax
import jax.numpy as jnp
import numpy as np
from jax import lax
from jax.experimental import pallas as pl
from jax.experimental.pallas import tpu as pltpu
from jax.sharding import PartitionSpec as P

BLK = 4
NY = 64
NZ = 64
LANES = 128
SUB = 8
CHUNKS = 2
COUPLING = 0.25
SCREENING = 0.1

precise = lax.Precision.HIGHEST
f32 = jnp.float32
bf16 = jnp.bfloat16

VM = pl.BlockSpec(memory_space=pltpu.VMEM)
SM = pl.BlockSpec(memory_space=pltpu.SMEM)
ANY = pl.BlockSpec(memory_space=pl.ANY)
HBM = pl.BlockSpec(memory_space=pltpu.HBM)
DMA = pltpu.SemaphoreType.DMA


def grant(mib):
    return pltpu.CompilerParams(vmem_limit_bytes=mib << 20)


def sine_np(n):
    k = np.arange(1, n + 1, dtype=np.float64)
    return np.sqrt(2.0 / (n + 1)) * np.sin(np.pi * k[:, None] * k[None, :] / (n + 1))


def eigen_np(n):
    k = np.arange(1, n + 1, dtype=np.float64)
    return 2.0 - 2.0 * np.cos(np.pi * k / (n + 1))


def halves_np(table):
    high = np.asarray(table, np.float32).astype(jnp.bfloat16)
    low = (np.asarray(table, np.float64) - high.astype(np.float64)).astype(jnp.bfloat16)
    return jnp.asarray(high), jnp.asarray(low)


def y_order():
    rows = LANES // NZ
    return np.arange(NY).reshape(NY // rows, rows).T.reshape(-1)


def y_table():
    order = y_order()
    return np.kron(sine_np(NY)[order][:, order], sine_np(SUB))


def z_table():
    half = LANES // NZ
    sine = sine_np(NZ)
    table = np.zeros((2, half, NZ, half, 2, NZ))
    for pair in range(2):
        for h in range(half):
            table[pair, h, :, h, pair, :] = sine
    return table.reshape(2 * half * NZ, half * 2 * NZ)


def line_np():
    c = eigen_np(NY)[y_order()][:, None] + eigen_np(NZ)[None, :] + SCREENING
    c = np.concatenate([c, c], axis=1)
    return c, 2.0 / (2.0 + c + np.sqrt(c * (c + 4.0)))


def host_np(chips):
    table = np.zeros((chips**chips, chips), np.int32)
    for owners in itertools.product(range(chips), repeat=chips):
        best = None
        for tiles in itertools.permutations(range(chips)):
            hops = [bin(chip ^ owners[tile]).count("1") for chip, tile in enumerate(tiles)]
            cost = (max(hops), sum(hops))
            if best is None or cost < best[0]:
                best = (cost, tiles)
        table[sum(own * chips**t for t, own in enumerate(owners))] = best[1]
    return table


def dot(a, b):
    return jnp.dot(a, b, preferred_element_type=f32)


def split(x):
    high = x.astype(bf16)
    return high, (x - high.astype(f32)).astype(bf16)


def dot3(a, b):
    return dot(a[0], b[0]) + dot(a[0], b[1]) + dot(a[1], b[0])


def my_core():
    return lax.rem(lax.axis_index("orb"), 2)


def my_place():
    o = lax.axis_index("orb")
    return o, lax.rem(o, 2), lax.div(o, 2)


def take_kernel(flip, start, source, *rest):
    out, sem = rest[-2:]
    core = my_core()
    side = 1 - core if flip else core
    at = pl.multiple_of(side * (source.shape[2] // 2) + start, LANES)
    copy = pltpu.make_async_copy(source.at[:, :, pl.ds(at, out.shape[2])], out, sem)
    copy.start()
    copy.wait()


def setup_kernel(per_device, tiles, host, rotation, mask, high, low, flags, match, alone):
    o, core, chip = my_place()
    chips = tiles.shape[0] // 2
    owners = [lax.div(tiles[2 * t] * BLK, 2 * per_device) for t in range(chips)]
    key = 0
    for t in range(chips):
        key = key + owners[t] * chips**t
    same = owners[0] == owners[1]
    for t in range(2, chips):
        same = same & (owners[t] == owners[0])
    alone[0] = same.astype(jnp.int32)
    bit_1 = jnp.where(core == 0, 1, 2)
    bit_2 = 3 - bit_1
    pair = BLK // 2
    order = [chip ^ 3, chip ^ bit_1, chip ^ bit_2, chip]
    heads = []
    for where in order:
        tile = host[key * chips + where]
        heads.append((BLK * tiles[2 * tile], BLK * tiles[2 * tile + 1]))
    wanted = []
    for a, b in heads:
        wanted += [a + (1 - core) * pair] + [b + w for w in range(BLK)] + [a + core * pair]
    for u in range(1, pair):
        for a, b in heads:
            wanted += [a + (1 - core) * pair + u, a + core * pair + u]
    lane = lax.broadcasted_iota(jnp.int32, (SUB, LANES), 1)
    chosen = jnp.concatenate([jnp.where(lane == n, 1.0, 0.0) for n in wanted]).astype(bf16)
    count = chosen.shape[0]
    row = lax.broadcasted_iota(jnp.int32, (LANES, LANES), 0)
    column = lax.broadcasted_iota(jnp.int32, (LANES, LANES), 1)
    columns = [
        jnp.where(row - (o ^ e) * per_device == jnp.right_shift(column, 3), 1.0, 0.0).astype(bf16)
        for e in range(2)
    ]
    keep = (lax.broadcasted_iota(jnp.int32, (count, LANES), 0) & (SUB - 1)) == (
        lax.broadcasted_iota(jnp.int32, (count, LANES), 1) & (SUB - 1)
    )
    for out, values in zip((high, low), split(rotation[...])):
        picked = lax.dot_general(chosen, values, (((1,), (1,)), ((), ())), preferred_element_type=f32).astype(bf16)
        for e in range(2):
            out[:, e * LANES:(e + 1) * LANES] = jnp.where(keep, dot(picked, columns[e]), 0.0).astype(bf16)
    a, b = heads[-1]
    live = mask[...].astype(f32)
    for u in range(pair):
        line = jnp.sum(jnp.where(row == a + core * pair + u, live, 0.0), axis=0, keepdims=True)
        for w in range(BLK):
            flags[u * BLK + w] = jnp.sum(jnp.where(column[:1] == b + w, line, 0.0))
    blocks = per_device // BLK
    parts = [chip, chip ^ bit_1, chip ^ bit_2, chip ^ 3, chip, chip ^ bit_2, chip ^ bit_1, chip ^ 3]
    for n, where in enumerate(parts):
        home = tiles[2 * host[key * chips + where]]
        for block in range(blocks):
            hit = home == o * blocks + block
            if n % 4 == 3:
                hit = hit & same
            match[block * len(parts) + n] = hit.astype(jnp.int32)


def rotate_kernel(first, high, low, *rest):
    send, keep = rest[-2:]
    rows = send.shape[0] * SUB
    part = pl.ds(first, 2 * rows)
    table = (high[part, :], low[part, :])
    at = 0
    step = 2 * LANES
    while at < send.shape[2]:
        width = rest[0].shape[2]
        n, inner = at // width, at % width
        lanes = slice(inner, inner + step)
        mine, theirs = rest[2 * n], rest[2 * n + 1]
        depth = mine.shape[0] * SUB
        cells = jnp.concatenate([mine[:, :, lanes].reshape(depth, step), theirs[:, :, lanes].reshape(depth, step)])
        total = dot3(table, split(cells))
        lanes = slice(at, at + step)
        send[:, :, lanes] = total[:rows].reshape(send.shape[0], SUB, step)
        keep[:, :, lanes] = total[rows:].reshape(keep.shape[0], SUB, step)
        at += step


def pass_kernel(keep, got, *rest):
    out = rest[-1]
    count = out.shape[0]
    out[...] = keep[:count] + got[:count]


def finish_kernel(keep, got, passed, *rest):
    out = rest[-1]
    count = out.shape[0]
    out[...] = keep[count:] + got[count:] + passed[...]


def clear_kernel(*refs):
    out, zeros, sem = refs[-3:]
    zeros[...] = jnp.zeros(zeros.shape, f32)
    step = zeros.shape[0]
    copies = [
        pltpu.make_async_copy(zeros, out.at[pl.ds(n * step, step)], sem.at[n]) for n in range(out.shape[0] // step)
    ]
    for copy in copies:
        copy.start()
    for copy in copies:
        copy.wait()


def sub_sums(values):
    row = lax.broadcasted_iota(jnp.int32, values[0].shape, 0)
    for s in (4, 2):
        low = (row & s) == 0
        paired = []
        for n in range(s):
            a, b = values[n], values[n + s]
            paired.append(jnp.where(low, a, pltpu.roll(b, s, 0)) + jnp.where(low, pltpu.roll(a, SUB - s, 0), b))
        values = paired
    even = (row & 1) == 0
    a, b = values
    return jnp.where(even, a, pltpu.roll(b, 1, 0)), jnp.where(even, pltpu.roll(a, SUB - 1, 0), b)


def fields(u, own, other, first_own, first_other):
    table = []
    for side, sources, targets in ((0, first_own, own), (1, first_other, other)):
        for n, ref in enumerate(sources):
            if u == 0:
                table.append((side, n, ref, targets[n], BLK + 1 if side == 0 else 0, 0))
            else:
                table.append((side, n, ref, targets[0], 1 if side == 0 else 0, n * ref.shape[2]))
    return table


def forward_kernel(u, counts, *refs):
    groups = []
    for count in counts[:-1]:
        groups.append(refs[:count])
        refs = refs[count:]
    first_own, first_other, own, other = groups[:4]
    y_hi, y_lo, z_hi, z_lo, ends, powers = refs[:6]
    messages, (spectrum, a_out, b_out, dens) = refs[-4 - counts[-1]:-4], refs[-4:]
    if u == 0:
        own, other = first_own, first_other
    core, g = my_core(), lax.axis_index("grid")
    tiles = first_own[0].shape[2] // LANES
    for side, n, source, target, slot, offset in fields(u, own, other, first_own, first_other):
        half = (core if side == 0 else 1 - core) * (len(first_own) * tiles * SUB)
        for t in range(tiles):
            lanes = pl.ds(t * LANES, LANES)
            value = target[slot, :, pl.ds(offset + t * LANES, LANES)]
            rows = pl.ds(pl.multiple_of(half + (n * tiles + t) * SUB, SUB), SUB)
            for w in range(BLK):
                dens[rows, w * LANES:(w + 1) * LANES] = value * source[1 + w, :, lanes]
    z = (z_hi[...], z_lo[...])
    half = dens.shape[0]
    for q in range(BLK // 2):
        out = dot3(split(dens[:, q * 2 * LANES:(q + 1) * 2 * LANES]), z)
        spectrum[:half, q * LANES:(q + 1) * LANES] = out[:, :LANES]
        spectrum[half:, q * LANES:(q + 1) * LANES] = out[:, LANES:]
    spectrum[...] = dot3((y_hi[...], y_lo[...]), split(spectrum[...]))

    def reduce(group, carry):
        lines = pl.ds(pl.multiple_of(group * SUB, SUB), SUB)
        near, far = powers[0, lines, :], powers[1, lines, :]
        for q in range(BLK // 2):
            lanes = slice(q * LANES, (q + 1) * LANES)
            values = []
            for k in range(SUB):
                rows = pl.ds(pl.multiple_of((group * SUB + k) * SUB, SUB), SUB)
                values.append(ends[rows, :] * spectrum[rows, lanes])
            even, odd = sub_sums(values)
            rightward = (even + odd) - near * (even - odd)
            leftward = (even - odd) - far * (even + odd)
            a_out[lines, lanes] = rightward
            b_out[lines, lanes] = leftward
            for k, out in enumerate(messages, 1):
                out[lines, lanes] = jnp.where((g ^ k) > g, rightward, leftward)
        return carry

    lax.fori_loop(0, NY // SUB, reduce, 0)


def backward_kernel(u, counts, flags, *refs):
    groups = []
    for count in counts:
        groups.append(refs[:count])
        refs = refs[count:]
    own, other, received = groups
    (y_hi, y_lo, z_hi, z_lo, inverse, basis, powers, steady, spectrum, a_in, b_in) = refs[:11]
    out, work, pot = refs[-3:]
    core, g = my_core(), lax.axis_index("grid")
    tiles = own[0].shape[2] // LANES
    first, last = basis[0], basis[1]

    def ends(group, carry):
        lines = pl.ds(pl.multiple_of(group * SUB, SUB), SUB)
        scale, r, slab = steady[0, lines, :], steady[1, lines, :], steady[2, lines, :]
        decays = [None, jnp.ones((SUB, LANES), f32), slab]
        while len(decays) <= len(received):
            decays.append(decays[-1] * slab)
        for q in range(BLK // 2):
            lanes = slice(q * LANES, (q + 1) * LANES)
            from_left = from_right = jnp.zeros((SUB, LANES), f32)
            for n, ref in enumerate(received, 1):
                distance = jnp.abs((g ^ n) - g)
                factor = decays[n]
                for d in range(1, n):
                    factor = jnp.where(distance == d, decays[d], factor)
                value = factor * ref[lines, lanes]
                is_left = (g ^ n) < g
                from_left = from_left + jnp.where(is_left, value, 0.0)
                from_right = from_right + jnp.where(is_left, 0.0, value)
            before = scale * (powers[2, lines, :] * from_left
                              + r * powers[3, lines, :] * (b_in[lines, lanes] + slab * from_right))
            after = scale * (powers[4, lines, :] * from_right
                             + r * powers[5, lines, :] * (a_in[lines, lanes] + slab * from_left))
            for k in range(SUB):
                rows = pl.ds(pl.multiple_of((group * SUB + k) * SUB, SUB), SUB)
                edge = first * before[k:k + 1] + last * after[k:k + 1]
                work[rows, lanes] = inverse[rows, :] * (spectrum[rows, lanes] + edge)
        return carry

    lax.fori_loop(0, NY // SUB, ends, 0)
    work[...] = dot3((y_hi[...], y_lo[...]), split(work[...]))
    z = (z_hi[...], z_lo[...])
    half = pot.shape[0]
    for q in range(BLK // 2):
        lanes = slice(q * LANES, (q + 1) * LANES)
        rows = jnp.concatenate([work[:half, lanes], work[half:, lanes]], axis=1)
        pot[:, q * 2 * LANES:(q + 1) * 2 * LANES] = dot3(split(rows), z)
    for side, group in ((0, own), (1, other)):
        half = (core if side == 0 else 1 - core) * (len(own) * tiles)
        for n, ref in enumerate(group):
            for t in range(tiles):
                lanes = pl.ds(t * LANES, LANES)
                at = half + n * tiles + t
                rows = pl.ds(pl.multiple_of(at * SUB, SUB), SUB)
                total = None
                for w in range(BLK):
                    term = flags[u * BLK + w] * (pot[rows, w * LANES:(w + 1) * LANES] * ref[1 + w, :, lanes])
                    total = term if total is None else total + term
                out[:, pl.ds(pl.multiple_of(at * LANES, LANES), LANES)] = -total


def place_kernel(stride, match, *refs):
    parts, (out, rows, sem) = refs[:-4], refs[-3:]
    pair = BLK // 2
    blocks, count = out.shape[0] // BLK, len(parts) // pair
    core = my_core()

    def hits(b, side):
        return [(match[b * stride + side * stride // 2 + n], side * count // 2 + n) for n in range(count // 2)]

    def found(b, side):
        return sum(hit for hit, n in hits(b, side)) > 0

    def move(b, side):
        which = core if side == 0 else 1 - core
        at = b * BLK + which * pair
        return pltpu.make_async_copy(rows.at[b, side], out.at[pl.ds(at, pair)], sem.at[b, side])

    for b in range(blocks):
        for side in range(2):

            @pl.when(found(b, side))
            def _():
                rows[b, side] = jnp.zeros(rows.shape[2:], f32)
                for hit, n in hits(b, side):

                    @pl.when(hit > 0)
                    def _():
                        for u in range(pair):
                            rows[b, side, u] += parts[u * count + n][...]

                move(b, side).start()

    for b in range(blocks):
        for side in range(2):

            @pl.when(found(b, side))
            def _():
                move(b, side).wait()


def tile_device(orbitals, rotation, tile_list, pair_mask):
    per_device, planes, width = orbitals.shape
    n_orb, n_grid = lax.axis_size("orb"), lax.axis_size("grid")
    size_x = planes * n_grid
    half = width // 2
    chips = n_orb // 2
    axes = ("orb", "grid")
    o, g = lax.axis_index("orb"), lax.axis_index("grid")
    core, chip = o % 2, o // 2

    def swap(x, even, odd):
        moves = []
        for a in range(n_orb):
            flip = even if a % 2 == 0 else odd
            moves += [(a * n_grid + b, (a ^ flip) * n_grid + b) for b in range(n_grid)]
        return lax.ppermute(x, axes, moves)

    def cross(x, k):
        moves = [(a * n_grid + b, a * n_grid + (b ^ k)) for a in range(n_orb) for b in range(n_grid)]
        return lax.ppermute(x, axes, moves)

    chunk = half // CHUNKS

    def take(flip, start, lanes, *after):
        return pl.pallas_call(
            functools.partial(take_kernel, flip, start),
            out_shape=jax.ShapeDtypeStruct((per_device, planes, lanes), f32),
            in_specs=[HBM] + [ANY] * len(after), out_specs=VM, scratch_shapes=[DMA], name=f"take_{int(flip)}_{start}",
            compiler_params=grant(4),
        )(orbitals, *after)

    theirs, mine, last = [], [], ()
    for n in range(CHUNKS):
        taken = take(True, n * chunk, chunk, *last)
        theirs.append(swap(taken, 1, 1))
        last = (taken,)
    for n in range(CHUNKS):
        mine.append(take(False, n * chunk, chunk, *last))

    pair = BLK // 2
    firsts = (BLK + 2) * chips
    rows = (firsts + 2 * (pair - 1) * chips) * SUB
    wide_table = jax.ShapeDtypeStruct((rows, 2 * LANES), bf16)
    blocks = per_device // BLK
    high, low, flags, match, alone = pl.pallas_call(
        functools.partial(setup_kernel, per_device),
        out_shape=(wide_table, wide_table, jax.ShapeDtypeStruct((pair * BLK,), f32),
                   jax.ShapeDtypeStruct((blocks * 8,), jnp.int32), jax.ShapeDtypeStruct((1,), jnp.int32)),
        in_specs=[SM, SM, VM, VM], out_specs=(VM, VM, SM, SM, SM), name="setup", compiler_params=grant(8),
    )(tile_list.reshape(-1), jnp.asarray(host_np(chips).reshape(-1)), rotation, pair_mask)

    def rotate(first, count, fields, name, *after):
        part = jax.ShapeDtypeStruct((count, planes, chunk * (len(fields) // 2)), f32)
        send, keep = pl.pallas_call(
            functools.partial(rotate_kernel, first * SUB), out_shape=(part, part),
            in_specs=[VM] * (2 + len(fields)) + [ANY] * len(after),
            out_specs=(VM, VM), name=name, compiler_params=grant(8),
        )(high, low, *fields, *after)
        return send, keep, swap(send, 2, 4)

    sums, last = [], ()
    for n in range(CHUNKS):
        sums.append(rotate(0, firsts // 2, [mine[n], theirs[n]], f"rotate_{n}", *last))
        last = (sums[-1][0],)
    both = [x for n in range(CHUNKS) for x in (mine[n], theirs[n])]
    sums.append(rotate(firsts, (pair - 1) * chips, both, "rotate_rest", *last))
    empty = pl.pallas_call(
        clear_kernel, out_shape=jax.ShapeDtypeStruct(orbitals.shape, f32), in_specs=[ANY], out_specs=HBM,
        scratch_shapes=[pltpu.VMEM((pair, planes, width), f32), DMA((per_device // pair,))], name="clear",
        compiler_params=grant(4),
    )(sums[-1][0])
    passing, last, specs = [], (empty,), [HBM]
    for n, (send, keep, got) in enumerate(sums):
        shape = (keep.shape[0] // 2,) + keep.shape[1:]
        value = pl.pallas_call(
            pass_kernel, out_shape=jax.ShapeDtypeStruct(shape, f32), in_specs=[VM] * 2 + specs, out_specs=VM,
            name=f"pass_{n}", compiler_params=grant(4),
        )(keep, got, *last)
        last, specs = (value,), [ANY]
        passing.append((keep, got, swap(value, 4, 2)))
    own, other = [], []
    for n, (keep, got, passed) in enumerate(passing):
        own.append(pl.pallas_call(
            finish_kernel, out_shape=jax.ShapeDtypeStruct(passed.shape, f32), in_specs=[VM] * 3 + [ANY] * len(own[-1:]),
            out_specs=VM, name=f"finish_{n}", compiler_params=grant(4),
        )(keep, got, passed, *own[-1:]))
        other.append(swap(own[-1], 1, 1))

    c, r = line_np()
    sine_x, eigen_x = sine_np(planes), eigen_np(planes)
    ends = jnp.asarray(np.einsum("jp,pkl->kjl", sine_x, r[None] ** np.arange(planes - 1, -1, -1)[:, None, None])
                       .reshape(-1, LANES), f32)
    inverse = jnp.asarray((COUPLING / (eigen_x[None, :, None] + c[:, None, :])).reshape(-1, LANES), f32)
    basis = jnp.asarray(np.broadcast_to(sine_x[:, [0, -1]].T[:, :, None], (2, planes, LANES)), f32)
    steady = jnp.asarray(np.stack([r / ((1 - r**2) * (1 - r ** (2 * size_x + 2))), r, r**planes]), f32)
    at = planes * g
    exponents = jnp.stack([
        2 * at + planes + 1,
        2 * size_x + 1 - planes - 2 * at,
        2 * size_x + 2 - 2 * at,
        2 * at,
        2 * at + 2 * planes + 2,
        2 * size_x - 2 * planes - 2 * at,
    ]).astype(f32)
    powers = jnp.exp(exponents[:, None, None] * jnp.asarray(np.log(r), f32)[None])
    powers = jnp.where(jnp.arange(6)[:, None, None] < 2, powers, 1.0 - powers)

    y_hi, y_lo = halves_np(y_table())
    z_hi, z_lo = halves_np(z_table())
    zt_hi, zt_lo = halves_np(z_table().T)
    solved = []
    lines = jax.ShapeDtypeStruct((NY, 2 * LANES), f32)
    cube = (NY * SUB, 2 * LANES)
    wide = pltpu.VMEM((width // LANES * SUB, BLK * LANES), f32)
    base_own, base_other = own[:CHUNKS], other[:CHUNKS]
    last = ()
    for u in range(pair):
        more_own, more_other = own[CHUNKS:][:u], other[CHUNKS:][:u]
        counts = (CHUNKS, CHUNKS, len(more_own), len(more_other))
        inputs = [*base_own, *base_other, *more_own, *more_other, y_hi, y_lo, z_hi, z_lo, ends, powers]
        *messages, spectrum, a, b = pl.pallas_call(
            functools.partial(forward_kernel, u, counts + (n_grid - 1,)),
            out_shape=[lines] * (n_grid - 1) + [jax.ShapeDtypeStruct(cube, f32), lines, lines],
            in_specs=[VM] * len(inputs) + [ANY] * len(last),
            out_specs=[VM] * (n_grid + 2),
            scratch_shapes=[wide],
            name=f"forward_{u}",
            compiler_params=grant(16),
        )(*inputs, *last)
        last = (spectrum,)
        solved.append((spectrum, a, b, [cross(m, k) for k, m in enumerate(messages, 1)]))

    terms, last = [], ()
    for u, (spectrum, a, b, received) in enumerate(solved):
        inputs = [*base_own, *base_other, *received, y_hi, y_lo, zt_hi, zt_lo, inverse, basis, powers, steady,
                  spectrum, a, b]
        terms.append(pl.pallas_call(
            functools.partial(backward_kernel, u, (CHUNKS, CHUNKS, len(received))),
            out_shape=jax.ShapeDtypeStruct((planes, width), f32),
            in_specs=[SM] + [VM] * len(inputs) + [ANY] * len(last),
            out_specs=VM,
            scratch_shapes=[pltpu.VMEM(cube, f32), wide],
            name=f"backward_{u}",
            compiler_params=grant(16),
        )(flags, *inputs, *last))
        last = (terms[-1],)

    near_1 = [swap(term, 2, 4) for term in terms]
    near_2 = [swap(term, 4, 2) for term in terms]
    own_parts = [[term, x, y] for term, x, y in zip(terms, near_1, near_2)]
    sib_parts = [[swap(v, 1, 1) for v in group] for group in own_parts]

    def place(target, groups):
        parts = [part for group in groups for part in group]
        return pl.pallas_call(
            functools.partial(place_kernel, 8),
            out_shape=jax.ShapeDtypeStruct(orbitals.shape, f32),
            in_specs=[SM] + [VM] * len(parts) + [HBM],
            out_specs=HBM,
            input_output_aliases={len(parts) + 1: 0},
            scratch_shapes=[pltpu.VMEM((blocks, 2, pair, planes, width), f32), DMA((blocks, 2))],
            name="place",
            compiler_params=grant(8),
        )(match, *parts, target)

    def place_near(target, mine, sibs):
        return place(target, [a + b for a, b in zip(mine, sibs)])

    def place_far(target, mine, sibs):
        far = [swap(group[1], 4, 2) for group in mine]
        return place(target, [a + [x] + b + [swap(x, 1, 1)] for a, b, x in zip(mine, sibs, far)])

    return lax.cond(alone[0] != 0, place_far, place_near, empty, own_parts, sib_parts)


def sine_table(length):
    wave_index = jnp.arange(length, dtype=f32) + 1.0
    return jnp.sqrt(2.0 / (length + 1.0)) * jnp.sin(
        jnp.pi * wave_index[:, None] * wave_index[None, :] / (length + 1.0)
    )


def eigen_values(length):
    wave_index = jnp.arange(length, dtype=f32) + 1.0
    return 2.0 - 2.0 * jnp.cos(jnp.pi * wave_index / (length + 1.0))


def green_kernel(size_x, size_y, size_z):
    summed = (
        eigen_values(size_x)[:, None, None]
        + eigen_values(size_y)[None, :, None]
        + eigen_values(size_z)[None, None, :]
    )
    return COUPLING / (summed + SCREENING)


def pair_lists(tile_list, pair_mask):
    within = jnp.arange(BLK * BLK, dtype=jnp.int32)
    targets = (BLK * tile_list[:, 0:1] + within[None, :] // BLK).reshape(-1)
    sources = (BLK * tile_list[:, 1:2] + within[None, :] % BLK).reshape(-1)
    return (targets, sources, pair_mask[targets, sources])


def compact(targets, sources, live_flags, number):
    ranking = jnp.cumsum(live_flags) - 1
    places = jnp.where(live_flags == 1, ranking, number)
    picked = (
        jnp.zeros((number,), jnp.int32)
        .at[places]
        .set(jnp.arange(live_flags.shape[0], dtype=jnp.int32), mode="drop")
    )
    return (targets[picked], sources[picked])


def along_z(values, matrix):
    number, planes, width_yz = values.shape
    size_z = matrix.shape[0]
    shaped = values.reshape(number, planes, width_yz // size_z, size_z)
    return jnp.einsum("pxrz,zk->pxrk", shaped, matrix, precision=precise).reshape(number, planes, width_yz)


def along_y(values, matrix):
    number, planes, width_yz = values.shape
    size_y = matrix.shape[0]
    shaped = values.reshape(number, planes, size_y, width_yz // size_y)
    return jnp.einsum("pxyz,yk->pxkz", shaped, matrix, precision=precise).reshape(number, planes, width_yz)


def along_x(values, matrix):
    return jnp.einsum("pxc,xk->pkc", values, matrix, precision=precise)


def any_device(orbitals, rotation, tile_list, pair_mask):
    n_orb, n_grid = lax.axis_size("orb"), lax.axis_size("grid")
    number_orbitals, size_x = rotation.shape[0], orbitals.shape[1] * n_grid
    rotated = jnp.einsum(
        "ij,ixc->jxc",
        rotation,
        lax.all_to_all(orbitals, "orb", split_axis=2, concat_axis=0, tiled=True),
        precision=precise,
    )
    planes, width_yz = rotated.shape[1:]
    targets, sources, live_flags = pair_lists(tile_list, pair_mask)
    matrix_x, matrix_y, matrix_z = sine_table(size_x), sine_table(NY), sine_table(NZ)
    kernel = green_kernel(size_x, NY, NZ).reshape(size_x, NY * NZ)
    orbital_ids = jnp.arange(number_orbitals, dtype=jnp.int32)
    targets, sources = compact(targets, sources, live_flags, targets.shape[0] // 2)
    density = rotated[targets] * rotated[sources]
    number = density.shape[0]
    spectrum = along_z(density, matrix_z)
    spectrum = lax.all_to_all(spectrum, "orb", split_axis=0, concat_axis=2, tiled=True)
    spectrum = along_y(spectrum, matrix_y)
    spectrum = lax.all_to_all(spectrum, "grid", split_axis=0, concat_axis=1, tiled=True)
    spectrum = along_x(along_x(spectrum, matrix_x) * kernel, matrix_x)
    spectrum = lax.all_to_all(spectrum, "grid", split_axis=1, concat_axis=0, tiled=True)
    spectrum = along_y(spectrum, matrix_y)
    spectrum = lax.all_to_all(spectrum, "orb", split_axis=2, concat_axis=0, tiled=True)
    potential = along_z(spectrum, matrix_z)
    products = potential * rotated[sources]
    selector = (targets[None, :] == orbital_ids[:, None]).astype(f32)
    partial_value = -jnp.dot(selector, products.reshape(number, planes * width_yz), precision=precise)
    partial_value = partial_value.reshape(number_orbitals, planes, width_yz)
    return lax.all_to_all(partial_value, "orb", split_axis=0, concat_axis=2, tiled=True)


def solution(mesh):
    n_orb, n_grid = mesh.shape["orb"], mesh.shape["grid"]

    def on_device(orbitals, rotation, tile_list, pair_mask):
        per_device, planes, width = orbitals.shape
        fits = n_orb == 8 and 2 * tile_list.shape[0] == n_orb and planes == SUB and per_device % BLK == 0
        fits = fits and width == NY * NZ and 2 * NZ == LANES and n_grid in (2, 4, 8)
        fits = fits and per_device * SUB == LANES and rotation.shape == (LANES, LANES)
        body = tile_device if fits else any_device
        return body(orbitals, rotation, tile_list, pair_mask)

    in_specs = (P("orb", "grid", None), P(), P(), P())
    out_specs = P("orb", "grid", None)
    return jax.shard_map(on_device, mesh=mesh, in_specs=in_specs, out_specs=out_specs, check_vma=False)
```

```python
import functools
import itertools

import jax
import jax.numpy as jnp
import numpy as np
from jax import lax
from jax.experimental import pallas as pl
from jax.experimental.pallas import tpu as pltpu
from jax.sharding import PartitionSpec as P

BLK = 4
NY = 64
NZ = 64
LANES = 128
SUB = 8
CHUNKS = 2
COUPLING = 0.25
SCREENING = 0.1

precise = lax.Precision.HIGHEST
f32 = jnp.float32
bf16 = jnp.bfloat16

VM = pl.BlockSpec(memory_space=pltpu.VMEM)
SM = pl.BlockSpec(memory_space=pltpu.SMEM)
ANY = pl.BlockSpec(memory_space=pl.ANY)
HBM = pl.BlockSpec(memory_space=pltpu.HBM)
DMA = pltpu.SemaphoreType.DMA


def grant(mib):
    return pltpu.CompilerParams(vmem_limit_bytes=mib << 20)


def sine_np(n):
    k = np.arange(1, n + 1, dtype=np.float64)
    return np.sqrt(2.0 / (n + 1)) * np.sin(np.pi * k[:, None] * k[None, :] / (n + 1))


def eigen_np(n):
    k = np.arange(1, n + 1, dtype=np.float64)
    return 2.0 - 2.0 * np.cos(np.pi * k / (n + 1))


def halves_np(table):
    high = np.asarray(table, np.float32).astype(jnp.bfloat16)
    low = (np.asarray(table, np.float64) - high.astype(np.float64)).astype(jnp.bfloat16)
    return jnp.asarray(high), jnp.asarray(low)


def y_order():
    rows = LANES // NZ
    return np.arange(NY).reshape(NY // rows, rows).T.reshape(-1)


def y_table():
    order = y_order()
    return np.kron(sine_np(NY)[order][:, order], sine_np(SUB))


def z_table():
    half = LANES // NZ
    sine = sine_np(NZ)
    table = np.zeros((2, half, NZ, half, 2, NZ))
    for pair in range(2):
        for h in range(half):
            table[pair, h, :, h, pair, :] = sine
    return table.reshape(2 * half * NZ, half * 2 * NZ)


def line_np():
    c = eigen_np(NY)[y_order()][:, None] + eigen_np(NZ)[None, :] + SCREENING
    c = np.concatenate([c, c], axis=1)
    return c, 2.0 / (2.0 + c + np.sqrt(c * (c + 4.0)))


def host_np(chips):
    table = np.zeros((chips**chips, chips), np.int32)
    for owners in itertools.product(range(chips), repeat=chips):
        best = None
        for tiles in itertools.permutations(range(chips)):
            hops = [bin(chip ^ owners[tile]).count("1") for chip, tile in enumerate(tiles)]
            cost = (max(hops), sum(hops))
            if best is None or cost < best[0]:
                best = (cost, tiles)
        table[sum(own * chips**t for t, own in enumerate(owners))] = best[1]
    return table


def dot(a, b):
    return jnp.dot(a, b, preferred_element_type=f32)


def split(x):
    high = x.astype(bf16)
    return high, (x - high.astype(f32)).astype(bf16)


def dot3(a, b):
    return dot(a[0], b[0]) + dot(a[0], b[1]) + dot(a[1], b[0])


def my_core():
    return lax.rem(lax.axis_index("orb"), 2)


def my_place():
    o = lax.axis_index("orb")
    return o, lax.rem(o, 2), lax.div(o, 2)


def take_kernel(flip, start, source, *rest):
    out, sem = rest[-2:]
    core = my_core()
    side = 1 - core if flip else core
    at = pl.multiple_of(side * (source.shape[2] // 2) + start, LANES)
    copy = pltpu.make_async_copy(source.at[:, :, pl.ds(at, out.shape[2])], out, sem)
    copy.start()
    copy.wait()


def setup_kernel(per_device, n_grid, tiles, host, rotation, mask, log_r, high, low, powers, flags, match, alone):
    o, core, chip = my_place()
    at, size_x = SUB * lax.axis_index("grid"), SUB * n_grid
    exponents = (
        2 * at + SUB + 1,
        2 * size_x + 1 - SUB - 2 * at,
        2 * size_x + 2 - 2 * at,
        2 * at,
        2 * at + 2 * SUB + 2,
        2 * size_x - 2 * SUB - 2 * at,
    )
    for n, exponent in enumerate(exponents):
        power = jnp.exp(exponent.astype(f32) * log_r[...])
        powers[n] = power if n < 2 else 1.0 - power
    chips = tiles.shape[0]
    owners = [lax.div(tiles[t, 0] * BLK, 2 * per_device) for t in range(chips)]
    key = 0
    for t in range(chips):
        key = key + owners[t] * chips**t
    same = owners[0] == owners[1]
    for t in range(2, chips):
        same = same & (owners[t] == owners[0])
    alone[0] = same.astype(jnp.int32)
    bit_1 = jnp.where(core == 0, 1, 2)
    bit_2 = 3 - bit_1
    pair = BLK // 2
    order = [chip ^ 3, chip ^ bit_1, chip ^ bit_2, chip]
    heads = []
    for where in order:
        tile = host[key * chips + where]
        heads.append((BLK * tiles[tile, 0], BLK * tiles[tile, 1]))
    wanted = []
    for a, b in heads:
        wanted += [a + (1 - core) * pair] + [b + w for w in range(BLK)] + [a + core * pair]
    for u in range(1, pair):
        for a, b in heads:
            wanted += [a + (1 - core) * pair + u, a + core * pair + u]
    lane = lax.broadcasted_iota(jnp.int32, (SUB, LANES), 1)
    chosen = jnp.concatenate([jnp.where(lane == n, 1.0, 0.0) for n in wanted]).astype(bf16)
    count = chosen.shape[0]
    row = lax.broadcasted_iota(jnp.int32, (LANES, LANES), 0)
    column = lax.broadcasted_iota(jnp.int32, (LANES, LANES), 1)
    columns = [
        jnp.where(row - (o ^ e) * per_device == jnp.right_shift(column, 3), 1.0, 0.0).astype(bf16)
        for e in range(2)
    ]
    keep = (lax.broadcasted_iota(jnp.int32, (count, LANES), 0) & (SUB - 1)) == (
        lax.broadcasted_iota(jnp.int32, (count, LANES), 1) & (SUB - 1)
    )
    for out, values in zip((high, low), split(rotation[...])):
        picked = lax.dot_general(chosen, values, (((1,), (1,)), ((), ())), preferred_element_type=f32).astype(bf16)
        for e in range(2):
            out[:, e * LANES:(e + 1) * LANES] = jnp.where(keep, dot(picked, columns[e]), 0.0).astype(bf16)
    a, b = heads[-1]
    live = mask[...].astype(f32)
    for u in range(pair):
        line = jnp.sum(jnp.where(row == a + core * pair + u, live, 0.0), axis=0, keepdims=True)
        for w in range(BLK):
            flags[u * BLK + w] = jnp.sum(jnp.where(column[:1] == b + w, line, 0.0))
    blocks = per_device // BLK
    parts = [chip, chip ^ bit_1, chip ^ bit_2, chip ^ 3, chip, chip ^ bit_2, chip ^ bit_1, chip ^ 3]
    for n, where in enumerate(parts):
        home = tiles[host[key * chips + where], 0]
        for block in range(blocks):
            hit = home == o * blocks + block
            if n % 4 == 3:
                hit = hit & same
            match[block * len(parts) + n] = hit.astype(jnp.int32)


def rotate_kernel(first, high, low, *rest):
    send, keep = rest[-2:]
    rows = send.shape[0] * SUB
    part = pl.ds(first, 2 * rows)
    table = (high[part, :], low[part, :])
    at = 0
    step = 2 * LANES
    while at < send.shape[2]:
        width = rest[0].shape[2]
        n, inner = at // width, at % width
        lanes = slice(inner, inner + step)
        mine, theirs = rest[2 * n], rest[2 * n + 1]
        depth = mine.shape[0] * SUB
        cells = jnp.concatenate([mine[:, :, lanes].reshape(depth, step), theirs[:, :, lanes].reshape(depth, step)])
        total = dot3(table, split(cells))
        lanes = slice(at, at + step)
        send[:, :, lanes] = total[:rows].reshape(send.shape[0], SUB, step)
        keep[:, :, lanes] = total[rows:].reshape(keep.shape[0], SUB, step)
        at += step


def pass_kernel(keep, got, *rest):
    out = rest[-1]
    count = out.shape[0]
    out[...] = keep[:count] + got[:count]


def finish_kernel(keep, got, passed, *rest):
    out = rest[-1]
    count = out.shape[0]
    out[...] = keep[count:] + got[count:] + passed[...]


def clear_kernel(*refs):
    out, zeros, sem = refs[-3:]
    zeros[...] = jnp.zeros(zeros.shape, f32)
    step = zeros.shape[0]
    copies = [
        pltpu.make_async_copy(zeros, out.at[pl.ds(n * step, step)], sem.at[n]) for n in range(out.shape[0] // step)
    ]
    for copy in copies:
        copy.start()
    for copy in copies:
        copy.wait()


def sub_sums(values):
    row = lax.broadcasted_iota(jnp.int32, values[0].shape, 0)
    for s in (4, 2):
        low = (row & s) == 0
        paired = []
        for n in range(s):
            a, b = values[n], values[n + s]
            paired.append(jnp.where(low, a, pltpu.roll(b, s, 0)) + jnp.where(low, pltpu.roll(a, SUB - s, 0), b))
        values = paired
    even = (row & 1) == 0
    a, b = values
    return jnp.where(even, a, pltpu.roll(b, 1, 0)), jnp.where(even, pltpu.roll(a, SUB - 1, 0), b)


def fields(u, own, other, first_own, first_other):
    table = []
    for side, sources, targets in ((0, first_own, own), (1, first_other, other)):
        for n, ref in enumerate(sources):
            if u == 0:
                table.append((side, n, ref, targets[n], BLK + 1 if side == 0 else 0, 0))
            else:
                table.append((side, n, ref, targets[0], 1 if side == 0 else 0, n * ref.shape[2]))
    return table


def forward_kernel(u, counts, *refs):
    groups = []
    for count in counts[:-1]:
        groups.append(refs[:count])
        refs = refs[count:]
    first_own, first_other, own, other = groups[:4]
    y_hi, y_lo, z_hi, z_lo, ends, powers = refs[:6]
    messages, (spectrum, a_out, b_out, dens) = refs[-4 - counts[-1]:-4], refs[-4:]
    if u == 0:
        own, other = first_own, first_other
    core, g = my_core(), lax.axis_index("grid")
    tiles = first_own[0].shape[2] // LANES
    for side, n, source, target, slot, offset in fields(u, own, other, first_own, first_other):
        half = (core if side == 0 else 1 - core) * (len(first_own) * tiles * SUB)
        for t in range(tiles):
            lanes = pl.ds(t * LANES, LANES)
            value = target[slot, :, pl.ds(offset + t * LANES, LANES)]
            rows = pl.ds(pl.multiple_of(half + (n * tiles + t) * SUB, SUB), SUB)
            for w in range(BLK):
                dens[rows, w * LANES:(w + 1) * LANES] = value * source[1 + w, :, lanes]
    z = (z_hi[...], z_lo[...])
    half = dens.shape[0]
    for q in range(BLK // 2):
        out = dot3(split(dens[:, q * 2 * LANES:(q + 1) * 2 * LANES]), z)
        spectrum[:half, q * LANES:(q + 1) * LANES] = out[:, :LANES]
        spectrum[half:, q * LANES:(q + 1) * LANES] = out[:, LANES:]
    spectrum[...] = dot3((y_hi[...], y_lo[...]), split(spectrum[...]))

    def reduce(group, carry):
        lines = pl.ds(pl.multiple_of(group * SUB, SUB), SUB)
        near, far = powers[0, lines, :], powers[1, lines, :]
        for q in range(BLK // 2):
            lanes = slice(q * LANES, (q + 1) * LANES)
            values = []
            for k in range(SUB):
                rows = pl.ds(pl.multiple_of((group * SUB + k) * SUB, SUB), SUB)
                values.append(ends[rows, :] * spectrum[rows, lanes])
            even, odd = sub_sums(values)
            rightward = (even + odd) - near * (even - odd)
            leftward = (even - odd) - far * (even + odd)
            a_out[lines, lanes] = rightward
            b_out[lines, lanes] = leftward
            for k, out in enumerate(messages, 1):
                out[lines, lanes] = jnp.where((g ^ k) > g, rightward, leftward)
        return carry

    lax.fori_loop(0, NY // SUB, reduce, 0)


def backward_kernel(u, counts, flags, *refs):
    groups = []
    for count in counts:
        groups.append(refs[:count])
        refs = refs[count:]
    own, other, received = groups
    (y_hi, y_lo, z_hi, z_lo, inverse, basis, powers, steady, spectrum, a_in, b_in) = refs[:11]
    out, work, pot = refs[-3:]
    core, g = my_core(), lax.axis_index("grid")
    tiles = own[0].shape[2] // LANES
    first, last = basis[0], basis[1]

    def ends(group, carry):
        lines = pl.ds(pl.multiple_of(group * SUB, SUB), SUB)
        scale, r, slab = steady[0, lines, :], steady[1, lines, :], steady[2, lines, :]
        decays = [None, jnp.ones((SUB, LANES), f32), slab]
        while len(decays) <= len(received):
            decays.append(decays[-1] * slab)
        for q in range(BLK // 2):
            lanes = slice(q * LANES, (q + 1) * LANES)
            from_left = from_right = jnp.zeros((SUB, LANES), f32)
            for n, ref in enumerate(received, 1):
                distance = jnp.abs((g ^ n) - g)
                factor = decays[n]
                for d in range(1, n):
                    factor = jnp.where(distance == d, decays[d], factor)
                value = factor * ref[lines, lanes]
                is_left = (g ^ n) < g
                from_left = from_left + jnp.where(is_left, value, 0.0)
                from_right = from_right + jnp.where(is_left, 0.0, value)
            before = scale * (powers[2, lines, :] * from_left
                              + r * powers[3, lines, :] * (b_in[lines, lanes] + slab * from_right))
            after = scale * (powers[4, lines, :] * from_right
                             + r * powers[5, lines, :] * (a_in[lines, lanes] + slab * from_left))
            for k in range(SUB):
                rows = pl.ds(pl.multiple_of((group * SUB + k) * SUB, SUB), SUB)
                edge = first * before[k:k + 1] + last * after[k:k + 1]
                work[rows, lanes] = inverse[rows, :] * (spectrum[rows, lanes] + edge)
        return carry

    lax.fori_loop(0, NY // SUB, ends, 0)
    work[...] = dot3((y_hi[...], y_lo[...]), split(work[...]))
    z = (z_hi[...], z_lo[...])
    half = pot.shape[0]
    for q in range(BLK // 2):
        lanes = slice(q * LANES, (q + 1) * LANES)
        rows = jnp.concatenate([work[:half, lanes], work[half:, lanes]], axis=1)
        pot[:, q * 2 * LANES:(q + 1) * 2 * LANES] = dot3(split(rows), z)
    for side, group in ((0, own), (1, other)):
        half = (core if side == 0 else 1 - core) * (len(own) * tiles)
        for n, ref in enumerate(group):
            for t in range(tiles):
                lanes = pl.ds(t * LANES, LANES)
                at = half + n * tiles + t
                rows = pl.ds(pl.multiple_of(at * SUB, SUB), SUB)
                total = None
                for w in range(BLK):
                    term = flags[u * BLK + w] * (pot[rows, w * LANES:(w + 1) * LANES] * ref[1 + w, :, lanes])
                    total = term if total is None else total + term
                out[:, pl.ds(pl.multiple_of(at * LANES, LANES), LANES)] = -total


def place_kernel(stride, match, *refs):
    parts, (out, rows, sem) = refs[:-4], refs[-3:]
    pair = BLK // 2
    blocks, count = out.shape[0] // BLK, len(parts) // pair
    core = my_core()

    def hits(b, side):
        return [(match[b * stride + side * stride // 2 + n], side * count // 2 + n) for n in range(count // 2)]

    def found(b, side):
        return sum(hit for hit, n in hits(b, side)) > 0

    def move(b, side):
        which = core if side == 0 else 1 - core
        at = b * BLK + which * pair
        return pltpu.make_async_copy(rows.at[b, side], out.at[pl.ds(at, pair)], sem.at[b, side])

    for b in range(blocks):
        for side in range(2):

            @pl.when(found(b, side))
            def _():
                rows[b, side] = jnp.zeros(rows.shape[2:], f32)
                for hit, n in hits(b, side):

                    @pl.when(hit > 0)
                    def _():
                        for u in range(pair):
                            rows[b, side, u] += parts[u * count + n][...]

                move(b, side).start()

    for b in range(blocks):
        for side in range(2):

            @pl.when(found(b, side))
            def _():
                move(b, side).wait()


def tile_device(orbitals, rotation, tile_list, pair_mask):
    shape = per_device, planes, width = orbitals.shape
    n_orb, n_grid = lax.axis_size("orb"), lax.axis_size("grid")
    size_x = planes * n_grid
    half = width // 2
    chips = n_orb // 2
    axes = ("orb", "grid")
    o, g = lax.axis_index("orb"), lax.axis_index("grid")
    core, chip = o % 2, o // 2

    def swap(x, even, odd):
        moves = []
        for a in range(n_orb):
            flip = even if a % 2 == 0 else odd
            moves += [(a * n_grid + b, (a ^ flip) * n_grid + b) for b in range(n_grid)]
        return lax.ppermute(x, axes, moves)

    def cross(x, k):
        moves = [(a * n_grid + b, a * n_grid + (b ^ k)) for a in range(n_orb) for b in range(n_grid)]
        return lax.ppermute(x, axes, moves)

    chunk = half // CHUNKS
    orbitals = pltpu.with_memory_space_constraint(orbitals, pltpu.HBM)

    def take(flip, start, lanes, *after):
        return pl.pallas_call(
            functools.partial(take_kernel, flip, start),
            out_shape=jax.ShapeDtypeStruct((per_device, planes, lanes), f32),
            in_specs=[HBM] + [ANY] * len(after), out_specs=VM, scratch_shapes=[DMA], name=f"take_{int(flip)}_{start}",
            compiler_params=grant(4),
        )(orbitals, *after)

    theirs, mine, last = [], [], ()
    for n in range(CHUNKS):
        taken = take(True, n * chunk, chunk, *last)
        theirs.append(swap(taken, 1, 1))
        last = (taken,)
    for n in range(CHUNKS):
        mine.append(take(False, n * chunk, chunk, *last))

    pair = BLK // 2
    firsts = (BLK + 2) * chips
    rows = (firsts + 2 * (pair - 1) * chips) * SUB
    wide_table = jax.ShapeDtypeStruct((rows, 2 * LANES), bf16)
    blocks = per_device // BLK
    c, r = line_np()
    high, low, powers, flags, match, alone = pl.pallas_call(
        functools.partial(setup_kernel, per_device, n_grid),
        out_shape=(wide_table, wide_table, jax.ShapeDtypeStruct((6, NY, LANES), f32), jax.ShapeDtypeStruct((pair * BLK,), f32),
                   jax.ShapeDtypeStruct((blocks * 8,), jnp.int32), jax.ShapeDtypeStruct((1,), jnp.int32)),
        in_specs=[SM, SM, VM, VM, VM], out_specs=(VM, VM, VM, SM, SM, SM), name="setup", compiler_params=grant(4),
    )(tile_list, jnp.asarray(host_np(chips).reshape(-1)), rotation, pair_mask, jnp.asarray(np.log(r), f32))

    def rotate(first, count, fields, name, *after):
        part = jax.ShapeDtypeStruct((count, planes, chunk * (len(fields) // 2)), f32)
        send, keep = pl.pallas_call(
            functools.partial(rotate_kernel, first * SUB), out_shape=(part, part),
            in_specs=[VM] * (2 + len(fields)) + [ANY] * len(after),
            out_specs=(VM, VM), name=name, compiler_params=grant(8),
        )(high, low, *fields, *after)
        return send, keep, swap(send, 2, 4)

    sums, last = [], ()
    for n in range(CHUNKS):
        sums.append(rotate(0, firsts // 2, [mine[n], theirs[n]], f"rotate_{n}", *last))
        last = (sums[-1][0],)
    both = [x for n in range(CHUNKS) for x in (mine[n], theirs[n])]
    sums.append(rotate(firsts, (pair - 1) * chips, both, "rotate_rest", *last))
    empty = pl.pallas_call(
        clear_kernel, out_shape=pltpu.HBM(shape, f32), in_specs=[ANY], out_specs=HBM,
        scratch_shapes=[pltpu.VMEM((pair, planes, width), f32), DMA((per_device // pair,))], name="clear",
        compiler_params=grant(4),
    )(sums[-1][0])
    passing, own, other = [], [], []

    def pass_on(n, *after, spec=ANY):
        send, keep, got = sums[n]
        count = keep.shape[0] // 2
        value = pl.pallas_call(
            pass_kernel, out_shape=jax.ShapeDtypeStruct((count,) + keep.shape[1:], f32),
            in_specs=[VM] * 2 + [spec] * len(after), out_specs=VM, name=f"pass_{n}", compiler_params=grant(4),
        )(keep, got, *after)
        passing.append((keep, got, swap(value, 4, 2)))
        return value

    def finish(n, *after):
        keep, got, passed = passing[n]
        own.append(pl.pallas_call(
            finish_kernel, out_shape=jax.ShapeDtypeStruct(passed.shape, f32), in_specs=[VM] * 3 + [ANY] * len(after),
            out_specs=VM, name=f"finish_{n}", compiler_params=grant(4),
        )(keep, got, passed, *after))
        other.append(swap(own[-1], 1, 1))
        return own[-1]

    step = pass_on(0, empty, spec=HBM)
    for n in range(1, CHUNKS):
        step = pass_on(n, step)
    step = finish(0, step)
    step = pass_on(CHUNKS, step)
    for n in range(1, CHUNKS):
        step = finish(n, step)

    sine_x, eigen_x = sine_np(planes), eigen_np(planes)
    ends = jnp.asarray(np.einsum("jp,pkl->kjl", sine_x, r[None] ** np.arange(planes - 1, -1, -1)[:, None, None])
                       .reshape(-1, LANES), f32)
    inverse = jnp.asarray((COUPLING / (eigen_x[None, :, None] + c[:, None, :])).reshape(-1, LANES), f32)
    basis = jnp.asarray(np.broadcast_to(sine_x[:, [0, -1]].T[:, :, None], (2, planes, LANES)), f32)
    steady = jnp.asarray(np.stack([r / ((1 - r**2) * (1 - r ** (2 * size_x + 2))), r, r**planes]), f32)

    y_hi, y_lo = halves_np(y_table())
    z_hi, z_lo = halves_np(z_table())
    zt_hi, zt_lo = halves_np(z_table().T)
    solved = []
    lines = jax.ShapeDtypeStruct((NY, 2 * LANES), f32)
    cube = (NY * SUB, 2 * LANES)
    wide = pltpu.VMEM((width // LANES * SUB, BLK * LANES), f32)
    base_own, base_other = own[:CHUNKS], other[:CHUNKS]
    last = ()
    for u in range(pair):
        if u:
            finish(CHUNKS, *last)
        more_own, more_other = own[CHUNKS:][:u], other[CHUNKS:][:u]
        counts = (CHUNKS, CHUNKS, len(more_own), len(more_other))
        inputs = [*base_own, *base_other, *more_own, *more_other, y_hi, y_lo, z_hi, z_lo, ends, powers]
        *messages, spectrum, a, b = pl.pallas_call(
            functools.partial(forward_kernel, u, counts + (n_grid - 1,)),
            out_shape=[lines] * (n_grid - 1) + [jax.ShapeDtypeStruct(cube, f32), lines, lines],
            in_specs=[VM] * len(inputs) + [ANY] * len(last),
            out_specs=[VM] * (n_grid + 2),
            scratch_shapes=[wide],
            name=f"forward_{u}",
            compiler_params=grant(16),
        )(*inputs, *last)
        last = (spectrum,)
        solved.append((spectrum, a, b, [cross(m, k) for k, m in enumerate(messages, 1)]))

    terms, last = [], ()
    for u, (spectrum, a, b, received) in enumerate(solved):
        inputs = [*base_own, *base_other, *received, y_hi, y_lo, zt_hi, zt_lo, inverse, basis, powers, steady,
                  spectrum, a, b]
        terms.append(pl.pallas_call(
            functools.partial(backward_kernel, u, (CHUNKS, CHUNKS, len(received))),
            out_shape=jax.ShapeDtypeStruct((planes, width), f32),
            in_specs=[SM] + [VM] * len(inputs) + [ANY] * len(last),
            out_specs=VM,
            scratch_shapes=[pltpu.VMEM(cube, f32), wide],
            name=f"backward_{u}",
            compiler_params=grant(16),
        )(flags, *inputs, *last))
        last = (terms[-1],)

    near_1 = [swap(term, 2, 4) for term in terms]
    near_2 = [swap(term, 4, 2) for term in terms]
    own_parts = [[term, x, y] for term, x, y in zip(terms, near_1, near_2)]
    sib_parts = [[swap(v, 1, 1) for v in group] for group in own_parts]

    def place(target, groups):
        parts = [part for group in groups for part in group]
        return pl.pallas_call(
            functools.partial(place_kernel, 8),
            out_shape=pltpu.HBM(shape, f32),
            in_specs=[SM] + [VM] * len(parts) + [HBM],
            out_specs=HBM,
            input_output_aliases={len(parts) + 1: 0},
            scratch_shapes=[pltpu.VMEM((blocks, 2, pair, planes, width), f32), DMA((blocks, 2))],
            name="place",
            compiler_params=grant(8),
        )(match, *parts, target)

    def place_near(target, mine, sibs):
        return place(target, [a + b for a, b in zip(mine, sibs)])

    def place_far(target, mine, sibs):
        far = [swap(group[1], 4, 2) for group in mine]
        return place(target, [a + [x] + b + [swap(x, 1, 1)] for a, b, x in zip(mine, sibs, far)])

    return lax.cond(alone[0] != 0, place_far, place_near, empty, own_parts, sib_parts)


def sine_table(length):
    wave_index = jnp.arange(length, dtype=f32) + 1.0
    return jnp.sqrt(2.0 / (length + 1.0)) * jnp.sin(
        jnp.pi * wave_index[:, None] * wave_index[None, :] / (length + 1.0)
    )


def eigen_values(length):
    wave_index = jnp.arange(length, dtype=f32) + 1.0
    return 2.0 - 2.0 * jnp.cos(jnp.pi * wave_index / (length + 1.0))


def green_kernel(size_x, size_y, size_z):
    summed = (
        eigen_values(size_x)[:, None, None]
        + eigen_values(size_y)[None, :, None]
        + eigen_values(size_z)[None, None, :]
    )
    return COUPLING / (summed + SCREENING)


def pair_lists(tile_list, pair_mask):
    within = jnp.arange(BLK * BLK, dtype=jnp.int32)
    targets = (BLK * tile_list[:, 0:1] + within[None, :] // BLK).reshape(-1)
    sources = (BLK * tile_list[:, 1:2] + within[None, :] % BLK).reshape(-1)
    return (targets, sources, pair_mask[targets, sources])


def compact(targets, sources, live_flags, number):
    ranking = jnp.cumsum(live_flags) - 1
    places = jnp.where(live_flags == 1, ranking, number)
    picked = (
        jnp.zeros((number,), jnp.int32)
        .at[places]
        .set(jnp.arange(live_flags.shape[0], dtype=jnp.int32), mode="drop")
    )
    return (targets[picked], sources[picked])


def along_z(values, matrix):
    number, planes, width_yz = values.shape
    size_z = matrix.shape[0]
    shaped = values.reshape(number, planes, width_yz // size_z, size_z)
    return jnp.einsum("pxrz,zk->pxrk", shaped, matrix, precision=precise).reshape(number, planes, width_yz)


def along_y(values, matrix):
    number, planes, width_yz = values.shape
    size_y = matrix.shape[0]
    shaped = values.reshape(number, planes, size_y, width_yz // size_y)
    return jnp.einsum("pxyz,yk->pxkz", shaped, matrix, precision=precise).reshape(number, planes, width_yz)


def along_x(values, matrix):
    return jnp.einsum("pxc,xk->pkc", values, matrix, precision=precise)


def any_device(orbitals, rotation, tile_list, pair_mask):
    n_orb, n_grid = lax.axis_size("orb"), lax.axis_size("grid")
    number_orbitals, size_x = rotation.shape[0], orbitals.shape[1] * n_grid
    rotated = jnp.einsum(
        "ij,ixc->jxc",
        rotation,
        lax.all_to_all(orbitals, "orb", split_axis=2, concat_axis=0, tiled=True),
        precision=precise,
    )
    planes, width_yz = rotated.shape[1:]
    targets, sources, live_flags = pair_lists(tile_list, pair_mask)
    matrix_x, matrix_y, matrix_z = sine_table(size_x), sine_table(NY), sine_table(NZ)
    kernel = green_kernel(size_x, NY, NZ).reshape(size_x, NY * NZ)
    orbital_ids = jnp.arange(number_orbitals, dtype=jnp.int32)
    targets, sources = compact(targets, sources, live_flags, targets.shape[0] // 2)
    density = rotated[targets] * rotated[sources]
    number = density.shape[0]
    spectrum = along_z(density, matrix_z)
    spectrum = lax.all_to_all(spectrum, "orb", split_axis=0, concat_axis=2, tiled=True)
    spectrum = along_y(spectrum, matrix_y)
    spectrum = lax.all_to_all(spectrum, "grid", split_axis=0, concat_axis=1, tiled=True)
    spectrum = along_x(along_x(spectrum, matrix_x) * kernel, matrix_x)
    spectrum = lax.all_to_all(spectrum, "grid", split_axis=1, concat_axis=0, tiled=True)
    spectrum = along_y(spectrum, matrix_y)
    spectrum = lax.all_to_all(spectrum, "orb", split_axis=2, concat_axis=0, tiled=True)
    potential = along_z(spectrum, matrix_z)
    products = potential * rotated[sources]
    selector = (targets[None, :] == orbital_ids[:, None]).astype(f32)
    partial_value = -jnp.dot(selector, products.reshape(number, planes * width_yz), precision=precise)
    partial_value = partial_value.reshape(number_orbitals, planes, width_yz)
    return lax.all_to_all(partial_value, "orb", split_axis=0, concat_axis=2, tiled=True)


def solution(mesh):
    n_orb, n_grid = mesh.shape["orb"], mesh.shape["grid"]

    def on_device(orbitals, rotation, tile_list, pair_mask):
        per_device, planes, width = orbitals.shape
        fits = n_orb == 8 and 2 * tile_list.shape[0] == n_orb and planes == SUB and per_device % BLK == 0
        fits = fits and width == NY * NZ and 2 * NZ == LANES and n_grid in (2, 4, 8)
        fits = fits and per_device * SUB == LANES and rotation.shape == (LANES, LANES)
        body = tile_device if fits else any_device
        return body(orbitals, rotation, tile_list, pair_mask)

    in_specs = (P("orb", "grid", None), P(), P(), P())
    out_specs = P("orb", "grid", None)
    return jax.shard_map(on_device, mesh=mesh, in_specs=in_specs, out_specs=out_specs, check_vma=False)
```

```python
import functools
import itertools

import jax
import jax.numpy as jnp
import numpy as np
from jax import lax
from jax.experimental import pallas as pl
from jax.experimental.pallas import tpu as pltpu
from jax.sharding import PartitionSpec as P


BLK = 4
NY = 64
NZ = 64
LANES = 128
SUB = 8
CHUNKS = 2
COUPLING = 0.25
SCREENING = 0.1

precise = lax.Precision.HIGHEST
f32 = jnp.float32
bf16 = jnp.bfloat16

VM = pl.BlockSpec(memory_space=pltpu.VMEM)
SM = pl.BlockSpec(memory_space=pltpu.SMEM)
ANY = pl.BlockSpec(memory_space=pl.ANY)
HBM = pl.BlockSpec(memory_space=pltpu.HBM)
DMA = pltpu.SemaphoreType.DMA


def grant(mib):
    return pltpu.CompilerParams(vmem_limit_bytes=mib << 20)


def sine_np(n):
    k = np.arange(1, n + 1, dtype=np.float64)
    return np.sqrt(2.0 / (n + 1)) * np.sin(np.pi * k[:, None] * k[None, :] / (n + 1))


def eigen_np(n):
    k = np.arange(1, n + 1, dtype=np.float64)
    return 2.0 - 2.0 * np.cos(np.pi * k / (n + 1))


def halves_np(table):
    high = np.asarray(table, np.float32).astype(jnp.bfloat16)
    low = (np.asarray(table, np.float64) - high.astype(np.float64)).astype(jnp.bfloat16)
    return jnp.asarray(high), jnp.asarray(low)


def y_order():
    rows = LANES // NZ
    return np.arange(NY).reshape(NY // rows, rows).T.reshape(-1)


def y_table():
    order = y_order()
    return np.kron(sine_np(NY)[order][:, order], sine_np(SUB))


def z_table():
    half = LANES // NZ
    sine = sine_np(NZ)
    table = np.zeros((2, half, NZ, half, 2, NZ))
    for pair in range(2):
        for h in range(half):
            table[pair, h, :, h, pair, :] = sine
    return table.reshape(2 * half * NZ, half * 2 * NZ)


def line_np():
    c = eigen_np(NY)[y_order()][:, None] + eigen_np(NZ)[None, :] + SCREENING
    c = np.concatenate([c, c], axis=1)
    return c, 2.0 / (2.0 + c + np.sqrt(c * (c + 4.0)))


def host_np(chips):
    table = np.zeros((chips**chips, chips), np.int32)
    for owners in itertools.product(range(chips), repeat=chips):
        best = None
        for tiles in itertools.permutations(range(chips)):
            hops = [bin(chip ^ owners[tile]).count("1") for chip, tile in enumerate(tiles)]
            cost = (max(hops), sum(hops))
            if best is None or cost < best[0]:
                best = (cost, tiles)
        table[sum(own * chips**t for t, own in enumerate(owners))] = best[1]
    return table


def dot(a, b):
    return jnp.dot(a, b, preferred_element_type=f32)


def split(x):
    high = x.astype(bf16)
    return high, (x - high.astype(f32)).astype(bf16)


def dot3(a, b):
    return dot(a[0], b[0]) + dot(a[0], b[1]) + dot(a[1], b[0])


def my_core():
    return lax.rem(lax.axis_index("orb"), 2)


def my_place():
    o = lax.axis_index("orb")
    return o, lax.rem(o, 2), lax.div(o, 2)


def fetch(source, out, sem, side, start, number):
    at = pl.multiple_of(side * (source.shape[2] // 2) + start, LANES)
    step = out.shape[0] // number
    return [
        pltpu.make_async_copy(
            source.at[pl.ds(n * step, step), :, pl.ds(at, out.shape[2])], out.at[pl.ds(n * step, step)], sem.at[n]
        )
        for n in range(number)
    ]


def take_kernel(start, source, *rest):
    out, sem = rest[-2:]
    copies = fetch(source, out, sem, 1 - my_core(), start, sem.shape[0])
    for copy in copies:
        copy.start()
    for copy in copies:
        copy.wait()


class Place:
    def __init__(self, per_device, tiles, host):
        self.o, self.core, self.chip = my_place()
        self.tiles, self.host = tiles, host
        self.chips = tiles.shape[0]
        owners = [lax.div(tiles[t, 0] * BLK, 2 * per_device) for t in range(self.chips)]
        key, same = 0, True
        for t in range(self.chips):
            key = key + owners[t] * self.chips**t
            same = same & (owners[t] == owners[0])
        self.key, self.same = key, same
        self.bit_1 = jnp.where(self.core == 0, 1, 2)
        self.bit_2 = 3 - self.bit_1

    def tile(self, chip):
        return self.host[self.key * self.chips + chip]

    def heads(self, chip):
        tile = self.tile(chip)
        return BLK * self.tiles[tile, 0], BLK * self.tiles[tile, 1]


def setup_kernel(per_device, tiles, host, rotation, source, after, *rest):
    count = len(rest) - 3
    mine, (high, low, sem) = rest[:count], rest[count:]
    core = my_core()
    copies = []
    for n, out in enumerate(mine):
        copies += fetch(source, out, sem.at[n], core, n * out.shape[2], sem.shape[1])
    for copy in copies:
        copy.start()
    at = Place(per_device, tiles, host)
    pair = BLK // 2
    heads = [at.heads(chip) for chip in (at.chip ^ 3, at.chip ^ at.bit_1, at.chip ^ at.bit_2, at.chip)]
    wanted = []
    for a, b in heads:
        wanted += [a + (1 - core) * pair] + [b + w for w in range(BLK)] + [a + core * pair]
    for u in range(1, pair):
        for a, b in heads:
            wanted += [a + (1 - core) * pair + u, a + core * pair + u]
    lane = lax.broadcasted_iota(jnp.int32, (SUB, LANES), 1)
    chosen = jnp.concatenate([jnp.where(lane == n, 1.0, 0.0) for n in wanted]).astype(bf16)
    rows = chosen.shape[0]
    row = lax.broadcasted_iota(jnp.int32, (LANES, LANES), 0)
    column = lax.broadcasted_iota(jnp.int32, (LANES, LANES), 1)
    columns = [
        jnp.where(row - (at.o ^ e) * per_device == jnp.right_shift(column, 3), 1.0, 0.0).astype(bf16)
        for e in range(2)
    ]
    keep = (lax.broadcasted_iota(jnp.int32, (rows, LANES), 0) & (SUB - 1)) == (
        lax.broadcasted_iota(jnp.int32, (rows, LANES), 1) & (SUB - 1)
    )
    for out, values in zip((high, low), split(rotation[...])):
        picked = lax.dot_general(chosen, values, (((1,), (1,)), ((), ())), preferred_element_type=f32).astype(bf16)
        for e in range(2):
            out[:, e * LANES:(e + 1) * LANES] = jnp.where(keep, dot(picked, columns[e]), 0.0).astype(bf16)
    for copy in copies:
        copy.wait()


def ready_kernel(per_device, n_grid, tiles, host, mask, log_r, *rest):
    out, powers, flags, match, alone, zeros, sem = rest[-7:]
    zeros[...] = jnp.zeros(zeros.shape, f32)
    step = zeros.shape[0]
    copies = [
        pltpu.make_async_copy(zeros, out.at[pl.ds(n * step, step)], sem.at[n]) for n in range(out.shape[0] // step)
    ]
    for copy in copies:
        copy.start()
    begin, size_x = SUB * lax.axis_index("grid"), SUB * n_grid
    exponents = (
        2 * begin + SUB + 1,
        2 * size_x + 1 - SUB - 2 * begin,
        2 * size_x + 2 - 2 * begin,
        2 * begin,
        2 * begin + 2 * SUB + 2,
        2 * size_x - 2 * SUB - 2 * begin,
    )
    for n, exponent in enumerate(exponents):
        power = jnp.exp(exponent.astype(f32) * log_r[...])
        powers[n] = power if n < 2 else 1.0 - power
    at = Place(per_device, tiles, host)
    alone[0] = at.same.astype(jnp.int32)
    a, b = at.heads(at.chip)
    pair = BLK // 2
    live = mask[...].astype(f32)
    row = lax.broadcasted_iota(jnp.int32, live.shape, 0)
    column = lax.broadcasted_iota(jnp.int32, (1, live.shape[1]), 1)
    for u in range(pair):
        line = jnp.sum(jnp.where(row == a + at.core * pair + u, live, 0.0), axis=0, keepdims=True)
        for w in range(BLK):
            flags[u * BLK + w] = jnp.sum(jnp.where(column == b + w, line, 0.0))
    blocks = per_device // BLK
    parts = [0, at.bit_1, at.bit_2, 3, 0, at.bit_2, at.bit_1, 3]
    for n, flip in enumerate(parts):
        home = tiles[at.tile(at.chip ^ flip), 0]
        for block in range(blocks):
            hit = home == at.o * blocks + block
            if n % 4 == 3:
                hit = hit & at.same
            match[block * len(parts) + n] = hit.astype(jnp.int32)
    for copy in copies:
        copy.wait()


def join_kernel(x, y, out):
    out[0] = x[...]
    out[1] = y[...]


def rotate_kernel(first, high, low, *rest):
    send, keep = rest[-2:]
    rows = send.shape[0] * SUB
    part = pl.ds(first, 2 * rows)
    table = (high[part, :], low[part, :])
    at = 0
    step = 2 * LANES
    while at < send.shape[2]:
        width = rest[0].shape[2]
        n, inner = at // width, at % width
        lanes = slice(inner, inner + step)
        mine, theirs = rest[2 * n], rest[2 * n + 1]
        depth = mine.shape[0] * SUB
        cells = jnp.concatenate([mine[:, :, lanes].reshape(depth, step), theirs[:, :, lanes].reshape(depth, step)])
        total = dot3(table, split(cells))
        lanes = slice(at, at + step)
        send[:, :, lanes] = total[:rows].reshape(send.shape[0], SUB, step)
        keep[:, :, lanes] = total[rows:].reshape(keep.shape[0], SUB, step)
        at += step


def pass_kernel(keep, got, *rest):
    out = rest[-1]
    count = out.shape[0]
    out[...] = keep[:count] + got[:count]


def finish_kernel(keep, got, passed, *rest):
    out = rest[-1]
    count = out.shape[0]
    out[...] = keep[count:] + got[count:] + passed[...]


def sub_sums(values):
    row = lax.broadcasted_iota(jnp.int32, values[0].shape, 0)
    for s in (4, 2):
        low = (row & s) == 0
        paired = []
        for n in range(s):
            a, b = values[n], values[n + s]
            paired.append(jnp.where(low, a, pltpu.roll(b, s, 0)) + jnp.where(low, pltpu.roll(a, SUB - s, 0), b))
        values = paired
    even = (row & 1) == 0
    a, b = values
    return jnp.where(even, a, pltpu.roll(b, 1, 0)), jnp.where(even, pltpu.roll(a, SUB - 1, 0), b)


def fields(u, own, other, first_own, first_other):
    table = []
    for side, sources, targets in ((0, first_own, own), (1, first_other, other)):
        for n, ref in enumerate(sources):
            if u == 0:
                table.append((side, n, ref, targets[n], BLK + 1 if side == 0 else 0, 0))
            else:
                table.append((side, n, ref, targets[0], 1 if side == 0 else 0, n * ref.shape[2]))
    return table


def forward_kernel(u, counts, *refs):
    groups = []
    for count in counts[:-1]:
        groups.append(refs[:count])
        refs = refs[count:]
    first_own, first_other, own, other = groups[:4]
    y_hi, y_lo, z_hi, z_lo, ends, powers = refs[:6]
    messages, (spectrum, a_out, b_out, dens) = refs[-4 - counts[-1]:-4], refs[-4:]
    if u == 0:
        own, other = first_own, first_other
    core, g = my_core(), lax.axis_index("grid")
    tiles = first_own[0].shape[2] // LANES
    for side, n, source, target, slot, offset in fields(u, own, other, first_own, first_other):
        half = (core if side == 0 else 1 - core) * (len(first_own) * tiles * SUB)
        for t in range(tiles):
            lanes = pl.ds(t * LANES, LANES)
            value = target[slot, :, pl.ds(offset + t * LANES, LANES)]
            rows = pl.ds(pl.multiple_of(half + (n * tiles + t) * SUB, SUB), SUB)
            for w in range(BLK):
                dens[rows, w * LANES:(w + 1) * LANES] = value * source[1 + w, :, lanes]
    z = (z_hi[...], z_lo[...])
    half = dens.shape[0]
    for q in range(BLK // 2):
        out = dot3(split(dens[:, q * 2 * LANES:(q + 1) * 2 * LANES]), z)
        spectrum[:half, q * LANES:(q + 1) * LANES] = out[:, :LANES]
        spectrum[half:, q * LANES:(q + 1) * LANES] = out[:, LANES:]
    spectrum[...] = dot3((y_hi[...], y_lo[...]), split(spectrum[...]))

    def reduce(group, carry):
        lines = pl.ds(pl.multiple_of(group * SUB, SUB), SUB)
        near, far = powers[0, lines, :], powers[1, lines, :]
        for q in range(BLK // 2):
            lanes = slice(q * LANES, (q + 1) * LANES)
            values = []
            for k in range(SUB):
                rows = pl.ds(pl.multiple_of((group * SUB + k) * SUB, SUB), SUB)
                values.append(ends[rows, :] * spectrum[rows, lanes])
            even, odd = sub_sums(values)
            rightward = (even + odd) - near * (even - odd)
            leftward = (even - odd) - far * (even + odd)
            a_out[lines, lanes] = rightward
            b_out[lines, lanes] = leftward
            for k, out in enumerate(messages, 1):
                out[lines, lanes] = jnp.where((g ^ k) > g, rightward, leftward)
        return carry

    lax.fori_loop(0, NY // SUB, reduce, 0)


def backward_kernel(u, counts, flags, *refs):
    groups = []
    for count in counts:
        groups.append(refs[:count])
        refs = refs[count:]
    own, other, received = groups
    (y_hi, y_lo, z_hi, z_lo, inverse, basis, powers, steady, spectrum, a_in, b_in) = refs[:11]
    out, work, pot = refs[-3:]
    core, g = my_core(), lax.axis_index("grid")
    tiles = own[0].shape[2] // LANES
    first, last = basis[0], basis[1]

    def ends(group, carry):
        lines = pl.ds(pl.multiple_of(group * SUB, SUB), SUB)
        scale, r, slab = steady[0, lines, :], steady[1, lines, :], steady[2, lines, :]
        decays = [None, jnp.ones((SUB, LANES), f32), slab]
        while len(decays) <= len(received):
            decays.append(decays[-1] * slab)
        for q in range(BLK // 2):
            lanes = slice(q * LANES, (q + 1) * LANES)
            from_left = from_right = jnp.zeros((SUB, LANES), f32)
            for n, ref in enumerate(received, 1):
                distance = jnp.abs((g ^ n) - g)
                factor = decays[n]
                for d in range(1, n):
                    factor = jnp.where(distance == d, decays[d], factor)
                value = factor * ref[lines, lanes]
                is_left = (g ^ n) < g
                from_left = from_left + jnp.where(is_left, value, 0.0)
                from_right = from_right + jnp.where(is_left, 0.0, value)
            before = scale * (powers[2, lines, :] * from_left
                              + r * powers[3, lines, :] * (b_in[lines, lanes] + slab * from_right))
            after = scale * (powers[4, lines, :] * from_right
                             + r * powers[5, lines, :] * (a_in[lines, lanes] + slab * from_left))
            for k in range(SUB):
                rows = pl.ds(pl.multiple_of((group * SUB + k) * SUB, SUB), SUB)
                edge = first * before[k:k + 1] + last * after[k:k + 1]
                work[rows, lanes] = inverse[rows, :] * (spectrum[rows, lanes] + edge)
        return carry

    lax.fori_loop(0, NY // SUB, ends, 0)
    work[...] = dot3((y_hi[...], y_lo[...]), split(work[...]))
    z = (z_hi[...], z_lo[...])
    half = pot.shape[0]
    for q in range(BLK // 2):
        lanes = slice(q * LANES, (q + 1) * LANES)
        rows = jnp.concatenate([work[:half, lanes], work[half:, lanes]], axis=1)
        pot[:, q * 2 * LANES:(q + 1) * 2 * LANES] = dot3(split(rows), z)
    for side, group in ((0, own), (1, other)):
        half = (core if side == 0 else 1 - core) * (len(own) * tiles)
        for n, ref in enumerate(group):
            for t in range(tiles):
                lanes = pl.ds(t * LANES, LANES)
                at = half + n * tiles + t
                rows = pl.ds(pl.multiple_of(at * SUB, SUB), SUB)
                total = None
                for w in range(BLK):
                    term = flags[u * BLK + w] * (pot[rows, w * LANES:(w + 1) * LANES] * ref[1 + w, :, lanes])
                    total = term if total is None else total + term
                out[:, pl.ds(pl.multiple_of(at * LANES, LANES), LANES)] = -total


def place_kernel(stride, match, *refs):
    parts, (out, rows, sem) = refs[:-4], refs[-3:]
    pair = BLK // 2
    blocks = out.shape[0] // BLK
    core = my_core()
    values = []
    for part in parts:
        values += [part] if len(part.shape) == 2 else [part.at[n] for n in range(part.shape[0])]
    parts, count = values, len(values) // pair

    def hits(b, side):
        return [(match[b * stride + side * stride // 2 + n], side * count // 2 + n) for n in range(count // 2)]

    def found(b, side):
        return sum(hit for hit, n in hits(b, side)) > 0

    def move(b, side):
        which = core if side == 0 else 1 - core
        at = b * BLK + which * pair
        return pltpu.make_async_copy(rows.at[b, side], out.at[pl.ds(at, pair)], sem.at[b, side])

    for b in range(blocks):
        for side in range(2):

            @pl.when(found(b, side))
            def _():
                rows[b, side] = jnp.zeros(rows.shape[2:], f32)
                for hit, n in hits(b, side):

                    @pl.when(hit > 0)
                    def _():
                        for u in range(pair):
                            rows[b, side, u] += parts[u * count + n][...]

                move(b, side).start()

    for b in range(blocks):
        for side in range(2):

            @pl.when(found(b, side))
            def _():
                move(b, side).wait()


def tile_device(orbitals, rotation, tile_list, pair_mask):
    shape = per_device, planes, width = orbitals.shape
    n_orb, n_grid = lax.axis_size("orb"), lax.axis_size("grid")
    size_x = planes * n_grid
    half = width // 2
    chips = n_orb // 2
    axes = ("orb", "grid")

    def swap(x, even, odd):
        moves = []
        for a in range(n_orb):
            flip = even if a % 2 == 0 else odd
            moves += [(a * n_grid + b, (a ^ flip) * n_grid + b) for b in range(n_grid)]
        return lax.ppermute(x, axes, moves)

    def cross(x, k):
        moves = [(a * n_grid + b, a * n_grid + (b ^ k)) for a in range(n_orb) for b in range(n_grid)]
        return lax.ppermute(x, axes, moves)

    chunk = half // CHUNKS
    orbitals = pltpu.with_memory_space_constraint(orbitals, pltpu.HBM)

    part = jax.ShapeDtypeStruct((per_device, planes, chunk), f32)
    copies = per_device // 2
    theirs, last = [], ()
    for n in range(CHUNKS):
        taken = pl.pallas_call(
            functools.partial(take_kernel, n * chunk), out_shape=part, in_specs=[HBM] + [ANY] * len(last), out_specs=VM,
            scratch_shapes=[DMA((copies,))], compiler_params=grant(4),
        )(orbitals, *last)
        theirs.append(swap(taken, 1, 1))
        last = (taken,)

    pair = BLK // 2
    firsts = (BLK + 2) * chips
    rows = (firsts + 2 * (pair - 1) * chips) * SUB
    wide_table = jax.ShapeDtypeStruct((rows, 2 * LANES), bf16)
    blocks = per_device // BLK
    c, r = line_np()
    c, r = line_np()
    host = jnp.asarray(host_np(chips).reshape(-1))
    *mine, high, low = pl.pallas_call(
        functools.partial(setup_kernel, per_device),
        out_shape=[part] * CHUNKS + [wide_table] * 2,
        in_specs=[SM, SM, VM, HBM, ANY], out_specs=[VM] * (CHUNKS + 2),
        scratch_shapes=[DMA((CHUNKS, copies))], name="setup", compiler_params=grant(6),
    )(tile_list, host, rotation, orbitals, *last)

    def rotate(first, count, fields, *after):
        part = jax.ShapeDtypeStruct((count, planes, chunk * (len(fields) // 2)), f32)
        send, keep = pl.pallas_call(
            functools.partial(rotate_kernel, first * SUB), out_shape=(part, part),
            in_specs=[VM] * (2 + len(fields)) + [ANY] * len(after),
            out_specs=(VM, VM), compiler_params=grant(8),
        )(high, low, *fields, *after)
        return send, keep, swap(send, 2, 4)

    sums, last = [], ()
    for n in range(CHUNKS):
        sums.append(rotate(0, firsts // 2, [mine[n], theirs[n]], *last))
        last = (sums[-1][0],)
    both = [x for n in range(CHUNKS) for x in (mine[n], theirs[n])]
    sums.append(rotate(firsts, (pair - 1) * chips, both, *last))
    empty, powers, flags, match, alone = pl.pallas_call(
        functools.partial(ready_kernel, per_device, n_grid),
        out_shape=(pltpu.HBM(shape, f32), jax.ShapeDtypeStruct((6, NY, LANES), f32),
                   jax.ShapeDtypeStruct((pair * BLK,), f32), jax.ShapeDtypeStruct((blocks * 8,), jnp.int32),
                   jax.ShapeDtypeStruct((1,), jnp.int32)),
        in_specs=[SM, SM, VM, VM, ANY], out_specs=(HBM, VM, SM, SM, SM),
        scratch_shapes=[pltpu.VMEM((pair, planes, width), f32), DMA((per_device // pair,))], name="ready",
        compiler_params=grant(4),
    )(tile_list, host, pair_mask, jnp.asarray(np.log(r), f32), sums[-1][0])
    passing, own, other = [], [], []

    def pass_on(n, *after, spec=ANY):
        _, keep, got = sums[n]
        count = keep.shape[0] // 2
        value = pl.pallas_call(
            pass_kernel, out_shape=jax.ShapeDtypeStruct((count,) + keep.shape[1:], f32),
            in_specs=[VM] * 2 + [spec] * len(after), out_specs=VM, compiler_params=grant(4),
        )(keep, got, *after)
        passing.append((keep, got, swap(value, 4, 2)))
        return value

    def finish(n, *after):
        keep, got, passed = passing[n]
        own.append(pl.pallas_call(
            finish_kernel, out_shape=jax.ShapeDtypeStruct(passed.shape, f32), in_specs=[VM] * 3 + [ANY] * len(after),
            out_specs=VM, compiler_params=grant(4),
        )(keep, got, passed, *after))
        other.append(swap(own[-1], 1, 1))
        return own[-1]

    step = pass_on(0, empty, spec=HBM)
    for n in range(1, CHUNKS):
        step = pass_on(n, step)
    step = finish(0, step)
    step = pass_on(CHUNKS, step)
    for n in range(1, CHUNKS):
        step = finish(n, step)

    sine_x, eigen_x = sine_np(planes), eigen_np(planes)
    ends = jnp.asarray(np.einsum("jp,pkl->kjl", sine_x, r[None] ** np.arange(planes - 1, -1, -1)[:, None, None])
                       .reshape(-1, LANES), f32)
    inverse = jnp.asarray((COUPLING / (eigen_x[None, :, None] + c[:, None, :])).reshape(-1, LANES), f32)
    basis = jnp.asarray(np.broadcast_to(sine_x[:, [0, -1]].T[:, :, None], (2, planes, LANES)), f32)
    steady = jnp.asarray(np.stack([r / ((1 - r**2) * (1 - r ** (2 * size_x + 2))), r, r**planes]), f32)

    y_hi, y_lo = halves_np(y_table())
    z_hi, z_lo = halves_np(z_table())
    zt_hi, zt_lo = halves_np(z_table().T)
    solved = []
    lines = jax.ShapeDtypeStruct((NY, 2 * LANES), f32)
    cube = (NY * SUB, 2 * LANES)
    wide = pltpu.VMEM((width // LANES * SUB, BLK * LANES), f32)
    base_own, base_other = own[:CHUNKS], other[:CHUNKS]
    last = ()
    for u in range(pair):
        if u:
            finish(CHUNKS, *last)
        more_own, more_other = own[CHUNKS:][:u], other[CHUNKS:][:u]
        counts = (CHUNKS, CHUNKS, len(more_own), len(more_other))
        inputs = [*base_own, *base_other, *more_own, *more_other, y_hi, y_lo, z_hi, z_lo, ends, powers]
        *messages, spectrum, a, b = pl.pallas_call(
            functools.partial(forward_kernel, u, counts + (n_grid - 1,)),
            out_shape=[lines] * (n_grid - 1) + [jax.ShapeDtypeStruct(cube, f32), lines, lines],
            in_specs=[VM] * len(inputs) + [ANY] * len(last),
            out_specs=[VM] * (n_grid + 2),
            scratch_shapes=[wide],
            compiler_params=grant(16),
        )(*inputs, *last)
        last = (spectrum,)
        solved.append((spectrum, a, b, [cross(m, k) for k, m in enumerate(messages, 1)]))

    terms, last = [], ()
    for u, (spectrum, a, b, received) in enumerate(solved):
        inputs = [*base_own, *base_other, *received, y_hi, y_lo, zt_hi, zt_lo, inverse, basis, powers, steady,
                  spectrum, a, b]
        terms.append(pl.pallas_call(
            functools.partial(backward_kernel, u, (CHUNKS, CHUNKS, len(received))),
            out_shape=jax.ShapeDtypeStruct((planes, width), f32),
            in_specs=[SM] + [VM] * len(inputs) + [ANY] * len(last),
            out_specs=VM,
            scratch_shapes=[pltpu.VMEM(cube, f32), wide],
            compiler_params=grant(16),
        )(flags, *inputs, *last))
        last = (terms[-1],)

    near_1 = [swap(term, 2, 4) for term in terms]
    near_2 = [swap(term, 4, 2) for term in terms]
    own_parts = [[term, x, y] for term, x, y in zip(terms, near_1, near_2)]
    sib_parts = []
    for term, x, y in own_parts:
        joined = pl.pallas_call(
            join_kernel, out_shape=jax.ShapeDtypeStruct((2,) + term.shape, f32), in_specs=[VM] * 2, out_specs=VM,
            compiler_params=grant(4),
        )(x, y)
        sib_parts.append([swap(term, 1, 1), swap(joined, 1, 1)])

    def place(target, groups):
        parts = [part for group in groups for part in group]
        return pl.pallas_call(
            functools.partial(place_kernel, 8),
            out_shape=pltpu.HBM(shape, f32),
            in_specs=[SM] + [VM] * len(parts) + [HBM],
            out_specs=HBM,
            input_output_aliases={len(parts) + 1: 0},
            scratch_shapes=[pltpu.VMEM((blocks, 2, pair, planes, width), f32), DMA((blocks, 2))],
            name="place",
            compiler_params=grant(8),
        )(match, *parts, target)

    def place_near(target, mine, sibs):
        return place(target, [a + b for a, b in zip(mine, sibs)])

    def place_far(target, mine, sibs):
        far = [swap(group[1], 4, 2) for group in mine]
        return place(target, [a + [x] + b + [swap(x, 1, 1)] for a, b, x in zip(mine, sibs, far)])

    return lax.cond(alone[0] != 0, place_far, place_near, empty, own_parts, sib_parts)


def sine_table(length):
    wave_index = jnp.arange(length, dtype=f32) + 1.0
    return jnp.sqrt(2.0 / (length + 1.0)) * jnp.sin(
        jnp.pi * wave_index[:, None] * wave_index[None, :] / (length + 1.0)
    )


def eigen_values(length):
    wave_index = jnp.arange(length, dtype=f32) + 1.0
    return 2.0 - 2.0 * jnp.cos(jnp.pi * wave_index / (length + 1.0))


def green_kernel(size_x, size_y, size_z):
    summed = (
        eigen_values(size_x)[:, None, None]
        + eigen_values(size_y)[None, :, None]
        + eigen_values(size_z)[None, None, :]
    )
    return COUPLING / (summed + SCREENING)


def pair_lists(tile_list, pair_mask):
    within = jnp.arange(BLK * BLK, dtype=jnp.int32)
    targets = (BLK * tile_list[:, 0:1] + within[None, :] // BLK).reshape(-1)
    sources = (BLK * tile_list[:, 1:2] + within[None, :] % BLK).reshape(-1)
    return (targets, sources, pair_mask[targets, sources])


def compact(targets, sources, live_flags, number):
    ranking = jnp.cumsum(live_flags) - 1
    places = jnp.where(live_flags == 1, ranking, number)
    picked = (
        jnp.zeros((number,), jnp.int32)
        .at[places]
        .set(jnp.arange(live_flags.shape[0], dtype=jnp.int32), mode="drop")
    )
    return (targets[picked], sources[picked])


def along_z(values, matrix):
    number, planes, width_yz = values.shape
    size_z = matrix.shape[0]
    shaped = values.reshape(number, planes, width_yz // size_z, size_z)
    return jnp.einsum("pxrz,zk->pxrk", shaped, matrix, precision=precise).reshape(number, planes, width_yz)


def along_y(values, matrix):
    number, planes, width_yz = values.shape
    size_y = matrix.shape[0]
    shaped = values.reshape(number, planes, size_y, width_yz // size_y)
    return jnp.einsum("pxyz,yk->pxkz", shaped, matrix, precision=precise).reshape(number, planes, width_yz)


def along_x(values, matrix):
    return jnp.einsum("pxc,xk->pkc", values, matrix, precision=precise)


def any_device(orbitals, rotation, tile_list, pair_mask):
    n_grid = lax.axis_size("grid")
    number_orbitals, size_x = rotation.shape[0], orbitals.shape[1] * n_grid
    rotated = jnp.einsum(
        "ij,ixc->jxc",
        rotation,
        lax.all_to_all(orbitals, "orb", split_axis=2, concat_axis=0, tiled=True),
        precision=precise,
    )
    planes, width_yz = rotated.shape[1:]
    targets, sources, live_flags = pair_lists(tile_list, pair_mask)
    matrix_x, matrix_y, matrix_z = sine_table(size_x), sine_table(NY), sine_table(NZ)
    kernel = green_kernel(size_x, NY, NZ).reshape(size_x, NY * NZ)
    orbital_ids = jnp.arange(number_orbitals, dtype=jnp.int32)
    targets, sources = compact(targets, sources, live_flags, targets.shape[0] // 2)
    density = rotated[targets] * rotated[sources]
    number = density.shape[0]
    spectrum = along_z(density, matrix_z)
    spectrum = lax.all_to_all(spectrum, "orb", split_axis=0, concat_axis=2, tiled=True)
    spectrum = along_y(spectrum, matrix_y)
    spectrum = lax.all_to_all(spectrum, "grid", split_axis=0, concat_axis=1, tiled=True)
    spectrum = along_x(along_x(spectrum, matrix_x) * kernel, matrix_x)
    spectrum = lax.all_to_all(spectrum, "grid", split_axis=1, concat_axis=0, tiled=True)
    spectrum = along_y(spectrum, matrix_y)
    spectrum = lax.all_to_all(spectrum, "orb", split_axis=2, concat_axis=0, tiled=True)
    potential = along_z(spectrum, matrix_z)
    products = potential * rotated[sources]
    selector = (targets[None, :] == orbital_ids[:, None]).astype(f32)
    partial_value = -jnp.dot(selector, products.reshape(number, planes * width_yz), precision=precise)
    partial_value = partial_value.reshape(number_orbitals, planes, width_yz)
    return lax.all_to_all(partial_value, "orb", split_axis=0, concat_axis=2, tiled=True)


def solution(mesh):
    n_orb, n_grid = mesh.shape["orb"], mesh.shape["grid"]

    def on_device(orbitals, rotation, tile_list, pair_mask):
        per_device, planes, width = orbitals.shape
        fits = n_orb == 8 and 2 * tile_list.shape[0] == n_orb and planes == SUB and per_device % BLK == 0
        fits = fits and width == NY * NZ and 2 * NZ == LANES and n_grid in (2, 4, 8)
        fits = fits and per_device * SUB == LANES and rotation.shape == (LANES, LANES)
        if not fits:
            return any_device(orbitals, rotation, tile_list, pair_mask)
        return tile_device(orbitals, rotation, tile_list, pair_mask)

    in_specs = (P("orb", "grid", None), P(), P(), P())
    out_specs = P("orb", "grid", None)
    return jax.shard_map(on_device, mesh=mesh, in_specs=in_specs, out_specs=out_specs, check_vma=False)
```

```python
import functools
import itertools

import jax
import jax.numpy as jnp
import numpy as np
from jax import lax
from jax.experimental import pallas as pl
from jax.experimental.pallas import tpu as pltpu
from jax.sharding import PartitionSpec as P


BLK = 4
NY = 64
NZ = 64
LANES = 128
SUB = 8
CHUNKS = 2
COUPLING = 0.25
SCREENING = 0.1

precise = lax.Precision.HIGHEST
f32 = jnp.float32
bf16 = jnp.bfloat16

VM = pl.BlockSpec(memory_space=pltpu.VMEM)
SM = pl.BlockSpec(memory_space=pltpu.SMEM)
ANY = pl.BlockSpec(memory_space=pl.ANY)
HBM = pl.BlockSpec(memory_space=pltpu.HBM)
DMA = pltpu.SemaphoreType.DMA


def grant(mib):
    return pltpu.CompilerParams(vmem_limit_bytes=mib << 20)


def sine_np(n):
    k = np.arange(1, n + 1, dtype=np.float64)
    return np.sqrt(2.0 / (n + 1)) * np.sin(np.pi * k[:, None] * k[None, :] / (n + 1))


def eigen_np(n):
    k = np.arange(1, n + 1, dtype=np.float64)
    return 2.0 - 2.0 * np.cos(np.pi * k / (n + 1))


def halves_np(table):
    high = np.asarray(table, np.float32).astype(jnp.bfloat16)
    low = (np.asarray(table, np.float64) - high.astype(np.float64)).astype(jnp.bfloat16)
    return jnp.asarray(high), jnp.asarray(low)


def y_order():
    rows = LANES // NZ
    return np.arange(NY).reshape(NY // rows, rows).T.reshape(-1)


def y_table():
    order = y_order()
    return np.kron(sine_np(NY)[order][:, order], sine_np(SUB))


def z_table():
    half = LANES // NZ
    sine = sine_np(NZ)
    table = np.zeros((2, half, NZ, half, 2, NZ))
    for pair in range(2):
        for h in range(half):
            table[pair, h, :, h, pair, :] = sine
    return table.reshape(2 * half * NZ, half * 2 * NZ)


def line_np():
    c = eigen_np(NY)[y_order()][:, None] + eigen_np(NZ)[None, :] + SCREENING
    c = np.concatenate([c, c], axis=1)
    return c, 2.0 / (2.0 + c + np.sqrt(c * (c + 4.0)))


def host_np(chips):
    table = np.zeros((chips**chips, chips), np.int32)
    for owners in itertools.product(range(chips), repeat=chips):
        best = None
        for tiles in itertools.permutations(range(chips)):
            hops = [bin(chip ^ owners[tile]).count("1") for chip, tile in enumerate(tiles)]
            cost = (max(hops), sum(hops))
            if best is None or cost < best[0]:
                best = (cost, tiles)
        table[sum(own * chips**t for t, own in enumerate(owners))] = best[1]
    return table


def dot(a, b):
    return jnp.dot(a, b, preferred_element_type=f32)


def split(x):
    high = x.astype(bf16)
    return high, (x - high.astype(f32)).astype(bf16)


def dot3(a, b):
    return dot(a[0], b[0]) + dot(a[0], b[1]) + dot(a[1], b[0])


def my_core():
    return lax.rem(lax.axis_index("orb"), 2)


def my_place():
    o = lax.axis_index("orb")
    return o, lax.rem(o, 2), lax.div(o, 2)


def fetch(source, out, sem, side, start, number):
    at = pl.multiple_of(side * (source.shape[2] // 2) + start, LANES)
    step = out.shape[0] // number
    return [
        pltpu.make_async_copy(
            source.at[pl.ds(n * step, step), :, pl.ds(at, out.shape[2])], out.at[pl.ds(n * step, step)], sem.at[n]
        )
        for n in range(number)
    ]


def take_kernel(start, source, *rest):
    out, sem = rest[-2:]
    copies = fetch(source, out, sem, 1 - my_core(), start, sem.shape[0])
    for copy in copies:
        copy.start()
    for copy in copies:
        copy.wait()


class Place:
    def __init__(self, per_device, tiles, host):
        self.o, self.core, self.chip = my_place()
        self.tiles, self.host = tiles, host
        self.chips = tiles.shape[0]
        owners = [lax.div(tiles[t, 0] * BLK, 2 * per_device) for t in range(self.chips)]
        key, same = 0, True
        for t in range(self.chips):
            key = key + owners[t] * self.chips**t
            same = same & (owners[t] == owners[0])
        self.key, self.same = key, same
        self.bit_1 = jnp.where(self.core == 0, 1, 2)
        self.bit_2 = 3 - self.bit_1

    def tile(self, chip):
        return self.host[self.key * self.chips + chip]

    def heads(self, chip):
        tile = self.tile(chip)
        return BLK * self.tiles[tile, 0], BLK * self.tiles[tile, 1]


def setup_kernel(per_device, tiles, host, rotation, source, after, *rest):
    fetched, (high, low, sem) = rest[:-3], rest[-3:]
    core = my_core()
    copies = []
    for n, out in enumerate(fetched):
        side, chunk = (1 - core, n + 1) if n < CHUNKS - 1 else (core, n - CHUNKS + 1)
        copies += fetch(source, out, sem.at[n], side, chunk * out.shape[2], sem.shape[1])
    for copy in copies:
        copy.start()
    at = Place(per_device, tiles, host)
    pair = BLK // 2
    heads = [at.heads(chip) for chip in (at.chip ^ 3, at.chip ^ at.bit_1, at.chip ^ at.bit_2, at.chip)]
    wanted = []
    for a, b in heads:
        wanted += [a + (1 - core) * pair] + [b + w for w in range(BLK)] + [a + core * pair]
    for u in range(1, pair):
        for a, b in heads:
            wanted += [a + (1 - core) * pair + u, a + core * pair + u]
    lane = lax.broadcasted_iota(jnp.int32, (SUB, LANES), 1)
    chosen = jnp.concatenate([jnp.where(lane == n, 1.0, 0.0) for n in wanted]).astype(bf16)
    rows = chosen.shape[0]
    row = lax.broadcasted_iota(jnp.int32, (LANES, LANES), 0)
    column = lax.broadcasted_iota(jnp.int32, (LANES, LANES), 1)
    columns = [
        jnp.where(row - (at.o ^ e) * per_device == jnp.right_shift(column, 3), 1.0, 0.0).astype(bf16)
        for e in range(2)
    ]
    keep = (lax.broadcasted_iota(jnp.int32, (rows, LANES), 0) & (SUB - 1)) == (
        lax.broadcasted_iota(jnp.int32, (rows, LANES), 1) & (SUB - 1)
    )
    for out, values in zip((high, low), split(rotation[...])):
        picked = lax.dot_general(chosen, values, (((1,), (1,)), ((), ())), preferred_element_type=f32).astype(bf16)
        for e in range(2):
            out[:, e * LANES:(e + 1) * LANES] = jnp.where(keep, dot(picked, columns[e]), 0.0).astype(bf16)
    for copy in copies:
        copy.wait()


def ready_kernel(per_device, n_grid, tiles, host, mask, log_r, *rest):
    out, powers, flags, match, alone, zeros, sem = rest[-7:]
    zeros[...] = jnp.zeros(zeros.shape, f32)
    step = zeros.shape[0]
    copies = [
        pltpu.make_async_copy(zeros, out.at[pl.ds(n * step, step)], sem.at[n]) for n in range(out.shape[0] // step)
    ]
    for copy in copies:
        copy.start()
    begin, size_x = SUB * lax.axis_index("grid"), SUB * n_grid
    exponents = (
        2 * begin + SUB + 1,
        2 * size_x + 1 - SUB - 2 * begin,
        2 * size_x + 2 - 2 * begin,
        2 * begin,
        2 * begin + 2 * SUB + 2,
        2 * size_x - 2 * SUB - 2 * begin,
    )
    for n, exponent in enumerate(exponents):
        power = jnp.exp(exponent.astype(f32) * log_r[...])
        powers[n] = power if n < 2 else 1.0 - power
    at = Place(per_device, tiles, host)
    alone[0] = at.same.astype(jnp.int32)
    a, b = at.heads(at.chip)
    pair = BLK // 2
    live = mask[...].astype(f32)
    row = lax.broadcasted_iota(jnp.int32, live.shape, 0)
    column = lax.broadcasted_iota(jnp.int32, (1, live.shape[1]), 1)
    for u in range(pair):
        line = jnp.sum(jnp.where(row == a + at.core * pair + u, live, 0.0), axis=0, keepdims=True)
        for w in range(BLK):
            flags[u * BLK + w] = jnp.sum(jnp.where(column == b + w, line, 0.0))
    blocks = per_device // BLK
    parts = [0, at.bit_1, at.bit_2, 3, 0, at.bit_2, at.bit_1, 3]
    for n, flip in enumerate(parts):
        home = tiles[at.tile(at.chip ^ flip), 0]
        for block in range(blocks):
            hit = home == at.o * blocks + block
            if n % 4 == 3:
                hit = hit & at.same
            match[block * len(parts) + n] = hit.astype(jnp.int32)
    for copy in copies:
        copy.wait()


def join_kernel(x, y, out):
    out[0] = x[...]
    out[1] = y[...]


def rotate_kernel(first, high, low, *rest):
    send, keep = rest[-2:]
    rows = send.shape[0] * SUB
    part = pl.ds(first, 2 * rows)
    table = (high[part, :], low[part, :])
    at = 0
    step = 2 * LANES
    while at < send.shape[2]:
        width = rest[0].shape[2]
        n, inner = at // width, at % width
        lanes = slice(inner, inner + step)
        mine, theirs = rest[2 * n], rest[2 * n + 1]
        depth = mine.shape[0] * SUB
        cells = jnp.concatenate([mine[:, :, lanes].reshape(depth, step), theirs[:, :, lanes].reshape(depth, step)])
        total = dot3(table, split(cells))
        lanes = slice(at, at + step)
        send[:, :, lanes] = total[:rows].reshape(send.shape[0], SUB, step)
        keep[:, :, lanes] = total[rows:].reshape(keep.shape[0], SUB, step)
        at += step


def pass_kernel(keep, got, *rest):
    out = rest[-1]
    count = out.shape[0]
    out[...] = keep[:count] + got[:count]


def finish_kernel(keep, got, passed, *rest):
    out = rest[-1]
    count = out.shape[0]
    out[...] = keep[count:] + got[count:] + passed[...]


def sub_sums(values):
    row = lax.broadcasted_iota(jnp.int32, values[0].shape, 0)
    for s in (4, 2):
        low = (row & s) == 0
        paired = []
        for n in range(s):
            a, b = values[n], values[n + s]
            paired.append(jnp.where(low, a, pltpu.roll(b, s, 0)) + jnp.where(low, pltpu.roll(a, SUB - s, 0), b))
        values = paired
    even = (row & 1) == 0
    a, b = values
    return jnp.where(even, a, pltpu.roll(b, 1, 0)), jnp.where(even, pltpu.roll(a, SUB - 1, 0), b)


def fields(u, own, other, first_own, first_other):
    table = []
    for side, sources, targets in ((0, first_own, own), (1, first_other, other)):
        for n, ref in enumerate(sources):
            if u == 0:
                table.append((side, n, ref, targets[n], BLK + 1 if side == 0 else 0, 0))
            else:
                table.append((side, n, ref, targets[0], 1 if side == 0 else 0, n * ref.shape[2]))
    return table


def forward_kernel(u, counts, *refs):
    groups = []
    for count in counts:
        groups.append(refs[:count])
        refs = refs[count:]
    first_own, first_other, own, other = groups[:4]
    y_hi, y_lo, z_hi, z_lo, ends, powers = refs[:6]
    message, spectrum, a_out, b_out, dens = refs[-5:]
    if u == 0:
        own, other = first_own, first_other
    core, g = my_core(), lax.axis_index("grid")
    tiles = first_own[0].shape[2] // LANES
    for side, n, source, target, slot, offset in fields(u, own, other, first_own, first_other):
        half = (core if side == 0 else 1 - core) * (len(first_own) * tiles * SUB)
        for t in range(tiles):
            lanes = pl.ds(t * LANES, LANES)
            value = target[slot, :, pl.ds(offset + t * LANES, LANES)]
            rows = pl.ds(pl.multiple_of(half + (n * tiles + t) * SUB, SUB), SUB)
            for w in range(BLK):
                dens[rows, w * LANES:(w + 1) * LANES] = value * source[1 + w, :, lanes]
    z = (z_hi[...], z_lo[...])
    half = dens.shape[0]
    for q in range(BLK // 2):
        out = dot3(split(dens[:, q * 2 * LANES:(q + 1) * 2 * LANES]), z)
        spectrum[:half, q * LANES:(q + 1) * LANES] = out[:, :LANES]
        spectrum[half:, q * LANES:(q + 1) * LANES] = out[:, LANES:]
    spectrum[...] = dot3((y_hi[...], y_lo[...]), split(spectrum[...]))

    def reduce(group, carry):
        lines = pl.ds(pl.multiple_of(group * SUB, SUB), SUB)
        near, far = powers[0, lines, :], powers[1, lines, :]
        for q in range(BLK // 2):
            lanes = slice(q * LANES, (q + 1) * LANES)
            values = []
            for k in range(SUB):
                rows = pl.ds(pl.multiple_of((group * SUB + k) * SUB, SUB), SUB)
                values.append(ends[rows, :] * spectrum[rows, lanes])
            even, odd = sub_sums(values)
            rightward = (even + odd) - near * (even - odd)
            leftward = (even - odd) - far * (even + odd)
            a_out[lines, lanes] = rightward
            b_out[lines, lanes] = leftward
            message[lines, lanes] = jnp.where((g & 1) == 0, rightward, leftward)
        return carry

    lax.fori_loop(0, NY // SUB, reduce, 0)


def backward_kernel(u, counts, flags, *refs):
    groups = []
    for count in counts:
        groups.append(refs[:count])
        refs = refs[count:]
    own, other, received = groups
    (y_hi, y_lo, z_hi, z_lo, inverse, basis, powers, steady, spectrum, a_in, b_in) = refs[:11]
    out, work, pot = refs[-3:]
    core, g = my_core(), lax.axis_index("grid")
    tiles = own[0].shape[2] // LANES
    first, last = basis[0], basis[1]
    odd, inner = (g & 1) == 1, (g == 1) | (g == 2)

    def ends(group, carry):
        lines = pl.ds(pl.multiple_of(group * SUB, SUB), SUB)
        scale, r, slab = steady[0, lines, :], steady[1, lines, :], steady[2, lines, :]
        for q in range(BLK // 2):
            lanes = slice(q * LANES, (q + 1) * LANES)
            same = received[0][lines, lanes] + jnp.where(inner, 0.0, slab * received[2][lines, lanes])
            across = jnp.where(inner, received[1][lines, lanes], 0.0)
            from_left = jnp.where(odd, same, across)
            from_right = jnp.where(odd, across, same)
            before = scale * (powers[2, lines, :] * from_left
                              + r * powers[3, lines, :] * (b_in[lines, lanes] + slab * from_right))
            after = scale * (powers[4, lines, :] * from_right
                             + r * powers[5, lines, :] * (a_in[lines, lanes] + slab * from_left))
            for k in range(SUB):
                rows = pl.ds(pl.multiple_of((group * SUB + k) * SUB, SUB), SUB)
                edge = first * before[k:k + 1] + last * after[k:k + 1]
                work[rows, lanes] = inverse[rows, :] * (spectrum[rows, lanes] + edge)
        return carry

    lax.fori_loop(0, NY // SUB, ends, 0)
    work[...] = dot3((y_hi[...], y_lo[...]), split(work[...]))
    z = (z_hi[...], z_lo[...])
    half = pot.shape[0]
    for q in range(BLK // 2):
        lanes = slice(q * LANES, (q + 1) * LANES)
        rows = jnp.concatenate([work[:half, lanes], work[half:, lanes]], axis=1)
        pot[:, q * 2 * LANES:(q + 1) * 2 * LANES] = dot3(split(rows), z)
    for side, group in ((0, own), (1, other)):
        half = (core if side == 0 else 1 - core) * (len(own) * tiles)
        for n, ref in enumerate(group):
            for t in range(tiles):
                lanes = pl.ds(t * LANES, LANES)
                at = half + n * tiles + t
                rows = pl.ds(pl.multiple_of(at * SUB, SUB), SUB)
                total = None
                for w in range(BLK):
                    term = flags[u * BLK + w] * (pot[rows, w * LANES:(w + 1) * LANES] * ref[1 + w, :, lanes])
                    total = term if total is None else total + term
                out[:, pl.ds(pl.multiple_of(at * LANES, LANES), LANES)] = -total


def relay_kernel(got, a, b, steady, out):
    g = lax.axis_index("grid")
    for q in range(BLK // 2):
        lanes = slice(q * LANES, (q + 1) * LANES)
        out[:, lanes] = jnp.where((g & 1) == 1, a[:, lanes], b[:, lanes]) + steady[2] * got[:, lanes]


def place_kernel(stride, match, *refs):
    parts, (out, rows, sem) = refs[:-4], refs[-3:]
    pair = BLK // 2
    blocks = out.shape[0] // BLK
    core = my_core()
    values = []
    for part in parts:
        values += [part] if len(part.shape) == 2 else [part.at[n] for n in range(part.shape[0])]
    parts, count = values, len(values) // pair

    def hits(b, side):
        return [(match[b * stride + side * stride // 2 + n], side * count // 2 + n) for n in range(count // 2)]

    def found(b, side):
        return sum(hit for hit, n in hits(b, side)) > 0

    def move(b, side):
        which = core if side == 0 else 1 - core
        at = b * BLK + which * pair
        return pltpu.make_async_copy(rows.at[b, side], out.at[pl.ds(at, pair)], sem.at[b, side])

    for b in range(blocks):
        for side in range(2):

            @pl.when(found(b, side))
            def _():
                rows[b, side] = jnp.zeros(rows.shape[2:], f32)
                for hit, n in hits(b, side):

                    @pl.when(hit > 0)
                    def _():
                        for u in range(pair):
                            rows[b, side, u] += parts[u * count + n][...]

                move(b, side).start()

    for b in range(blocks):
        for side in range(2):

            @pl.when(found(b, side))
            def _():
                move(b, side).wait()


def tile_device(orbitals, rotation, tile_list, pair_mask):
    shape = per_device, planes, width = orbitals.shape
    n_orb, n_grid = lax.axis_size("orb"), lax.axis_size("grid")
    size_x = planes * n_grid
    half = width // 2
    chips = n_orb // 2
    axes = ("orb", "grid")

    def swap(x, even, odd):
        moves = []
        for a in range(n_orb):
            flip = even if a % 2 == 0 else odd
            moves += [(a * n_grid + b, (a ^ flip) * n_grid + b) for b in range(n_grid)]
        return lax.ppermute(x, axes, moves)

    def along(x, target):
        return lax.ppermute(x, axes, [(a * n_grid + b, a * n_grid + t) for a in range(n_orb) for b, t in enumerate(target)])

    chunk = half // CHUNKS
    orbitals = pltpu.with_memory_space_constraint(orbitals, pltpu.HBM)

    part = jax.ShapeDtypeStruct((per_device, planes, chunk), f32)
    copies = per_device // 2
    taken = pl.pallas_call(
        functools.partial(take_kernel, 0), out_shape=part, in_specs=[HBM], out_specs=VM,
        scratch_shapes=[DMA((copies,))], name="take", compiler_params=grant(4),
    )(orbitals)
    theirs = [swap(taken, 1, 1)]

    pair = BLK // 2
    firsts = (BLK + 2) * chips
    rows = (firsts + 2 * (pair - 1) * chips) * SUB
    wide_table = jax.ShapeDtypeStruct((rows, 2 * LANES), bf16)
    blocks = per_device // BLK
    c, r = line_np()
    c, r = line_np()
    host = jnp.asarray(host_np(chips).reshape(-1))
    *fetched, high, low = pl.pallas_call(
        functools.partial(setup_kernel, per_device),
        out_shape=[part] * (2 * CHUNKS - 1) + [wide_table] * 2,
        in_specs=[SM, SM, VM, HBM, ANY], out_specs=[VM] * (2 * CHUNKS + 1),
        scratch_shapes=[DMA((2 * CHUNKS - 1, copies))], name="setup", compiler_params=grant(8),
    )(tile_list, host, rotation, orbitals, taken)
    mine = fetched[CHUNKS - 1:]
    for n, taken in enumerate(fetched[:CHUNKS - 1], 1):
        theirs.append(swap(taken, 1, 1))

    def rotate(first, count, fields, *after):
        part = jax.ShapeDtypeStruct((count, planes, chunk * (len(fields) // 2)), f32)
        send, keep = pl.pallas_call(
            functools.partial(rotate_kernel, first * SUB), out_shape=(part, part),
            in_specs=[VM] * (2 + len(fields)) + [ANY] * len(after),
            out_specs=(VM, VM), compiler_params=grant(8),
        )(high, low, *fields, *after)
        return send, keep, swap(send, 2, 4)

    sums, last = [], ()
    for n in range(CHUNKS):
        sums.append(rotate(0, firsts // 2, [mine[n], theirs[n]], *last))
        last = (sums[-1][0],)
    both = [x for n in range(CHUNKS) for x in (mine[n], theirs[n])]
    empty, powers, flags, match, alone = pl.pallas_call(
        functools.partial(ready_kernel, per_device, n_grid),
        out_shape=(pltpu.HBM(shape, f32), jax.ShapeDtypeStruct((6, NY, LANES), f32),
                   jax.ShapeDtypeStruct((pair * BLK,), f32), jax.ShapeDtypeStruct((blocks * 8,), jnp.int32),
                   jax.ShapeDtypeStruct((1,), jnp.int32)),
        in_specs=[SM, SM, VM, VM, ANY], out_specs=(HBM, VM, SM, SM, SM),
        scratch_shapes=[pltpu.VMEM((pair, planes, width), f32), DMA((per_device // pair,))], name="ready",
        compiler_params=grant(4),
    )(tile_list, host, pair_mask, jnp.asarray(np.log(r), f32), sums[-1][0])
    passing, own, other = [], [], []

    def pass_on(n, *after, spec=ANY):
        _, keep, got = sums[n]
        count = keep.shape[0] // 2
        value = pl.pallas_call(
            pass_kernel, out_shape=jax.ShapeDtypeStruct((count,) + keep.shape[1:], f32),
            in_specs=[VM] * 2 + [spec] * len(after), out_specs=VM, compiler_params=grant(4),
        )(keep, got, *after)
        passing.append((keep, got, swap(value, 4, 2)))
        return value

    def finish(n, *after):
        keep, got, passed = passing[n]
        own.append(pl.pallas_call(
            finish_kernel, out_shape=jax.ShapeDtypeStruct(passed.shape, f32), in_specs=[VM] * 3 + [ANY] * len(after),
            out_specs=VM, compiler_params=grant(4),
        )(keep, got, passed, *after))
        other.append(swap(own[-1], 1, 1))
        return own[-1]

    step = pass_on(0, empty, spec=HBM)
    for n in range(1, CHUNKS):
        step = pass_on(n, step)
    sums.append(rotate(firsts, (pair - 1) * chips, both, step))
    step = sums[-1][0]
    for n in range(CHUNKS):
        step = finish(n, step)
    last = (pass_on(CHUNKS, step),)

    sine_x, eigen_x = sine_np(planes), eigen_np(planes)
    ends = jnp.asarray(np.einsum("jp,pkl->kjl", sine_x, r[None] ** np.arange(planes - 1, -1, -1)[:, None, None])
                       .reshape(-1, LANES), f32)
    inverse = jnp.asarray((COUPLING / (eigen_x[None, :, None] + c[:, None, :])).reshape(-1, LANES), f32)
    basis = jnp.asarray(np.broadcast_to(sine_x[:, [0, -1]].T[:, :, None], (2, planes, LANES)), f32)
    steady = jnp.asarray(np.stack([r / ((1 - r**2) * (1 - r ** (2 * size_x + 2))), r, r**planes]), f32)

    y_hi, y_lo = halves_np(y_table())
    z_hi, z_lo = halves_np(z_table())
    zt_hi, zt_lo = halves_np(z_table().T)
    solved = []
    lines = jax.ShapeDtypeStruct((NY, 2 * LANES), f32)
    cube = (NY * SUB, 2 * LANES)
    wide = pltpu.VMEM((width // LANES * SUB, BLK * LANES), f32)
    base_own, base_other = own[:CHUNKS], other[:CHUNKS]
    for u in range(pair):
        if u:
            finish(CHUNKS, *last)
        more_own, more_other = own[CHUNKS:][:u], other[CHUNKS:][:u]
        counts = (CHUNKS, CHUNKS, len(more_own), len(more_other))
        inputs = [*base_own, *base_other, *more_own, *more_other, y_hi, y_lo, z_hi, z_lo, ends, powers]
        message, spectrum, a, b = pl.pallas_call(
            functools.partial(forward_kernel, u, counts),
            out_shape=[lines, jax.ShapeDtypeStruct(cube, f32), lines, lines],
            in_specs=[VM] * len(inputs) + [ANY] * len(last),
            out_specs=[VM] * 4,
            scratch_shapes=[wide],
            compiler_params=grant(16),
        )(*inputs, *last)
        near = along(message, (1, 0, 3, 2))
        relayed = pl.pallas_call(
            relay_kernel, out_shape=lines, in_specs=[VM] * 4, out_specs=VM, compiler_params=grant(4),
        )(near, a, b, steady)
        far_pair = along(relayed, (0, 2, 1, 3))
        handed = along(far_pair, (1, 0, 3, 2))
        last = (spectrum,)
        solved.append((spectrum, a, b, [near, far_pair, handed]))

    terms, last = [], ()
    for u, (spectrum, a, b, received) in enumerate(solved):
        inputs = [*base_own, *base_other, *received, y_hi, y_lo, zt_hi, zt_lo, inverse, basis, powers, steady,
                  spectrum, a, b]
        terms.append(pl.pallas_call(
            functools.partial(backward_kernel, u, (CHUNKS, CHUNKS, len(received))),
            out_shape=jax.ShapeDtypeStruct((planes, width), f32),
            in_specs=[SM] + [VM] * len(inputs) + [ANY] * len(last),
            out_specs=VM,
            scratch_shapes=[pltpu.VMEM(cube, f32), wide],
            compiler_params=grant(16),
        )(flags, *inputs, *last))
        last = (terms[-1],)

    near_1 = [swap(term, 2, 4) for term in terms]
    near_2 = [swap(term, 4, 2) for term in terms]
    own_parts = [[term, x, y] for term, x, y in zip(terms, near_1, near_2)]
    sib_parts = []
    for term, x, y in own_parts:
        joined = pl.pallas_call(
            join_kernel, out_shape=jax.ShapeDtypeStruct((2,) + term.shape, f32), in_specs=[VM] * 2, out_specs=VM,
            compiler_params=grant(4),
        )(x, y)
        sib_parts.append([swap(term, 1, 1), swap(joined, 1, 1)])

    def place(target, groups):
        parts = [part for group in groups for part in group]
        return pl.pallas_call(
            functools.partial(place_kernel, 8),
            out_shape=pltpu.HBM(shape, f32),
            in_specs=[SM] + [VM] * len(parts) + [HBM],
            out_specs=HBM,
            input_output_aliases={len(parts) + 1: 0},
            scratch_shapes=[pltpu.VMEM((blocks, 2, pair, planes, width), f32), DMA((blocks, 2))],
            name="place",
            compiler_params=grant(8),
        )(match, *parts, target)

    def place_near(target, mine, sibs):
        return place(target, [a + b for a, b in zip(mine, sibs)])

    def place_far(target, mine, sibs):
        far = [swap(group[1], 4, 2) for group in mine]
        return place(target, [a + [x] + b + [swap(x, 1, 1)] for a, b, x in zip(mine, sibs, far)])

    return lax.cond(alone[0] != 0, place_far, place_near, empty, own_parts, sib_parts)


def sine_table(length):
    wave_index = jnp.arange(length, dtype=f32) + 1.0
    return jnp.sqrt(2.0 / (length + 1.0)) * jnp.sin(
        jnp.pi * wave_index[:, None] * wave_index[None, :] / (length + 1.0)
    )


def eigen_values(length):
    wave_index = jnp.arange(length, dtype=f32) + 1.0
    return 2.0 - 2.0 * jnp.cos(jnp.pi * wave_index / (length + 1.0))


def green_kernel(size_x, size_y, size_z):
    summed = (
        eigen_values(size_x)[:, None, None]
        + eigen_values(size_y)[None, :, None]
        + eigen_values(size_z)[None, None, :]
    )
    return COUPLING / (summed + SCREENING)


def pair_lists(tile_list, pair_mask):
    within = jnp.arange(BLK * BLK, dtype=jnp.int32)
    targets = (BLK * tile_list[:, 0:1] + within[None, :] // BLK).reshape(-1)
    sources = (BLK * tile_list[:, 1:2] + within[None, :] % BLK).reshape(-1)
    return (targets, sources, pair_mask[targets, sources])


def compact(targets, sources, live_flags, number):
    ranking = jnp.cumsum(live_flags) - 1
    places = jnp.where(live_flags == 1, ranking, number)
    picked = (
        jnp.zeros((number,), jnp.int32)
        .at[places]
        .set(jnp.arange(live_flags.shape[0], dtype=jnp.int32), mode="drop")
    )
    return (targets[picked], sources[picked])


def along_z(values, matrix):
    number, planes, width_yz = values.shape
    size_z = matrix.shape[0]
    shaped = values.reshape(number, planes, width_yz // size_z, size_z)
    return jnp.einsum("pxrz,zk->pxrk", shaped, matrix, precision=precise).reshape(number, planes, width_yz)


def along_y(values, matrix):
    number, planes, width_yz = values.shape
    size_y = matrix.shape[0]
    shaped = values.reshape(number, planes, size_y, width_yz // size_y)
    return jnp.einsum("pxyz,yk->pxkz", shaped, matrix, precision=precise).reshape(number, planes, width_yz)


def along_x(values, matrix):
    return jnp.einsum("pxc,xk->pkc", values, matrix, precision=precise)


def any_device(orbitals, rotation, tile_list, pair_mask):
    n_grid = lax.axis_size("grid")
    number_orbitals, size_x = rotation.shape[0], orbitals.shape[1] * n_grid
    rotated = jnp.einsum(
        "ij,ixc->jxc",
        rotation,
        lax.all_to_all(orbitals, "orb", split_axis=2, concat_axis=0, tiled=True),
        precision=precise,
    )
    planes, width_yz = rotated.shape[1:]
    targets, sources, live_flags = pair_lists(tile_list, pair_mask)
    matrix_x, matrix_y, matrix_z = sine_table(size_x), sine_table(NY), sine_table(NZ)
    kernel = green_kernel(size_x, NY, NZ).reshape(size_x, NY * NZ)
    orbital_ids = jnp.arange(number_orbitals, dtype=jnp.int32)
    targets, sources = compact(targets, sources, live_flags, targets.shape[0] // 2)
    density = rotated[targets] * rotated[sources]
    number = density.shape[0]
    spectrum = along_z(density, matrix_z)
    spectrum = lax.all_to_all(spectrum, "orb", split_axis=0, concat_axis=2, tiled=True)
    spectrum = along_y(spectrum, matrix_y)
    spectrum = lax.all_to_all(spectrum, "grid", split_axis=0, concat_axis=1, tiled=True)
    spectrum = along_x(along_x(spectrum, matrix_x) * kernel, matrix_x)
    spectrum = lax.all_to_all(spectrum, "grid", split_axis=1, concat_axis=0, tiled=True)
    spectrum = along_y(spectrum, matrix_y)
    spectrum = lax.all_to_all(spectrum, "orb", split_axis=2, concat_axis=0, tiled=True)
    potential = along_z(spectrum, matrix_z)
    products = potential * rotated[sources]
    selector = (targets[None, :] == orbital_ids[:, None]).astype(f32)
    partial_value = -jnp.dot(selector, products.reshape(number, planes * width_yz), precision=precise)
    partial_value = partial_value.reshape(number_orbitals, planes, width_yz)
    return lax.all_to_all(partial_value, "orb", split_axis=0, concat_axis=2, tiled=True)


def solution(mesh):
    n_orb, n_grid = mesh.shape["orb"], mesh.shape["grid"]

    def on_device(orbitals, rotation, tile_list, pair_mask):
        per_device, planes, width = orbitals.shape
        fits = n_orb == 8 and 2 * tile_list.shape[0] == n_orb and planes == SUB and per_device % BLK == 0
        fits = fits and width == NY * NZ and 2 * NZ == LANES and n_grid == 4
        fits = fits and per_device * SUB == LANES and rotation.shape == (LANES, LANES)
        if not fits:
            return any_device(orbitals, rotation, tile_list, pair_mask)
        return tile_device(orbitals, rotation, tile_list, pair_mask)

    in_specs = (P("orb", "grid", None), P(), P(), P())
    out_specs = P("orb", "grid", None)
    return jax.shard_map(on_device, mesh=mesh, in_specs=in_specs, out_specs=out_specs, check_vma=False)
```

```python
import functools
import itertools

import jax
import jax.numpy as jnp
import numpy as np
from jax import lax
from jax.experimental import pallas as pl
from jax.experimental.pallas import tpu as pltpu
from jax.sharding import PartitionSpec as P


BLK = 4
NY = 64
NZ = 64
LANES = 128
SUB = 8
CHUNKS = 2
COUPLING = 0.25
SCREENING = 0.1

precise = lax.Precision.HIGHEST
f32 = jnp.float32
bf16 = jnp.bfloat16

VM = pl.BlockSpec(memory_space=pltpu.VMEM)
SM = pl.BlockSpec(memory_space=pltpu.SMEM)
ANY = pl.BlockSpec(memory_space=pl.ANY)
HBM = pl.BlockSpec(memory_space=pltpu.HBM)
DMA = pltpu.SemaphoreType.DMA


def grant(mib):
    return pltpu.CompilerParams(vmem_limit_bytes=mib << 20)


def sine_np(n):
    k = np.arange(1, n + 1, dtype=np.float64)
    return np.sqrt(2.0 / (n + 1)) * np.sin(np.pi * k[:, None] * k[None, :] / (n + 1))


def eigen_np(n):
    k = np.arange(1, n + 1, dtype=np.float64)
    return 2.0 - 2.0 * np.cos(np.pi * k / (n + 1))


def halves_np(table):
    high = np.asarray(table, np.float32).astype(jnp.bfloat16)
    low = (np.asarray(table, np.float64) - high.astype(np.float64)).astype(jnp.bfloat16)
    return jnp.asarray(high), jnp.asarray(low)


def y_order():
    rows = LANES // NZ
    return np.arange(NY).reshape(NY // rows, rows).T.reshape(-1)


def y_tables():
    sine, planes = sine_np(NY), sine_np(SUB)
    even, odd = np.kron(sine[0::2, 0::2], planes), np.kron(sine[1::2, 0::2], planes)
    return np.stack([even, odd]), np.stack([even, odd.T])


def turned(x):
    count = x.shape[0] // SUB
    return jnp.concatenate([x[(count - 1 - t) * SUB:(count - t) * SUB] for t in range(count)])


def z_table():
    half = LANES // NZ
    sine = sine_np(NZ)
    table = np.zeros((2, half, NZ, half, 2, NZ))
    for pair in range(2):
        for h in range(half):
            table[pair, h, :, h, pair, :] = sine
    return table.reshape(2 * half * NZ, half * 2 * NZ)


def line_np():
    c = eigen_np(NY)[y_order()][:, None] + eigen_np(NZ)[None, :] + SCREENING
    c = np.concatenate([c, c], axis=1)
    return c, 2.0 / (2.0 + c + np.sqrt(c * (c + 4.0)))


def host_np(chips):
    table = np.zeros((chips**chips, chips), np.int32)
    for owners in itertools.product(range(chips), repeat=chips):
        best = None
        for tiles in itertools.permutations(range(chips)):
            hops = [bin(chip ^ owners[tile]).count("1") for chip, tile in enumerate(tiles)]
            cost = (max(hops), sum(hops))
            if best is None or cost < best[0]:
                best = (cost, tiles)
        table[sum(own * chips**t for t, own in enumerate(owners))] = best[1]
    return table


def dot(a, b):
    return jnp.dot(a, b, preferred_element_type=f32)


def split(x):
    high = x.astype(bf16)
    return high, (x - high.astype(f32)).astype(bf16)


def dot3(a, b):
    return dot(a[0], b[0]) + dot(a[0], b[1]) + dot(a[1], b[0])


def my_core():
    return lax.rem(lax.axis_index("orb"), 2)


def my_place():
    o = lax.axis_index("orb")
    return o, lax.rem(o, 2), lax.div(o, 2)


def fetch(source, out, sem, side, start, number):
    at = pl.multiple_of(side * (source.shape[2] // 2) + start, LANES)
    step = out.shape[0] // number
    return [
        pltpu.make_async_copy(
            source.at[pl.ds(n * step, step), :, pl.ds(at, out.shape[2])], out.at[pl.ds(n * step, step)], sem.at[n]
        )
        for n in range(number)
    ]


def take_kernel(start, source, *rest):
    out, sem = rest[-2:]
    copies = fetch(source, out, sem, 1 - my_core(), start, sem.shape[0])
    for copy in copies:
        copy.start()
    for copy in copies:
        copy.wait()


class Place:
    def __init__(self, per_device, tiles, host):
        self.o, self.core, self.chip = my_place()
        self.tiles, self.host = tiles, host
        self.chips = tiles.shape[0]
        owners = [lax.div(tiles[t, 0] * BLK, 2 * per_device) for t in range(self.chips)]
        key, same = 0, True
        for t in range(self.chips):
            key = key + owners[t] * self.chips**t
            same = same & (owners[t] == owners[0])
        self.key, self.same = key, same
        self.bit_1 = jnp.where(self.core == 0, 1, 2)
        self.bit_2 = 3 - self.bit_1

    def tile(self, chip):
        return self.host[self.key * self.chips + chip]

    def heads(self, chip):
        tile = self.tile(chip)
        return BLK * self.tiles[tile, 0], BLK * self.tiles[tile, 1]


def setup_kernel(per_device, tiles, host, rotation, source, after, *rest):
    fetched, (high, low, sem) = rest[:-3], rest[-3:]
    core = my_core()
    copies = []
    for n, out in enumerate(fetched):
        side, chunk = (1 - core, n + 1) if n < CHUNKS - 1 else (core, n - CHUNKS + 1)
        copies += fetch(source, out, sem.at[n], side, chunk * out.shape[2], sem.shape[1])
    for copy in copies:
        copy.start()
    at = Place(per_device, tiles, host)
    pair = BLK // 2
    heads = [at.heads(chip) for chip in (at.chip ^ 3, at.chip ^ at.bit_1, at.chip ^ at.bit_2, at.chip)]
    wanted = []
    for a, b in heads:
        wanted += [a + (1 - core) * pair] + [b + w for w in range(BLK)] + [a + core * pair]
    for u in range(1, pair):
        for a, b in heads:
            wanted += [a + (1 - core) * pair + u, a + core * pair + u]
    lane = lax.broadcasted_iota(jnp.int32, (SUB, LANES), 1)
    chosen = jnp.concatenate([jnp.where(lane == n, 1.0, 0.0) for n in wanted]).astype(bf16)
    rows = chosen.shape[0]
    row = lax.broadcasted_iota(jnp.int32, (LANES, LANES), 0)
    column = lax.broadcasted_iota(jnp.int32, (LANES, LANES), 1)
    columns = [
        jnp.where(row - (at.o ^ e) * per_device == jnp.right_shift(column, 3), 1.0, 0.0).astype(bf16)
        for e in range(2)
    ]
    keep = (lax.broadcasted_iota(jnp.int32, (rows, LANES), 0) & (SUB - 1)) == (
        lax.broadcasted_iota(jnp.int32, (rows, LANES), 1) & (SUB - 1)
    )
    for out, values in zip((high, low), split(rotation[...])):
        picked = lax.dot_general(chosen, values, (((1,), (1,)), ((), ())), preferred_element_type=f32).astype(bf16)
        for e in range(2):
            out[:, e * LANES:(e + 1) * LANES] = jnp.where(keep, dot(picked, columns[e]), 0.0).astype(bf16)
    for copy in copies:
        copy.wait()


def ready_kernel(per_device, n_grid, tiles, host, mask, log_r, *rest):
    out, powers, flags, match, alone, zeros, sem = rest[-7:]
    zeros[...] = jnp.zeros(zeros.shape, f32)
    step = zeros.shape[0]
    copies = [
        pltpu.make_async_copy(zeros, out.at[pl.ds(n * step, step)], sem.at[n]) for n in range(out.shape[0] // step)
    ]
    for copy in copies:
        copy.start()
    begin, size_x = SUB * lax.axis_index("grid"), SUB * n_grid
    exponents = (
        2 * begin + SUB + 1,
        2 * size_x + 1 - SUB - 2 * begin,
        2 * size_x + 2 - 2 * begin,
        2 * begin,
        2 * begin + 2 * SUB + 2,
        2 * size_x - 2 * SUB - 2 * begin,
    )
    for n, exponent in enumerate(exponents):
        power = jnp.exp(exponent.astype(f32) * log_r[...])
        powers[n] = power if n < 2 else 1.0 - power
    at = Place(per_device, tiles, host)
    alone[0] = at.same.astype(jnp.int32)
    a, b = at.heads(at.chip)
    pair = BLK // 2
    live = mask[...].astype(f32)
    row = lax.broadcasted_iota(jnp.int32, live.shape, 0)
    column = lax.broadcasted_iota(jnp.int32, (1, live.shape[1]), 1)
    for u in range(pair):
        line = jnp.sum(jnp.where(row == a + at.core * pair + u, live, 0.0), axis=0, keepdims=True)
        for w in range(BLK):
            flags[u * BLK + w] = jnp.sum(jnp.where(column == b + w, line, 0.0))
    blocks = per_device // BLK
    parts = [0, at.bit_1, at.bit_2, 3, 0, at.bit_2, at.bit_1, 3]
    for n, flip in enumerate(parts):
        home = tiles[at.tile(at.chip ^ flip), 0]
        for block in range(blocks):
            hit = home == at.o * blocks + block
            if n % 4 == 3:
                hit = hit & at.same
            match[block * len(parts) + n] = hit.astype(jnp.int32)
    for copy in copies:
        copy.wait()


def join_kernel(x, y, out):
    out[0] = x[...]
    out[1] = y[...]


def rotate_kernel(first, high, low, *rest):
    send, keep = rest[-2:]
    rows = send.shape[0] * SUB
    part = pl.ds(first, 2 * rows)
    table = (high[part, :], low[part, :])
    at = 0
    step = 2 * LANES
    while at < send.shape[2]:
        width = rest[0].shape[2]
        n, inner = at // width, at % width
        lanes = slice(inner, inner + step)
        mine, theirs = rest[2 * n], rest[2 * n + 1]
        depth = mine.shape[0] * SUB
        cells = jnp.concatenate([mine[:, :, lanes].reshape(depth, step), theirs[:, :, lanes].reshape(depth, step)])
        total = dot3(table, split(cells))
        lanes = slice(at, at + step)
        send[:, :, lanes] = total[:rows].reshape(send.shape[0], SUB, step)
        keep[:, :, lanes] = total[rows:].reshape(keep.shape[0], SUB, step)
        at += step


def pass_kernel(keep, got, *rest):
    out = rest[-1]
    count = out.shape[0]
    out[...] = keep[:count] + got[:count]


def finish_kernel(keep, got, passed, *rest):
    out = rest[-1]
    count = out.shape[0]
    out[...] = keep[count:] + got[count:] + passed[...]


def sub_sums(values):
    row = lax.broadcasted_iota(jnp.int32, values[0].shape, 0)
    for s in (4, 2):
        low = (row & s) == 0
        paired = []
        for n in range(s):
            a, b = values[n], values[n + s]
            paired.append(jnp.where(low, a, pltpu.roll(b, s, 0)) + jnp.where(low, pltpu.roll(a, SUB - s, 0), b))
        values = paired
    even = (row & 1) == 0
    a, b = values
    return jnp.where(even, a, pltpu.roll(b, 1, 0)), jnp.where(even, pltpu.roll(a, SUB - 1, 0), b)


def fields(u, own, other, first_own, first_other):
    table = []
    for side, sources, targets in ((0, first_own, own), (1, first_other, other)):
        for n, ref in enumerate(sources):
            if u == 0:
                table.append((side, n, ref, targets[n], BLK + 1 if side == 0 else 0, 0))
            else:
                table.append((side, n, ref, targets[0], 1 if side == 0 else 0, n * ref.shape[2]))
    return table


def forward_kernel(u, counts, *refs):
    groups = []
    for count in counts[:-1]:
        groups.append(refs[:count])
        refs = refs[count:]
    first_own, first_other, own, other = groups[:4]
    y_hi, y_lo, z_hi, z_lo, ends, powers = refs[:6]
    messages, (spectrum, a_out, b_out, dens) = refs[-4 - counts[-1]:-4], refs[-4:]
    if u == 0:
        own, other = first_own, first_other
    core, g = my_core(), lax.axis_index("grid")
    tiles = first_own[0].shape[2] // LANES
    for side, n, source, target, slot, offset in fields(u, own, other, first_own, first_other):
        half = (core if side == 0 else 1 - core) * (len(first_own) * tiles * SUB)
        for t in range(tiles):
            lanes = pl.ds(t * LANES, LANES)
            value = target[slot, :, pl.ds(offset + t * LANES, LANES)]
            rows = pl.ds(pl.multiple_of(half + (n * tiles + t) * SUB, SUB), SUB)
            for w in range(BLK):
                dens[rows, w * LANES:(w + 1) * LANES] = value * source[1 + w, :, lanes]
    z = (z_hi[...], z_lo[...])
    half = dens.shape[0]
    for q in range(BLK // 2):
        out = dot3(split(dens[:, q * 2 * LANES:(q + 1) * 2 * LANES]), z)
        mirror = turned(out[:, LANES:])
        spectrum[:half, q * LANES:(q + 1) * LANES] = out[:, :LANES] + mirror
        spectrum[half:, q * LANES:(q + 1) * LANES] = out[:, :LANES] - mirror
    for parity in range(2):
        part = pl.ds(parity * half, half)
        spectrum[part, :] = dot3((y_hi[parity], y_lo[parity]), split(spectrum[part, :]))

    def reduce(group, carry):
        lines = pl.ds(pl.multiple_of(group * SUB, SUB), SUB)
        near, far = powers[0, lines, :], powers[1, lines, :]
        for q in range(BLK // 2):
            lanes = slice(q * LANES, (q + 1) * LANES)
            values = []
            for k in range(SUB):
                rows = pl.ds(pl.multiple_of((group * SUB + k) * SUB, SUB), SUB)
                values.append(ends[rows, :] * spectrum[rows, lanes])
            even, odd = sub_sums(values)
            rightward = (even + odd) - near * (even - odd)
            leftward = (even - odd) - far * (even + odd)
            a_out[lines, lanes] = rightward
            b_out[lines, lanes] = leftward
            for k, out in enumerate(messages, 1):
                out[lines, lanes] = jnp.where((g ^ k) > g, rightward, leftward)
        return carry

    lax.fori_loop(0, NY // SUB, reduce, 0)


def backward_kernel(u, counts, flags, *refs):
    groups = []
    for count in counts:
        groups.append(refs[:count])
        refs = refs[count:]
    own, other, received = groups
    (y_hi, y_lo, z_hi, z_lo, inverse, basis, powers, steady, spectrum, a_in, b_in) = refs[:11]
    out, work, pot = refs[-3:]
    core, g = my_core(), lax.axis_index("grid")
    tiles = own[0].shape[2] // LANES
    first, last = basis[0], basis[1]

    def ends(group, carry):
        lines = pl.ds(pl.multiple_of(group * SUB, SUB), SUB)
        scale, r, slab = steady[0, lines, :], steady[1, lines, :], steady[2, lines, :]
        decays = [None, jnp.ones((SUB, LANES), f32), slab]
        while len(decays) <= len(received):
            decays.append(decays[-1] * slab)
        for q in range(BLK // 2):
            lanes = slice(q * LANES, (q + 1) * LANES)
            from_left = from_right = jnp.zeros((SUB, LANES), f32)
            for n, ref in enumerate(received, 1):
                distance = jnp.abs((g ^ n) - g)
                factor = decays[n]
                for d in range(1, n):
                    factor = jnp.where(distance == d, decays[d], factor)
                value = factor * ref[lines, lanes]
                is_left = (g ^ n) < g
                from_left = from_left + jnp.where(is_left, value, 0.0)
                from_right = from_right + jnp.where(is_left, 0.0, value)
            before = scale * (powers[2, lines, :] * from_left
                              + r * powers[3, lines, :] * (b_in[lines, lanes] + slab * from_right))
            after = scale * (powers[4, lines, :] * from_right
                             + r * powers[5, lines, :] * (a_in[lines, lanes] + slab * from_left))
            for k in range(SUB):
                rows = pl.ds(pl.multiple_of((group * SUB + k) * SUB, SUB), SUB)
                edge = first * before[k:k + 1] + last * after[k:k + 1]
                work[rows, lanes] = inverse[rows, :] * (spectrum[rows, lanes] + edge)
        return carry

    lax.fori_loop(0, NY // SUB, ends, 0)
    z = (z_hi[...], z_lo[...])
    half = pot.shape[0]
    for parity in range(2):
        part = pl.ds(parity * half, half)
        work[part, :] = dot3((y_hi[parity], y_lo[parity]), split(work[part, :]))
    for q in range(BLK // 2):
        lanes = slice(q * LANES, (q + 1) * LANES)
        even, odd = work[:half, lanes], work[half:, lanes]
        rows = jnp.concatenate([even + odd, turned(even - odd)], axis=1)
        pot[:, q * 2 * LANES:(q + 1) * 2 * LANES] = dot3(split(rows), z)
    for side, group in ((0, own), (1, other)):
        half = (core if side == 0 else 1 - core) * (len(own) * tiles)
        for n, ref in enumerate(group):
            for t in range(tiles):
                lanes = pl.ds(t * LANES, LANES)
                at = half + n * tiles + t
                rows = pl.ds(pl.multiple_of(at * SUB, SUB), SUB)
                total = None
                for w in range(BLK):
                    term = flags[u * BLK + w] * (pot[rows, w * LANES:(w + 1) * LANES] * ref[1 + w, :, lanes])
                    total = term if total is None else total + term
                out[:, pl.ds(pl.multiple_of(at * LANES, LANES), LANES)] = -total


def place_kernel(stride, match, *refs):
    parts, (out, rows, sem) = refs[:-4], refs[-3:]
    pair = BLK // 2
    blocks = out.shape[0] // BLK
    core = my_core()
    values = []
    for part in parts:
        values += [part] if len(part.shape) == 2 else [part.at[n] for n in range(part.shape[0])]
    parts, count = values, len(values) // pair

    def hits(b, side):
        return [(match[b * stride + side * stride // 2 + n], side * count // 2 + n) for n in range(count // 2)]

    def found(b, side):
        return sum(hit for hit, n in hits(b, side)) > 0

    def move(b, side):
        which = core if side == 0 else 1 - core
        at = b * BLK + which * pair
        return pltpu.make_async_copy(rows.at[b, side], out.at[pl.ds(at, pair)], sem.at[b, side])

    for b in range(blocks):
        for side in range(2):

            @pl.when(found(b, side))
            def _():
                rows[b, side] = jnp.zeros(rows.shape[2:], f32)
                for hit, n in hits(b, side):

                    @pl.when(hit > 0)
                    def _():
                        for u in range(pair):
                            rows[b, side, u] += parts[u * count + n][...]

                move(b, side).start()

    for b in range(blocks):
        for side in range(2):

            @pl.when(found(b, side))
            def _():
                move(b, side).wait()


def tile_device(orbitals, rotation, tile_list, pair_mask):
    shape = per_device, planes, width = orbitals.shape
    n_orb, n_grid = lax.axis_size("orb"), lax.axis_size("grid")
    size_x = planes * n_grid
    half = width // 2
    chips = n_orb // 2
    axes = ("orb", "grid")

    def swap(x, even, odd):
        moves = []
        for a in range(n_orb):
            flip = even if a % 2 == 0 else odd
            moves += [(a * n_grid + b, (a ^ flip) * n_grid + b) for b in range(n_grid)]
        return lax.ppermute(x, axes, moves)

    def cross(x, k):
        moves = [(a * n_grid + b, a * n_grid + (b ^ k)) for a in range(n_orb) for b in range(n_grid)]
        return lax.ppermute(x, axes, moves)

    chunk = half // CHUNKS
    orbitals = pltpu.with_memory_space_constraint(orbitals, pltpu.HBM)

    part = jax.ShapeDtypeStruct((per_device, planes, chunk), f32)
    copies = per_device // 2
    taken = pl.pallas_call(
        functools.partial(take_kernel, 0), out_shape=part, in_specs=[HBM], out_specs=VM,
        scratch_shapes=[DMA((copies,))], name="take", compiler_params=grant(4),
    )(orbitals)
    theirs = [swap(taken, 1, 1)]

    pair = BLK // 2
    firsts = (BLK + 2) * chips
    rows = (firsts + 2 * (pair - 1) * chips) * SUB
    wide_table = jax.ShapeDtypeStruct((rows, 2 * LANES), bf16)
    blocks = per_device // BLK
    c, r = line_np()
    c, r = line_np()
    host = jnp.asarray(host_np(chips).reshape(-1))
    *fetched, high, low = pl.pallas_call(
        functools.partial(setup_kernel, per_device),
        out_shape=[part] * (2 * CHUNKS - 1) + [wide_table] * 2,
        in_specs=[SM, SM, VM, HBM, ANY], out_specs=[VM] * (2 * CHUNKS + 1),
        scratch_shapes=[DMA((2 * CHUNKS - 1, copies))], name="setup", compiler_params=grant(8),
    )(tile_list, host, rotation, orbitals, taken)
    mine = fetched[CHUNKS - 1:]
    for n, taken in enumerate(fetched[:CHUNKS - 1], 1):
        theirs.append(swap(taken, 1, 1))

    def rotate(first, count, fields, *after):
        part = jax.ShapeDtypeStruct((count, planes, chunk * (len(fields) // 2)), f32)
        send, keep = pl.pallas_call(
            functools.partial(rotate_kernel, first * SUB), out_shape=(part, part),
            in_specs=[VM] * (2 + len(fields)) + [ANY] * len(after),
            out_specs=(VM, VM), compiler_params=grant(8),
        )(high, low, *fields, *after)
        return send, keep, swap(send, 2, 4)

    sums, last = [], ()
    for n in range(CHUNKS):
        sums.append(rotate(0, firsts // 2, [mine[n], theirs[n]], *last))
        last = (sums[-1][0],)
    both = [x for n in range(CHUNKS) for x in (mine[n], theirs[n])]
    sums.append(rotate(firsts, (pair - 1) * chips, both, *last))
    empty, powers, flags, match, alone = pl.pallas_call(
        functools.partial(ready_kernel, per_device, n_grid),
        out_shape=(pltpu.HBM(shape, f32), jax.ShapeDtypeStruct((6, NY, LANES), f32),
                   jax.ShapeDtypeStruct((pair * BLK,), f32), jax.ShapeDtypeStruct((blocks * 8,), jnp.int32),
                   jax.ShapeDtypeStruct((1,), jnp.int32)),
        in_specs=[SM, SM, VM, VM, ANY], out_specs=(HBM, VM, SM, SM, SM),
        scratch_shapes=[pltpu.VMEM((pair, planes, width), f32), DMA((per_device // pair,))], name="ready",
        compiler_params=grant(4),
    )(tile_list, host, pair_mask, jnp.asarray(np.log(r), f32), sums[-1][0])
    passing, own, other = [], [], []

    def pass_on(n, *after, spec=ANY):
        _, keep, got = sums[n]
        count = keep.shape[0] // 2
        value = pl.pallas_call(
            pass_kernel, out_shape=jax.ShapeDtypeStruct((count,) + keep.shape[1:], f32),
            in_specs=[VM] * 2 + [spec] * len(after), out_specs=VM, compiler_params=grant(4),
        )(keep, got, *after)
        passing.append((keep, got, swap(value, 4, 2)))
        return value

    def finish(n, *after):
        keep, got, passed = passing[n]
        own.append(pl.pallas_call(
            finish_kernel, out_shape=jax.ShapeDtypeStruct(passed.shape, f32), in_specs=[VM] * 3 + [ANY] * len(after),
            out_specs=VM, compiler_params=grant(4),
        )(keep, got, passed, *after))
        other.append(swap(own[-1], 1, 1))
        return own[-1]

    step = pass_on(0, empty, spec=HBM)
    for n in range(1, CHUNKS):
        step = pass_on(n, step)
    for n in range(CHUNKS):
        step = finish(n, step)
    last = (step,)

    sine_x, eigen_x = sine_np(planes), eigen_np(planes)
    ends = jnp.asarray(np.einsum("jp,pkl->kjl", sine_x, r[None] ** np.arange(planes - 1, -1, -1)[:, None, None])
                       .reshape(-1, LANES), f32)
    inverse = jnp.asarray((COUPLING / (eigen_x[None, :, None] + c[:, None, :])).reshape(-1, LANES), f32)
    basis = jnp.asarray(np.broadcast_to(sine_x[:, [0, -1]].T[:, :, None], (2, planes, LANES)), f32)
    steady = jnp.asarray(np.stack([r / ((1 - r**2) * (1 - r ** (2 * size_x + 2))), r, r**planes]), f32)

    y_there, y_back = y_tables()
    y_hi, y_lo = halves_np(y_there)
    yt_hi, yt_lo = halves_np(y_back)
    z_hi, z_lo = halves_np(z_table())
    zt_hi, zt_lo = halves_np(z_table().T)
    solved = []
    lines = jax.ShapeDtypeStruct((NY, 2 * LANES), f32)
    cube = (NY * SUB, 2 * LANES)
    wide = pltpu.VMEM((width // LANES * SUB, BLK * LANES), f32)
    base_own, base_other = own[:CHUNKS], other[:CHUNKS]
    for u in range(pair):
        if u:
            pass_on(CHUNKS, *last)
            finish(CHUNKS, *last)
        more_own, more_other = own[CHUNKS:][:u], other[CHUNKS:][:u]
        counts = (CHUNKS, CHUNKS, len(more_own), len(more_other))
        inputs = [*base_own, *base_other, *more_own, *more_other, y_hi, y_lo, z_hi, z_lo, ends, powers]
        *messages, spectrum, a, b = pl.pallas_call(
            functools.partial(forward_kernel, u, counts + (n_grid - 1,)),
            out_shape=[lines] * (n_grid - 1) + [jax.ShapeDtypeStruct(cube, f32), lines, lines],
            in_specs=[VM] * len(inputs) + [ANY] * len(last),
            out_specs=[VM] * (n_grid + 2),
            scratch_shapes=[wide],
            compiler_params=grant(16),
        )(*inputs, *last)
        last = (spectrum,)
        received = []
        for k, message in enumerate(messages, 1):
            received.append(cross(message, k))
        solved.append((spectrum, a, b, received))

    terms, last = [], ()
    for u, (spectrum, a, b, received) in enumerate(solved):
        inputs = [*base_own, *base_other, *received, yt_hi, yt_lo, zt_hi, zt_lo, inverse, basis, powers, steady,
                  spectrum, a, b]
        terms.append(pl.pallas_call(
            functools.partial(backward_kernel, u, (CHUNKS, CHUNKS, len(received))),
            out_shape=jax.ShapeDtypeStruct((planes, width), f32),
            in_specs=[SM] + [VM] * len(inputs) + [ANY] * len(last),
            out_specs=VM,
            scratch_shapes=[pltpu.VMEM(cube, f32), wide],
            compiler_params=grant(16),
        )(flags, *inputs, *last))
        last = (terms[-1],)

    near_1 = [swap(term, 2, 4) for term in terms]
    near_2 = [swap(term, 4, 2) for term in terms]
    own_parts = [[term, x, y] for term, x, y in zip(terms, near_1, near_2)]
    sib_parts = []
    for term, x, y in own_parts:
        joined = pl.pallas_call(
            join_kernel, out_shape=jax.ShapeDtypeStruct((2,) + term.shape, f32), in_specs=[VM] * 2, out_specs=VM,
            compiler_params=grant(4),
        )(x, y)
        given = swap(term, 1, 1)
        sib_parts.append([given, swap(joined, 1, 1)])

    def place(target, groups):
        parts = [part for group in groups for part in group]
        return pl.pallas_call(
            functools.partial(place_kernel, 8),
            out_shape=pltpu.HBM(shape, f32),
            in_specs=[SM] + [VM] * len(parts) + [HBM],
            out_specs=HBM,
            input_output_aliases={len(parts) + 1: 0},
            scratch_shapes=[pltpu.VMEM((blocks, 2, pair, planes, width), f32), DMA((blocks, 2))],
            name="place",
            compiler_params=grant(8),
        )(match, *parts, target)

    def place_near(target, mine, sibs):
        return place(target, [a + b for a, b in zip(mine, sibs)])

    def place_far(target, mine, sibs):
        far = [swap(group[1], 4, 2) for group in mine]
        return place(target, [a + [x] + b + [swap(x, 1, 1)] for a, b, x in zip(mine, sibs, far)])

    return lax.cond(alone[0] != 0, place_far, place_near, empty, own_parts, sib_parts)


def sine_table(length):
    wave_index = jnp.arange(length, dtype=f32) + 1.0
    return jnp.sqrt(2.0 / (length + 1.0)) * jnp.sin(
        jnp.pi * wave_index[:, None] * wave_index[None, :] / (length + 1.0)
    )


def eigen_values(length):
    wave_index = jnp.arange(length, dtype=f32) + 1.0
    return 2.0 - 2.0 * jnp.cos(jnp.pi * wave_index / (length + 1.0))


def green_kernel(size_x, size_y, size_z):
    summed = (
        eigen_values(size_x)[:, None, None]
        + eigen_values(size_y)[None, :, None]
        + eigen_values(size_z)[None, None, :]
    )
    return COUPLING / (summed + SCREENING)


def pair_lists(tile_list, pair_mask):
    within = jnp.arange(BLK * BLK, dtype=jnp.int32)
    targets = (BLK * tile_list[:, 0:1] + within[None, :] // BLK).reshape(-1)
    sources = (BLK * tile_list[:, 1:2] + within[None, :] % BLK).reshape(-1)
    return (targets, sources, pair_mask[targets, sources])


def compact(targets, sources, live_flags, number):
    ranking = jnp.cumsum(live_flags) - 1
    places = jnp.where(live_flags == 1, ranking, number)
    picked = (
        jnp.zeros((number,), jnp.int32)
        .at[places]
        .set(jnp.arange(live_flags.shape[0], dtype=jnp.int32), mode="drop")
    )
    return (targets[picked], sources[picked])


def along_z(values, matrix):
    number, planes, width_yz = values.shape
    size_z = matrix.shape[0]
    shaped = values.reshape(number, planes, width_yz // size_z, size_z)
    return jnp.einsum("pxrz,zk->pxrk", shaped, matrix, precision=precise).reshape(number, planes, width_yz)


def along_y(values, matrix):
    number, planes, width_yz = values.shape
    size_y = matrix.shape[0]
    shaped = values.reshape(number, planes, size_y, width_yz // size_y)
    return jnp.einsum("pxyz,yk->pxkz", shaped, matrix, precision=precise).reshape(number, planes, width_yz)


def along_x(values, matrix):
    return jnp.einsum("pxc,xk->pkc", values, matrix, precision=precise)


def any_device(orbitals, rotation, tile_list, pair_mask):
    n_grid = lax.axis_size("grid")
    number_orbitals, size_x = rotation.shape[0], orbitals.shape[1] * n_grid
    rotated = jnp.einsum(
        "ij,ixc->jxc",
        rotation,
        lax.all_to_all(orbitals, "orb", split_axis=2, concat_axis=0, tiled=True),
        precision=precise,
    )
    planes, width_yz = rotated.shape[1:]
    targets, sources, live_flags = pair_lists(tile_list, pair_mask)
    matrix_x, matrix_y, matrix_z = sine_table(size_x), sine_table(NY), sine_table(NZ)
    kernel = green_kernel(size_x, NY, NZ).reshape(size_x, NY * NZ)
    orbital_ids = jnp.arange(number_orbitals, dtype=jnp.int32)
    targets, sources = compact(targets, sources, live_flags, targets.shape[0] // 2)
    density = rotated[targets] * rotated[sources]
    number = density.shape[0]
    spectrum = along_z(density, matrix_z)
    spectrum = lax.all_to_all(spectrum, "orb", split_axis=0, concat_axis=2, tiled=True)
    spectrum = along_y(spectrum, matrix_y)
    spectrum = lax.all_to_all(spectrum, "grid", split_axis=0, concat_axis=1, tiled=True)
    spectrum = along_x(along_x(spectrum, matrix_x) * kernel, matrix_x)
    spectrum = lax.all_to_all(spectrum, "grid", split_axis=1, concat_axis=0, tiled=True)
    spectrum = along_y(spectrum, matrix_y)
    spectrum = lax.all_to_all(spectrum, "orb", split_axis=2, concat_axis=0, tiled=True)
    potential = along_z(spectrum, matrix_z)
    products = potential * rotated[sources]
    selector = (targets[None, :] == orbital_ids[:, None]).astype(f32)
    partial_value = -jnp.dot(selector, products.reshape(number, planes * width_yz), precision=precise)
    partial_value = partial_value.reshape(number_orbitals, planes, width_yz)
    return lax.all_to_all(partial_value, "orb", split_axis=0, concat_axis=2, tiled=True)


def solution(mesh):
    n_orb, n_grid = mesh.shape["orb"], mesh.shape["grid"]

    def on_device(orbitals, rotation, tile_list, pair_mask):
        per_device, planes, width = orbitals.shape
        fits = n_orb == 8 and 2 * tile_list.shape[0] == n_orb and planes == SUB and per_device % BLK == 0
        fits = fits and width == NY * NZ and 2 * NZ == LANES and n_grid in (2, 4, 8)
        fits = fits and per_device * SUB == LANES and rotation.shape == (LANES, LANES)
        if not fits:
            return any_device(orbitals, rotation, tile_list, pair_mask)
        return tile_device(orbitals, rotation, tile_list, pair_mask)

    in_specs = (P("orb", "grid", None), P(), P(), P())
    out_specs = P("orb", "grid", None)
    return jax.shard_map(on_device, mesh=mesh, in_specs=in_specs, out_specs=out_specs, check_vma=False)
```

```python
import functools
import itertools

import jax
import jax.numpy as jnp
import numpy as np
from jax import lax
from jax.experimental import pallas as pl
from jax.experimental.pallas import tpu as pltpu
from jax.sharding import PartitionSpec as P


BLK = 4
NY = 64
NZ = 64
LANES = 128
SUB = 8
CHUNKS = 2
COUPLING = 0.25
SCREENING = 0.1

precise = lax.Precision.HIGHEST
f32 = jnp.float32
bf16 = jnp.bfloat16

VM = pl.BlockSpec(memory_space=pltpu.VMEM)
SM = pl.BlockSpec(memory_space=pltpu.SMEM)
ANY = pl.BlockSpec(memory_space=pl.ANY)
HBM = pl.BlockSpec(memory_space=pltpu.HBM)
DMA = pltpu.SemaphoreType.DMA


def grant(mib):
    return pltpu.CompilerParams(vmem_limit_bytes=mib << 20)


def sine_np(n):
    k = np.arange(1, n + 1, dtype=np.float64)
    return np.sqrt(2.0 / (n + 1)) * np.sin(np.pi * k[:, None] * k[None, :] / (n + 1))


def eigen_np(n):
    k = np.arange(1, n + 1, dtype=np.float64)
    return 2.0 - 2.0 * np.cos(np.pi * k / (n + 1))


def halves_np(table):
    high = np.asarray(table, np.float32).astype(jnp.bfloat16)
    low = (np.asarray(table, np.float64) - high.astype(np.float64)).astype(jnp.bfloat16)
    return jnp.asarray(high), jnp.asarray(low)


def y_order():
    rows = LANES // NZ
    return np.arange(NY).reshape(NY // rows, rows).T.reshape(-1)


def y_tables():
    sine, planes = sine_np(NY), sine_np(SUB)
    even, odd = np.kron(sine[0::2, 0::2], planes), np.kron(sine[1::2, 0::2], planes)
    return np.stack([even, odd]), np.stack([even, odd.T])


def turned(x):
    count = x.shape[0] // SUB
    return jnp.concatenate([x[(count - 1 - t) * SUB:(count - t) * SUB] for t in range(count)])


def z_table():
    half = LANES // NZ
    sine = sine_np(NZ)
    table = np.zeros((2, half, NZ, half, 2, NZ))
    for pair in range(2):
        for h in range(half):
            table[pair, h, :, h, pair, :] = sine
    return table.reshape(2 * half * NZ, half * 2 * NZ)


def line_np():
    c = eigen_np(NY)[y_order()][:, None] + eigen_np(NZ)[None, :] + SCREENING
    c = np.concatenate([c, c], axis=1)
    return c, 2.0 / (2.0 + c + np.sqrt(c * (c + 4.0)))


def host_np(chips):
    table = np.zeros((chips**chips, chips), np.int32)
    for owners in itertools.product(range(chips), repeat=chips):
        best = None
        for tiles in itertools.permutations(range(chips)):
            hops = [bin(chip ^ owners[tile]).count("1") for chip, tile in enumerate(tiles)]
            cost = (max(hops), sum(hops))
            if best is None or cost < best[0]:
                best = (cost, tiles)
        table[sum(own * chips**t for t, own in enumerate(owners))] = best[1]
    return table


def dot(a, b):
    return jnp.dot(a, b, preferred_element_type=f32)


def split(x):
    high = x.astype(bf16)
    return high, (x - high.astype(f32)).astype(bf16)


def dot3(a, b):
    return dot(a[0], b[0]) + dot(a[0], b[1]) + dot(a[1], b[0])


def my_core():
    return lax.rem(lax.axis_index("orb"), 2)


def my_place():
    o = lax.axis_index("orb")
    return o, lax.rem(o, 2), lax.div(o, 2)


def take_kernel(start, source, *rest):
    out = rest[-1]
    at = (1 - my_core()) * (source.shape[2] // 2) + start
    out[...] = source[:, :, pl.ds(pl.multiple_of(at, LANES), out.shape[2])]


class Place:
    def __init__(self, per_device, tiles, host):
        self.o, self.core, self.chip = my_place()
        self.tiles, self.host = tiles, host
        self.chips = tiles.shape[0]
        owners = [lax.div(tiles[t, 0] * BLK, 2 * per_device) for t in range(self.chips)]
        key, same = 0, True
        for t in range(self.chips):
            key = key + owners[t] * self.chips**t
            same = same & (owners[t] == owners[0])
        self.key, self.same = key, same
        self.bit_1 = jnp.where(self.core == 0, 1, 2)
        self.bit_2 = 3 - self.bit_1

    def tile(self, chip):
        return self.host[self.key * self.chips + chip]

    def heads(self, chip):
        tile = self.tile(chip)
        return BLK * self.tiles[tile, 0], BLK * self.tiles[tile, 1]


def setup_kernel(per_device, tiles, host, rotation, source, loaded, high, low, sem):
    core = my_core()
    step = per_device // sem.shape[0]
    copies = [
        pltpu.make_async_copy(source.at[pl.ds(n * step, step)], loaded.at[pl.ds(n * step, step)], sem.at[n])
        for n in range(sem.shape[0])
    ]
    for copy in copies:
        copy.start()
    at = Place(per_device, tiles, host)
    pair = BLK // 2
    heads = [at.heads(chip) for chip in (at.chip ^ 3, at.chip ^ at.bit_1, at.chip ^ at.bit_2, at.chip)]
    wanted = []
    for a, b in heads:
        wanted += [a + (1 - core) * pair] + [b + w for w in range(BLK)] + [a + core * pair]
    for u in range(1, pair):
        for a, b in heads:
            wanted += [a + (1 - core) * pair + u, a + core * pair + u]
    lane = lax.broadcasted_iota(jnp.int32, (SUB, LANES), 1)
    chosen = jnp.concatenate([jnp.where(lane == n, 1.0, 0.0) for n in wanted]).astype(bf16)
    rows = chosen.shape[0]
    row = lax.broadcasted_iota(jnp.int32, (LANES, LANES), 0)
    column = lax.broadcasted_iota(jnp.int32, (LANES, LANES), 1)
    columns = [
        jnp.where(row - (at.o ^ e) * per_device == jnp.right_shift(column, 3), 1.0, 0.0).astype(bf16)
        for e in range(2)
    ]
    keep = (lax.broadcasted_iota(jnp.int32, (rows, LANES), 0) & (SUB - 1)) == (
        lax.broadcasted_iota(jnp.int32, (rows, LANES), 1) & (SUB - 1)
    )
    for out, values in zip((high, low), split(rotation[...])):
        picked = lax.dot_general(chosen, values, (((1,), (1,)), ((), ())), preferred_element_type=f32).astype(bf16)
        for e in range(2):
            out[:, e * LANES:(e + 1) * LANES] = jnp.where(keep, dot(picked, columns[e]), 0.0).astype(bf16)
    for copy in copies:
        copy.wait()


def ready_kernel(per_device, n_grid, tiles, host, mask, log_r, *rest):
    out, powers, flags, match, alone, zeros, sem = rest[-7:]
    zeros[...] = jnp.zeros(zeros.shape, f32)
    step = zeros.shape[0]
    copies = [
        pltpu.make_async_copy(zeros, out.at[pl.ds(n * step, step)], sem.at[n]) for n in range(out.shape[0] // step)
    ]
    for copy in copies:
        copy.start()
    begin, size_x = SUB * lax.axis_index("grid"), SUB * n_grid
    exponents = (
        2 * begin + SUB + 1,
        2 * size_x + 1 - SUB - 2 * begin,
        2 * size_x + 2 - 2 * begin,
        2 * begin,
        2 * begin + 2 * SUB + 2,
        2 * size_x - 2 * SUB - 2 * begin,
    )
    for n, exponent in enumerate(exponents):
        power = jnp.exp(exponent.astype(f32) * log_r[...])
        powers[n] = power if n < 2 else 1.0 - power
    at = Place(per_device, tiles, host)
    alone[0] = at.same.astype(jnp.int32)
    a, b = at.heads(at.chip)
    pair = BLK // 2
    live = mask[...].astype(f32)
    row = lax.broadcasted_iota(jnp.int32, live.shape, 0)
    column = lax.broadcasted_iota(jnp.int32, (1, live.shape[1]), 1)
    for u in range(pair):
        line = jnp.sum(jnp.where(row == a + at.core * pair + u, live, 0.0), axis=0, keepdims=True)
        for w in range(BLK):
            flags[u * BLK + w] = jnp.sum(jnp.where(column == b + w, line, 0.0))
    blocks = per_device // BLK
    parts = [0, at.bit_1, at.bit_2, 3, 0, at.bit_2, at.bit_1, 3]
    for n, flip in enumerate(parts):
        home = tiles[at.tile(at.chip ^ flip), 0]
        for block in range(blocks):
            hit = home == at.o * blocks + block
            if n % 4 == 3:
                hit = hit & at.same
            match[block * len(parts) + n] = hit.astype(jnp.int32)
    for copy in copies:
        copy.wait()


def join_kernel(x, y, out):
    out[0] = x[...]
    out[1] = y[...]


def rotate_kernel(first, start, high, low, mine, *rest):
    send, keep = rest[-2:]
    begin = my_core() * (mine.shape[2] // 2) + start
    rows = send.shape[0] * SUB
    part = pl.ds(first, 2 * rows)
    table = (high[part, :], low[part, :])
    at = 0
    step = 2 * LANES
    while at < send.shape[2]:
        width = rest[0].shape[2]
        n, inner = at // width, at % width
        theirs = rest[n]
        depth = theirs.shape[0] * SUB
        own = pl.ds(pl.multiple_of(begin + at, LANES), step)
        cells = jnp.concatenate([
            mine[:, :, own].reshape(depth, step), theirs[:, :, inner:inner + step].reshape(depth, step)
        ])
        total = dot3(table, split(cells))
        lanes = slice(at, at + step)
        send[:, :, lanes] = total[:rows].reshape(send.shape[0], SUB, step)
        keep[:, :, lanes] = total[rows:].reshape(keep.shape[0], SUB, step)
        at += step


def pass_kernel(keep, got, *rest):
    out = rest[-1]
    count = out.shape[0]
    out[...] = keep[:count] + got[:count]


def finish_kernel(keep, got, passed, *rest):
    out = rest[-1]
    count = out.shape[0]
    out[...] = keep[count:] + got[count:] + passed[...]


def sub_sums(values):
    row = lax.broadcasted_iota(jnp.int32, values[0].shape, 0)
    for s in (4, 2):
        low = (row & s) == 0
        paired = []
        for n in range(s):
            a, b = values[n], values[n + s]
            paired.append(jnp.where(low, a, pltpu.roll(b, s, 0)) + jnp.where(low, pltpu.roll(a, SUB - s, 0), b))
        values = paired
    even = (row & 1) == 0
    a, b = values
    return jnp.where(even, a, pltpu.roll(b, 1, 0)), jnp.where(even, pltpu.roll(a, SUB - 1, 0), b)


def fields(u, own, other, first_own, first_other):
    table = []
    for side, sources, targets in ((0, first_own, own), (1, first_other, other)):
        for n, ref in enumerate(sources):
            if u == 0:
                table.append((side, n, ref, targets[n], BLK + 1 if side == 0 else 0, 0))
            else:
                table.append((side, n, ref, targets[0], 1 if side == 0 else 0, n * ref.shape[2]))
    return table


def forward_kernel(u, counts, *refs):
    groups = []
    for count in counts[:-1]:
        groups.append(refs[:count])
        refs = refs[count:]
    first_own, first_other, own, other = groups[:4]
    y_hi, y_lo, z_hi, z_lo, ends, powers = refs[:6]
    messages, (spectrum, a_out, b_out, dens) = refs[-4 - counts[-1]:-4], refs[-4:]
    if u == 0:
        own, other = first_own, first_other
    core, g = my_core(), lax.axis_index("grid")
    tiles = first_own[0].shape[2] // LANES
    for side, n, source, target, slot, offset in fields(u, own, other, first_own, first_other):
        half = (core if side == 0 else 1 - core) * (len(first_own) * tiles * SUB)
        for t in range(tiles):
            lanes = pl.ds(t * LANES, LANES)
            value = target[slot, :, pl.ds(offset + t * LANES, LANES)]
            rows = pl.ds(pl.multiple_of(half + (n * tiles + t) * SUB, SUB), SUB)
            for w in range(BLK):
                dens[rows, w * LANES:(w + 1) * LANES] = value * source[1 + w, :, lanes]
    z = (z_hi[...], z_lo[...])
    half = dens.shape[0]
    for q in range(BLK // 2):
        out = dot3(split(dens[:, q * 2 * LANES:(q + 1) * 2 * LANES]), z)
        mirror = turned(out[:, LANES:])
        spectrum[:half, q * LANES:(q + 1) * LANES] = out[:, :LANES] + mirror
        spectrum[half:, q * LANES:(q + 1) * LANES] = out[:, :LANES] - mirror
    for parity in range(2):
        part = pl.ds(parity * half, half)
        spectrum[part, :] = dot3((y_hi[parity], y_lo[parity]), split(spectrum[part, :]))

    def reduce(group, carry):
        lines = pl.ds(pl.multiple_of(group * SUB, SUB), SUB)
        near, far = powers[0, lines, :], powers[1, lines, :]
        for q in range(BLK // 2):
            lanes = slice(q * LANES, (q + 1) * LANES)
            values = []
            for k in range(SUB):
                rows = pl.ds(pl.multiple_of((group * SUB + k) * SUB, SUB), SUB)
                values.append(ends[rows, :] * spectrum[rows, lanes])
            even, odd = sub_sums(values)
            rightward = (even + odd) - near * (even - odd)
            leftward = (even - odd) - far * (even + odd)
            a_out[lines, lanes] = rightward
            b_out[lines, lanes] = leftward
            for k, out in enumerate(messages, 1):
                out[lines, lanes] = jnp.where((g ^ k) > g, rightward, leftward)
        return carry

    lax.fori_loop(0, NY // SUB, reduce, 0)


def backward_kernel(u, counts, flags, *refs):
    groups = []
    for count in counts:
        groups.append(refs[:count])
        refs = refs[count:]
    own, other, received = groups
    (y_hi, y_lo, z_hi, z_lo, inverse, basis, powers, steady, spectrum, a_in, b_in) = refs[:11]
    out, work, pot = refs[-3:]
    core, g = my_core(), lax.axis_index("grid")
    tiles = own[0].shape[2] // LANES
    first, last = basis[0], basis[1]

    def ends(group, carry):
        lines = pl.ds(pl.multiple_of(group * SUB, SUB), SUB)
        scale, r, slab = steady[0, lines, :], steady[1, lines, :], steady[2, lines, :]
        decays = [None, jnp.ones((SUB, LANES), f32), slab]
        while len(decays) <= len(received):
            decays.append(decays[-1] * slab)
        for q in range(BLK // 2):
            lanes = slice(q * LANES, (q + 1) * LANES)
            from_left = from_right = jnp.zeros((SUB, LANES), f32)
            for n, ref in enumerate(received, 1):
                distance = jnp.abs((g ^ n) - g)
                factor = decays[n]
                for d in range(1, n):
                    factor = jnp.where(distance == d, decays[d], factor)
                value = factor * ref[lines, lanes]
                is_left = (g ^ n) < g
                from_left = from_left + jnp.where(is_left, value, 0.0)
                from_right = from_right + jnp.where(is_left, 0.0, value)
            before = scale * (powers[2, lines, :] * from_left
                              + r * powers[3, lines, :] * (b_in[lines, lanes] + slab * from_right))
            after = scale * (powers[4, lines, :] * from_right
                             + r * powers[5, lines, :] * (a_in[lines, lanes] + slab * from_left))
            for k in range(SUB):
                rows = pl.ds(pl.multiple_of((group * SUB + k) * SUB, SUB), SUB)
                edge = first * before[k:k + 1] + last * after[k:k + 1]
                work[rows, lanes] = inverse[rows, :] * (spectrum[rows, lanes] + edge)
        return carry

    lax.fori_loop(0, NY // SUB, ends, 0)
    z = (z_hi[...], z_lo[...])
    half = pot.shape[0]
    for parity in range(2):
        part = pl.ds(parity * half, half)
        work[part, :] = dot3((y_hi[parity], y_lo[parity]), split(work[part, :]))
    for q in range(BLK // 2):
        lanes = slice(q * LANES, (q + 1) * LANES)
        even, odd = work[:half, lanes], work[half:, lanes]
        rows = jnp.concatenate([even + odd, turned(even - odd)], axis=1)
        pot[:, q * 2 * LANES:(q + 1) * 2 * LANES] = dot3(split(rows), z)
    for side, group in ((0, own), (1, other)):
        half = (core if side == 0 else 1 - core) * (len(own) * tiles)
        for n, ref in enumerate(group):
            for t in range(tiles):
                lanes = pl.ds(t * LANES, LANES)
                at = half + n * tiles + t
                rows = pl.ds(pl.multiple_of(at * SUB, SUB), SUB)
                total = None
                for w in range(BLK):
                    term = flags[u * BLK + w] * (pot[rows, w * LANES:(w + 1) * LANES] * ref[1 + w, :, lanes])
                    total = term if total is None else total + term
                out[:, pl.ds(pl.multiple_of(at * LANES, LANES), LANES)] = -total


def place_kernel(stride, sides, match, *refs):
    parts, (out, rows, sem) = refs[:-4], refs[-3:]
    pair = BLK // 2
    blocks = out.shape[0] // BLK
    core = my_core()
    values = []
    for part in parts:
        values += [part] if len(part.shape) == 2 else [part.at[n] for n in range(part.shape[0])]
    count = len(values) // (pair * len(sides))

    def hits(b, side):
        return [match[b * stride + side * stride // 2 + n] for n in range(count)]

    def move(b, at):
        which = core if sides[at] == 0 else 1 - core
        begin = b * BLK + which * pair
        return pltpu.make_async_copy(rows.at[b, at], out.at[pl.ds(begin, pair)], sem.at[b, at])

    for b in range(blocks):
        for at, side in enumerate(sides):

            @pl.when(sum(hits(b, side)) > 0)
            def _():
                rows[b, at] = jnp.zeros(rows.shape[2:], f32)
                for n, hit in enumerate(hits(b, side)):

                    @pl.when(hit > 0)
                    def _():
                        for u in range(pair):
                            rows[b, at, u] += values[(at * pair + u) * count + n][...]

                move(b, at).start()

    for b in range(blocks):
        for at, side in enumerate(sides):

            @pl.when(sum(hits(b, side)) > 0)
            def _():
                move(b, at).wait()


def tile_device(orbitals, rotation, tile_list, pair_mask):
    shape = per_device, planes, width = orbitals.shape
    n_orb, n_grid = lax.axis_size("orb"), lax.axis_size("grid")
    size_x = planes * n_grid
    half = width // 2
    chips = n_orb // 2
    axes = ("orb", "grid")

    def swap(x, even, odd):
        moves = []
        for a in range(n_orb):
            flip = even if a % 2 == 0 else odd
            moves += [(a * n_grid + b, (a ^ flip) * n_grid + b) for b in range(n_grid)]
        return lax.ppermute(x, axes, moves)

    def cross(x, k):
        moves = [(a * n_grid + b, a * n_grid + (b ^ k)) for a in range(n_orb) for b in range(n_grid)]
        return lax.ppermute(x, axes, moves)

    chunk = half // CHUNKS
    orbitals = pltpu.with_memory_space_constraint(orbitals, pltpu.HBM)
    part = jax.ShapeDtypeStruct((per_device, planes, chunk), f32)

    pair = BLK // 2
    firsts = (BLK + 2) * chips
    rows = (firsts + 2 * (pair - 1) * chips) * SUB
    wide_table = jax.ShapeDtypeStruct((rows, 2 * LANES), bf16)
    blocks = per_device // BLK
    c, r = line_np()
    c, r = line_np()
    host = jnp.asarray(host_np(chips).reshape(-1))
    loaded, high, low = pl.pallas_call(
        functools.partial(setup_kernel, per_device),
        out_shape=[jax.ShapeDtypeStruct(shape, f32)] + [wide_table] * 2,
        in_specs=[SM, SM, VM, HBM], out_specs=[VM] * 3, scratch_shapes=[DMA((4,))], name="setup",
        compiler_params=grant(8),
    )(tile_list, host, rotation, orbitals)
    theirs, last = [], ()
    for n in range(CHUNKS):
        taken = pl.pallas_call(
            functools.partial(take_kernel, n * chunk), out_shape=part, in_specs=[VM] + [ANY] * len(last), out_specs=VM,
            compiler_params=grant(8),
        )(loaded, *last)
        theirs.append(swap(taken, 1, 1))
        last = (taken,)

    def rotate(first, count, start, fields, *after):
        part = jax.ShapeDtypeStruct((count, planes, chunk * len(fields)), f32)
        send, keep = pl.pallas_call(
            functools.partial(rotate_kernel, first * SUB, start), out_shape=(part, part),
            in_specs=[VM] * (3 + len(fields)) + [ANY] * len(after),
            out_specs=(VM, VM), compiler_params=grant(8),
        )(high, low, loaded, *fields, *after)
        return send, keep, swap(send, 2, 4)

    sums, last = [], ()
    for n in range(CHUNKS):
        sums.append(rotate(0, firsts // 2, n * chunk, [theirs[n]], *last))
        last = (sums[-1][0],)
    sums.append(rotate(firsts, (pair - 1) * chips, 0, theirs, *last))
    empty, powers, flags, match, alone = pl.pallas_call(
        functools.partial(ready_kernel, per_device, n_grid),
        out_shape=(pltpu.HBM(shape, f32), jax.ShapeDtypeStruct((6, NY, LANES), f32),
                   jax.ShapeDtypeStruct((pair * BLK,), f32), jax.ShapeDtypeStruct((blocks * 8,), jnp.int32),
                   jax.ShapeDtypeStruct((1,), jnp.int32)),
        in_specs=[SM, SM, VM, VM, ANY], out_specs=(HBM, VM, SM, SM, SM),
        scratch_shapes=[pltpu.VMEM((pair, planes, width), f32), DMA((per_device // pair,))], name="ready",
        compiler_params=grant(4),
    )(tile_list, host, pair_mask, jnp.asarray(np.log(r), f32), sums[-1][0])
    passing, own, other = [], [], []

    def pass_on(n, *after, spec=ANY):
        _, keep, got = sums[n]
        count = keep.shape[0] // 2
        value = pl.pallas_call(
            pass_kernel, out_shape=jax.ShapeDtypeStruct((count,) + keep.shape[1:], f32),
            in_specs=[VM] * 2 + [spec] * len(after), out_specs=VM, compiler_params=grant(4),
        )(keep, got, *after)
        passing.append((keep, got, swap(value, 4, 2)))
        return value

    def finish(n, *after):
        keep, got, passed = passing[n]
        own.append(pl.pallas_call(
            finish_kernel, out_shape=jax.ShapeDtypeStruct(passed.shape, f32), in_specs=[VM] * 3 + [ANY] * len(after),
            out_specs=VM, compiler_params=grant(4),
        )(keep, got, passed, *after))
        other.append(swap(own[-1], 1, 1))
        return own[-1]

    step = pass_on(0, empty, spec=HBM)
    for n in range(1, CHUNKS):
        step = pass_on(n, step)
    for n in range(CHUNKS):
        step = finish(n, step)
    last = (pass_on(CHUNKS, step),)

    sine_x, eigen_x = sine_np(planes), eigen_np(planes)
    ends = jnp.asarray(np.einsum("jp,pkl->kjl", sine_x, r[None] ** np.arange(planes - 1, -1, -1)[:, None, None])
                       .reshape(-1, LANES), f32)
    inverse = jnp.asarray((COUPLING / (eigen_x[None, :, None] + c[:, None, :])).reshape(-1, LANES), f32)
    basis = jnp.asarray(np.broadcast_to(sine_x[:, [0, -1]].T[:, :, None], (2, planes, LANES)), f32)
    steady = jnp.asarray(np.stack([r / ((1 - r**2) * (1 - r ** (2 * size_x + 2))), r, r**planes]), f32)

    y_there, y_back = y_tables()
    y_hi, y_lo = halves_np(y_there)
    yt_hi, yt_lo = halves_np(y_back)
    z_hi, z_lo = halves_np(z_table())
    zt_hi, zt_lo = halves_np(z_table().T)
    solved = []
    lines = jax.ShapeDtypeStruct((NY, 2 * LANES), f32)
    cube = (NY * SUB, 2 * LANES)
    wide = pltpu.VMEM((width // LANES * SUB, BLK * LANES), f32)
    base_own, base_other = own[:CHUNKS], other[:CHUNKS]
    for u in range(pair):
        if u:
            finish(CHUNKS, *last)
        more_own, more_other = own[CHUNKS:][:u], other[CHUNKS:][:u]
        counts = (CHUNKS, CHUNKS, len(more_own), len(more_other))
        inputs = [*base_own, *base_other, *more_own, *more_other, y_hi, y_lo, z_hi, z_lo, ends, powers]
        *messages, spectrum, a, b = pl.pallas_call(
            functools.partial(forward_kernel, u, counts + (n_grid - 1,)),
            out_shape=[lines] * (n_grid - 1) + [jax.ShapeDtypeStruct(cube, f32), lines, lines],
            in_specs=[VM] * len(inputs) + [ANY] * len(last),
            out_specs=[VM] * (n_grid + 2),
            scratch_shapes=[wide],
            compiler_params=grant(16),
        )(*inputs, *last)
        last = (spectrum,)
        received = []
        for k, message in enumerate(messages, 1):
            received.append(cross(message, k))
        solved.append((spectrum, a, b, received))

    terms, last = [], ()
    for u, (spectrum, a, b, received) in enumerate(solved):
        inputs = [*base_own, *base_other, *received, yt_hi, yt_lo, zt_hi, zt_lo, inverse, basis, powers, steady,
                  spectrum, a, b]
        terms.append(pl.pallas_call(
            functools.partial(backward_kernel, u, (CHUNKS, CHUNKS, len(received))),
            out_shape=jax.ShapeDtypeStruct((planes, width), f32),
            in_specs=[SM] + [VM] * len(inputs) + [ANY] * len(last),
            out_specs=VM,
            scratch_shapes=[pltpu.VMEM(cube, f32), wide],
            compiler_params=grant(16),
        )(flags, *inputs, *last))
        last = (terms[-1],)

    near_1 = [swap(term, 2, 4) for term in terms]
    near_2 = [swap(term, 4, 2) for term in terms]
    own_parts = [[term, x, y] for term, x, y in zip(terms, near_1, near_2)]
    sib_parts = []
    for term, x, y in own_parts:
        joined = pl.pallas_call(
            join_kernel, out_shape=jax.ShapeDtypeStruct((2,) + term.shape, f32), in_specs=[VM] * 2, out_specs=VM,
            compiler_params=grant(4),
        )(x, y)
        given = swap(term, 1, 1)
        sib_parts.append([given, swap(joined, 1, 1)])

    def place(target, sides, groups):
        parts = [part for group in groups for part in group]
        return pl.pallas_call(
            functools.partial(place_kernel, 8, sides),
            out_shape=pltpu.HBM(shape, f32),
            in_specs=[SM] + [VM] * len(parts) + [HBM],
            out_specs=HBM,
            input_output_aliases={len(parts) + 1: 0},
            scratch_shapes=[pltpu.VMEM((blocks, len(sides), pair, planes, width), f32), DMA((blocks, len(sides)))],
            compiler_params=grant(8),
        )(match, *parts, target)

    def place_near(target, mine, sibs):
        return place(target, (1,), sibs)

    def place_far(target, mine, sibs):
        far = [swap(group[1], 4, 2) for group in mine]
        groups = [a + [x] for a, x in zip(mine, far)] + [b + [swap(x, 1, 1)] for b, x in zip(sibs, far)]
        return place(target, (0, 1), groups)

    empty = place(empty, (0,), own_parts)
    return lax.cond(alone[0] != 0, place_far, place_near, empty, own_parts, sib_parts)


def sine_table(length):
    wave_index = jnp.arange(length, dtype=f32) + 1.0
    return jnp.sqrt(2.0 / (length + 1.0)) * jnp.sin(
        jnp.pi * wave_index[:, None] * wave_index[None, :] / (length + 1.0)
    )


def eigen_values(length):
    wave_index = jnp.arange(length, dtype=f32) + 1.0
    return 2.0 - 2.0 * jnp.cos(jnp.pi * wave_index / (length + 1.0))


def green_kernel(size_x, size_y, size_z):
    summed = (
        eigen_values(size_x)[:, None, None]
        + eigen_values(size_y)[None, :, None]
        + eigen_values(size_z)[None, None, :]
    )
    return COUPLING / (summed + SCREENING)


def pair_lists(tile_list, pair_mask):
    within = jnp.arange(BLK * BLK, dtype=jnp.int32)
    targets = (BLK * tile_list[:, 0:1] + within[None, :] // BLK).reshape(-1)
    sources = (BLK * tile_list[:, 1:2] + within[None, :] % BLK).reshape(-1)
    return (targets, sources, pair_mask[targets, sources])


def compact(targets, sources, live_flags, number):
    ranking = jnp.cumsum(live_flags) - 1
    places = jnp.where(live_flags == 1, ranking, number)
    picked = (
        jnp.zeros((number,), jnp.int32)
        .at[places]
        .set(jnp.arange(live_flags.shape[0], dtype=jnp.int32), mode="drop")
    )
    return (targets[picked], sources[picked])


def along_z(values, matrix):
    number, planes, width_yz = values.shape
    size_z = matrix.shape[0]
    shaped = values.reshape(number, planes, width_yz // size_z, size_z)
    return jnp.einsum("pxrz,zk->pxrk", shaped, matrix, precision=precise).reshape(number, planes, width_yz)


def along_y(values, matrix):
    number, planes, width_yz = values.shape
    size_y = matrix.shape[0]
    shaped = values.reshape(number, planes, size_y, width_yz // size_y)
    return jnp.einsum("pxyz,yk->pxkz", shaped, matrix, precision=precise).reshape(number, planes, width_yz)


def along_x(values, matrix):
    return jnp.einsum("pxc,xk->pkc", values, matrix, precision=precise)


def any_device(orbitals, rotation, tile_list, pair_mask):
    n_grid = lax.axis_size("grid")
    number_orbitals, size_x = rotation.shape[0], orbitals.shape[1] * n_grid
    rotated = jnp.einsum(
        "ij,ixc->jxc",
        rotation,
        lax.all_to_all(orbitals, "orb", split_axis=2, concat_axis=0, tiled=True),
        precision=precise,
    )
    planes, width_yz = rotated.shape[1:]
    targets, sources, live_flags = pair_lists(tile_list, pair_mask)
    matrix_x, matrix_y, matrix_z = sine_table(size_x), sine_table(NY), sine_table(NZ)
    kernel = green_kernel(size_x, NY, NZ).reshape(size_x, NY * NZ)
    orbital_ids = jnp.arange(number_orbitals, dtype=jnp.int32)
    targets, sources = compact(targets, sources, live_flags, targets.shape[0] // 2)
    density = rotated[targets] * rotated[sources]
    number = density.shape[0]
    spectrum = along_z(density, matrix_z)
    spectrum = lax.all_to_all(spectrum, "orb", split_axis=0, concat_axis=2, tiled=True)
    spectrum = along_y(spectrum, matrix_y)
    spectrum = lax.all_to_all(spectrum, "grid", split_axis=0, concat_axis=1, tiled=True)
    spectrum = along_x(along_x(spectrum, matrix_x) * kernel, matrix_x)
    spectrum = lax.all_to_all(spectrum, "grid", split_axis=1, concat_axis=0, tiled=True)
    spectrum = along_y(spectrum, matrix_y)
    spectrum = lax.all_to_all(spectrum, "orb", split_axis=2, concat_axis=0, tiled=True)
    potential = along_z(spectrum, matrix_z)
    products = potential * rotated[sources]
    selector = (targets[None, :] == orbital_ids[:, None]).astype(f32)
    partial_value = -jnp.dot(selector, products.reshape(number, planes * width_yz), precision=precise)
    partial_value = partial_value.reshape(number_orbitals, planes, width_yz)
    return lax.all_to_all(partial_value, "orb", split_axis=0, concat_axis=2, tiled=True)


def solution(mesh):
    n_orb, n_grid = mesh.shape["orb"], mesh.shape["grid"]

    def on_device(orbitals, rotation, tile_list, pair_mask):
        per_device, planes, width = orbitals.shape
        fits = n_orb == 8 and 2 * tile_list.shape[0] == n_orb and planes == SUB and per_device % BLK == 0
        fits = fits and width == NY * NZ and 2 * NZ == LANES and n_grid in (2, 4, 8)
        fits = fits and per_device * SUB == LANES and rotation.shape == (LANES, LANES)
        if not fits:
            return any_device(orbitals, rotation, tile_list, pair_mask)
        return tile_device(orbitals, rotation, tile_list, pair_mask)

    in_specs = (P("orb", "grid", None), P(), P(), P())
    out_specs = P("orb", "grid", None)
    return jax.shard_map(on_device, mesh=mesh, in_specs=in_specs, out_specs=out_specs, check_vma=False)
```

```python
import functools
import itertools

import jax
import jax.numpy as jnp
import numpy as np
from jax import lax
from jax.experimental import pallas as pl
from jax.experimental.pallas import tpu as pltpu
from jax.sharding import PartitionSpec as P


BLK = 4
NY = 64
NZ = 64
LANES = 128
SUB = 8
CHUNKS = 2
COUPLING = 0.25
SCREENING = 0.1

precise = lax.Precision.HIGHEST
f32 = jnp.float32
bf16 = jnp.bfloat16

VM = pl.BlockSpec(memory_space=pltpu.VMEM)
SM = pl.BlockSpec(memory_space=pltpu.SMEM)
ANY = pl.BlockSpec(memory_space=pl.ANY)
HBM = pl.BlockSpec(memory_space=pltpu.HBM)
DMA = pltpu.SemaphoreType.DMA


def grant(mib):
    return pltpu.CompilerParams(vmem_limit_bytes=mib << 20)


def sine_np(n):
    k = np.arange(1, n + 1, dtype=np.float64)
    return np.sqrt(2.0 / (n + 1)) * np.sin(np.pi * k[:, None] * k[None, :] / (n + 1))


def eigen_np(n):
    k = np.arange(1, n + 1, dtype=np.float64)
    return 2.0 - 2.0 * np.cos(np.pi * k / (n + 1))


def halves_np(table):
    high = np.asarray(table, np.float32).astype(jnp.bfloat16)
    low = (np.asarray(table, np.float64) - high.astype(np.float64)).astype(jnp.bfloat16)
    return jnp.asarray(high), jnp.asarray(low)


def y_order():
    rows = LANES // NZ
    return np.arange(NY).reshape(NY // rows, rows).T.reshape(-1)


def y_tables():
    sine, planes = sine_np(NY), sine_np(SUB)
    even, odd = np.kron(sine[0::2, 0::2], planes), np.kron(sine[1::2, 0::2], planes)
    return np.stack([even, odd]), np.stack([even, odd.T])


def turned(x):
    count = x.shape[0] // SUB
    return jnp.concatenate([x[(count - 1 - t) * SUB:(count - t) * SUB] for t in range(count)])


def z_table():
    half = LANES // NZ
    sine = sine_np(NZ)
    table = np.zeros((2, half, NZ, half, 2, NZ))
    for pair in range(2):
        for h in range(half):
            table[pair, h, :, h, pair, :] = sine
    return table.reshape(2 * half * NZ, half * 2 * NZ)


def line_np():
    c = eigen_np(NY)[y_order()][:, None] + eigen_np(NZ)[None, :] + SCREENING
    c = np.concatenate([c, c], axis=1)
    return c, 2.0 / (2.0 + c + np.sqrt(c * (c + 4.0)))


def host_np(chips):
    table = np.zeros((chips**chips, chips), np.int32)
    for owners in itertools.product(range(chips), repeat=chips):
        best = None
        for tiles in itertools.permutations(range(chips)):
            hops = [bin(chip ^ owners[tile]).count("1") for chip, tile in enumerate(tiles)]
            cost = (max(hops), sum(hops))
            if best is None or cost < best[0]:
                best = (cost, tiles)
        table[sum(own * chips**t for t, own in enumerate(owners))] = best[1]
    return table


def dot(a, b):
    return jnp.dot(a, b, preferred_element_type=f32)


def split(x):
    high = x.astype(bf16)
    return high, (x - high.astype(f32)).astype(bf16)


def dot3(a, b):
    return dot(a[0], b[0]) + dot(a[0], b[1]) + dot(a[1], b[0])


def my_core():
    return lax.rem(lax.axis_index("orb"), 2)


def my_place():
    o = lax.axis_index("orb")
    return o, lax.rem(o, 2), lax.div(o, 2)


def fetch_kernel(source, out, sem):
    step = out.shape[0] // sem.shape[0]
    copies = [
        pltpu.make_async_copy(source.at[pl.ds(n * step, step)], out.at[pl.ds(n * step, step)], sem.at[n])
        for n in range(sem.shape[0])
    ]
    for copy in copies:
        copy.start()
    for copy in copies:
        copy.wait()


def take_kernel(start, source, *rest):
    out = rest[-1]
    at = (1 - my_core()) * (source.shape[2] // 2) + start
    out[...] = source[:, :, pl.ds(pl.multiple_of(at, LANES), out.shape[2])]


class Place:
    def __init__(self, per_device, tiles, host):
        self.o, self.core, self.chip = my_place()
        self.tiles, self.host = tiles, host
        self.chips = tiles.shape[0]
        owners = [lax.div(tiles[t, 0] * BLK, 2 * per_device) for t in range(self.chips)]
        key, same = 0, True
        for t in range(self.chips):
            key = key + owners[t] * self.chips**t
            same = same & (owners[t] == owners[0])
        self.key, self.same = key, same
        self.bit_1 = jnp.where(self.core == 0, 1, 2)
        self.bit_2 = 3 - self.bit_1

    def tile(self, chip):
        return self.host[self.key * self.chips + chip]

    def heads(self, chip):
        tile = self.tile(chip)
        return BLK * self.tiles[tile, 0], BLK * self.tiles[tile, 1]


def setup_kernel(per_device, tiles, host, rotation, after, high, low):
    core = my_core()
    at = Place(per_device, tiles, host)
    pair = BLK // 2
    heads = [at.heads(chip) for chip in (at.chip ^ 3, at.chip ^ at.bit_1, at.chip ^ at.bit_2, at.chip)]
    wanted = []
    for a, b in heads:
        wanted += [a + (1 - core) * pair] + [b + w for w in range(BLK)] + [a + core * pair]
    for u in range(1, pair):
        for a, b in heads:
            wanted += [a + (1 - core) * pair + u, a + core * pair + u]
    lane = lax.broadcasted_iota(jnp.int32, (SUB, LANES), 1)
    chosen = jnp.concatenate([jnp.where(lane == n, 1.0, 0.0) for n in wanted]).astype(bf16)
    rows = chosen.shape[0]
    row = lax.broadcasted_iota(jnp.int32, (LANES, LANES), 0)
    column = lax.broadcasted_iota(jnp.int32, (LANES, LANES), 1)
    columns = [
        jnp.where(row - (at.o ^ e) * per_device == jnp.right_shift(column, 3), 1.0, 0.0).astype(bf16)
        for e in range(2)
    ]
    keep = (lax.broadcasted_iota(jnp.int32, (rows, LANES), 0) & (SUB - 1)) == (
        lax.broadcasted_iota(jnp.int32, (rows, LANES), 1) & (SUB - 1)
    )
    for out, values in zip((high, low), split(rotation[...])):
        picked = lax.dot_general(chosen, values, (((1,), (1,)), ((), ())), preferred_element_type=f32).astype(bf16)
        for e in range(2):
            out[:, e * LANES:(e + 1) * LANES] = jnp.where(keep, dot(picked, columns[e]), 0.0).astype(bf16)


def ready_kernel(per_device, n_grid, tiles, host, mask, log_r, *rest):
    out, powers, flags, match, alone, zeros, sem = rest[-7:]
    zeros[...] = jnp.zeros(zeros.shape, f32)
    step = zeros.shape[0]
    copies = [
        pltpu.make_async_copy(zeros, out.at[pl.ds(n * step, step)], sem.at[n]) for n in range(out.shape[0] // step)
    ]
    for copy in copies:
        copy.start()
    begin, size_x = SUB * lax.axis_index("grid"), SUB * n_grid
    exponents = (
        2 * begin + SUB + 1,
        2 * size_x + 1 - SUB - 2 * begin,
        2 * size_x + 2 - 2 * begin,
        2 * begin,
        2 * begin + 2 * SUB + 2,
        2 * size_x - 2 * SUB - 2 * begin,
    )
    for n, exponent in enumerate(exponents):
        power = jnp.exp(exponent.astype(f32) * log_r[...])
        powers[n] = power if n < 2 else 1.0 - power
    at = Place(per_device, tiles, host)
    alone[0] = at.same.astype(jnp.int32)
    a, b = at.heads(at.chip)
    pair = BLK // 2
    live = mask[...].astype(f32)
    row = lax.broadcasted_iota(jnp.int32, live.shape, 0)
    column = lax.broadcasted_iota(jnp.int32, (1, live.shape[1]), 1)
    for u in range(pair):
        line = jnp.sum(jnp.where(row == a + at.core * pair + u, live, 0.0), axis=0, keepdims=True)
        for w in range(BLK):
            flags[u * BLK + w] = jnp.sum(jnp.where(column == b + w, line, 0.0))
    blocks = per_device // BLK
    parts = [0, at.bit_1, at.bit_2, 3, 0, at.bit_2, at.bit_1, 3]
    for n, flip in enumerate(parts):
        home = tiles[at.tile(at.chip ^ flip), 0]
        for block in range(blocks):
            hit = home == at.o * blocks + block
            if n % 4 == 3:
                hit = hit & at.same
            found = hit.astype(jnp.int32)
            match[block * len(parts) + n] = found
            total = blocks * len(parts) + 2 * block + n // 4
            match[total] = found if n % 4 == 0 else match[total] + found
    for copy in copies:
        copy.wait()


def join_kernel(x, y, out):
    out[0] = x[...]
    out[1] = y[...]


def rotate_kernel(first, start, high, low, mine, *rest):
    send, keep = rest[-2:]
    begin = my_core() * (mine.shape[2] // 2) + start
    rows = send.shape[0] * SUB
    part = pl.ds(first, 2 * rows)
    table = (high[part, :], low[part, :])
    at = 0
    step = 2 * LANES
    while at < send.shape[2]:
        width = rest[0].shape[2]
        n, inner = at // width, at % width
        theirs = rest[n]
        depth = theirs.shape[0] * SUB
        own = pl.ds(pl.multiple_of(begin + at, LANES), step)
        cells = jnp.concatenate([
            mine[:, :, own].reshape(depth, step), theirs[:, :, inner:inner + step].reshape(depth, step)
        ])
        total = dot3(table, split(cells))
        lanes = slice(at, at + step)
        send[:, :, lanes] = total[:rows].reshape(send.shape[0], SUB, step)
        keep[:, :, lanes] = total[rows:].reshape(keep.shape[0], SUB, step)
        at += step


def pass_kernel(keep, got, *rest):
    out = rest[-1]
    count = out.shape[0]
    out[...] = keep[:count] + got[:count]


def finish_kernel(keep, got, passed, *rest):
    out = rest[-1]
    count = out.shape[0]
    out[...] = keep[count:] + got[count:] + passed[...]


def sub_sums(values):
    row = lax.broadcasted_iota(jnp.int32, values[0].shape, 0)
    for s in (4, 2):
        low = (row & s) == 0
        paired = []
        for n in range(s):
            a, b = values[n], values[n + s]
            paired.append(jnp.where(low, a, pltpu.roll(b, s, 0)) + jnp.where(low, pltpu.roll(a, SUB - s, 0), b))
        values = paired
    even = (row & 1) == 0
    a, b = values
    return jnp.where(even, a, pltpu.roll(b, 1, 0)), jnp.where(even, pltpu.roll(a, SUB - 1, 0), b)


def fields(u, own, other, first_own, first_other):
    table = []
    for side, sources, targets in ((0, first_own, own), (1, first_other, other)):
        for n, ref in enumerate(sources):
            if u == 0:
                table.append((side, n, ref, targets[n], BLK + 1 if side == 0 else 0, 0))
            else:
                table.append((side, n, ref, targets[0], 1 if side == 0 else 0, n * ref.shape[2]))
    return table


def forward_kernel(u, counts, *refs):
    groups = []
    for count in counts[:-1]:
        groups.append(refs[:count])
        refs = refs[count:]
    first_own, first_other, own, other = groups[:4]
    y_hi, y_lo, z_hi, z_lo, ends, powers = refs[:6]
    messages, (spectrum, a_out, b_out, dens) = refs[-4 - counts[-1]:-4], refs[-4:]
    if u == 0:
        own, other = first_own, first_other
    core, g = my_core(), lax.axis_index("grid")
    tiles = first_own[0].shape[2] // LANES
    for side, n, source, target, slot, offset in fields(u, own, other, first_own, first_other):
        half = (core if side == 0 else 1 - core) * (len(first_own) * tiles * SUB)
        for t in range(tiles):
            lanes = pl.ds(t * LANES, LANES)
            value = target[slot, :, pl.ds(offset + t * LANES, LANES)]
            rows = pl.ds(pl.multiple_of(half + (n * tiles + t) * SUB, SUB), SUB)
            for w in range(BLK):
                dens[rows, w * LANES:(w + 1) * LANES] = value * source[1 + w, :, lanes]
    z = (z_hi[...], z_lo[...])
    half = dens.shape[0]
    for q in range(BLK // 2):
        out = dot3(split(dens[:, q * 2 * LANES:(q + 1) * 2 * LANES]), z)
        mirror = turned(out[:, LANES:])
        spectrum[:half, q * LANES:(q + 1) * LANES] = out[:, :LANES] + mirror
        spectrum[half:, q * LANES:(q + 1) * LANES] = out[:, :LANES] - mirror
    for parity in range(2):
        part = pl.ds(parity * half, half)
        spectrum[part, :] = dot3((y_hi[parity], y_lo[parity]), split(spectrum[part, :]))

    def reduce(group, carry):
        lines = pl.ds(pl.multiple_of(group * SUB, SUB), SUB)
        near, far = powers[0, lines, :], powers[1, lines, :]
        for q in range(BLK // 2):
            lanes = slice(q * LANES, (q + 1) * LANES)
            values = []
            for k in range(SUB):
                rows = pl.ds(pl.multiple_of((group * SUB + k) * SUB, SUB), SUB)
                values.append(ends[rows, :] * spectrum[rows, lanes])
            even, odd = sub_sums(values)
            rightward = (even + odd) - near * (even - odd)
            leftward = (even - odd) - far * (even + odd)
            a_out[lines, lanes] = rightward
            b_out[lines, lanes] = leftward
            for k, out in enumerate(messages, 1):
                out[lines, lanes] = jnp.where((g ^ k) > g, rightward, leftward)
        return carry

    lax.fori_loop(0, NY // SUB, reduce, 0)


def backward_kernel(u, counts, flags, *refs):
    groups = []
    for count in counts:
        groups.append(refs[:count])
        refs = refs[count:]
    own, other, received = groups
    (y_hi, y_lo, z_hi, z_lo, inverse, basis, powers, steady, spectrum, a_in, b_in) = refs[:11]
    out, work, pot = refs[-3:]
    core, g = my_core(), lax.axis_index("grid")
    tiles = own[0].shape[2] // LANES
    first, last = basis[0], basis[1]

    def ends(group, carry):
        lines = pl.ds(pl.multiple_of(group * SUB, SUB), SUB)
        scale, r, slab = steady[0, lines, :], steady[1, lines, :], steady[2, lines, :]
        decays = [None, jnp.ones((SUB, LANES), f32), slab]
        while len(decays) <= len(received):
            decays.append(decays[-1] * slab)
        for q in range(BLK // 2):
            lanes = slice(q * LANES, (q + 1) * LANES)
            from_left = from_right = jnp.zeros((SUB, LANES), f32)
            for n, ref in enumerate(received, 1):
                distance = jnp.abs((g ^ n) - g)
                factor = decays[n]
                for d in range(1, n):
                    factor = jnp.where(distance == d, decays[d], factor)
                value = factor * ref[lines, lanes]
                is_left = (g ^ n) < g
                from_left = from_left + jnp.where(is_left, value, 0.0)
                from_right = from_right + jnp.where(is_left, 0.0, value)
            before = scale * (powers[2, lines, :] * from_left
                              + r * powers[3, lines, :] * (b_in[lines, lanes] + slab * from_right))
            after = scale * (powers[4, lines, :] * from_right
                             + r * powers[5, lines, :] * (a_in[lines, lanes] + slab * from_left))
            for k in range(SUB):
                rows = pl.ds(pl.multiple_of((group * SUB + k) * SUB, SUB), SUB)
                edge = first * before[k:k + 1] + last * after[k:k + 1]
                work[rows, lanes] = inverse[rows, :] * (spectrum[rows, lanes] + edge)
        return carry

    lax.fori_loop(0, NY // SUB, ends, 0)
    z = (z_hi[...], z_lo[...])
    half = pot.shape[0]
    for parity in range(2):
        part = pl.ds(parity * half, half)
        work[part, :] = dot3((y_hi[parity], y_lo[parity]), split(work[part, :]))
    for q in range(BLK // 2):
        lanes = slice(q * LANES, (q + 1) * LANES)
        even, odd = work[:half, lanes], work[half:, lanes]
        rows = jnp.concatenate([even + odd, turned(even - odd)], axis=1)
        pot[:, q * 2 * LANES:(q + 1) * 2 * LANES] = dot3(split(rows), z)
    for side, group in ((0, own), (1, other)):
        half = (core if side == 0 else 1 - core) * (len(own) * tiles)
        for n, ref in enumerate(group):
            for t in range(tiles):
                lanes = pl.ds(t * LANES, LANES)
                at = half + n * tiles + t
                rows = pl.ds(pl.multiple_of(at * SUB, SUB), SUB)
                total = None
                for w in range(BLK):
                    term = flags[u * BLK + w] * (pot[rows, w * LANES:(w + 1) * LANES] * ref[1 + w, :, lanes])
                    total = term if total is None else total + term
                out[:, pl.ds(pl.multiple_of(at * LANES, LANES), LANES)] = -total


def place_kernel(stride, match, *refs):
    parts, (out, rows, sem) = refs[:-4], refs[-3:]
    pair = BLK // 2
    blocks = out.shape[0] // BLK
    core = my_core()
    values = []
    for part in parts:
        values += [part] if len(part.shape) == 2 else [part.at[n] for n in range(part.shape[0])]
    parts, count = values, len(values) // pair

    def hits(b, side):
        return [(match[b * stride + side * stride // 2 + n], side * count // 2 + n) for n in range(count // 2)]

    def found(b, side):
        return match[blocks * stride + 2 * b + side] > 0

    def move(b, side):
        which = core if side == 0 else 1 - core
        at = b * BLK + which * pair
        return pltpu.make_async_copy(rows.at[b, side], out.at[pl.ds(at, pair)], sem.at[b, side])

    for b in range(blocks):
        for side in range(2):

            @pl.when(found(b, side))
            def _():
                rows[b, side] = jnp.zeros(rows.shape[2:], f32)
                for hit, n in hits(b, side):

                    @pl.when(hit > 0)
                    def _():
                        for u in range(pair):
                            rows[b, side, u] += parts[u * count + n][...]

                move(b, side).start()

    for b in range(blocks):
        for side in range(2):

            @pl.when(found(b, side))
            def _():
                move(b, side).wait()


def tile_device(orbitals, rotation, tile_list, pair_mask):
    shape = per_device, planes, width = orbitals.shape
    n_orb, n_grid = lax.axis_size("orb"), lax.axis_size("grid")
    size_x = planes * n_grid
    half = width // 2
    chips = n_orb // 2
    axes = ("orb", "grid")

    def swap(x, even, odd):
        moves = []
        for a in range(n_orb):
            flip = even if a % 2 == 0 else odd
            moves += [(a * n_grid + b, (a ^ flip) * n_grid + b) for b in range(n_grid)]
        return lax.ppermute(x, axes, moves)

    def cross(x, k):
        moves = [(a * n_grid + b, a * n_grid + (b ^ k)) for a in range(n_orb) for b in range(n_grid)]
        return lax.ppermute(x, axes, moves)

    chunk = half // CHUNKS
    orbitals = pltpu.with_memory_space_constraint(orbitals, pltpu.HBM)

    part = jax.ShapeDtypeStruct((per_device, planes, chunk), f32)
    loaded = pl.pallas_call(
        fetch_kernel, out_shape=jax.ShapeDtypeStruct(shape, f32), in_specs=[HBM], out_specs=VM,
        scratch_shapes=[DMA((4,))], name="fetch", compiler_params=grant(8),
    )(orbitals)
    theirs, last = [], ()
    for n in range(CHUNKS):
        taken = pl.pallas_call(
            functools.partial(take_kernel, n * chunk), out_shape=part, in_specs=[VM] + [ANY] * len(last), out_specs=VM,
            compiler_params=grant(8),
        )(loaded, *last)
        theirs.append(swap(taken, 1, 1))
        last = (taken,)

    pair = BLK // 2
    firsts = (BLK + 2) * chips
    rows = (firsts + 2 * (pair - 1) * chips) * SUB
    wide_table = jax.ShapeDtypeStruct((rows, 2 * LANES), bf16)
    blocks = per_device // BLK
    c, r = line_np()
    c, r = line_np()
    host = jnp.asarray(host_np(chips).reshape(-1))
    high, low = pl.pallas_call(
        functools.partial(setup_kernel, per_device), out_shape=[wide_table] * 2,
        in_specs=[SM, SM, VM, ANY], out_specs=[VM] * 2, name="setup", compiler_params=grant(8),
    )(tile_list, host, rotation, taken)

    def rotate(first, count, start, fields, *after):
        part = jax.ShapeDtypeStruct((count, planes, chunk * len(fields)), f32)
        send, keep = pl.pallas_call(
            functools.partial(rotate_kernel, first * SUB, start), out_shape=(part, part),
            in_specs=[VM] * (3 + len(fields)) + [ANY] * len(after),
            out_specs=(VM, VM), compiler_params=grant(8),
        )(high, low, loaded, *fields, *after)
        return send, keep, swap(send, 2, 4)

    sums, last = [], ()
    for n in range(CHUNKS):
        sums.append(rotate(0, firsts // 2, n * chunk, [theirs[n]], *last))
        last = (sums[-1][0],)
    sums.append(rotate(firsts, (pair - 1) * chips, 0, theirs, *last))
    passing, own, other = [], [], []

    def pass_on(n, *after, spec=ANY):
        _, keep, got = sums[n]
        count = keep.shape[0] // 2
        value = pl.pallas_call(
            pass_kernel, out_shape=jax.ShapeDtypeStruct((count,) + keep.shape[1:], f32),
            in_specs=[VM] * 2 + [spec] * len(after), out_specs=VM, compiler_params=grant(4),
        )(keep, got, *after)
        passing.append((keep, got, swap(value, 4, 2)))
        return value

    def finish(n, *after):
        keep, got, passed = passing[n]
        own.append(pl.pallas_call(
            finish_kernel, out_shape=jax.ShapeDtypeStruct(passed.shape, f32), in_specs=[VM] * 3 + [ANY] * len(after),
            out_specs=VM, compiler_params=grant(4),
        )(keep, got, passed, *after))
        other.append(swap(own[-1], 1, 1))
        return own[-1]

    step = pass_on(0, sums[-1][0])
    empty, powers, flags, match, alone = pl.pallas_call(
        functools.partial(ready_kernel, per_device, n_grid),
        out_shape=(pltpu.HBM(shape, f32), jax.ShapeDtypeStruct((6, NY, LANES), f32),
                   jax.ShapeDtypeStruct((pair * BLK,), f32), jax.ShapeDtypeStruct((blocks * 10,), jnp.int32),
                   jax.ShapeDtypeStruct((1,), jnp.int32)),
        in_specs=[SM, SM, VM, VM, ANY], out_specs=(HBM, VM, SM, SM, SM),
        scratch_shapes=[pltpu.VMEM((pair, planes, width), f32), DMA((per_device // pair,))], name="ready",
        compiler_params=grant(4),
    )(tile_list, host, pair_mask, jnp.asarray(np.log(r), f32), step)
    step = pass_on(1, empty, spec=HBM)
    for n in range(2, CHUNKS):
        step = pass_on(n, step)
    for n in range(CHUNKS):
        step = finish(n, step)
    last = (pass_on(CHUNKS, step),)

    sine_x, eigen_x = sine_np(planes), eigen_np(planes)
    ends = jnp.asarray(np.einsum("jp,pkl->kjl", sine_x, r[None] ** np.arange(planes - 1, -1, -1)[:, None, None])
                       .reshape(-1, LANES), f32)
    inverse = jnp.asarray((COUPLING / (eigen_x[None, :, None] + c[:, None, :])).reshape(-1, LANES), f32)
    basis = jnp.asarray(np.broadcast_to(sine_x[:, [0, -1]].T[:, :, None], (2, planes, LANES)), f32)
    steady = jnp.asarray(np.stack([r / ((1 - r**2) * (1 - r ** (2 * size_x + 2))), r, r**planes]), f32)

    y_there, y_back = y_tables()
    y_hi, y_lo = halves_np(y_there)
    yt_hi, yt_lo = halves_np(y_back)
    z_hi, z_lo = halves_np(z_table())
    zt_hi, zt_lo = halves_np(z_table().T)
    solved = []
    lines = jax.ShapeDtypeStruct((NY, 2 * LANES), f32)
    cube = (NY * SUB, 2 * LANES)
    wide = pltpu.VMEM((width // LANES * SUB, BLK * LANES), f32)
    base_own, base_other = own[:CHUNKS], other[:CHUNKS]
    for u in range(pair):
        if u:
            finish(CHUNKS, *last)
        more_own, more_other = own[CHUNKS:][:u], other[CHUNKS:][:u]
        counts = (CHUNKS, CHUNKS, len(more_own), len(more_other))
        inputs = [*base_own, *base_other, *more_own, *more_other, y_hi, y_lo, z_hi, z_lo, ends, powers]
        *messages, spectrum, a, b = pl.pallas_call(
            functools.partial(forward_kernel, u, counts + (n_grid - 1,)),
            out_shape=[lines] * (n_grid - 1) + [jax.ShapeDtypeStruct(cube, f32), lines, lines],
            in_specs=[VM] * len(inputs) + [ANY] * len(last),
            out_specs=[VM] * (n_grid + 2),
            scratch_shapes=[wide],
            compiler_params=grant(16),
        )(*inputs, *last)
        last = (spectrum,)
        received = []
        for k, message in enumerate(messages, 1):
            received.append(cross(message, k))
        solved.append((spectrum, a, b, received))

    terms, last = [], ()
    for u, (spectrum, a, b, received) in enumerate(solved):
        inputs = [*base_own, *base_other, *received, yt_hi, yt_lo, zt_hi, zt_lo, inverse, basis, powers, steady,
                  spectrum, a, b]
        terms.append(pl.pallas_call(
            functools.partial(backward_kernel, u, (CHUNKS, CHUNKS, len(received))),
            out_shape=jax.ShapeDtypeStruct((planes, width), f32),
            in_specs=[SM] + [VM] * len(inputs) + [ANY] * len(last),
            out_specs=VM,
            scratch_shapes=[pltpu.VMEM(cube, f32), wide],
            compiler_params=grant(16),
        )(flags, *inputs, *last))
        last = (terms[-1],)

    near_1 = [swap(term, 2, 4) for term in terms]
    near_2 = [swap(term, 4, 2) for term in terms]
    own_parts = [[term, x, y] for term, x, y in zip(terms, near_1, near_2)]
    sib_parts = []
    for term, x, y in own_parts:
        joined = pl.pallas_call(
            join_kernel, out_shape=jax.ShapeDtypeStruct((2,) + term.shape, f32), in_specs=[VM] * 2, out_specs=VM,
            compiler_params=grant(4),
        )(x, y)
        given = swap(term, 1, 1)
        sib_parts.append([given, swap(joined, 1, 1)])

    def place(target, groups):
        parts = [part for group in groups for part in group]
        return pl.pallas_call(
            functools.partial(place_kernel, 8),
            out_shape=pltpu.HBM(shape, f32),
            in_specs=[SM] + [VM] * len(parts) + [HBM],
            out_specs=HBM,
            input_output_aliases={len(parts) + 1: 0},
            scratch_shapes=[pltpu.VMEM((blocks, 2, pair, planes, width), f32), DMA((blocks, 2))],
            name="place",
            compiler_params=grant(8),
        )(match, *parts, target)

    def place_near(target, mine, sibs):
        return place(target, [a + b for a, b in zip(mine, sibs)])

    def place_far(target, mine, sibs):
        far = [swap(group[1], 4, 2) for group in mine]
        return place(target, [a + [x] + b + [swap(x, 1, 1)] for a, b, x in zip(mine, sibs, far)])

    return lax.cond(alone[0] != 0, place_far, place_near, empty, own_parts, sib_parts)


def sine_table(length):
    wave_index = jnp.arange(length, dtype=f32) + 1.0
    return jnp.sqrt(2.0 / (length + 1.0)) * jnp.sin(
        jnp.pi * wave_index[:, None] * wave_index[None, :] / (length + 1.0)
    )


def eigen_values(length):
    wave_index = jnp.arange(length, dtype=f32) + 1.0
    return 2.0 - 2.0 * jnp.cos(jnp.pi * wave_index / (length + 1.0))


def green_kernel(size_x, size_y, size_z):
    summed = (
        eigen_values(size_x)[:, None, None]
        + eigen_values(size_y)[None, :, None]
        + eigen_values(size_z)[None, None, :]
    )
    return COUPLING / (summed + SCREENING)


def pair_lists(tile_list, pair_mask):
    within = jnp.arange(BLK * BLK, dtype=jnp.int32)
    targets = (BLK * tile_list[:, 0:1] + within[None, :] // BLK).reshape(-1)
    sources = (BLK * tile_list[:, 1:2] + within[None, :] % BLK).reshape(-1)
    return (targets, sources, pair_mask[targets, sources])


def compact(targets, sources, live_flags, number):
    ranking = jnp.cumsum(live_flags) - 1
    places = jnp.where(live_flags == 1, ranking, number)
    picked = (
        jnp.zeros((number,), jnp.int32)
        .at[places]
        .set(jnp.arange(live_flags.shape[0], dtype=jnp.int32), mode="drop")
    )
    return (targets[picked], sources[picked])


def along_z(values, matrix):
    number, planes, width_yz = values.shape
    size_z = matrix.shape[0]
    shaped = values.reshape(number, planes, width_yz // size_z, size_z)
    return jnp.einsum("pxrz,zk->pxrk", shaped, matrix, precision=precise).reshape(number, planes, width_yz)


def along_y(values, matrix):
    number, planes, width_yz = values.shape
    size_y = matrix.shape[0]
    shaped = values.reshape(number, planes, size_y, width_yz // size_y)
    return jnp.einsum("pxyz,yk->pxkz", shaped, matrix, precision=precise).reshape(number, planes, width_yz)


def along_x(values, matrix):
    return jnp.einsum("pxc,xk->pkc", values, matrix, precision=precise)


def any_device(orbitals, rotation, tile_list, pair_mask):
    n_grid = lax.axis_size("grid")
    number_orbitals, size_x = rotation.shape[0], orbitals.shape[1] * n_grid
    rotated = jnp.einsum(
        "ij,ixc->jxc",
        rotation,
        lax.all_to_all(orbitals, "orb", split_axis=2, concat_axis=0, tiled=True),
        precision=precise,
    )
    planes, width_yz = rotated.shape[1:]
    targets, sources, live_flags = pair_lists(tile_list, pair_mask)
    matrix_x, matrix_y, matrix_z = sine_table(size_x), sine_table(NY), sine_table(NZ)
    kernel = green_kernel(size_x, NY, NZ).reshape(size_x, NY * NZ)
    orbital_ids = jnp.arange(number_orbitals, dtype=jnp.int32)
    targets, sources = compact(targets, sources, live_flags, targets.shape[0] // 2)
    density = rotated[targets] * rotated[sources]
    number = density.shape[0]
    spectrum = along_z(density, matrix_z)
    spectrum = lax.all_to_all(spectrum, "orb", split_axis=0, concat_axis=2, tiled=True)
    spectrum = along_y(spectrum, matrix_y)
    spectrum = lax.all_to_all(spectrum, "grid", split_axis=0, concat_axis=1, tiled=True)
    spectrum = along_x(along_x(spectrum, matrix_x) * kernel, matrix_x)
    spectrum = lax.all_to_all(spectrum, "grid", split_axis=1, concat_axis=0, tiled=True)
    spectrum = along_y(spectrum, matrix_y)
    spectrum = lax.all_to_all(spectrum, "orb", split_axis=2, concat_axis=0, tiled=True)
    potential = along_z(spectrum, matrix_z)
    products = potential * rotated[sources]
    selector = (targets[None, :] == orbital_ids[:, None]).astype(f32)
    partial_value = -jnp.dot(selector, products.reshape(number, planes * width_yz), precision=precise)
    partial_value = partial_value.reshape(number_orbitals, planes, width_yz)
    return lax.all_to_all(partial_value, "orb", split_axis=0, concat_axis=2, tiled=True)


def solution(mesh):
    n_orb, n_grid = mesh.shape["orb"], mesh.shape["grid"]

    def on_device(orbitals, rotation, tile_list, pair_mask):
        per_device, planes, width = orbitals.shape
        fits = n_orb == 8 and 2 * tile_list.shape[0] == n_orb and planes == SUB and per_device % BLK == 0
        fits = fits and width == NY * NZ and 2 * NZ == LANES and n_grid in (2, 4, 8)
        fits = fits and per_device * SUB == LANES and rotation.shape == (LANES, LANES)
        if not fits:
            return any_device(orbitals, rotation, tile_list, pair_mask)
        return tile_device(orbitals, rotation, tile_list, pair_mask)

    in_specs = (P("orb", "grid", None), P(), P(), P())
    out_specs = P("orb", "grid", None)
    return jax.shard_map(on_device, mesh=mesh, in_specs=in_specs, out_specs=out_specs, check_vma=False)
```

```python
import functools
import itertools

import jax
import jax.numpy as jnp
import numpy as np
from jax import lax
from jax.experimental import pallas as pl
from jax.experimental.pallas import tpu as pltpu
from jax.sharding import PartitionSpec as P


BLK = 4
NY = 64
NZ = 64
LANES = 128
SUB = 8
CHUNKS = 2
COUPLING = 0.25
SCREENING = 0.1

precise = lax.Precision.HIGHEST
f32 = jnp.float32
bf16 = jnp.bfloat16

VM = pl.BlockSpec(memory_space=pltpu.VMEM)
SM = pl.BlockSpec(memory_space=pltpu.SMEM)
ANY = pl.BlockSpec(memory_space=pl.ANY)
HBM = pl.BlockSpec(memory_space=pltpu.HBM)
DMA = pltpu.SemaphoreType.DMA


def grant(mib):
    return pltpu.CompilerParams(vmem_limit_bytes=mib << 20)


def sine_np(n):
    k = np.arange(1, n + 1, dtype=np.float64)
    return np.sqrt(2.0 / (n + 1)) * np.sin(np.pi * k[:, None] * k[None, :] / (n + 1))


def eigen_np(n):
    k = np.arange(1, n + 1, dtype=np.float64)
    return 2.0 - 2.0 * np.cos(np.pi * k / (n + 1))


def halves_np(table):
    high = np.asarray(table, np.float32).astype(jnp.bfloat16)
    low = (np.asarray(table, np.float64) - high.astype(np.float64)).astype(jnp.bfloat16)
    return jnp.asarray(high), jnp.asarray(low)


def y_order():
    rows = LANES // NZ
    return np.arange(NY).reshape(NY // rows, rows).T.reshape(-1)


def y_tables():
    sine, planes = sine_np(NY), sine_np(SUB)
    even, odd = np.kron(sine[0::2, 0::2], planes), np.kron(sine[1::2, 0::2], planes)
    return np.stack([even, odd]), np.stack([even, odd.T])


def turned(x):
    count = x.shape[0] // SUB
    return jnp.concatenate([x[(count - 1 - t) * SUB:(count - t) * SUB] for t in range(count)])


def z_table():
    half = LANES // NZ
    sine = sine_np(NZ)
    table = np.zeros((2, half, NZ, half, 2, NZ))
    for pair in range(2):
        for h in range(half):
            table[pair, h, :, h, pair, :] = sine
    return table.reshape(2 * half * NZ, half * 2 * NZ)


def line_np():
    c = eigen_np(NY)[y_order()][:, None] + eigen_np(NZ)[None, :] + SCREENING
    c = np.concatenate([c, c], axis=1)
    return c, 2.0 / (2.0 + c + np.sqrt(c * (c + 4.0)))


def host_np(chips):
    table = np.zeros((chips**chips, chips), np.int32)
    for owners in itertools.product(range(chips), repeat=chips):
        best = None
        for tiles in itertools.permutations(range(chips)):
            hops = [bin(chip ^ owners[tile]).count("1") for chip, tile in enumerate(tiles)]
            cost = (max(hops), sum(hops))
            if best is None or cost < best[0]:
                best = (cost, tiles)
        table[sum(own * chips**t for t, own in enumerate(owners))] = best[1]
    return table


def dot(a, b):
    return jnp.dot(a, b, preferred_element_type=f32)


def split(x):
    high = x.astype(bf16)
    return high, (x - high.astype(f32)).astype(bf16)


def dot3(a, b):
    return dot(a[0], b[0]) + dot(a[0], b[1]) + dot(a[1], b[0])


def my_core():
    return lax.rem(lax.axis_index("orb"), 2)


def my_place():
    o = lax.axis_index("orb")
    return o, lax.rem(o, 2), lax.div(o, 2)


def fetch_kernel(source, out, sem):
    step = out.shape[0] // sem.shape[0]
    copies = [
        pltpu.make_async_copy(source.at[pl.ds(n * step, step)], out.at[pl.ds(n * step, step)], sem.at[n])
        for n in range(sem.shape[0])
    ]
    for copy in copies:
        copy.start()
    for copy in copies:
        copy.wait()


def take_kernel(flip, start, source, *rest):
    out, sem = rest[-2:]
    core = my_core()
    at = (1 - core if flip else core) * (source.shape[2] // 2) + start
    copy = pltpu.make_async_copy(source.at[:, :, pl.ds(pl.multiple_of(at, LANES), out.shape[2])], out, sem)
    copy.start()
    copy.wait()


class Place:
    def __init__(self, per_device, tiles, host):
        self.o, self.core, self.chip = my_place()
        self.tiles, self.host = tiles, host
        self.chips = tiles.shape[0]
        owners = [lax.div(tiles[t, 0] * BLK, 2 * per_device) for t in range(self.chips)]
        key, same = 0, True
        for t in range(self.chips):
            key = key + owners[t] * self.chips**t
            same = same & (owners[t] == owners[0])
        self.key, self.same = key, same
        self.bit_1 = jnp.where(self.core == 0, 1, 2)
        self.bit_2 = 3 - self.bit_1

    def tile(self, chip):
        return self.host[self.key * self.chips + chip]

    def heads(self, chip):
        tile = self.tile(chip)
        return BLK * self.tiles[tile, 0], BLK * self.tiles[tile, 1]


def setup_kernel(per_device, tiles, host, rotation, after, high, low):
    core = my_core()
    at = Place(per_device, tiles, host)
    pair = BLK // 2
    heads = [at.heads(chip) for chip in (at.chip ^ 3, at.chip ^ at.bit_1, at.chip ^ at.bit_2, at.chip)]
    wanted = []
    for a, b in heads:
        wanted += [a + (1 - core) * pair] + [b + w for w in range(BLK)] + [a + core * pair]
    for u in range(1, pair):
        for a, b in heads:
            wanted += [a + (1 - core) * pair + u, a + core * pair + u]
    lane = lax.broadcasted_iota(jnp.int32, (SUB, LANES), 1)
    chosen = jnp.concatenate([jnp.where(lane == n, 1.0, 0.0) for n in wanted]).astype(bf16)
    rows = chosen.shape[0]
    row = lax.broadcasted_iota(jnp.int32, (LANES, LANES), 0)
    column = lax.broadcasted_iota(jnp.int32, (LANES, LANES), 1)
    columns = [
        jnp.where(row - (at.o ^ e) * per_device == jnp.right_shift(column, 3), 1.0, 0.0).astype(bf16)
        for e in range(2)
    ]
    keep = (lax.broadcasted_iota(jnp.int32, (rows, LANES), 0) & (SUB - 1)) == (
        lax.broadcasted_iota(jnp.int32, (rows, LANES), 1) & (SUB - 1)
    )
    for out, values in zip((high, low), split(rotation[...])):
        picked = lax.dot_general(chosen, values, (((1,), (1,)), ((), ())), preferred_element_type=f32).astype(bf16)
        for e in range(2):
            out[:, e * LANES:(e + 1) * LANES] = jnp.where(keep, dot(picked, columns[e]), 0.0).astype(bf16)


def ready_kernel(per_device, n_grid, tiles, host, mask, log_r, *rest):
    out, powers, flags, match, alone, zeros, sem = rest[-7:]
    zeros[...] = jnp.zeros(zeros.shape, f32)
    step = zeros.shape[0]
    copies = [
        pltpu.make_async_copy(zeros, out.at[pl.ds(n * step, step)], sem.at[n]) for n in range(out.shape[0] // step)
    ]
    for copy in copies:
        copy.start()
    begin, size_x = SUB * lax.axis_index("grid"), SUB * n_grid
    exponents = (
        2 * begin + SUB + 1,
        2 * size_x + 1 - SUB - 2 * begin,
        2 * size_x + 2 - 2 * begin,
        2 * begin,
        2 * begin + 2 * SUB + 2,
        2 * size_x - 2 * SUB - 2 * begin,
    )
    for n, exponent in enumerate(exponents):
        power = jnp.exp(exponent.astype(f32) * log_r[...])
        powers[n] = power if n < 2 else 1.0 - power
    at = Place(per_device, tiles, host)
    alone[0] = at.same.astype(jnp.int32)
    a, b = at.heads(at.chip)
    pair = BLK // 2
    live = mask[...].astype(f32)
    row = lax.broadcasted_iota(jnp.int32, live.shape, 0)
    column = lax.broadcasted_iota(jnp.int32, (1, live.shape[1]), 1)
    for u in range(pair):
        line = jnp.sum(jnp.where(row == a + at.core * pair + u, live, 0.0), axis=0, keepdims=True)
        for w in range(BLK):
            flags[u * BLK + w] = jnp.sum(jnp.where(column == b + w, line, 0.0))
    blocks = per_device // BLK
    parts = [0, at.bit_1, at.bit_2, 3, 0, at.bit_2, at.bit_1, 3]
    for n, flip in enumerate(parts):
        home = tiles[at.tile(at.chip ^ flip), 0]
        for block in range(blocks):
            hit = home == at.o * blocks + block
            if n % 4 == 3:
                hit = hit & at.same
            found = hit.astype(jnp.int32)
            match[block * len(parts) + n] = found
            total = blocks * len(parts) + 2 * block + n // 4
            match[total] = found if n % 4 == 0 else match[total] + found
    for copy in copies:
        copy.wait()


def join_kernel(x, y, out):
    out[0] = x[...]
    out[1] = y[...]


def rotate_kernel(first, high, low, *rest):
    send, keep = rest[-2:]
    rows = send.shape[0] * SUB
    part = pl.ds(first, 2 * rows)
    table = (high[part, :], low[part, :])
    at = 0
    step = 2 * LANES
    while at < send.shape[2]:
        width = rest[0].shape[2]
        n, inner = at // width, at % width
        lanes = slice(inner, inner + step)
        mine, theirs = rest[2 * n], rest[2 * n + 1]
        depth = mine.shape[0] * SUB
        cells = jnp.concatenate([mine[:, :, lanes].reshape(depth, step), theirs[:, :, lanes].reshape(depth, step)])
        total = dot3(table, split(cells))
        lanes = slice(at, at + step)
        send[:, :, lanes] = total[:rows].reshape(send.shape[0], SUB, step)
        keep[:, :, lanes] = total[rows:].reshape(keep.shape[0], SUB, step)
        at += step


def pass_kernel(keep, got, *rest):
    out = rest[-1]
    count = out.shape[0]
    out[...] = keep[:count] + got[:count]


def finish_kernel(keep, got, passed, *rest):
    out = rest[-1]
    count = out.shape[0]
    out[...] = keep[count:] + got[count:] + passed[...]


def sub_sums(values):
    row = lax.broadcasted_iota(jnp.int32, values[0].shape, 0)
    for s in (4, 2):
        low = (row & s) == 0
        paired = []
        for n in range(s):
            a, b = values[n], values[n + s]
            paired.append(jnp.where(low, a, pltpu.roll(b, s, 0)) + jnp.where(low, pltpu.roll(a, SUB - s, 0), b))
        values = paired
    even = (row & 1) == 0
    a, b = values
    return jnp.where(even, a, pltpu.roll(b, 1, 0)), jnp.where(even, pltpu.roll(a, SUB - 1, 0), b)


def fields(u, own, other, first_own, first_other):
    table = []
    for side, sources, targets in ((0, first_own, own), (1, first_other, other)):
        for n, ref in enumerate(sources):
            if u == 0:
                table.append((side, n, ref, targets[n], BLK + 1 if side == 0 else 0, 0))
            else:
                table.append((side, n, ref, targets[0], 1 if side == 0 else 0, n * ref.shape[2]))
    return table


def forward_kernel(u, counts, *refs):
    groups = []
    for count in counts[:-1]:
        groups.append(refs[:count])
        refs = refs[count:]
    first_own, first_other, own, other = groups[:4]
    y_hi, y_lo, z_hi, z_lo, ends, powers = refs[:6]
    messages, (spectrum, a_out, b_out, dens) = refs[-4 - counts[-1]:-4], refs[-4:]
    if u == 0:
        own, other = first_own, first_other
    core, g = my_core(), lax.axis_index("grid")
    tiles = first_own[0].shape[2] // LANES
    for side, n, source, target, slot, offset in fields(u, own, other, first_own, first_other):
        half = (core if side == 0 else 1 - core) * (len(first_own) * tiles * SUB)
        for t in range(tiles):
            lanes = pl.ds(t * LANES, LANES)
            value = target[slot, :, pl.ds(offset + t * LANES, LANES)]
            rows = pl.ds(pl.multiple_of(half + (n * tiles + t) * SUB, SUB), SUB)
            for w in range(BLK):
                dens[rows, w * LANES:(w + 1) * LANES] = value * source[1 + w, :, lanes]
    z = (z_hi[...], z_lo[...])
    half = dens.shape[0]
    for q in range(BLK // 2):
        out = dot3(split(dens[:, q * 2 * LANES:(q + 1) * 2 * LANES]), z)
        mirror = turned(out[:, LANES:])
        spectrum[:half, q * LANES:(q + 1) * LANES] = out[:, :LANES] + mirror
        spectrum[half:, q * LANES:(q + 1) * LANES] = out[:, :LANES] - mirror
    for parity in range(2):
        part = pl.ds(parity * half, half)
        spectrum[part, :] = dot3((y_hi[parity], y_lo[parity]), split(spectrum[part, :]))

    def reduce(group, carry):
        lines = pl.ds(pl.multiple_of(group * SUB, SUB), SUB)
        near, far = powers[0, lines, :], powers[1, lines, :]
        for q in range(BLK // 2):
            lanes = slice(q * LANES, (q + 1) * LANES)
            values = []
            for k in range(SUB):
                rows = pl.ds(pl.multiple_of((group * SUB + k) * SUB, SUB), SUB)
                values.append(ends[rows, :] * spectrum[rows, lanes])
            even, odd = sub_sums(values)
            rightward = (even + odd) - near * (even - odd)
            leftward = (even - odd) - far * (even + odd)
            a_out[lines, lanes] = rightward
            b_out[lines, lanes] = leftward
            for k, out in enumerate(messages, 1):
                out[lines, lanes] = jnp.where((g ^ k) > g, rightward, leftward)
        return carry

    lax.fori_loop(0, NY // SUB, reduce, 0)


def backward_kernel(u, counts, flags, *refs):
    groups = []
    for count in counts:
        groups.append(refs[:count])
        refs = refs[count:]
    own, other, received = groups
    (y_hi, y_lo, z_hi, z_lo, inverse, basis, powers, steady, spectrum, a_in, b_in) = refs[:11]
    out, work, pot = refs[-3:]
    core, g = my_core(), lax.axis_index("grid")
    tiles = own[0].shape[2] // LANES
    first, last = basis[0], basis[1]

    def ends(group, carry):
        lines = pl.ds(pl.multiple_of(group * SUB, SUB), SUB)
        scale, r, slab = steady[0, lines, :], steady[1, lines, :], steady[2, lines, :]
        decays = [None, jnp.ones((SUB, LANES), f32), slab]
        while len(decays) <= len(received):
            decays.append(decays[-1] * slab)
        for q in range(BLK // 2):
            lanes = slice(q * LANES, (q + 1) * LANES)
            from_left = from_right = jnp.zeros((SUB, LANES), f32)
            for n, ref in enumerate(received, 1):
                distance = jnp.abs((g ^ n) - g)
                factor = decays[n]
                for d in range(1, n):
                    factor = jnp.where(distance == d, decays[d], factor)
                value = factor * ref[lines, lanes]
                is_left = (g ^ n) < g
                from_left = from_left + jnp.where(is_left, value, 0.0)
                from_right = from_right + jnp.where(is_left, 0.0, value)
            before = scale * (powers[2, lines, :] * from_left
                              + r * powers[3, lines, :] * (b_in[lines, lanes] + slab * from_right))
            after = scale * (powers[4, lines, :] * from_right
                             + r * powers[5, lines, :] * (a_in[lines, lanes] + slab * from_left))
            for k in range(SUB):
                rows = pl.ds(pl.multiple_of((group * SUB + k) * SUB, SUB), SUB)
                edge = first * before[k:k + 1] + last * after[k:k + 1]
                work[rows, lanes] = inverse[rows, :] * (spectrum[rows, lanes] + edge)
        return carry

    lax.fori_loop(0, NY // SUB, ends, 0)
    z = (z_hi[...], z_lo[...])
    half = pot.shape[0]
    for parity in range(2):
        part = pl.ds(parity * half, half)
        work[part, :] = dot3((y_hi[parity], y_lo[parity]), split(work[part, :]))
    for q in range(BLK // 2):
        lanes = slice(q * LANES, (q + 1) * LANES)
        even, odd = work[:half, lanes], work[half:, lanes]
        rows = jnp.concatenate([even + odd, turned(even - odd)], axis=1)
        pot[:, q * 2 * LANES:(q + 1) * 2 * LANES] = dot3(split(rows), z)
    for side, group in ((0, own), (1, other)):
        half = (core if side == 0 else 1 - core) * (len(own) * tiles)
        for n, ref in enumerate(group):
            for t in range(tiles):
                lanes = pl.ds(t * LANES, LANES)
                at = half + n * tiles + t
                rows = pl.ds(pl.multiple_of(at * SUB, SUB), SUB)
                total = None
                for w in range(BLK):
                    term = flags[u * BLK + w] * (pot[rows, w * LANES:(w + 1) * LANES] * ref[1 + w, :, lanes])
                    total = term if total is None else total + term
                out[:, pl.ds(pl.multiple_of(at * LANES, LANES), LANES)] = -total


def place_kernel(stride, match, *refs):
    parts, (out, rows, sem) = refs[:-4], refs[-3:]
    pair = BLK // 2
    blocks = out.shape[0] // BLK
    core = my_core()
    values = []
    for part in parts:
        values += [part] if len(part.shape) == 2 else [part.at[n] for n in range(part.shape[0])]
    parts, count = values, len(values) // pair

    def hits(b, side):
        return [(match[b * stride + side * stride // 2 + n], side * count // 2 + n) for n in range(count // 2)]

    def found(b, side):
        return match[blocks * stride + 2 * b + side] > 0

    def move(b, side):
        which = core if side == 0 else 1 - core
        at = b * BLK + which * pair
        return pltpu.make_async_copy(rows.at[b, side], out.at[pl.ds(at, pair)], sem.at[b, side])

    for b in range(blocks):
        for side in range(2):

            @pl.when(found(b, side))
            def _():
                rows[b, side] = jnp.zeros(rows.shape[2:], f32)
                for hit, n in hits(b, side):

                    @pl.when(hit > 0)
                    def _():
                        for u in range(pair):
                            rows[b, side, u] += parts[u * count + n][...]

                move(b, side).start()

    for b in range(blocks):
        for side in range(2):

            @pl.when(found(b, side))
            def _():
                move(b, side).wait()


def tile_device(orbitals, rotation, tile_list, pair_mask):
    shape = per_device, planes, width = orbitals.shape
    n_orb, n_grid = lax.axis_size("orb"), lax.axis_size("grid")
    size_x = planes * n_grid
    half = width // 2
    chips = n_orb // 2
    axes = ("orb", "grid")

    def swap(x, even, odd):
        moves = []
        for a in range(n_orb):
            flip = even if a % 2 == 0 else odd
            moves += [(a * n_grid + b, (a ^ flip) * n_grid + b) for b in range(n_grid)]
        return lax.ppermute(x, axes, moves)

    def cross(x, k):
        moves = [(a * n_grid + b, a * n_grid + (b ^ k)) for a in range(n_orb) for b in range(n_grid)]
        return lax.ppermute(x, axes, moves)

    chunk = half // CHUNKS
    orbitals = pltpu.with_memory_space_constraint(orbitals, pltpu.HBM)

    part = jax.ShapeDtypeStruct((per_device, planes, chunk), f32)
    loaded = pl.pallas_call(
        fetch_kernel, out_shape=jax.ShapeDtypeStruct(shape, f32), in_specs=[HBM], out_specs=VM,
        scratch_shapes=[DMA((4,))], name="fetch", compiler_params=grant(8),
    )(orbitals)

    def take(flip, n, *after):
        return pl.pallas_call(
            functools.partial(take_kernel, flip, n * chunk), out_shape=part, in_specs=[VM] + [ANY] * len(after),
            out_specs=VM, scratch_shapes=[DMA], compiler_params=grant(8),
        )(loaded, *after)

    theirs, last = [], ()
    for n in range(CHUNKS):
        taken = take(True, n, *last)
        theirs.append(swap(taken, 1, 1))
        last = (taken,)
    mine = [take(False, n, taken) for n in range(CHUNKS)]

    pair = BLK // 2
    firsts = (BLK + 2) * chips
    rows = (firsts + 2 * (pair - 1) * chips) * SUB
    wide_table = jax.ShapeDtypeStruct((rows, 2 * LANES), bf16)
    blocks = per_device // BLK
    c, r = line_np()
    c, r = line_np()
    host = jnp.asarray(host_np(chips).reshape(-1))
    high, low = pl.pallas_call(
        functools.partial(setup_kernel, per_device), out_shape=[wide_table] * 2,
        in_specs=[SM, SM, VM, ANY], out_specs=[VM] * 2, name="setup", compiler_params=grant(8),
    )(tile_list, host, rotation, taken)

    def rotate(first, count, fields, *after):
        part = jax.ShapeDtypeStruct((count, planes, chunk * (len(fields) // 2)), f32)
        send, keep = pl.pallas_call(
            functools.partial(rotate_kernel, first * SUB), out_shape=(part, part),
            in_specs=[VM] * (2 + len(fields)) + [ANY] * len(after),
            out_specs=(VM, VM), compiler_params=grant(8),
        )(high, low, *fields, *after)
        return send, keep, swap(send, 2, 4)

    sums, last = [], ()
    for n in range(CHUNKS):
        sums.append(rotate(0, firsts // 2, [mine[n], theirs[n]], *last))
        last = (sums[-1][0],)
    both = [x for n in range(CHUNKS) for x in (mine[n], theirs[n])]
    sums.append(rotate(firsts, (pair - 1) * chips, both, *last))
    passing, own, other = [], [], []

    def pass_on(n, *after, spec=ANY):
        _, keep, got = sums[n]
        count = keep.shape[0] // 2
        value = pl.pallas_call(
            pass_kernel, out_shape=jax.ShapeDtypeStruct((count,) + keep.shape[1:], f32),
            in_specs=[VM] * 2 + [spec] * len(after), out_specs=VM, compiler_params=grant(4),
        )(keep, got, *after)
        passing.append((keep, got, swap(value, 4, 2)))
        return value

    def finish(n, *after):
        keep, got, passed = passing[n]
        own.append(pl.pallas_call(
            finish_kernel, out_shape=jax.ShapeDtypeStruct(passed.shape, f32), in_specs=[VM] * 3 + [ANY] * len(after),
            out_specs=VM, compiler_params=grant(4),
        )(keep, got, passed, *after))
        other.append(swap(own[-1], 1, 1))
        return own[-1]

    step = pass_on(0, sums[-1][0])
    empty, powers, flags, match, alone = pl.pallas_call(
        functools.partial(ready_kernel, per_device, n_grid),
        out_shape=(pltpu.HBM(shape, f32), jax.ShapeDtypeStruct((6, NY, LANES), f32),
                   jax.ShapeDtypeStruct((pair * BLK,), f32), jax.ShapeDtypeStruct((blocks * 10,), jnp.int32),
                   jax.ShapeDtypeStruct((1,), jnp.int32)),
        in_specs=[SM, SM, VM, VM, ANY], out_specs=(HBM, VM, SM, SM, SM),
        scratch_shapes=[pltpu.VMEM((pair, planes, width), f32), DMA((per_device // pair,))], name="ready",
        compiler_params=grant(4),
    )(tile_list, host, pair_mask, jnp.asarray(np.log(r), f32), step)
    step = pass_on(1, empty, spec=HBM)
    for n in range(2, CHUNKS):
        step = pass_on(n, step)
    for n in range(CHUNKS):
        step = finish(n, step)
    last = (pass_on(CHUNKS, step),)

    sine_x, eigen_x = sine_np(planes), eigen_np(planes)
    ends = jnp.asarray(np.einsum("jp,pkl->kjl", sine_x, r[None] ** np.arange(planes - 1, -1, -1)[:, None, None])
                       .reshape(-1, LANES), f32)
    inverse = jnp.asarray((COUPLING / (eigen_x[None, :, None] + c[:, None, :])).reshape(-1, LANES), f32)
    basis = jnp.asarray(np.broadcast_to(sine_x[:, [0, -1]].T[:, :, None], (2, planes, LANES)), f32)
    steady = jnp.asarray(np.stack([r / ((1 - r**2) * (1 - r ** (2 * size_x + 2))), r, r**planes]), f32)

    y_there, y_back = y_tables()
    y_hi, y_lo = halves_np(y_there)
    yt_hi, yt_lo = halves_np(y_back)
    z_hi, z_lo = halves_np(z_table())
    zt_hi, zt_lo = halves_np(z_table().T)
    solved = []
    lines = jax.ShapeDtypeStruct((NY, 2 * LANES), f32)
    cube = (NY * SUB, 2 * LANES)
    wide = pltpu.VMEM((width // LANES * SUB, BLK * LANES), f32)
    base_own, base_other = own[:CHUNKS], other[:CHUNKS]
    for u in range(pair):
        if u:
            finish(CHUNKS, *last)
        more_own, more_other = own[CHUNKS:][:u], other[CHUNKS:][:u]
        counts = (CHUNKS, CHUNKS, len(more_own), len(more_other))
        inputs = [*base_own, *base_other, *more_own, *more_other, y_hi, y_lo, z_hi, z_lo, ends, powers]
        *messages, spectrum, a, b = pl.pallas_call(
            functools.partial(forward_kernel, u, counts + (n_grid - 1,)),
            out_shape=[lines] * (n_grid - 1) + [jax.ShapeDtypeStruct(cube, f32), lines, lines],
            in_specs=[VM] * len(inputs) + [ANY] * len(last),
            out_specs=[VM] * (n_grid + 2),
            scratch_shapes=[wide],
            compiler_params=grant(16),
        )(*inputs, *last)
        last = (spectrum,)
        received = []
        for k, message in enumerate(messages, 1):
            received.append(cross(message, k))
        solved.append((spectrum, a, b, received))

    terms, last = [], ()
    for u, (spectrum, a, b, received) in enumerate(solved):
        inputs = [*base_own, *base_other, *received, yt_hi, yt_lo, zt_hi, zt_lo, inverse, basis, powers, steady,
                  spectrum, a, b]
        terms.append(pl.pallas_call(
            functools.partial(backward_kernel, u, (CHUNKS, CHUNKS, len(received))),
            out_shape=jax.ShapeDtypeStruct((planes, width), f32),
            in_specs=[SM] + [VM] * len(inputs) + [ANY] * len(last),
            out_specs=VM,
            scratch_shapes=[pltpu.VMEM(cube, f32), wide],
            compiler_params=grant(16),
        )(flags, *inputs, *last))
        last = (terms[-1],)

    near_1 = [swap(term, 2, 4) for term in terms]
    near_2 = [swap(term, 4, 2) for term in terms]
    own_parts = [[term, x, y] for term, x, y in zip(terms, near_1, near_2)]
    sib_parts = []
    for term, x, y in own_parts:
        joined = pl.pallas_call(
            join_kernel, out_shape=jax.ShapeDtypeStruct((2,) + term.shape, f32), in_specs=[VM] * 2, out_specs=VM,
            compiler_params=grant(4),
        )(x, y)
        given = swap(term, 1, 1)
        sib_parts.append([given, swap(joined, 1, 1)])

    def place(target, groups):
        parts = [part for group in groups for part in group]
        return pl.pallas_call(
            functools.partial(place_kernel, 8),
            out_shape=pltpu.HBM(shape, f32),
            in_specs=[SM] + [VM] * len(parts) + [HBM],
            out_specs=HBM,
            input_output_aliases={len(parts) + 1: 0},
            scratch_shapes=[pltpu.VMEM((blocks, 2, pair, planes, width), f32), DMA((blocks, 2))],
            name="place",
            compiler_params=grant(8),
        )(match, *parts, target)

    def place_near(target, mine, sibs):
        return place(target, [a + b for a, b in zip(mine, sibs)])

    def place_far(target, mine, sibs):
        far = [swap(group[1], 4, 2) for group in mine]
        return place(target, [a + [x] + b + [swap(x, 1, 1)] for a, b, x in zip(mine, sibs, far)])

    return lax.cond(alone[0] != 0, place_far, place_near, empty, own_parts, sib_parts)


def sine_table(length):
    wave_index = jnp.arange(length, dtype=f32) + 1.0
    return jnp.sqrt(2.0 / (length + 1.0)) * jnp.sin(
        jnp.pi * wave_index[:, None] * wave_index[None, :] / (length + 1.0)
    )


def eigen_values(length):
    wave_index = jnp.arange(length, dtype=f32) + 1.0
    return 2.0 - 2.0 * jnp.cos(jnp.pi * wave_index / (length + 1.0))


def green_kernel(size_x, size_y, size_z):
    summed = (
        eigen_values(size_x)[:, None, None]
        + eigen_values(size_y)[None, :, None]
        + eigen_values(size_z)[None, None, :]
    )
    return COUPLING / (summed + SCREENING)


def pair_lists(tile_list, pair_mask):
    within = jnp.arange(BLK * BLK, dtype=jnp.int32)
    targets = (BLK * tile_list[:, 0:1] + within[None, :] // BLK).reshape(-1)
    sources = (BLK * tile_list[:, 1:2] + within[None, :] % BLK).reshape(-1)
    return (targets, sources, pair_mask[targets, sources])


def compact(targets, sources, live_flags, number):
    ranking = jnp.cumsum(live_flags) - 1
    places = jnp.where(live_flags == 1, ranking, number)
    picked = (
        jnp.zeros((number,), jnp.int32)
        .at[places]
        .set(jnp.arange(live_flags.shape[0], dtype=jnp.int32), mode="drop")
    )
    return (targets[picked], sources[picked])


def along_z(values, matrix):
    number, planes, width_yz = values.shape
    size_z = matrix.shape[0]
    shaped = values.reshape(number, planes, width_yz // size_z, size_z)
    return jnp.einsum("pxrz,zk->pxrk", shaped, matrix, precision=precise).reshape(number, planes, width_yz)


def along_y(values, matrix):
    number, planes, width_yz = values.shape
    size_y = matrix.shape[0]
    shaped = values.reshape(number, planes, size_y, width_yz // size_y)
    return jnp.einsum("pxyz,yk->pxkz", shaped, matrix, precision=precise).reshape(number, planes, width_yz)


def along_x(values, matrix):
    return jnp.einsum("pxc,xk->pkc", values, matrix, precision=precise)


def any_device(orbitals, rotation, tile_list, pair_mask):
    n_grid = lax.axis_size("grid")
    number_orbitals, size_x = rotation.shape[0], orbitals.shape[1] * n_grid
    rotated = jnp.einsum(
        "ij,ixc->jxc",
        rotation,
        lax.all_to_all(orbitals, "orb", split_axis=2, concat_axis=0, tiled=True),
        precision=precise,
    )
    planes, width_yz = rotated.shape[1:]
    targets, sources, live_flags = pair_lists(tile_list, pair_mask)
    matrix_x, matrix_y, matrix_z = sine_table(size_x), sine_table(NY), sine_table(NZ)
    kernel = green_kernel(size_x, NY, NZ).reshape(size_x, NY * NZ)
    orbital_ids = jnp.arange(number_orbitals, dtype=jnp.int32)
    targets, sources = compact(targets, sources, live_flags, targets.shape[0] // 2)
    density = rotated[targets] * rotated[sources]
    number = density.shape[0]
    spectrum = along_z(density, matrix_z)
    spectrum = lax.all_to_all(spectrum, "orb", split_axis=0, concat_axis=2, tiled=True)
    spectrum = along_y(spectrum, matrix_y)
    spectrum = lax.all_to_all(spectrum, "grid", split_axis=0, concat_axis=1, tiled=True)
    spectrum = along_x(along_x(spectrum, matrix_x) * kernel, matrix_x)
    spectrum = lax.all_to_all(spectrum, "grid", split_axis=1, concat_axis=0, tiled=True)
    spectrum = along_y(spectrum, matrix_y)
    spectrum = lax.all_to_all(spectrum, "orb", split_axis=2, concat_axis=0, tiled=True)
    potential = along_z(spectrum, matrix_z)
    products = potential * rotated[sources]
    selector = (targets[None, :] == orbital_ids[:, None]).astype(f32)
    partial_value = -jnp.dot(selector, products.reshape(number, planes * width_yz), precision=precise)
    partial_value = partial_value.reshape(number_orbitals, planes, width_yz)
    return lax.all_to_all(partial_value, "orb", split_axis=0, concat_axis=2, tiled=True)


def solution(mesh):
    n_orb, n_grid = mesh.shape["orb"], mesh.shape["grid"]

    def on_device(orbitals, rotation, tile_list, pair_mask):
        per_device, planes, width = orbitals.shape
        fits = n_orb == 8 and 2 * tile_list.shape[0] == n_orb and planes == SUB and per_device % BLK == 0
        fits = fits and width == NY * NZ and 2 * NZ == LANES and n_grid in (2, 4, 8)
        fits = fits and per_device * SUB == LANES and rotation.shape == (LANES, LANES)
        if not fits:
            return any_device(orbitals, rotation, tile_list, pair_mask)
        return tile_device(orbitals, rotation, tile_list, pair_mask)

    in_specs = (P("orb", "grid", None), P(), P(), P())
    out_specs = P("orb", "grid", None)
    return jax.shard_map(on_device, mesh=mesh, in_specs=in_specs, out_specs=out_specs, check_vma=False)
```

```python
import functools
import itertools

import jax
import jax.numpy as jnp
import numpy as np
from jax import lax
from jax.experimental import pallas as pl
from jax.experimental.pallas import tpu as pltpu
from jax.sharding import PartitionSpec as P


BLK = 4
NY = 64
NZ = 64
LANES = 128
SUB = 8
CHUNKS = 2
COUPLING = 0.25
SCREENING = 0.1

precise = lax.Precision.HIGHEST
f32 = jnp.float32
bf16 = jnp.bfloat16

VM = pl.BlockSpec(memory_space=pltpu.VMEM)
SM = pl.BlockSpec(memory_space=pltpu.SMEM)
ANY = pl.BlockSpec(memory_space=pl.ANY)
HBM = pl.BlockSpec(memory_space=pltpu.HBM)
DMA = pltpu.SemaphoreType.DMA


def grant(mib):
    return pltpu.CompilerParams(vmem_limit_bytes=mib << 20)


def sine_np(n):
    k = np.arange(1, n + 1, dtype=np.float64)
    return np.sqrt(2.0 / (n + 1)) * np.sin(np.pi * k[:, None] * k[None, :] / (n + 1))


def eigen_np(n):
    k = np.arange(1, n + 1, dtype=np.float64)
    return 2.0 - 2.0 * np.cos(np.pi * k / (n + 1))


def halves_np(table):
    high = np.asarray(table, np.float32).astype(jnp.bfloat16)
    low = (np.asarray(table, np.float64) - high.astype(np.float64)).astype(jnp.bfloat16)
    return jnp.asarray(high), jnp.asarray(low)


def y_order():
    rows = LANES // NZ
    return np.arange(NY).reshape(NY // rows, rows).T.reshape(-1)


def y_tables():
    sine, planes = sine_np(NY), sine_np(SUB)
    even, odd = np.kron(sine[0::2, 0::2], planes), np.kron(sine[1::2, 0::2], planes)
    return np.stack([even, odd]), np.stack([even, odd.T])


def turned(x):
    count = x.shape[0] // SUB
    return jnp.concatenate([x[(count - 1 - t) * SUB:(count - t) * SUB] for t in range(count)])


def z_table():
    half = LANES // NZ
    sine = sine_np(NZ)
    table = np.zeros((2, half, NZ, half, 2, NZ))
    for pair in range(2):
        for h in range(half):
            table[pair, h, :, h, pair, :] = sine
    return table.reshape(2 * half * NZ, half * 2 * NZ)


def line_np():
    c = eigen_np(NY)[y_order()][:, None] + eigen_np(NZ)[None, :] + SCREENING
    c = np.concatenate([c, c], axis=1)
    return c, 2.0 / (2.0 + c + np.sqrt(c * (c + 4.0)))


def host_np(chips):
    table = np.zeros((chips**chips, chips), np.int32)
    for owners in itertools.product(range(chips), repeat=chips):
        best = None
        for tiles in itertools.permutations(range(chips)):
            hops = [bin(chip ^ owners[tile]).count("1") for chip, tile in enumerate(tiles)]
            cost = (max(hops), sum(hops))
            if best is None or cost < best[0]:
                best = (cost, tiles)
        table[sum(own * chips**t for t, own in enumerate(owners))] = best[1]
    return table


def dot(a, b):
    return jnp.dot(a, b, preferred_element_type=f32)


def split(x):
    high = x.astype(bf16)
    return high, (x - high.astype(f32)).astype(bf16)


def dot3(a, b):
    return dot(a[0], b[0]) + dot(a[0], b[1]) + dot(a[1], b[0])


def my_core():
    return lax.rem(lax.axis_index("orb"), 2)


def my_place():
    o = lax.axis_index("orb")
    return o, lax.rem(o, 2), lax.div(o, 2)


def fetch_kernel(source, *rest):
    outs, (whole, sem) = rest[:-2], rest[-2:]
    step = whole.shape[0] // len(outs)
    copies = [
        pltpu.make_async_copy(source.at[pl.ds(n * step, step)], whole.at[pl.ds(n * step, step)], sem.at[n])
        for n in range(len(outs))
    ]
    for copy in copies:
        copy.start()
    for copy in copies:
        copy.wait()
    core = my_core()
    copies = []
    for n, out in enumerate(outs):
        side = 1 - core if n < CHUNKS else core
        at = side * (whole.shape[2] // 2) + n % CHUNKS * out.shape[2]
        lanes = pl.ds(pl.multiple_of(at, LANES), out.shape[2])
        copies.append(pltpu.make_async_copy(whole.at[:, :, lanes], out, sem.at[n]))
    for copy in copies:
        copy.start()
    for copy in copies:
        copy.wait()


class Place:
    def __init__(self, per_device, tiles, host):
        self.o, self.core, self.chip = my_place()
        self.tiles, self.host = tiles, host
        self.chips = tiles.shape[0]
        owners = [lax.div(tiles[t, 0] * BLK, 2 * per_device) for t in range(self.chips)]
        key, same = 0, True
        for t in range(self.chips):
            key = key + owners[t] * self.chips**t
            same = same & (owners[t] == owners[0])
        self.key, self.same = key, same
        self.bit_1 = jnp.where(self.core == 0, 1, 2)
        self.bit_2 = 3 - self.bit_1

    def tile(self, chip):
        return self.host[self.key * self.chips + chip]

    def heads(self, chip):
        tile = self.tile(chip)
        return BLK * self.tiles[tile, 0], BLK * self.tiles[tile, 1]


def setup_kernel(per_device, tiles, host, rotation, after, high, low):
    core = my_core()
    at = Place(per_device, tiles, host)
    pair = BLK // 2
    heads = [at.heads(chip) for chip in (at.chip ^ 3, at.chip ^ at.bit_1, at.chip ^ at.bit_2, at.chip)]
    wanted = []
    for a, b in heads:
        wanted += [a + (1 - core) * pair] + [b + w for w in range(BLK)] + [a + core * pair]
    for u in range(1, pair):
        for a, b in heads:
            wanted += [a + (1 - core) * pair + u, a + core * pair + u]
    lane = lax.broadcasted_iota(jnp.int32, (SUB, LANES), 1)
    chosen = jnp.concatenate([jnp.where(lane == n, 1.0, 0.0) for n in wanted]).astype(bf16)
    rows = chosen.shape[0]
    row = lax.broadcasted_iota(jnp.int32, (LANES, LANES), 0)
    column = lax.broadcasted_iota(jnp.int32, (LANES, LANES), 1)
    columns = [
        jnp.where(row - (at.o ^ e) * per_device == jnp.right_shift(column, 3), 1.0, 0.0).astype(bf16)
        for e in range(2)
    ]
    keep = (lax.broadcasted_iota(jnp.int32, (rows, LANES), 0) & (SUB - 1)) == (
        lax.broadcasted_iota(jnp.int32, (rows, LANES), 1) & (SUB - 1)
    )
    for out, values in zip((high, low), split(rotation[...])):
        picked = lax.dot_general(chosen, values, (((1,), (1,)), ((), ())), preferred_element_type=f32).astype(bf16)
        for e in range(2):
            out[:, e * LANES:(e + 1) * LANES] = jnp.where(keep, dot(picked, columns[e]), 0.0).astype(bf16)


def ready_kernel(per_device, n_grid, tiles, host, mask, log_r, *rest):
    out, powers, flags, match, alone, zeros, sem = rest[-7:]
    zeros[...] = jnp.zeros(zeros.shape, f32)
    step = zeros.shape[0]
    copies = [
        pltpu.make_async_copy(zeros, out.at[pl.ds(n * step, step)], sem.at[n]) for n in range(out.shape[0] // step)
    ]
    for copy in copies:
        copy.start()
    begin, size_x = SUB * lax.axis_index("grid"), SUB * n_grid
    exponents = (
        2 * begin + SUB + 1,
        2 * size_x + 1 - SUB - 2 * begin,
        2 * size_x + 2 - 2 * begin,
        2 * begin,
        2 * begin + 2 * SUB + 2,
        2 * size_x - 2 * SUB - 2 * begin,
    )
    for n, exponent in enumerate(exponents):
        power = jnp.exp(exponent.astype(f32) * log_r[...])
        powers[n] = power if n < 2 else 1.0 - power
    at = Place(per_device, tiles, host)
    alone[0] = at.same.astype(jnp.int32)
    a, b = at.heads(at.chip)
    pair = BLK // 2
    live = mask[...].astype(f32)
    row = lax.broadcasted_iota(jnp.int32, live.shape, 0)
    column = lax.broadcasted_iota(jnp.int32, (1, live.shape[1]), 1)
    for u in range(pair):
        line = jnp.sum(jnp.where(row == a + at.core * pair + u, live, 0.0), axis=0, keepdims=True)
        for w in range(BLK):
            flags[u * BLK + w] = jnp.sum(jnp.where(column == b + w, line, 0.0))
    blocks = per_device // BLK
    parts = [0, at.bit_1, at.bit_2, 3, 0, at.bit_2, at.bit_1, 3]
    for n, flip in enumerate(parts):
        home = tiles[at.tile(at.chip ^ flip), 0]
        for block in range(blocks):
            hit = home == at.o * blocks + block
            if n % 4 == 3:
                hit = hit & at.same
            found = hit.astype(jnp.int32)
            match[block * len(parts) + n] = found
            total = blocks * len(parts) + 2 * block + n // 4
            match[total] = found if n % 4 == 0 else match[total] + found
    for copy in copies:
        copy.wait()


def join_kernel(x, y, out):
    out[0] = x[...]
    out[1] = y[...]


def rotate_kernel(first, high, low, *rest):
    send, keep = rest[-2:]
    rows = send.shape[0] * SUB
    part = pl.ds(first, 2 * rows)
    table = (high[part, :], low[part, :])
    at = 0
    step = 2 * LANES
    while at < send.shape[2]:
        width = rest[0].shape[2]
        n, inner = at // width, at % width
        lanes = slice(inner, inner + step)
        mine, theirs = rest[2 * n], rest[2 * n + 1]
        depth = mine.shape[0] * SUB
        cells = jnp.concatenate([mine[:, :, lanes].reshape(depth, step), theirs[:, :, lanes].reshape(depth, step)])
        total = dot3(table, split(cells))
        lanes = slice(at, at + step)
        send[:, :, lanes] = total[:rows].reshape(send.shape[0], SUB, step)
        keep[:, :, lanes] = total[rows:].reshape(keep.shape[0], SUB, step)
        at += step


def pass_kernel(keep, got, *rest):
    out = rest[-1]
    count = out.shape[0]
    out[...] = keep[:count] + got[:count]


def finish_kernel(keep, got, passed, *rest):
    out = rest[-1]
    count = out.shape[0]
    out[...] = keep[count:] + got[count:] + passed[...]


def sub_sums(values):
    row = lax.broadcasted_iota(jnp.int32, values[0].shape, 0)
    for s in (4, 2):
        low = (row & s) == 0
        paired = []
        for n in range(s):
            a, b = values[n], values[n + s]
            paired.append(jnp.where(low, a, pltpu.roll(b, s, 0)) + jnp.where(low, pltpu.roll(a, SUB - s, 0), b))
        values = paired
    even = (row & 1) == 0
    a, b = values
    return jnp.where(even, a, pltpu.roll(b, 1, 0)), jnp.where(even, pltpu.roll(a, SUB - 1, 0), b)


def fields(u, own, other, first_own, first_other):
    table = []
    for side, sources, targets in ((0, first_own, own), (1, first_other, other)):
        for n, ref in enumerate(sources):
            if u == 0:
                table.append((side, n, ref, targets[n], BLK + 1 if side == 0 else 0, 0))
            else:
                table.append((side, n, ref, targets[0], 1 if side == 0 else 0, n * ref.shape[2]))
    return table


def forward_kernel(u, counts, *refs):
    groups = []
    for count in counts[:-1]:
        groups.append(refs[:count])
        refs = refs[count:]
    first_own, first_other, own, other = groups[:4]
    y_hi, y_lo, z_hi, z_lo, ends, powers = refs[:6]
    messages, (spectrum, a_out, b_out, dens) = refs[-4 - counts[-1]:-4], refs[-4:]
    if u == 0:
        own, other = first_own, first_other
    core, g = my_core(), lax.axis_index("grid")
    tiles = first_own[0].shape[2] // LANES
    for side, n, source, target, slot, offset in fields(u, own, other, first_own, first_other):
        half = (core if side == 0 else 1 - core) * (len(first_own) * tiles * SUB)
        for t in range(tiles):
            lanes = pl.ds(t * LANES, LANES)
            value = target[slot, :, pl.ds(offset + t * LANES, LANES)]
            rows = pl.ds(pl.multiple_of(half + (n * tiles + t) * SUB, SUB), SUB)
            for w in range(BLK):
                dens[rows, w * LANES:(w + 1) * LANES] = value * source[1 + w, :, lanes]
    z = (z_hi[...], z_lo[...])
    half = dens.shape[0]
    for q in range(BLK // 2):
        out = dot3(split(dens[:, q * 2 * LANES:(q + 1) * 2 * LANES]), z)
        mirror = turned(out[:, LANES:])
        spectrum[:half, q * LANES:(q + 1) * LANES] = out[:, :LANES] + mirror
        spectrum[half:, q * LANES:(q + 1) * LANES] = out[:, :LANES] - mirror
    for parity in range(2):
        part = pl.ds(parity * half, half)
        spectrum[part, :] = dot3((y_hi[parity], y_lo[parity]), split(spectrum[part, :]))

    def reduce(group, carry):
        lines = pl.ds(pl.multiple_of(group * SUB, SUB), SUB)
        near, far = powers[0, lines, :], powers[1, lines, :]
        for q in range(BLK // 2):
            lanes = slice(q * LANES, (q + 1) * LANES)
            values = []
            for k in range(SUB):
                rows = pl.ds(pl.multiple_of((group * SUB + k) * SUB, SUB), SUB)
                values.append(ends[rows, :] * spectrum[rows, lanes])
            even, odd = sub_sums(values)
            rightward = (even + odd) - near * (even - odd)
            leftward = (even - odd) - far * (even + odd)
            a_out[lines, lanes] = rightward
            b_out[lines, lanes] = leftward
            for k, out in enumerate(messages, 1):
                out[lines, lanes] = jnp.where((g ^ k) > g, rightward, leftward)
        return carry

    lax.fori_loop(0, NY // SUB, reduce, 0)


def backward_kernel(u, counts, flags, *refs):
    groups = []
    for count in counts:
        groups.append(refs[:count])
        refs = refs[count:]
    own, other, received = groups
    (y_hi, y_lo, z_hi, z_lo, inverse, basis, powers, steady, spectrum, a_in, b_in) = refs[:11]
    out, work, pot = refs[-3:]
    core, g = my_core(), lax.axis_index("grid")
    tiles = own[0].shape[2] // LANES
    first, last = basis[0], basis[1]

    def ends(group, carry):
        lines = pl.ds(pl.multiple_of(group * SUB, SUB), SUB)
        scale, r, slab = steady[0, lines, :], steady[1, lines, :], steady[2, lines, :]
        decays = [None, jnp.ones((SUB, LANES), f32), slab]
        while len(decays) <= len(received):
            decays.append(decays[-1] * slab)
        for q in range(BLK // 2):
            lanes = slice(q * LANES, (q + 1) * LANES)
            from_left = from_right = jnp.zeros((SUB, LANES), f32)
            for n, ref in enumerate(received, 1):
                distance = jnp.abs((g ^ n) - g)
                factor = decays[n]
                for d in range(1, n):
                    factor = jnp.where(distance == d, decays[d], factor)
                value = factor * ref[lines, lanes]
                is_left = (g ^ n) < g
                from_left = from_left + jnp.where(is_left, value, 0.0)
                from_right = from_right + jnp.where(is_left, 0.0, value)
            before = scale * (powers[2, lines, :] * from_left
                              + r * powers[3, lines, :] * (b_in[lines, lanes] + slab * from_right))
            after = scale * (powers[4, lines, :] * from_right
                             + r * powers[5, lines, :] * (a_in[lines, lanes] + slab * from_left))
            for k in range(SUB):
                rows = pl.ds(pl.multiple_of((group * SUB + k) * SUB, SUB), SUB)
                edge = first * before[k:k + 1] + last * after[k:k + 1]
                work[rows, lanes] = inverse[rows, :] * (spectrum[rows, lanes] + edge)
        return carry

    lax.fori_loop(0, NY // SUB, ends, 0)
    z = (z_hi[...], z_lo[...])
    half = pot.shape[0]
    for parity in range(2):
        part = pl.ds(parity * half, half)
        work[part, :] = dot3((y_hi[parity], y_lo[parity]), split(work[part, :]))
    for q in range(BLK // 2):
        lanes = slice(q * LANES, (q + 1) * LANES)
        even, odd = work[:half, lanes], work[half:, lanes]
        rows = jnp.concatenate([even + odd, turned(even - odd)], axis=1)
        pot[:, q * 2 * LANES:(q + 1) * 2 * LANES] = dot3(split(rows), z)
    for side, group in ((0, own), (1, other)):
        half = (core if side == 0 else 1 - core) * (len(own) * tiles)
        for n, ref in enumerate(group):
            for t in range(tiles):
                lanes = pl.ds(t * LANES, LANES)
                at = half + n * tiles + t
                rows = pl.ds(pl.multiple_of(at * SUB, SUB), SUB)
                total = None
                for w in range(BLK):
                    term = flags[u * BLK + w] * (pot[rows, w * LANES:(w + 1) * LANES] * ref[1 + w, :, lanes])
                    total = term if total is None else total + term
                out[:, pl.ds(pl.multiple_of(at * LANES, LANES), LANES)] = -total


def place_kernel(stride, match, *refs):
    parts, (out, rows, sem) = refs[:-4], refs[-3:]
    pair = BLK // 2
    blocks = out.shape[0] // BLK
    core = my_core()
    values = []
    for part in parts:
        values += [part] if len(part.shape) == 2 else [part.at[n] for n in range(part.shape[0])]
    parts, count = values, len(values) // pair

    def hits(b, side):
        return [(match[b * stride + side * stride // 2 + n], side * count // 2 + n) for n in range(count // 2)]

    def found(b, side):
        return match[blocks * stride + 2 * b + side] > 0

    def move(b, side):
        which = core if side == 0 else 1 - core
        at = b * BLK + which * pair
        return pltpu.make_async_copy(rows.at[b, side], out.at[pl.ds(at, pair)], sem.at[b, side])

    for b in range(blocks):
        for side in range(2):

            @pl.when(found(b, side))
            def _():
                rows[b, side] = jnp.zeros(rows.shape[2:], f32)
                for hit, n in hits(b, side):

                    @pl.when(hit > 0)
                    def _():
                        for u in range(pair):
                            rows[b, side, u] += parts[u * count + n][...]

                move(b, side).start()

    for b in range(blocks):
        for side in range(2):

            @pl.when(found(b, side))
            def _():
                move(b, side).wait()


def tile_device(orbitals, rotation, tile_list, pair_mask):
    shape = per_device, planes, width = orbitals.shape
    n_orb, n_grid = lax.axis_size("orb"), lax.axis_size("grid")
    size_x = planes * n_grid
    half = width // 2
    chips = n_orb // 2
    axes = ("orb", "grid")

    def swap(x, even, odd):
        moves = []
        for a in range(n_orb):
            flip = even if a % 2 == 0 else odd
            moves += [(a * n_grid + b, (a ^ flip) * n_grid + b) for b in range(n_grid)]
        return lax.ppermute(x, axes, moves)

    def cross(x, k):
        moves = [(a * n_grid + b, a * n_grid + (b ^ k)) for a in range(n_orb) for b in range(n_grid)]
        return lax.ppermute(x, axes, moves)

    chunk = half // CHUNKS
    orbitals = pltpu.with_memory_space_constraint(orbitals, pltpu.HBM)

    part = jax.ShapeDtypeStruct((per_device, planes, chunk), f32)
    fetched = pl.pallas_call(
        fetch_kernel, out_shape=[part] * (2 * CHUNKS), in_specs=[HBM], out_specs=[VM] * (2 * CHUNKS),
        scratch_shapes=[pltpu.VMEM(shape, f32), DMA((2 * CHUNKS,))], name="fetch", compiler_params=grant(8),
    )(orbitals)
    theirs, mine = [], fetched[CHUNKS:]
    for taken in fetched[:CHUNKS]:
        theirs.append(swap(taken, 1, 1))

    pair = BLK // 2
    firsts = (BLK + 2) * chips
    rows = (firsts + 2 * (pair - 1) * chips) * SUB
    wide_table = jax.ShapeDtypeStruct((rows, 2 * LANES), bf16)
    blocks = per_device // BLK
    c, r = line_np()
    c, r = line_np()
    host = jnp.asarray(host_np(chips).reshape(-1))
    high, low = pl.pallas_call(
        functools.partial(setup_kernel, per_device), out_shape=[wide_table] * 2,
        in_specs=[SM, SM, VM, ANY], out_specs=[VM] * 2, name="setup", compiler_params=grant(8),
    )(tile_list, host, rotation, taken)

    def rotate(first, count, fields, *after):
        part = jax.ShapeDtypeStruct((count, planes, chunk * (len(fields) // 2)), f32)
        send, keep = pl.pallas_call(
            functools.partial(rotate_kernel, first * SUB), out_shape=(part, part),
            in_specs=[VM] * (2 + len(fields)) + [ANY] * len(after),
            out_specs=(VM, VM), compiler_params=grant(8),
        )(high, low, *fields, *after)
        return send, keep, swap(send, 2, 4)

    sums, last = [], ()
    for n in range(CHUNKS):
        sums.append(rotate(0, firsts // 2, [mine[n], theirs[n]], *last))
        last = (sums[-1][0],)
    both = [x for n in range(CHUNKS) for x in (mine[n], theirs[n])]
    sums.append(rotate(firsts, (pair - 1) * chips, both, *last))
    passing, own, other = [], [], []

    def pass_on(n, *after, spec=ANY):
        _, keep, got = sums[n]
        count = keep.shape[0] // 2
        value = pl.pallas_call(
            pass_kernel, out_shape=jax.ShapeDtypeStruct((count,) + keep.shape[1:], f32),
            in_specs=[VM] * 2 + [spec] * len(after), out_specs=VM, compiler_params=grant(4),
        )(keep, got, *after)
        passing.append((keep, got, swap(value, 4, 2)))
        return value

    def finish(n, *after):
        keep, got, passed = passing[n]
        own.append(pl.pallas_call(
            finish_kernel, out_shape=jax.ShapeDtypeStruct(passed.shape, f32), in_specs=[VM] * 3 + [ANY] * len(after),
            out_specs=VM, compiler_params=grant(4),
        )(keep, got, passed, *after))
        other.append(swap(own[-1], 1, 1))
        return own[-1]

    step = pass_on(0, sums[-1][0])
    empty, powers, flags, match, alone = pl.pallas_call(
        functools.partial(ready_kernel, per_device, n_grid),
        out_shape=(pltpu.HBM(shape, f32), jax.ShapeDtypeStruct((6, NY, LANES), f32),
                   jax.ShapeDtypeStruct((pair * BLK,), f32), jax.ShapeDtypeStruct((blocks * 10,), jnp.int32),
                   jax.ShapeDtypeStruct((1,), jnp.int32)),
        in_specs=[SM, SM, VM, VM, ANY], out_specs=(HBM, VM, SM, SM, SM),
        scratch_shapes=[pltpu.VMEM((pair, planes, width), f32), DMA((per_device // pair,))], name="ready",
        compiler_params=grant(4),
    )(tile_list, host, pair_mask, jnp.asarray(np.log(r), f32), step)
    step = pass_on(1, empty, spec=HBM)
    for n in range(2, CHUNKS):
        step = pass_on(n, step)
    for n in range(CHUNKS):
        step = finish(n, step)
    last = (pass_on(CHUNKS, step),)

    sine_x, eigen_x = sine_np(planes), eigen_np(planes)
    ends = jnp.asarray(np.einsum("jp,pkl->kjl", sine_x, r[None] ** np.arange(planes - 1, -1, -1)[:, None, None])
                       .reshape(-1, LANES), f32)
    inverse = jnp.asarray((COUPLING / (eigen_x[None, :, None] + c[:, None, :])).reshape(-1, LANES), f32)
    basis = jnp.asarray(np.broadcast_to(sine_x[:, [0, -1]].T[:, :, None], (2, planes, LANES)), f32)
    steady = jnp.asarray(np.stack([r / ((1 - r**2) * (1 - r ** (2 * size_x + 2))), r, r**planes]), f32)

    y_there, y_back = y_tables()
    y_hi, y_lo = halves_np(y_there)
    yt_hi, yt_lo = halves_np(y_back)
    z_hi, z_lo = halves_np(z_table())
    zt_hi, zt_lo = halves_np(z_table().T)
    solved = []
    lines = jax.ShapeDtypeStruct((NY, 2 * LANES), f32)
    cube = (NY * SUB, 2 * LANES)
    wide = pltpu.VMEM((width // LANES * SUB, BLK * LANES), f32)
    base_own, base_other = own[:CHUNKS], other[:CHUNKS]
    for u in range(pair):
        if u:
            finish(CHUNKS, *last)
        more_own, more_other = own[CHUNKS:][:u], other[CHUNKS:][:u]
        counts = (CHUNKS, CHUNKS, len(more_own), len(more_other))
        inputs = [*base_own, *base_other, *more_own, *more_other, y_hi, y_lo, z_hi, z_lo, ends, powers]
        *messages, spectrum, a, b = pl.pallas_call(
            functools.partial(forward_kernel, u, counts + (n_grid - 1,)),
            out_shape=[lines] * (n_grid - 1) + [jax.ShapeDtypeStruct(cube, f32), lines, lines],
            in_specs=[VM] * len(inputs) + [ANY] * len(last),
            out_specs=[VM] * (n_grid + 2),
            scratch_shapes=[wide],
            compiler_params=grant(16),
        )(*inputs, *last)
        last = (spectrum,)
        received = []
        for k, message in enumerate(messages, 1):
            received.append(cross(message, k))
        solved.append((spectrum, a, b, received))

    terms, last = [], ()
    for u, (spectrum, a, b, received) in enumerate(solved):
        inputs = [*base_own, *base_other, *received, yt_hi, yt_lo, zt_hi, zt_lo, inverse, basis, powers, steady,
                  spectrum, a, b]
        terms.append(pl.pallas_call(
            functools.partial(backward_kernel, u, (CHUNKS, CHUNKS, len(received))),
            out_shape=jax.ShapeDtypeStruct((planes, width), f32),
            in_specs=[SM] + [VM] * len(inputs) + [ANY] * len(last),
            out_specs=VM,
            scratch_shapes=[pltpu.VMEM(cube, f32), wide],
            compiler_params=grant(16),
        )(flags, *inputs, *last))
        last = (terms[-1],)

    near_1 = [swap(term, 2, 4) for term in terms]
    near_2 = [swap(term, 4, 2) for term in terms]
    own_parts = [[term, x, y] for term, x, y in zip(terms, near_1, near_2)]
    sib_parts = []
    for term, x, y in own_parts:
        joined = pl.pallas_call(
            join_kernel, out_shape=jax.ShapeDtypeStruct((2,) + term.shape, f32), in_specs=[VM] * 2, out_specs=VM,
            compiler_params=grant(4),
        )(x, y)
        given = swap(term, 1, 1)
        sib_parts.append([given, swap(joined, 1, 1)])

    def place(target, groups):
        parts = [part for group in groups for part in group]
        return pl.pallas_call(
            functools.partial(place_kernel, 8),
            out_shape=pltpu.HBM(shape, f32),
            in_specs=[SM] + [VM] * len(parts) + [HBM],
            out_specs=HBM,
            input_output_aliases={len(parts) + 1: 0},
            scratch_shapes=[pltpu.VMEM((blocks, 2, pair, planes, width), f32), DMA((blocks, 2))],
            name="place",
            compiler_params=grant(8),
        )(match, *parts, target)

    def place_near(target, mine, sibs):
        return place(target, [a + b for a, b in zip(mine, sibs)])

    def place_far(target, mine, sibs):
        far = [swap(group[1], 4, 2) for group in mine]
        return place(target, [a + [x] + b + [swap(x, 1, 1)] for a, b, x in zip(mine, sibs, far)])

    return lax.cond(alone[0] != 0, place_far, place_near, empty, own_parts, sib_parts)


def sine_table(length):
    wave_index = jnp.arange(length, dtype=f32) + 1.0
    return jnp.sqrt(2.0 / (length + 1.0)) * jnp.sin(
        jnp.pi * wave_index[:, None] * wave_index[None, :] / (length + 1.0)
    )


def eigen_values(length):
    wave_index = jnp.arange(length, dtype=f32) + 1.0
    return 2.0 - 2.0 * jnp.cos(jnp.pi * wave_index / (length + 1.0))


def green_kernel(size_x, size_y, size_z):
    summed = (
        eigen_values(size_x)[:, None, None]
        + eigen_values(size_y)[None, :, None]
        + eigen_values(size_z)[None, None, :]
    )
    return COUPLING / (summed + SCREENING)


def pair_lists(tile_list, pair_mask):
    within = jnp.arange(BLK * BLK, dtype=jnp.int32)
    targets = (BLK * tile_list[:, 0:1] + within[None, :] // BLK).reshape(-1)
    sources = (BLK * tile_list[:, 1:2] + within[None, :] % BLK).reshape(-1)
    return (targets, sources, pair_mask[targets, sources])


def compact(targets, sources, live_flags, number):
    ranking = jnp.cumsum(live_flags) - 1
    places = jnp.where(live_flags == 1, ranking, number)
    picked = (
        jnp.zeros((number,), jnp.int32)
        .at[places]
        .set(jnp.arange(live_flags.shape[0], dtype=jnp.int32), mode="drop")
    )
    return (targets[picked], sources[picked])


def along_z(values, matrix):
    number, planes, width_yz = values.shape
    size_z = matrix.shape[0]
    shaped = values.reshape(number, planes, width_yz // size_z, size_z)
    return jnp.einsum("pxrz,zk->pxrk", shaped, matrix, precision=precise).reshape(number, planes, width_yz)


def along_y(values, matrix):
    number, planes, width_yz = values.shape
    size_y = matrix.shape[0]
    shaped = values.reshape(number, planes, size_y, width_yz // size_y)
    return jnp.einsum("pxyz,yk->pxkz", shaped, matrix, precision=precise).reshape(number, planes, width_yz)


def along_x(values, matrix):
    return jnp.einsum("pxc,xk->pkc", values, matrix, precision=precise)


def any_device(orbitals, rotation, tile_list, pair_mask):
    n_grid = lax.axis_size("grid")
    number_orbitals, size_x = rotation.shape[0], orbitals.shape[1] * n_grid
    rotated = jnp.einsum(
        "ij,ixc->jxc",
        rotation,
        lax.all_to_all(orbitals, "orb", split_axis=2, concat_axis=0, tiled=True),
        precision=precise,
    )
    planes, width_yz = rotated.shape[1:]
    targets, sources, live_flags = pair_lists(tile_list, pair_mask)
    matrix_x, matrix_y, matrix_z = sine_table(size_x), sine_table(NY), sine_table(NZ)
    kernel = green_kernel(size_x, NY, NZ).reshape(size_x, NY * NZ)
    orbital_ids = jnp.arange(number_orbitals, dtype=jnp.int32)
    targets, sources = compact(targets, sources, live_flags, targets.shape[0] // 2)
    density = rotated[targets] * rotated[sources]
    number = density.shape[0]
    spectrum = along_z(density, matrix_z)
    spectrum = lax.all_to_all(spectrum, "orb", split_axis=0, concat_axis=2, tiled=True)
    spectrum = along_y(spectrum, matrix_y)
    spectrum = lax.all_to_all(spectrum, "grid", split_axis=0, concat_axis=1, tiled=True)
    spectrum = along_x(along_x(spectrum, matrix_x) * kernel, matrix_x)
    spectrum = lax.all_to_all(spectrum, "grid", split_axis=1, concat_axis=0, tiled=True)
    spectrum = along_y(spectrum, matrix_y)
    spectrum = lax.all_to_all(spectrum, "orb", split_axis=2, concat_axis=0, tiled=True)
    potential = along_z(spectrum, matrix_z)
    products = potential * rotated[sources]
    selector = (targets[None, :] == orbital_ids[:, None]).astype(f32)
    partial_value = -jnp.dot(selector, products.reshape(number, planes * width_yz), precision=precise)
    partial_value = partial_value.reshape(number_orbitals, planes, width_yz)
    return lax.all_to_all(partial_value, "orb", split_axis=0, concat_axis=2, tiled=True)


def solution(mesh):
    n_orb, n_grid = mesh.shape["orb"], mesh.shape["grid"]

    def on_device(orbitals, rotation, tile_list, pair_mask):
        per_device, planes, width = orbitals.shape
        fits = n_orb == 8 and 2 * tile_list.shape[0] == n_orb and planes == SUB and per_device % BLK == 0
        fits = fits and width == NY * NZ and 2 * NZ == LANES and n_grid in (2, 4, 8)
        fits = fits and per_device * SUB == LANES and rotation.shape == (LANES, LANES)
        if not fits:
            return any_device(orbitals, rotation, tile_list, pair_mask)
        return tile_device(orbitals, rotation, tile_list, pair_mask)

    in_specs = (P("orb", "grid", None), P(), P(), P())
    out_specs = P("orb", "grid", None)
    return jax.shard_map(on_device, mesh=mesh, in_specs=in_specs, out_specs=out_specs, check_vma=False)
```

```python
import functools
import itertools

import jax
import jax.numpy as jnp
import numpy as np
from jax import lax
from jax.experimental import pallas as pl
from jax.experimental.pallas import tpu as pltpu
from jax.sharding import PartitionSpec as P


BLK = 4
NY = 64
NZ = 64
LANES = 128
SUB = 8
CHUNKS = 2
COUPLING = 0.25
SCREENING = 0.1

precise = lax.Precision.HIGHEST
f32 = jnp.float32
bf16 = jnp.bfloat16

VM = pl.BlockSpec(memory_space=pltpu.VMEM)
SM = pl.BlockSpec(memory_space=pltpu.SMEM)
ANY = pl.BlockSpec(memory_space=pl.ANY)
HBM = pl.BlockSpec(memory_space=pltpu.HBM)
DMA = pltpu.SemaphoreType.DMA


def grant(mib):
    return pltpu.CompilerParams(vmem_limit_bytes=mib << 20)


def sine_np(n):
    k = np.arange(1, n + 1, dtype=np.float64)
    return np.sqrt(2.0 / (n + 1)) * np.sin(np.pi * k[:, None] * k[None, :] / (n + 1))


def eigen_np(n):
    k = np.arange(1, n + 1, dtype=np.float64)
    return 2.0 - 2.0 * np.cos(np.pi * k / (n + 1))


def halves_np(table):
    high = np.asarray(table, np.float32).astype(jnp.bfloat16)
    low = (np.asarray(table, np.float64) - high.astype(np.float64)).astype(jnp.bfloat16)
    return jnp.asarray(high), jnp.asarray(low)


def y_order():
    rows = LANES // NZ
    return np.arange(NY).reshape(NY // rows, rows).T.reshape(-1)


def y_tables():
    sine, planes = sine_np(NY), sine_np(SUB)
    even, odd = np.kron(sine[0::2, 0::2], planes), np.kron(sine[1::2, 0::2], planes)
    return np.stack([even, odd]), np.stack([even, odd.T])


def turned(x):
    count = x.shape[0] // SUB
    return jnp.concatenate([x[(count - 1 - t) * SUB:(count - t) * SUB] for t in range(count)])


def z_table():
    half = LANES // NZ
    sine = sine_np(NZ)
    table = np.zeros((2, half, NZ, half, 2, NZ))
    for pair in range(2):
        for h in range(half):
            table[pair, h, :, h, pair, :] = sine
    return table.reshape(2 * half * NZ, half * 2 * NZ)


def line_np():
    c = eigen_np(NY)[y_order()][:, None] + eigen_np(NZ)[None, :] + SCREENING
    c = np.concatenate([c, c], axis=1)
    return c, 2.0 / (2.0 + c + np.sqrt(c * (c + 4.0)))


def host_np(chips):
    table = np.zeros((chips**chips, chips), np.int32)
    for owners in itertools.product(range(chips), repeat=chips):
        best = None
        for tiles in itertools.permutations(range(chips)):
            hops = [bin(chip ^ owners[tile]).count("1") for chip, tile in enumerate(tiles)]
            cost = (max(hops), sum(hops))
            if best is None or cost < best[0]:
                best = (cost, tiles)
        table[sum(own * chips**t for t, own in enumerate(owners))] = best[1]
    return table


def dot(a, b):
    return jnp.dot(a, b, preferred_element_type=f32)


def split(x):
    high = x.astype(bf16)
    return high, (x - high.astype(f32)).astype(bf16)


def dot3(a, b):
    return dot(a[0], b[0]) + dot(a[0], b[1]) + dot(a[1], b[0])


def my_core():
    return lax.rem(lax.axis_index("orb"), 2)


def my_place():
    o = lax.axis_index("orb")
    return o, lax.rem(o, 2), lax.div(o, 2)


def fetch_kernel(source, *rest):
    outs, (whole, sem) = rest[:-2], rest[-2:]
    step = whole.shape[0] // len(outs)
    copies = [
        pltpu.make_async_copy(source.at[pl.ds(n * step, step)], whole.at[pl.ds(n * step, step)], sem.at[n])
        for n in range(len(outs))
    ]
    for copy in copies:
        copy.start()
    for copy in copies:
        copy.wait()
    core = my_core()
    copies = []
    for n, out in enumerate(outs):
        side = 1 - core if n < CHUNKS else core
        at = side * (whole.shape[2] // 2) + n % CHUNKS * out.shape[2]
        lanes = pl.ds(pl.multiple_of(at, LANES), out.shape[2])
        copies.append(pltpu.make_async_copy(whole.at[:, :, lanes], out, sem.at[n]))
    for copy in copies:
        copy.start()
    for copy in copies:
        copy.wait()


class Place:
    def __init__(self, per_device, tiles, host):
        self.o, self.core, self.chip = my_place()
        self.tiles, self.host = tiles, host
        self.chips = tiles.shape[0]
        owners = [lax.div(tiles[t, 0] * BLK, 2 * per_device) for t in range(self.chips)]
        key, same = 0, True
        for t in range(self.chips):
            key = key + owners[t] * self.chips**t
            same = same & (owners[t] == owners[0])
        self.key, self.same = key, same
        self.bit_1 = jnp.where(self.core == 0, 1, 2)
        self.bit_2 = 3 - self.bit_1

    def tile(self, chip):
        return self.host[self.key * self.chips + chip]

    def heads(self, chip):
        tile = self.tile(chip)
        return BLK * self.tiles[tile, 0], BLK * self.tiles[tile, 1]


def setup_kernel(per_device, tiles, host, rotation, after, high, low):
    core = my_core()
    at = Place(per_device, tiles, host)
    pair = BLK // 2
    heads = [at.heads(chip) for chip in (at.chip ^ 3, at.chip ^ at.bit_1, at.chip ^ at.bit_2, at.chip)]
    wanted = []
    for a, b in heads:
        wanted += [a + (1 - core) * pair] + [b + w for w in range(BLK)] + [a + core * pair]
    for u in range(1, pair):
        for a, b in heads:
            wanted += [a + (1 - core) * pair + u, a + core * pair + u]
    lane = lax.broadcasted_iota(jnp.int32, (SUB, LANES), 1)
    chosen = jnp.concatenate([jnp.where(lane == n, 1.0, 0.0) for n in wanted]).astype(bf16)
    rows = chosen.shape[0]
    row = lax.broadcasted_iota(jnp.int32, (LANES, LANES), 0)
    column = lax.broadcasted_iota(jnp.int32, (LANES, LANES), 1)
    columns = [
        jnp.where(row - (at.o ^ e) * per_device == jnp.right_shift(column, 3), 1.0, 0.0).astype(bf16)
        for e in range(2)
    ]
    keep = (lax.broadcasted_iota(jnp.int32, (rows, LANES), 0) & (SUB - 1)) == (
        lax.broadcasted_iota(jnp.int32, (rows, LANES), 1) & (SUB - 1)
    )
    for out, values in zip((high, low), split(rotation[...])):
        picked = lax.dot_general(chosen, values, (((1,), (1,)), ((), ())), preferred_element_type=f32).astype(bf16)
        for e in range(2):
            out[:, e * LANES:(e + 1) * LANES] = jnp.where(keep, dot(picked, columns[e]), 0.0).astype(bf16)


def ready_kernel(per_device, n_grid, tiles, host, mask, log_r, *rest):
    out, powers, flags, match, alone, zeros, sem = rest[-7:]
    zeros[...] = jnp.zeros(zeros.shape, f32)
    step = zeros.shape[0]
    copies = [
        pltpu.make_async_copy(zeros, out.at[pl.ds(n * step, step)], sem.at[n]) for n in range(out.shape[0] // step)
    ]
    for copy in copies:
        copy.start()
    begin, size_x = SUB * lax.axis_index("grid"), SUB * n_grid
    exponents = (
        2 * begin + SUB + 1,
        2 * size_x + 1 - SUB - 2 * begin,
        2 * size_x + 2 - 2 * begin,
        2 * begin,
        2 * begin + 2 * SUB + 2,
        2 * size_x - 2 * SUB - 2 * begin,
    )
    for n, exponent in enumerate(exponents):
        power = jnp.exp(exponent.astype(f32) * log_r[...])
        powers[n] = power if n < 2 else 1.0 - power
    at = Place(per_device, tiles, host)
    alone[0] = at.same.astype(jnp.int32)
    a, b = at.heads(at.chip)
    pair = BLK // 2
    live = mask[...].astype(f32)
    row = lax.broadcasted_iota(jnp.int32, live.shape, 0)
    column = lax.broadcasted_iota(jnp.int32, (1, live.shape[1]), 1)
    for u in range(pair):
        line = jnp.sum(jnp.where(row == a + at.core * pair + u, live, 0.0), axis=0, keepdims=True)
        for w in range(BLK):
            flags[u * BLK + w] = jnp.sum(jnp.where(column == b + w, line, 0.0))
    blocks = per_device // BLK
    parts = [0, at.bit_1, at.bit_2, 3, 0, at.bit_2, at.bit_1, 3]
    for n, flip in enumerate(parts):
        home = tiles[at.tile(at.chip ^ flip), 0]
        for block in range(blocks):
            hit = home == at.o * blocks + block
            if n % 4 == 3:
                hit = hit & at.same
            found = hit.astype(jnp.int32)
            match[block * len(parts) + n] = found
            total = blocks * len(parts) + 2 * block + n // 4
            match[total] = found if n % 4 == 0 else match[total] + found
    for copy in copies:
        copy.wait()


def join_kernel(x, y, out):
    out[0] = x[...]
    out[1] = y[...]


def rotate_kernel(first, high, low, *rest):
    send, keep = rest[-2:]
    rows = send.shape[0] * SUB
    part = pl.ds(first, 2 * rows)
    table = (high[part, :], low[part, :])
    at = 0
    step = 2 * LANES
    while at < send.shape[2]:
        width = rest[0].shape[2]
        n, inner = at // width, at % width
        lanes = slice(inner, inner + step)
        mine, theirs = rest[2 * n], rest[2 * n + 1]
        depth = mine.shape[0] * SUB
        cells = jnp.concatenate([mine[:, :, lanes].reshape(depth, step), theirs[:, :, lanes].reshape(depth, step)])
        total = dot3(table, split(cells))
        lanes = slice(at, at + step)
        send[:, :, lanes] = total[:rows].reshape(send.shape[0], SUB, step)
        keep[:, :, lanes] = total[rows:].reshape(keep.shape[0], SUB, step)
        at += step


def pass_kernel(keep, got, *rest):
    out = rest[-1]
    count = out.shape[0]
    out[...] = keep[:count] + got[:count]


def finish_kernel(keep, got, passed, *rest):
    out = rest[-1]
    count = out.shape[0]
    out[...] = keep[count:] + got[count:] + passed[...]


def sub_sums(values):
    row = lax.broadcasted_iota(jnp.int32, values[0].shape, 0)
    for s in (4, 2):
        low = (row & s) == 0
        paired = []
        for n in range(s):
            a, b = values[n], values[n + s]
            paired.append(jnp.where(low, a, pltpu.roll(b, s, 0)) + jnp.where(low, pltpu.roll(a, SUB - s, 0), b))
        values = paired
    even = (row & 1) == 0
    a, b = values
    return jnp.where(even, a, pltpu.roll(b, 1, 0)), jnp.where(even, pltpu.roll(a, SUB - 1, 0), b)


def fields(u, own, other, first_own, first_other):
    table = []
    for side, sources, targets in ((0, first_own, own), (1, first_other, other)):
        for n, ref in enumerate(sources):
            if u == 0:
                table.append((side, n, ref, targets[n], BLK + 1 if side == 0 else 0, 0))
            else:
                table.append((side, n, ref, targets[0], 1 if side == 0 else 0, n * ref.shape[2]))
    return table


def forward_kernel(u, counts, *refs):
    groups = []
    for count in counts[:-1]:
        groups.append(refs[:count])
        refs = refs[count:]
    first_own, first_other, own, other = groups[:4]
    y_hi, y_lo, z_hi, z_lo, ends, powers = refs[:6]
    messages, (spectrum, a_out, b_out, dens) = refs[-4 - counts[-1]:-4], refs[-4:]
    if u == 0:
        own, other = first_own, first_other
    core, g = my_core(), lax.axis_index("grid")
    tiles = first_own[0].shape[2] // LANES
    for side, n, source, target, slot, offset in fields(u, own, other, first_own, first_other):
        half = (core if side == 0 else 1 - core) * (len(first_own) * tiles * SUB)
        for t in range(tiles):
            lanes = pl.ds(t * LANES, LANES)
            value = target[slot, :, pl.ds(offset + t * LANES, LANES)]
            rows = pl.ds(pl.multiple_of(half + (n * tiles + t) * SUB, SUB), SUB)
            for w in range(BLK):
                dens[rows, w * LANES:(w + 1) * LANES] = value * source[1 + w, :, lanes]
    z = (z_hi[...], z_lo[...])
    half = dens.shape[0]
    for q in range(BLK // 2):
        out = dot3(split(dens[:, q * 2 * LANES:(q + 1) * 2 * LANES]), z)
        mirror = turned(out[:, LANES:])
        spectrum[:half, q * LANES:(q + 1) * LANES] = out[:, :LANES] + mirror
        spectrum[half:, q * LANES:(q + 1) * LANES] = out[:, :LANES] - mirror
    for parity in range(2):
        part = pl.ds(parity * half, half)
        spectrum[part, :] = dot3((y_hi[parity], y_lo[parity]), split(spectrum[part, :]))

    def reduce(group, carry):
        lines = pl.ds(pl.multiple_of(group * SUB, SUB), SUB)
        near, far = powers[0, lines, :], powers[1, lines, :]
        for q in range(BLK // 2):
            lanes = slice(q * LANES, (q + 1) * LANES)
            values = []
            for k in range(SUB):
                rows = pl.ds(pl.multiple_of((group * SUB + k) * SUB, SUB), SUB)
                values.append(ends[rows, :] * spectrum[rows, lanes])
            even, odd = sub_sums(values)
            rightward = (even + odd) - near * (even - odd)
            leftward = (even - odd) - far * (even + odd)
            a_out[lines, lanes] = rightward
            b_out[lines, lanes] = leftward
            for k, out in enumerate(messages, 1):
                out[lines, lanes] = jnp.where((g ^ k) > g, rightward, leftward)
        return carry

    lax.fori_loop(0, NY // SUB, reduce, 0)


def backward_kernel(u, counts, flags, *refs):
    groups = []
    for count in counts:
        groups.append(refs[:count])
        refs = refs[count:]
    own, other, received = groups
    (y_hi, y_lo, z_hi, z_lo, inverse, basis, powers, steady, spectrum, a_in, b_in) = refs[:11]
    out, work, pot = refs[-3:]
    core, g = my_core(), lax.axis_index("grid")
    tiles = own[0].shape[2] // LANES
    first, last = basis[0], basis[1]

    def ends(group, carry):
        lines = pl.ds(pl.multiple_of(group * SUB, SUB), SUB)
        scale, r, slab = steady[0, lines, :], steady[1, lines, :], steady[2, lines, :]
        decays = [None, jnp.ones((SUB, LANES), f32), slab]
        while len(decays) <= len(received):
            decays.append(decays[-1] * slab)
        for q in range(BLK // 2):
            lanes = slice(q * LANES, (q + 1) * LANES)
            from_left = from_right = jnp.zeros((SUB, LANES), f32)
            for n, ref in enumerate(received, 1):
                distance = jnp.abs((g ^ n) - g)
                factor = decays[n]
                for d in range(1, n):
                    factor = jnp.where(distance == d, decays[d], factor)
                value = factor * ref[lines, lanes]
                is_left = (g ^ n) < g
                from_left = from_left + jnp.where(is_left, value, 0.0)
                from_right = from_right + jnp.where(is_left, 0.0, value)
            before = scale * (powers[2, lines, :] * from_left
                              + r * powers[3, lines, :] * (b_in[lines, lanes] + slab * from_right))
            after = scale * (powers[4, lines, :] * from_right
                             + r * powers[5, lines, :] * (a_in[lines, lanes] + slab * from_left))
            for k in range(SUB):
                rows = pl.ds(pl.multiple_of((group * SUB + k) * SUB, SUB), SUB)
                edge = first * before[k:k + 1] + last * after[k:k + 1]
                work[rows, lanes] = inverse[rows, :] * (spectrum[rows, lanes] + edge)
        return carry

    lax.fori_loop(0, NY // SUB, ends, 0)
    z = (z_hi[...], z_lo[...])
    half = pot.shape[0]
    for parity in range(2):
        part = pl.ds(parity * half, half)
        work[part, :] = dot3((y_hi[parity], y_lo[parity]), split(work[part, :]))
    for q in range(BLK // 2):
        lanes = slice(q * LANES, (q + 1) * LANES)
        even, odd = work[:half, lanes], work[half:, lanes]
        rows = jnp.concatenate([even + odd, turned(even - odd)], axis=1)
        pot[:, q * 2 * LANES:(q + 1) * 2 * LANES] = dot3(split(rows), z)
    for side, group in ((0, own), (1, other)):
        half = (core if side == 0 else 1 - core) * (len(own) * tiles)
        for n, ref in enumerate(group):
            for t in range(tiles):
                lanes = pl.ds(t * LANES, LANES)
                at = half + n * tiles + t
                rows = pl.ds(pl.multiple_of(at * SUB, SUB), SUB)
                total = None
                for w in range(BLK):
                    term = flags[u * BLK + w] * (pot[rows, w * LANES:(w + 1) * LANES] * ref[1 + w, :, lanes])
                    total = term if total is None else total + term
                out[:, pl.ds(pl.multiple_of(at * LANES, LANES), LANES)] = -total


def place_kernel(stride, match, *refs):
    parts, (out, rows, sem) = refs[:-4], refs[-3:]
    pair = BLK // 2
    blocks = out.shape[0] // BLK
    core = my_core()
    values = []
    for part in parts:
        values += [part] if len(part.shape) == 2 else [part.at[n] for n in range(part.shape[0])]
    parts, count = values, len(values) // pair

    def hits(b, side):
        return [(match[b * stride + side * stride // 2 + n], side * count // 2 + n) for n in range(count // 2)]

    def found(b, side):
        return match[blocks * stride + 2 * b + side] > 0

    def move(b, side):
        which = core if side == 0 else 1 - core
        at = b * BLK + which * pair
        return pltpu.make_async_copy(rows.at[b, side], out.at[pl.ds(at, pair)], sem.at[b, side])

    for b in range(blocks):
        for side in range(2):

            @pl.when(found(b, side))
            def _():
                rows[b, side] = jnp.zeros(rows.shape[2:], f32)
                for hit, n in hits(b, side):

                    @pl.when(hit > 0)
                    def _():
                        for u in range(pair):
                            rows[b, side, u] += parts[u * count + n][...]

                move(b, side).start()

    for b in range(blocks):
        for side in range(2):

            @pl.when(found(b, side))
            def _():
                move(b, side).wait()


def tile_device(orbitals, rotation, tile_list, pair_mask):
    shape = per_device, planes, width = orbitals.shape
    n_orb, n_grid = lax.axis_size("orb"), lax.axis_size("grid")
    size_x = planes * n_grid
    half = width // 2
    chips = n_orb // 2
    axes = ("orb", "grid")

    def swap(x, even, odd):
        moves = []
        for a in range(n_orb):
            flip = even if a % 2 == 0 else odd
            moves += [(a * n_grid + b, (a ^ flip) * n_grid + b) for b in range(n_grid)]
        return lax.ppermute(x, axes, moves)

    def cross(x, k):
        moves = [(a * n_grid + b, a * n_grid + (b ^ k)) for a in range(n_orb) for b in range(n_grid)]
        return lax.ppermute(x, axes, moves)

    chunk = half // CHUNKS
    orbitals = pltpu.with_memory_space_constraint(orbitals, pltpu.HBM)

    part = jax.ShapeDtypeStruct((per_device, planes, chunk), f32)
    fetched = pl.pallas_call(
        fetch_kernel, out_shape=[part] * (2 * CHUNKS), in_specs=[HBM], out_specs=[VM] * (2 * CHUNKS),
        scratch_shapes=[pltpu.VMEM(shape, f32), DMA((2 * CHUNKS,))], name="fetch", compiler_params=grant(8),
    )(orbitals)
    theirs, mine = [], fetched[CHUNKS:]
    for taken in fetched[:CHUNKS]:
        theirs.append(swap(taken, 1, 1))

    pair = BLK // 2
    firsts = (BLK + 2) * chips
    rows = (firsts + 2 * (pair - 1) * chips) * SUB
    wide_table = jax.ShapeDtypeStruct((rows, 2 * LANES), bf16)
    blocks = per_device // BLK
    c, r = line_np()
    c, r = line_np()
    host = jnp.asarray(host_np(chips).reshape(-1))
    high, low = pl.pallas_call(
        functools.partial(setup_kernel, per_device), out_shape=[wide_table] * 2,
        in_specs=[SM, SM, VM, ANY], out_specs=[VM] * 2, name="setup", compiler_params=grant(8),
    )(tile_list, host, rotation, taken)

    def rotate(first, count, fields, *after):
        part = jax.ShapeDtypeStruct((count, planes, chunk * (len(fields) // 2)), f32)
        send, keep = pl.pallas_call(
            functools.partial(rotate_kernel, first * SUB), out_shape=(part, part),
            in_specs=[VM] * (2 + len(fields)) + [ANY] * len(after),
            out_specs=(VM, VM), compiler_params=grant(8),
        )(high, low, *fields, *after)
        return send, keep, swap(send, 2, 4)

    sums, last = [], ()
    for n in range(CHUNKS):
        sums.append(rotate(0, firsts // 2, [mine[n], theirs[n]], *last))
        last = (sums[-1][0],)
    both = [x for n in range(CHUNKS) for x in (mine[n], theirs[n])]
    sums.append(rotate(firsts, (pair - 1) * chips, both, *last))
    passing, own, other = [], [], []

    def pass_on(n, *after, spec=ANY):
        _, keep, got = sums[n]
        count = keep.shape[0] // 2
        value = pl.pallas_call(
            pass_kernel, out_shape=jax.ShapeDtypeStruct((count,) + keep.shape[1:], f32),
            in_specs=[VM] * 2 + [spec] * len(after), out_specs=VM, compiler_params=grant(4),
        )(keep, got, *after)
        passing.append((keep, got, swap(value, 4, 2)))
        return value

    def finish(n, *after):
        keep, got, passed = passing[n]
        own.append(pl.pallas_call(
            finish_kernel, out_shape=jax.ShapeDtypeStruct(passed.shape, f32), in_specs=[VM] * 3 + [ANY] * len(after),
            out_specs=VM, compiler_params=grant(4),
        )(keep, got, passed, *after))
        other.append(swap(own[-1], 1, 1))
        return own[-1]

    step = pass_on(0, sums[-1][0])
    empty, powers, flags, match, alone = pl.pallas_call(
        functools.partial(ready_kernel, per_device, n_grid),
        out_shape=(pltpu.HBM(shape, f32), jax.ShapeDtypeStruct((6, NY, LANES), f32),
                   jax.ShapeDtypeStruct((pair * BLK,), f32), jax.ShapeDtypeStruct((blocks * 10,), jnp.int32),
                   jax.ShapeDtypeStruct((1,), jnp.int32)),
        in_specs=[SM, SM, VM, VM, ANY], out_specs=(HBM, VM, SM, SM, SM),
        scratch_shapes=[pltpu.VMEM((pair, planes, width), f32), DMA((per_device // pair,))], name="ready",
        compiler_params=grant(4),
    )(tile_list, host, pair_mask, jnp.asarray(np.log(r), f32), step)
    step = pass_on(1, empty, spec=HBM)
    for n in range(2, CHUNKS):
        step = pass_on(n, step)
    for n in range(CHUNKS):
        step = finish(n, step)
    last = (pass_on(CHUNKS, step),)

    sine_x, eigen_x = sine_np(planes), eigen_np(planes)
    ends = jnp.asarray(np.einsum("jp,pkl->kjl", sine_x, r[None] ** np.arange(planes - 1, -1, -1)[:, None, None])
                       .reshape(-1, LANES), f32)
    inverse = jnp.asarray((COUPLING / (eigen_x[None, :, None] + c[:, None, :])).reshape(-1, LANES), f32)
    basis = jnp.asarray(np.broadcast_to(sine_x[:, [0, -1]].T[:, :, None], (2, planes, LANES)), f32)
    steady = jnp.asarray(np.stack([r / ((1 - r**2) * (1 - r ** (2 * size_x + 2))), r, r**planes]), f32)

    y_there, y_back = y_tables()
    y_hi, y_lo = halves_np(y_there)
    yt_hi, yt_lo = halves_np(y_back)
    z_hi, z_lo = halves_np(z_table())
    zt_hi, zt_lo = halves_np(z_table().T)
    solved = []
    lines = jax.ShapeDtypeStruct((NY, 2 * LANES), f32)
    cube = (NY * SUB, 2 * LANES)
    wide = pltpu.VMEM((width // LANES * SUB, BLK * LANES), f32)
    base_own, base_other = own[:CHUNKS], other[:CHUNKS]
    for u in range(pair):
        if u:
            finish(CHUNKS, *last)
        more_own, more_other = own[CHUNKS:][:u], other[CHUNKS:][:u]
        counts = (CHUNKS, CHUNKS, len(more_own), len(more_other))
        inputs = [*base_own, *base_other, *more_own, *more_other, y_hi, y_lo, z_hi, z_lo, ends, powers]
        *messages, spectrum, a, b = pl.pallas_call(
            functools.partial(forward_kernel, u, counts + (n_grid - 1,)),
            out_shape=[lines] * (n_grid - 1) + [jax.ShapeDtypeStruct(cube, f32), lines, lines],
            in_specs=[VM] * len(inputs) + [ANY] * len(last),
            out_specs=[VM] * (n_grid + 2),
            scratch_shapes=[wide],
            compiler_params=grant(16),
        )(*inputs, *last)
        last = (spectrum,)
        received = []
        for k, message in enumerate(messages, 1):
            received.append(cross(message, k))
        solved.append((spectrum, a, b, received))

    terms, last = [], ()
    for u, (spectrum, a, b, received) in enumerate(solved):
        inputs = [*base_own, *base_other, *received, yt_hi, yt_lo, zt_hi, zt_lo, inverse, basis, powers, steady,
                  spectrum, a, b]
        terms.append(pl.pallas_call(
            functools.partial(backward_kernel, u, (CHUNKS, CHUNKS, len(received))),
            out_shape=jax.ShapeDtypeStruct((planes, width), f32),
            in_specs=[SM] + [VM] * len(inputs) + [ANY] * len(last),
            out_specs=VM,
            scratch_shapes=[pltpu.VMEM(cube, f32), wide],
            compiler_params=grant(16),
        )(flags, *inputs, *last))
        last = (terms[-1],)

    near_1, near_2 = [], []
    for term in terms:
        near_1.append(swap(term, 2, 4))
        near_2.append(swap(term, 4, 2))
    own_parts = [[term, x, y] for term, x, y in zip(terms, near_1, near_2)]
    sib_parts = []
    for term, x, y in own_parts:
        joined = pl.pallas_call(
            join_kernel, out_shape=jax.ShapeDtypeStruct((2,) + term.shape, f32), in_specs=[VM] * 2, out_specs=VM,
            compiler_params=grant(4),
        )(x, y)
        given = swap(term, 1, 1)
        sib_parts.append([given, swap(joined, 1, 1)])

    def place(target, groups):
        parts = [part for group in groups for part in group]
        return pl.pallas_call(
            functools.partial(place_kernel, 8),
            out_shape=pltpu.HBM(shape, f32),
            in_specs=[SM] + [VM] * len(parts) + [HBM],
            out_specs=HBM,
            input_output_aliases={len(parts) + 1: 0},
            scratch_shapes=[pltpu.VMEM((blocks, 2, pair, planes, width), f32), DMA((blocks, 2))],
            name="place",
            compiler_params=grant(8),
        )(match, *parts, target)

    def place_near(target, mine, sibs):
        return place(target, [a + b for a, b in zip(mine, sibs)])

    def place_far(target, mine, sibs):
        far = [swap(group[1], 4, 2) for group in mine]
        return place(target, [a + [x] + b + [swap(x, 1, 1)] for a, b, x in zip(mine, sibs, far)])

    return lax.cond(alone[0] != 0, place_far, place_near, empty, own_parts, sib_parts)


def sine_table(length):
    wave_index = jnp.arange(length, dtype=f32) + 1.0
    return jnp.sqrt(2.0 / (length + 1.0)) * jnp.sin(
        jnp.pi * wave_index[:, None] * wave_index[None, :] / (length + 1.0)
    )


def eigen_values(length):
    wave_index = jnp.arange(length, dtype=f32) + 1.0
    return 2.0 - 2.0 * jnp.cos(jnp.pi * wave_index / (length + 1.0))


def green_kernel(size_x, size_y, size_z):
    summed = (
        eigen_values(size_x)[:, None, None]
        + eigen_values(size_y)[None, :, None]
        + eigen_values(size_z)[None, None, :]
    )
    return COUPLING / (summed + SCREENING)


def pair_lists(tile_list, pair_mask):
    within = jnp.arange(BLK * BLK, dtype=jnp.int32)
    targets = (BLK * tile_list[:, 0:1] + within[None, :] // BLK).reshape(-1)
    sources = (BLK * tile_list[:, 1:2] + within[None, :] % BLK).reshape(-1)
    return (targets, sources, pair_mask[targets, sources])


def compact(targets, sources, live_flags, number):
    ranking = jnp.cumsum(live_flags) - 1
    places = jnp.where(live_flags == 1, ranking, number)
    picked = (
        jnp.zeros((number,), jnp.int32)
        .at[places]
        .set(jnp.arange(live_flags.shape[0], dtype=jnp.int32), mode="drop")
    )
    return (targets[picked], sources[picked])


def along_z(values, matrix):
    number, planes, width_yz = values.shape
    size_z = matrix.shape[0]
    shaped = values.reshape(number, planes, width_yz // size_z, size_z)
    return jnp.einsum("pxrz,zk->pxrk", shaped, matrix, precision=precise).reshape(number, planes, width_yz)


def along_y(values, matrix):
    number, planes, width_yz = values.shape
    size_y = matrix.shape[0]
    shaped = values.reshape(number, planes, size_y, width_yz // size_y)
    return jnp.einsum("pxyz,yk->pxkz", shaped, matrix, precision=precise).reshape(number, planes, width_yz)


def along_x(values, matrix):
    return jnp.einsum("pxc,xk->pkc", values, matrix, precision=precise)


def any_device(orbitals, rotation, tile_list, pair_mask):
    n_grid = lax.axis_size("grid")
    number_orbitals, size_x = rotation.shape[0], orbitals.shape[1] * n_grid
    rotated = jnp.einsum(
        "ij,ixc->jxc",
        rotation,
        lax.all_to_all(orbitals, "orb", split_axis=2, concat_axis=0, tiled=True),
        precision=precise,
    )
    planes, width_yz = rotated.shape[1:]
    targets, sources, live_flags = pair_lists(tile_list, pair_mask)
    matrix_x, matrix_y, matrix_z = sine_table(size_x), sine_table(NY), sine_table(NZ)
    kernel = green_kernel(size_x, NY, NZ).reshape(size_x, NY * NZ)
    orbital_ids = jnp.arange(number_orbitals, dtype=jnp.int32)
    targets, sources = compact(targets, sources, live_flags, targets.shape[0] // 2)
    density = rotated[targets] * rotated[sources]
    number = density.shape[0]
    spectrum = along_z(density, matrix_z)
    spectrum = lax.all_to_all(spectrum, "orb", split_axis=0, concat_axis=2, tiled=True)
    spectrum = along_y(spectrum, matrix_y)
    spectrum = lax.all_to_all(spectrum, "grid", split_axis=0, concat_axis=1, tiled=True)
    spectrum = along_x(along_x(spectrum, matrix_x) * kernel, matrix_x)
    spectrum = lax.all_to_all(spectrum, "grid", split_axis=1, concat_axis=0, tiled=True)
    spectrum = along_y(spectrum, matrix_y)
    spectrum = lax.all_to_all(spectrum, "orb", split_axis=2, concat_axis=0, tiled=True)
    potential = along_z(spectrum, matrix_z)
    products = potential * rotated[sources]
    selector = (targets[None, :] == orbital_ids[:, None]).astype(f32)
    partial_value = -jnp.dot(selector, products.reshape(number, planes * width_yz), precision=precise)
    partial_value = partial_value.reshape(number_orbitals, planes, width_yz)
    return lax.all_to_all(partial_value, "orb", split_axis=0, concat_axis=2, tiled=True)


def solution(mesh):
    n_orb, n_grid = mesh.shape["orb"], mesh.shape["grid"]

    def on_device(orbitals, rotation, tile_list, pair_mask):
        per_device, planes, width = orbitals.shape
        fits = n_orb == 8 and 2 * tile_list.shape[0] == n_orb and planes == SUB and per_device % BLK == 0
        fits = fits and width == NY * NZ and 2 * NZ == LANES and n_grid in (2, 4, 8)
        fits = fits and per_device * SUB == LANES and rotation.shape == (LANES, LANES)
        if not fits:
            return any_device(orbitals, rotation, tile_list, pair_mask)
        return tile_device(orbitals, rotation, tile_list, pair_mask)

    in_specs = (P("orb", "grid", None), P(), P(), P())
    out_specs = P("orb", "grid", None)
    return jax.shard_map(on_device, mesh=mesh, in_specs=in_specs, out_specs=out_specs, check_vma=False)
```

```python
import functools
import itertools

import jax
import jax.numpy as jnp
import numpy as np
from jax import lax
from jax.experimental import pallas as pl
from jax.experimental.pallas import tpu as pltpu
from jax.sharding import PartitionSpec as P


BLK = 4
NY = 64
NZ = 64
LANES = 128
SUB = 8
CHUNKS = 2
COUPLING = 0.25
SCREENING = 0.1

precise = lax.Precision.HIGHEST
f32 = jnp.float32
bf16 = jnp.bfloat16

VM = pl.BlockSpec(memory_space=pltpu.VMEM)
SM = pl.BlockSpec(memory_space=pltpu.SMEM)
ANY = pl.BlockSpec(memory_space=pl.ANY)
HBM = pl.BlockSpec(memory_space=pltpu.HBM)
DMA = pltpu.SemaphoreType.DMA


def grant(mib):
    return pltpu.CompilerParams(vmem_limit_bytes=mib << 20)


def sine_np(n):
    k = np.arange(1, n + 1, dtype=np.float64)
    return np.sqrt(2.0 / (n + 1)) * np.sin(np.pi * k[:, None] * k[None, :] / (n + 1))


def eigen_np(n):
    k = np.arange(1, n + 1, dtype=np.float64)
    return 2.0 - 2.0 * np.cos(np.pi * k / (n + 1))


def halves_np(table):
    high = np.asarray(table, np.float32).astype(jnp.bfloat16)
    low = (np.asarray(table, np.float64) - high.astype(np.float64)).astype(jnp.bfloat16)
    return jnp.asarray(high), jnp.asarray(low)


def y_order():
    rows = LANES // NZ
    return np.arange(NY).reshape(NY // rows, rows).T.reshape(-1)


def y_tables():
    sine, planes = sine_np(NY), sine_np(SUB)
    even, odd = np.kron(sine[0::2, 0::2], planes), np.kron(sine[1::2, 0::2], planes)
    return np.stack([even, odd]), np.stack([even, odd.T])


def turned(x):
    count = x.shape[0] // SUB
    return jnp.concatenate([x[(count - 1 - t) * SUB:(count - t) * SUB] for t in range(count)])


def z_table():
    half = LANES // NZ
    sine = sine_np(NZ)
    table = np.zeros((2, half, NZ, half, 2, NZ))
    for pair in range(2):
        for h in range(half):
            table[pair, h, :, h, pair, :] = sine
    return table.reshape(2 * half * NZ, half * 2 * NZ)


def line_np():
    c = eigen_np(NY)[y_order()][:, None] + eigen_np(NZ)[None, :] + SCREENING
    c = np.concatenate([c, c], axis=1)
    return c, 2.0 / (2.0 + c + np.sqrt(c * (c + 4.0)))


def host_np(chips):
    table = np.zeros((chips**chips, chips), np.int32)
    for owners in itertools.product(range(chips), repeat=chips):
        best = None
        for tiles in itertools.permutations(range(chips)):
            hops = [bin(chip ^ owners[tile]).count("1") for chip, tile in enumerate(tiles)]
            cost = (max(hops), sum(hops))
            if best is None or cost < best[0]:
                best = (cost, tiles)
        table[sum(own * chips**t for t, own in enumerate(owners))] = best[1]
    return table


def dot(a, b):
    return jnp.dot(a, b, preferred_element_type=f32)


def split(x):
    high = x.astype(bf16)
    return high, (x - high.astype(f32)).astype(bf16)


def dot3(a, b):
    return dot(a[0], b[0]) + dot(a[0], b[1]) + dot(a[1], b[0])


def my_core():
    return lax.rem(lax.axis_index("orb"), 2)


def my_place():
    o = lax.axis_index("orb")
    return o, lax.rem(o, 2), lax.div(o, 2)


def fetch_kernel(source, *rest):
    outs, (whole, sem) = rest[:-2], rest[-2:]
    step = whole.shape[0] // len(outs)
    copies = [
        pltpu.make_async_copy(source.at[pl.ds(n * step, step)], whole.at[pl.ds(n * step, step)], sem.at[n])
        for n in range(len(outs))
    ]
    for copy in copies:
        copy.start()
    for copy in copies:
        copy.wait()
    core = my_core()
    copies = []
    for n, out in enumerate(outs):
        side = 1 - core if n < CHUNKS else core
        at = side * (whole.shape[2] // 2) + n % CHUNKS * out.shape[2]
        lanes = pl.ds(pl.multiple_of(at, LANES), out.shape[2])
        copies.append(pltpu.make_async_copy(whole.at[:, :, lanes], out, sem.at[n]))
    for copy in copies:
        copy.start()
    for copy in copies:
        copy.wait()


class Place:
    def __init__(self, per_device, tiles, host):
        self.o, self.core, self.chip = my_place()
        self.tiles, self.host = tiles, host
        self.chips = tiles.shape[0]
        owners = [lax.div(tiles[t, 0] * BLK, 2 * per_device) for t in range(self.chips)]
        key, same = 0, True
        for t in range(self.chips):
            key = key + owners[t] * self.chips**t
            same = same & (owners[t] == owners[0])
        self.key, self.same = key, same
        self.bit_1 = jnp.where(self.core == 0, 1, 2)
        self.bit_2 = 3 - self.bit_1

    def tile(self, chip):
        return self.host[self.key * self.chips + chip]

    def heads(self, chip):
        tile = self.tile(chip)
        return BLK * self.tiles[tile, 0], BLK * self.tiles[tile, 1]


def setup_kernel(per_device, tiles, host, rotation, after, high, low):
    core = my_core()
    at = Place(per_device, tiles, host)
    pair = BLK // 2
    heads = [at.heads(chip) for chip in (at.chip ^ 3, at.chip ^ at.bit_1, at.chip ^ at.bit_2, at.chip)]
    wanted = []
    for a, b in heads:
        wanted += [a + (1 - core) * pair] + [b + w for w in range(BLK)] + [a + core * pair]
    for u in range(1, pair):
        for a, b in heads:
            wanted += [a + (1 - core) * pair + u, a + core * pair + u]
    lane = lax.broadcasted_iota(jnp.int32, (SUB, LANES), 1)
    chosen = jnp.concatenate([jnp.where(lane == n, 1.0, 0.0) for n in wanted]).astype(bf16)
    rows = chosen.shape[0]
    row = lax.broadcasted_iota(jnp.int32, (LANES, LANES), 0)
    column = lax.broadcasted_iota(jnp.int32, (LANES, LANES), 1)
    columns = [
        jnp.where(row - (at.o ^ e) * per_device == jnp.right_shift(column, 3), 1.0, 0.0).astype(bf16)
        for e in range(2)
    ]
    keep = (lax.broadcasted_iota(jnp.int32, (rows, LANES), 0) & (SUB - 1)) == (
        lax.broadcasted_iota(jnp.int32, (rows, LANES), 1) & (SUB - 1)
    )
    for out, values in zip((high, low), split(rotation[...])):
        picked = lax.dot_general(chosen, values, (((1,), (1,)), ((), ())), preferred_element_type=f32).astype(bf16)
        for e in range(2):
            out[:, e * LANES:(e + 1) * LANES] = jnp.where(keep, dot(picked, columns[e]), 0.0).astype(bf16)


def ready_kernel(per_device, n_grid, tiles, host, mask, log_r, *rest):
    out, powers, flags, match, alone, zeros, sem = rest[-7:]
    zeros[...] = jnp.zeros(zeros.shape, f32)
    step = zeros.shape[0]
    copies = [
        pltpu.make_async_copy(zeros, out.at[pl.ds(n * step, step)], sem.at[n]) for n in range(out.shape[0] // step)
    ]
    for copy in copies:
        copy.start()
    begin, size_x = SUB * lax.axis_index("grid"), SUB * n_grid
    exponents = (
        2 * begin + SUB + 1,
        2 * size_x + 1 - SUB - 2 * begin,
        2 * size_x + 2 - 2 * begin,
        2 * begin,
        2 * begin + 2 * SUB + 2,
        2 * size_x - 2 * SUB - 2 * begin,
    )
    for n, exponent in enumerate(exponents):
        power = jnp.exp(exponent.astype(f32) * log_r[...])
        powers[n] = power if n < 2 else 1.0 - power
    at = Place(per_device, tiles, host)
    alone[0] = at.same.astype(jnp.int32)
    a, b = at.heads(at.chip)
    pair = BLK // 2
    live = mask[...].astype(f32)
    row = lax.broadcasted_iota(jnp.int32, live.shape, 0)
    column = lax.broadcasted_iota(jnp.int32, (1, live.shape[1]), 1)
    for u in range(pair):
        line = jnp.sum(jnp.where(row == a + at.core * pair + u, live, 0.0), axis=0, keepdims=True)
        for w in range(BLK):
            flag = jnp.sum(jnp.where(column == b + w, line, 0.0), axis=1, keepdims=True)
            flags[u * BLK + w:u * BLK + w + 1, :] = jnp.broadcast_to(flag, (1, LANES))
    blocks = per_device // BLK
    parts = [0, at.bit_1, at.bit_2, 3, 0, at.bit_2, at.bit_1, 3]
    for n, flip in enumerate(parts):
        home = tiles[at.tile(at.chip ^ flip), 0]
        for block in range(blocks):
            hit = home == at.o * blocks + block
            if n % 4 == 3:
                hit = hit & at.same
            found = hit.astype(jnp.int32)
            match[block * len(parts) + n] = found
            total = blocks * len(parts) + 2 * block + n // 4
            match[total] = found if n % 4 == 0 else match[total] + found
    for copy in copies:
        copy.wait()


def join_kernel(x, y, out):
    out[0] = x[...]
    out[1] = y[...]


def rotate_kernel(first, high, low, *rest):
    send, keep = rest[-2:]
    rows = send.shape[0] * SUB
    part = pl.ds(first, 2 * rows)
    table = (high[part, :], low[part, :])
    at = 0
    step = 2 * LANES
    while at < send.shape[2]:
        width = rest[0].shape[2]
        n, inner = at // width, at % width
        lanes = slice(inner, inner + step)
        mine, theirs = rest[2 * n], rest[2 * n + 1]
        depth = mine.shape[0] * SUB
        cells = jnp.concatenate([mine[:, :, lanes].reshape(depth, step), theirs[:, :, lanes].reshape(depth, step)])
        total = dot3(table, split(cells))
        lanes = slice(at, at + step)
        send[:, :, lanes] = total[:rows].reshape(send.shape[0], SUB, step)
        keep[:, :, lanes] = total[rows:].reshape(keep.shape[0], SUB, step)
        at += step


def pass_kernel(keep, got, *rest):
    out = rest[-1]
    count = out.shape[0]
    out[...] = keep[:count] + got[:count]


def finish_kernel(keep, got, passed, *rest):
    out = rest[-1]
    count = out.shape[0]
    out[...] = keep[count:] + got[count:] + passed[...]


def sub_sums(values):
    row = lax.broadcasted_iota(jnp.int32, values[0].shape, 0)
    for s in (4, 2):
        low = (row & s) == 0
        paired = []
        for n in range(s):
            a, b = values[n], values[n + s]
            paired.append(jnp.where(low, a, pltpu.roll(b, s, 0)) + jnp.where(low, pltpu.roll(a, SUB - s, 0), b))
        values = paired
    even = (row & 1) == 0
    a, b = values
    return jnp.where(even, a, pltpu.roll(b, 1, 0)), jnp.where(even, pltpu.roll(a, SUB - 1, 0), b)


def fields(u, own, other, first_own, first_other):
    table = []
    for side, sources, targets in ((0, first_own, own), (1, first_other, other)):
        for n, ref in enumerate(sources):
            if u == 0:
                table.append((side, n, ref, targets[n], BLK + 1 if side == 0 else 0, 0))
            else:
                table.append((side, n, ref, targets[0], 1 if side == 0 else 0, n * ref.shape[2]))
    return table


def forward_kernel(u, counts, *refs):
    groups = []
    for count in counts[:-1]:
        groups.append(refs[:count])
        refs = refs[count:]
    first_own, first_other, own, other = groups[:4]
    y_hi, y_lo, z_hi, z_lo, ends, powers = refs[:6]
    messages, (spectrum, a_out, b_out, dens) = refs[-4 - counts[-1]:-4], refs[-4:]
    if u == 0:
        own, other = first_own, first_other
    core, g = my_core(), lax.axis_index("grid")
    tiles = first_own[0].shape[2] // LANES
    for side, n, source, target, slot, offset in fields(u, own, other, first_own, first_other):
        half = (core if side == 0 else 1 - core) * (len(first_own) * tiles * SUB)
        for t in range(tiles):
            lanes = pl.ds(t * LANES, LANES)
            value = target[slot, :, pl.ds(offset + t * LANES, LANES)]
            rows = pl.ds(pl.multiple_of(half + (n * tiles + t) * SUB, SUB), SUB)
            for w in range(BLK):
                dens[rows, w * LANES:(w + 1) * LANES] = value * source[1 + w, :, lanes]
    z = (z_hi[...], z_lo[...])
    half = dens.shape[0]
    for q in range(BLK // 2):
        out = dot3(split(dens[:, q * 2 * LANES:(q + 1) * 2 * LANES]), z)
        mirror = turned(out[:, LANES:])
        spectrum[:half, q * LANES:(q + 1) * LANES] = out[:, :LANES] + mirror
        spectrum[half:, q * LANES:(q + 1) * LANES] = out[:, :LANES] - mirror
    for parity in range(2):
        part = pl.ds(parity * half, half)
        spectrum[part, :] = dot3((y_hi[parity], y_lo[parity]), split(spectrum[part, :]))

    def reduce(group, carry):
        lines = pl.ds(pl.multiple_of(group * SUB, SUB), SUB)
        near, far = powers[0, lines, :], powers[1, lines, :]
        for q in range(BLK // 2):
            lanes = slice(q * LANES, (q + 1) * LANES)
            values = []
            for k in range(SUB):
                rows = pl.ds(pl.multiple_of((group * SUB + k) * SUB, SUB), SUB)
                values.append(ends[rows, :] * spectrum[rows, lanes])
            even, odd = sub_sums(values)
            rightward = (even + odd) - near * (even - odd)
            leftward = (even - odd) - far * (even + odd)
            a_out[lines, lanes] = rightward
            b_out[lines, lanes] = leftward
            for k, out in enumerate(messages, 1):
                out[lines, lanes] = jnp.where((g ^ k) > g, rightward, leftward)
        return carry

    lax.fori_loop(0, NY // SUB, reduce, 0)


def backward_kernel(u, counts, flags, *refs):
    groups = []
    for count in counts:
        groups.append(refs[:count])
        refs = refs[count:]
    own, other, received = groups
    (y_hi, y_lo, z_hi, z_lo, inverse, basis, powers, steady, spectrum, a_in, b_in) = refs[:11]
    out, work, pot = refs[-3:]
    core, g = my_core(), lax.axis_index("grid")
    tiles = own[0].shape[2] // LANES
    first, last = basis[0], basis[1]

    def ends(group, carry):
        lines = pl.ds(pl.multiple_of(group * SUB, SUB), SUB)
        scale, r, slab = steady[0, lines, :], steady[1, lines, :], steady[2, lines, :]
        decays = [None, jnp.ones((SUB, LANES), f32), slab]
        while len(decays) <= len(received):
            decays.append(decays[-1] * slab)
        for q in range(BLK // 2):
            lanes = slice(q * LANES, (q + 1) * LANES)
            from_left = from_right = jnp.zeros((SUB, LANES), f32)
            for n, ref in enumerate(received, 1):
                distance = jnp.abs((g ^ n) - g)
                factor = decays[n]
                for d in range(1, n):
                    factor = jnp.where(distance == d, decays[d], factor)
                value = factor * ref[lines, lanes]
                is_left = (g ^ n) < g
                from_left = from_left + jnp.where(is_left, value, 0.0)
                from_right = from_right + jnp.where(is_left, 0.0, value)
            before = scale * (powers[2, lines, :] * from_left
                              + r * powers[3, lines, :] * (b_in[lines, lanes] + slab * from_right))
            after = scale * (powers[4, lines, :] * from_right
                             + r * powers[5, lines, :] * (a_in[lines, lanes] + slab * from_left))
            for k in range(SUB):
                rows = pl.ds(pl.multiple_of((group * SUB + k) * SUB, SUB), SUB)
                edge = first * before[k:k + 1] + last * after[k:k + 1]
                work[rows, lanes] = inverse[rows, :] * (spectrum[rows, lanes] + edge)
        return carry

    lax.fori_loop(0, NY // SUB, ends, 0)
    z = (z_hi[...], z_lo[...])
    half = pot.shape[0]
    for parity in range(2):
        part = pl.ds(parity * half, half)
        work[part, :] = dot3((y_hi[parity], y_lo[parity]), split(work[part, :]))
    for q in range(BLK // 2):
        lanes = slice(q * LANES, (q + 1) * LANES)
        even, odd = work[:half, lanes], work[half:, lanes]
        rows = jnp.concatenate([even + odd, turned(even - odd)], axis=1)
        pot[:, q * 2 * LANES:(q + 1) * 2 * LANES] = dot3(split(rows), z)
    live = [jnp.broadcast_to(flags[u * BLK + w:u * BLK + w + 1, :], (SUB, LANES)) for w in range(BLK)]
    for side, group in ((0, own), (1, other)):
        half = (core if side == 0 else 1 - core) * (len(own) * tiles)
        for n, ref in enumerate(group):
            for t in range(tiles):
                lanes = pl.ds(t * LANES, LANES)
                at = half + n * tiles + t
                rows = pl.ds(pl.multiple_of(at * SUB, SUB), SUB)
                total = None
                for w in range(BLK):
                    term = live[w] * (pot[rows, w * LANES:(w + 1) * LANES] * ref[1 + w, :, lanes])
                    total = term if total is None else total + term
                out[:, pl.ds(pl.multiple_of(at * LANES, LANES), LANES)] = -total


def place_kernel(stride, match, *refs):
    parts, (out, rows, sem) = refs[:-4], refs[-3:]
    pair = BLK // 2
    blocks = out.shape[0] // BLK
    core = my_core()
    values = []
    for part in parts:
        values += [part] if len(part.shape) == 2 else [part.at[n] for n in range(part.shape[0])]
    parts, count = values, len(values) // pair

    def hits(b, side):
        return [(match[b * stride + side * stride // 2 + n], side * count // 2 + n) for n in range(count // 2)]

    def found(b, side):
        return match[blocks * stride + 2 * b + side] > 0

    def move(b, side):
        which = core if side == 0 else 1 - core
        at = b * BLK + which * pair
        return pltpu.make_async_copy(rows.at[b, side], out.at[pl.ds(at, pair)], sem.at[b, side])

    for b in range(blocks):
        for side in range(2):

            @pl.when(found(b, side))
            def _():
                rows[b, side] = jnp.zeros(rows.shape[2:], f32)
                for hit, n in hits(b, side):

                    @pl.when(hit > 0)
                    def _():
                        for u in range(pair):
                            rows[b, side, u] += parts[u * count + n][...]

                move(b, side).start()

    for b in range(blocks):
        for side in range(2):

            @pl.when(found(b, side))
            def _():
                move(b, side).wait()


def tile_device(orbitals, rotation, tile_list, pair_mask):
    shape = per_device, planes, width = orbitals.shape
    n_orb, n_grid = lax.axis_size("orb"), lax.axis_size("grid")
    size_x = planes * n_grid
    half = width // 2
    chips = n_orb // 2
    axes = ("orb", "grid")

    def swap(x, even, odd):
        moves = []
        for a in range(n_orb):
            flip = even if a % 2 == 0 else odd
            moves += [(a * n_grid + b, (a ^ flip) * n_grid + b) for b in range(n_grid)]
        return lax.ppermute(x, axes, moves)

    def cross(x, k):
        moves = [(a * n_grid + b, a * n_grid + (b ^ k)) for a in range(n_orb) for b in range(n_grid)]
        return lax.ppermute(x, axes, moves)

    chunk = half // CHUNKS
    orbitals = pltpu.with_memory_space_constraint(orbitals, pltpu.HBM)

    part = jax.ShapeDtypeStruct((per_device, planes, chunk), f32)
    fetched = pl.pallas_call(
        fetch_kernel, out_shape=[part] * (2 * CHUNKS), in_specs=[HBM], out_specs=[VM] * (2 * CHUNKS),
        scratch_shapes=[pltpu.VMEM(shape, f32), DMA((2 * CHUNKS,))], name="fetch", compiler_params=grant(8),
    )(orbitals)
    theirs, mine = [], fetched[CHUNKS:]
    for taken in fetched[:CHUNKS]:
        theirs.append(swap(taken, 1, 1))

    pair = BLK // 2
    firsts = (BLK + 2) * chips
    rows = (firsts + 2 * (pair - 1) * chips) * SUB
    wide_table = jax.ShapeDtypeStruct((rows, 2 * LANES), bf16)
    blocks = per_device // BLK
    c, r = line_np()
    c, r = line_np()
    host = jnp.asarray(host_np(chips).reshape(-1))
    high, low = pl.pallas_call(
        functools.partial(setup_kernel, per_device), out_shape=[wide_table] * 2,
        in_specs=[SM, SM, VM, ANY], out_specs=[VM] * 2, name="setup", compiler_params=grant(8),
    )(tile_list, host, rotation, taken)

    def rotate(first, count, fields, *after):
        part = jax.ShapeDtypeStruct((count, planes, chunk * (len(fields) // 2)), f32)
        send, keep = pl.pallas_call(
            functools.partial(rotate_kernel, first * SUB), out_shape=(part, part),
            in_specs=[VM] * (2 + len(fields)) + [ANY] * len(after),
            out_specs=(VM, VM), compiler_params=grant(8),
        )(high, low, *fields, *after)
        return send, keep, swap(send, 2, 4)

    sums, last = [], ()
    for n in range(CHUNKS):
        sums.append(rotate(0, firsts // 2, [mine[n], theirs[n]], *last))
        last = (sums[-1][0],)
    both = [x for n in range(CHUNKS) for x in (mine[n], theirs[n])]
    sums.append(rotate(firsts, (pair - 1) * chips, both, *last))
    passing, own, other = [], [], []

    def pass_on(n, *after, spec=ANY):
        _, keep, got = sums[n]
        count = keep.shape[0] // 2
        value = pl.pallas_call(
            pass_kernel, out_shape=jax.ShapeDtypeStruct((count,) + keep.shape[1:], f32),
            in_specs=[VM] * 2 + [spec] * len(after), out_specs=VM, compiler_params=grant(4),
        )(keep, got, *after)
        passing.append((keep, got, swap(value, 4, 2)))
        return value

    def finish(n, *after):
        keep, got, passed = passing[n]
        own.append(pl.pallas_call(
            finish_kernel, out_shape=jax.ShapeDtypeStruct(passed.shape, f32), in_specs=[VM] * 3 + [ANY] * len(after),
            out_specs=VM, compiler_params=grant(4),
        )(keep, got, passed, *after))
        other.append(swap(own[-1], 1, 1))
        return own[-1]

    step = pass_on(0, sums[-1][0])
    empty, powers, flags, match, alone = pl.pallas_call(
        functools.partial(ready_kernel, per_device, n_grid),
        out_shape=(pltpu.HBM(shape, f32), jax.ShapeDtypeStruct((6, NY, LANES), f32),
                   jax.ShapeDtypeStruct((pair * BLK, LANES), f32), jax.ShapeDtypeStruct((blocks * 10,), jnp.int32),
                   jax.ShapeDtypeStruct((1,), jnp.int32)),
        in_specs=[SM, SM, VM, VM, ANY], out_specs=(HBM, VM, VM, SM, SM),
        scratch_shapes=[pltpu.VMEM((pair, planes, width), f32), DMA((per_device // pair,))], name="ready",
        compiler_params=grant(4),
    )(tile_list, host, pair_mask, jnp.asarray(np.log(r), f32), step)
    step = pass_on(1, empty, spec=HBM)
    for n in range(2, CHUNKS):
        step = pass_on(n, step)
    for n in range(CHUNKS):
        step = finish(n, step)
    last = (pass_on(CHUNKS, step),)

    sine_x, eigen_x = sine_np(planes), eigen_np(planes)
    ends = jnp.asarray(np.einsum("jp,pkl->kjl", sine_x, r[None] ** np.arange(planes - 1, -1, -1)[:, None, None])
                       .reshape(-1, LANES), f32)
    inverse = jnp.asarray((COUPLING / (eigen_x[None, :, None] + c[:, None, :])).reshape(-1, LANES), f32)
    basis = jnp.asarray(np.broadcast_to(sine_x[:, [0, -1]].T[:, :, None], (2, planes, LANES)), f32)
    steady = jnp.asarray(np.stack([r / ((1 - r**2) * (1 - r ** (2 * size_x + 2))), r, r**planes]), f32)

    y_there, y_back = y_tables()
    y_hi, y_lo = halves_np(y_there)
    yt_hi, yt_lo = halves_np(y_back)
    z_hi, z_lo = halves_np(z_table())
    zt_hi, zt_lo = halves_np(z_table().T)
    solved = []
    lines = jax.ShapeDtypeStruct((NY, 2 * LANES), f32)
    cube = (NY * SUB, 2 * LANES)
    wide = pltpu.VMEM((width // LANES * SUB, BLK * LANES), f32)
    base_own, base_other = own[:CHUNKS], other[:CHUNKS]
    for u in range(pair):
        if u:
            finish(CHUNKS, *last)
        more_own, more_other = own[CHUNKS:][:u], other[CHUNKS:][:u]
        counts = (CHUNKS, CHUNKS, len(more_own), len(more_other))
        inputs = [*base_own, *base_other, *more_own, *more_other, y_hi, y_lo, z_hi, z_lo, ends, powers]
        *messages, spectrum, a, b = pl.pallas_call(
            functools.partial(forward_kernel, u, counts + (n_grid - 1,)),
            out_shape=[lines] * (n_grid - 1) + [jax.ShapeDtypeStruct(cube, f32), lines, lines],
            in_specs=[VM] * len(inputs) + [ANY] * len(last),
            out_specs=[VM] * (n_grid + 2),
            scratch_shapes=[wide],
            compiler_params=grant(16),
        )(*inputs, *last)
        last = (spectrum,)
        received = []
        for k, message in enumerate(messages, 1):
            received.append(cross(message, k))
        solved.append((spectrum, a, b, received))

    terms, last = [], ()
    for u, (spectrum, a, b, received) in enumerate(solved):
        inputs = [*base_own, *base_other, *received, yt_hi, yt_lo, zt_hi, zt_lo, inverse, basis, powers, steady,
                  spectrum, a, b]
        terms.append(pl.pallas_call(
            functools.partial(backward_kernel, u, (CHUNKS, CHUNKS, len(received))),
            out_shape=jax.ShapeDtypeStruct((planes, width), f32),
            in_specs=[VM] * (1 + len(inputs)) + [ANY] * len(last),
            out_specs=VM,
            scratch_shapes=[pltpu.VMEM(cube, f32), wide],
            compiler_params=grant(16),
        )(flags, *inputs, *last))
        last = (terms[-1],)

    near_1 = [swap(term, 2, 4) for term in terms]
    near_2 = [swap(term, 4, 2) for term in terms]
    own_parts = [[term, x, y] for term, x, y in zip(terms, near_1, near_2)]
    sib_parts = []
    for term, x, y in own_parts:
        joined = pl.pallas_call(
            join_kernel, out_shape=jax.ShapeDtypeStruct((2,) + term.shape, f32), in_specs=[VM] * 2, out_specs=VM,
            compiler_params=grant(4),
        )(x, y)
        given = swap(term, 1, 1)
        sib_parts.append([given, swap(joined, 1, 1)])

    def place(target, groups):
        parts = [part for group in groups for part in group]
        return pl.pallas_call(
            functools.partial(place_kernel, 8),
            out_shape=pltpu.HBM(shape, f32),
            in_specs=[SM] + [VM] * len(parts) + [HBM],
            out_specs=HBM,
            input_output_aliases={len(parts) + 1: 0},
            scratch_shapes=[pltpu.VMEM((blocks, 2, pair, planes, width), f32), DMA((blocks, 2))],
            name="place",
            compiler_params=grant(8),
        )(match, *parts, target)

    def place_near(target, mine, sibs):
        return place(target, [a + b for a, b in zip(mine, sibs)])

    def place_far(target, mine, sibs):
        far = [swap(group[1], 4, 2) for group in mine]
        return place(target, [a + [x] + b + [swap(x, 1, 1)] for a, b, x in zip(mine, sibs, far)])

    return lax.cond(alone[0] != 0, place_far, place_near, empty, own_parts, sib_parts)


def sine_table(length):
    wave_index = jnp.arange(length, dtype=f32) + 1.0
    return jnp.sqrt(2.0 / (length + 1.0)) * jnp.sin(
        jnp.pi * wave_index[:, None] * wave_index[None, :] / (length + 1.0)
    )


def eigen_values(length):
    wave_index = jnp.arange(length, dtype=f32) + 1.0
    return 2.0 - 2.0 * jnp.cos(jnp.pi * wave_index / (length + 1.0))


def green_kernel(size_x, size_y, size_z):
    summed = (
        eigen_values(size_x)[:, None, None]
        + eigen_values(size_y)[None, :, None]
        + eigen_values(size_z)[None, None, :]
    )
    return COUPLING / (summed + SCREENING)


def pair_lists(tile_list, pair_mask):
    within = jnp.arange(BLK * BLK, dtype=jnp.int32)
    targets = (BLK * tile_list[:, 0:1] + within[None, :] // BLK).reshape(-1)
    sources = (BLK * tile_list[:, 1:2] + within[None, :] % BLK).reshape(-1)
    return (targets, sources, pair_mask[targets, sources])


def compact(targets, sources, live_flags, number):
    ranking = jnp.cumsum(live_flags) - 1
    places = jnp.where(live_flags == 1, ranking, number)
    picked = (
        jnp.zeros((number,), jnp.int32)
        .at[places]
        .set(jnp.arange(live_flags.shape[0], dtype=jnp.int32), mode="drop")
    )
    return (targets[picked], sources[picked])


def along_z(values, matrix):
    number, planes, width_yz = values.shape
    size_z = matrix.shape[0]
    shaped = values.reshape(number, planes, width_yz // size_z, size_z)
    return jnp.einsum("pxrz,zk->pxrk", shaped, matrix, precision=precise).reshape(number, planes, width_yz)


def along_y(values, matrix):
    number, planes, width_yz = values.shape
    size_y = matrix.shape[0]
    shaped = values.reshape(number, planes, size_y, width_yz // size_y)
    return jnp.einsum("pxyz,yk->pxkz", shaped, matrix, precision=precise).reshape(number, planes, width_yz)


def along_x(values, matrix):
    return jnp.einsum("pxc,xk->pkc", values, matrix, precision=precise)


def any_device(orbitals, rotation, tile_list, pair_mask):
    n_grid = lax.axis_size("grid")
    number_orbitals, size_x = rotation.shape[0], orbitals.shape[1] * n_grid
    rotated = jnp.einsum(
        "ij,ixc->jxc",
        rotation,
        lax.all_to_all(orbitals, "orb", split_axis=2, concat_axis=0, tiled=True),
        precision=precise,
    )
    planes, width_yz = rotated.shape[1:]
    targets, sources, live_flags = pair_lists(tile_list, pair_mask)
    matrix_x, matrix_y, matrix_z = sine_table(size_x), sine_table(NY), sine_table(NZ)
    kernel = green_kernel(size_x, NY, NZ).reshape(size_x, NY * NZ)
    orbital_ids = jnp.arange(number_orbitals, dtype=jnp.int32)
    targets, sources = compact(targets, sources, live_flags, targets.shape[0] // 2)
    density = rotated[targets] * rotated[sources]
    number = density.shape[0]
    spectrum = along_z(density, matrix_z)
    spectrum = lax.all_to_all(spectrum, "orb", split_axis=0, concat_axis=2, tiled=True)
    spectrum = along_y(spectrum, matrix_y)
    spectrum = lax.all_to_all(spectrum, "grid", split_axis=0, concat_axis=1, tiled=True)
    spectrum = along_x(along_x(spectrum, matrix_x) * kernel, matrix_x)
    spectrum = lax.all_to_all(spectrum, "grid", split_axis=1, concat_axis=0, tiled=True)
    spectrum = along_y(spectrum, matrix_y)
    spectrum = lax.all_to_all(spectrum, "orb", split_axis=2, concat_axis=0, tiled=True)
    potential = along_z(spectrum, matrix_z)
    products = potential * rotated[sources]
    selector = (targets[None, :] == orbital_ids[:, None]).astype(f32)
    partial_value = -jnp.dot(selector, products.reshape(number, planes * width_yz), precision=precise)
    partial_value = partial_value.reshape(number_orbitals, planes, width_yz)
    return lax.all_to_all(partial_value, "orb", split_axis=0, concat_axis=2, tiled=True)


def solution(mesh):
    n_orb, n_grid = mesh.shape["orb"], mesh.shape["grid"]

    def on_device(orbitals, rotation, tile_list, pair_mask):
        per_device, planes, width = orbitals.shape
        fits = n_orb == 8 and 2 * tile_list.shape[0] == n_orb and planes == SUB and per_device % BLK == 0
        fits = fits and width == NY * NZ and 2 * NZ == LANES and n_grid in (2, 4, 8)
        fits = fits and per_device * SUB == LANES and rotation.shape == (LANES, LANES)
        if not fits:
            return any_device(orbitals, rotation, tile_list, pair_mask)
        return tile_device(orbitals, rotation, tile_list, pair_mask)

    in_specs = (P("orb", "grid", None), P(), P(), P())
    out_specs = P("orb", "grid", None)
    return jax.shard_map(on_device, mesh=mesh, in_specs=in_specs, out_specs=out_specs, check_vma=False)
```

```python
import functools
import itertools

import jax
import jax.numpy as jnp
import numpy as np
from jax import lax
from jax.experimental import pallas as pl
from jax.experimental.pallas import tpu as pltpu
from jax.sharding import PartitionSpec as P


BLK = 4
NY = 64
NZ = 64
LANES = 128
SUB = 8
CHUNKS = 2
COUPLING = 0.25
SCREENING = 0.1

precise = lax.Precision.HIGHEST
f32 = jnp.float32
bf16 = jnp.bfloat16

VM = pl.BlockSpec(memory_space=pltpu.VMEM)
SM = pl.BlockSpec(memory_space=pltpu.SMEM)
ANY = pl.BlockSpec(memory_space=pl.ANY)
HBM = pl.BlockSpec(memory_space=pltpu.HBM)
DMA = pltpu.SemaphoreType.DMA


def grant(mib):
    return pltpu.CompilerParams(vmem_limit_bytes=mib << 20)


def sine_np(n):
    k = np.arange(1, n + 1, dtype=np.float64)
    return np.sqrt(2.0 / (n + 1)) * np.sin(np.pi * k[:, None] * k[None, :] / (n + 1))


def eigen_np(n):
    k = np.arange(1, n + 1, dtype=np.float64)
    return 2.0 - 2.0 * np.cos(np.pi * k / (n + 1))


def halves_np(table):
    high = np.asarray(table, np.float32).astype(jnp.bfloat16)
    low = (np.asarray(table, np.float64) - high.astype(np.float64)).astype(jnp.bfloat16)
    return jnp.asarray(high), jnp.asarray(low)


def y_order():
    rows = LANES // NZ
    return np.arange(NY).reshape(NY // rows, rows).T.reshape(-1)


def y_tables():
    sine, planes = sine_np(NY), sine_np(SUB)
    even, odd = np.kron(sine[0::2, 0::2], planes), np.kron(sine[1::2, 0::2], planes)
    return np.stack([even, odd]), np.stack([even, odd.T])


def turned(x):
    count = x.shape[0] // SUB
    return jnp.concatenate([x[(count - 1 - t) * SUB:(count - t) * SUB] for t in range(count)])


def z_table():
    half = LANES // NZ
    sine = sine_np(NZ)
    table = np.zeros((2, half, NZ, half, 2, NZ))
    for pair in range(2):
        for h in range(half):
            table[pair, h, :, h, pair, :] = sine
    return table.reshape(2 * half * NZ, half * 2 * NZ)


def line_np():
    c = eigen_np(NY)[y_order()][:, None] + eigen_np(NZ)[None, :] + SCREENING
    c = np.concatenate([c, c], axis=1)
    return c, 2.0 / (2.0 + c + np.sqrt(c * (c + 4.0)))


def host_np(chips):
    table = np.zeros((chips**chips, chips), np.int32)
    for owners in itertools.product(range(chips), repeat=chips):
        best = None
        for tiles in itertools.permutations(range(chips)):
            hops = [bin(chip ^ owners[tile]).count("1") for chip, tile in enumerate(tiles)]
            cost = (max(hops), sum(hops))
            if best is None or cost < best[0]:
                best = (cost, tiles)
        table[sum(own * chips**t for t, own in enumerate(owners))] = best[1]
    return table


def dot(a, b):
    return jnp.dot(a, b, preferred_element_type=f32)


def split(x):
    high = x.astype(bf16)
    return high, (x - high.astype(f32)).astype(bf16)


def dot3(a, b):
    return dot(a[0], b[0]) + dot(a[0], b[1]) + dot(a[1], b[0])


def my_core():
    return lax.rem(lax.axis_index("orb"), 2)


def my_place():
    o = lax.axis_index("orb")
    return o, lax.rem(o, 2), lax.div(o, 2)


def fetch_kernel(source, *rest):
    outs, (whole, sem) = rest[:-2], rest[-2:]
    step = whole.shape[0] // len(outs)
    copies = [
        pltpu.make_async_copy(source.at[pl.ds(n * step, step)], whole.at[pl.ds(n * step, step)], sem.at[n])
        for n in range(len(outs))
    ]
    for copy in copies:
        copy.start()
    for copy in copies:
        copy.wait()
    core = my_core()
    copies = []
    for n, out in enumerate(outs):
        side = 1 - core if n < CHUNKS else core
        at = side * (whole.shape[2] // 2) + n % CHUNKS * out.shape[2]
        lanes = pl.ds(pl.multiple_of(at, LANES), out.shape[2])
        copies.append(pltpu.make_async_copy(whole.at[:, :, lanes], out, sem.at[n]))
    for copy in copies:
        copy.start()
    for copy in copies:
        copy.wait()


class Place:
    def __init__(self, per_device, tiles, host):
        self.o, self.core, self.chip = my_place()
        self.tiles, self.host = tiles, host
        self.chips = tiles.shape[0]
        owners = [lax.div(tiles[t, 0] * BLK, 2 * per_device) for t in range(self.chips)]
        key, same = 0, True
        for t in range(self.chips):
            key = key + owners[t] * self.chips**t
            same = same & (owners[t] == owners[0])
        self.key, self.same = key, same
        self.bit_1 = jnp.where(self.core == 0, 1, 2)
        self.bit_2 = 3 - self.bit_1

    def tile(self, chip):
        return self.host[self.key * self.chips + chip]

    def heads(self, chip):
        tile = self.tile(chip)
        return BLK * self.tiles[tile, 0], BLK * self.tiles[tile, 1]


def setup_kernel(per_device, tiles, host, rotation, after, high, low):
    core = my_core()
    at = Place(per_device, tiles, host)
    pair = BLK // 2
    heads = [at.heads(chip) for chip in (at.chip ^ 3, at.chip ^ at.bit_1, at.chip ^ at.bit_2, at.chip)]
    wanted = []
    for a, b in heads:
        wanted += [a + (1 - core) * pair] + [b + w for w in range(BLK)] + [a + core * pair]
    for u in range(1, pair):
        for a, b in heads:
            wanted += [a + (1 - core) * pair + u, a + core * pair + u]
    lane = lax.broadcasted_iota(jnp.int32, (SUB, LANES), 1)
    chosen = jnp.concatenate([jnp.where(lane == n, 1.0, 0.0) for n in wanted]).astype(bf16)
    rows = chosen.shape[0]
    row = lax.broadcasted_iota(jnp.int32, (LANES, LANES), 0)
    column = lax.broadcasted_iota(jnp.int32, (LANES, LANES), 1)
    columns = [
        jnp.where(row - (at.o ^ e) * per_device == jnp.right_shift(column, 3), 1.0, 0.0).astype(bf16)
        for e in range(2)
    ]
    keep = (lax.broadcasted_iota(jnp.int32, (rows, LANES), 0) & (SUB - 1)) == (
        lax.broadcasted_iota(jnp.int32, (rows, LANES), 1) & (SUB - 1)
    )
    for out, values in zip((high, low), split(rotation[...])):
        picked = lax.dot_general(chosen, values, (((1,), (1,)), ((), ())), preferred_element_type=f32).astype(bf16)
        for e in range(2):
            out[:, e * LANES:(e + 1) * LANES] = jnp.where(keep, dot(picked, columns[e]), 0.0).astype(bf16)


def ready_kernel(per_device, n_grid, tiles, host, mask, log_r, *rest):
    out, powers, flags, match, alone, zeros, sem = rest[-7:]
    zeros[...] = jnp.zeros(zeros.shape, f32)
    step = zeros.shape[0]
    copies = [
        pltpu.make_async_copy(zeros, out.at[pl.ds(n * step, step)], sem.at[n]) for n in range(out.shape[0] // step)
    ]
    for copy in copies:
        copy.start()
    begin, size_x = SUB * lax.axis_index("grid"), SUB * n_grid
    exponents = (
        2 * begin + SUB + 1,
        2 * size_x + 1 - SUB - 2 * begin,
        2 * size_x + 2 - 2 * begin,
        2 * begin,
        2 * begin + 2 * SUB + 2,
        2 * size_x - 2 * SUB - 2 * begin,
    )
    for n, exponent in enumerate(exponents):
        power = jnp.exp(exponent.astype(f32) * log_r[...])
        powers[n] = power if n < 2 else 1.0 - power
    at = Place(per_device, tiles, host)
    alone[0] = at.same.astype(jnp.int32)
    a, b = at.heads(at.chip)
    pair = BLK // 2
    live = mask[...].astype(f32)
    row = lax.broadcasted_iota(jnp.int32, live.shape, 0)
    column = lax.broadcasted_iota(jnp.int32, (1, live.shape[1]), 1)
    for u in range(pair):
        line = jnp.sum(jnp.where(row == a + at.core * pair + u, live, 0.0), axis=0, keepdims=True)
        for w in range(BLK):
            flag = jnp.sum(jnp.where(column == b + w, line, 0.0), axis=1, keepdims=True)
            flags[u * BLK + w:u * BLK + w + 1, :] = jnp.broadcast_to(flag, (1, LANES))
    blocks = per_device // BLK
    flips = ((0, at.bit_1, at.bit_2), (0, at.bit_2, at.bit_1))
    near, far = 0, 0
    for side in range(2):
        homes = [tiles[at.tile(at.chip ^ flip), 0] for flip in flips[side] + (3,)]
        for block in range(blocks):
            bits = [(home == at.o * blocks + block).astype(jnp.int32) for home in homes]
            for n in range(3):
                near = near + bits[n] * (1 << ((2 * block + side) * 3 + n))
            far = far + bits[3] * (1 << (2 * block + side))
    match[0:1, :] = jnp.full((1, LANES), near.astype(f32))
    match[1:2, :] = jnp.full((1, LANES), far.astype(f32))
    for copy in copies:
        copy.wait()


def join_kernel(x, y, out):
    out[0] = x[...]
    out[1] = y[...]


def rotate_kernel(first, high, low, *rest):
    send, keep = rest[-2:]
    rows = send.shape[0] * SUB
    part = pl.ds(first, 2 * rows)
    table = (high[part, :], low[part, :])
    at = 0
    step = 2 * LANES
    while at < send.shape[2]:
        width = rest[0].shape[2]
        n, inner = at // width, at % width
        lanes = slice(inner, inner + step)
        mine, theirs = rest[2 * n], rest[2 * n + 1]
        depth = mine.shape[0] * SUB
        cells = jnp.concatenate([mine[:, :, lanes].reshape(depth, step), theirs[:, :, lanes].reshape(depth, step)])
        total = dot3(table, split(cells))
        lanes = slice(at, at + step)
        send[:, :, lanes] = total[:rows].reshape(send.shape[0], SUB, step)
        keep[:, :, lanes] = total[rows:].reshape(keep.shape[0], SUB, step)
        at += step


def pass_kernel(keep, got, *rest):
    out = rest[-1]
    count = out.shape[0]
    out[...] = keep[:count] + got[:count]


def finish_kernel(keep, got, passed, *rest):
    out = rest[-1]
    count = out.shape[0]
    out[...] = keep[count:] + got[count:] + passed[...]


def sub_sums(values):
    row = lax.broadcasted_iota(jnp.int32, values[0].shape, 0)
    for s in (4, 2):
        low = (row & s) == 0
        paired = []
        for n in range(s):
            a, b = values[n], values[n + s]
            paired.append(jnp.where(low, a, pltpu.roll(b, s, 0)) + jnp.where(low, pltpu.roll(a, SUB - s, 0), b))
        values = paired
    even = (row & 1) == 0
    a, b = values
    return jnp.where(even, a, pltpu.roll(b, 1, 0)), jnp.where(even, pltpu.roll(a, SUB - 1, 0), b)


def fields(u, own, other, first_own, first_other):
    table = []
    for side, sources, targets in ((0, first_own, own), (1, first_other, other)):
        for n, ref in enumerate(sources):
            if u == 0:
                table.append((side, n, ref, targets[n], BLK + 1 if side == 0 else 0, 0))
            else:
                table.append((side, n, ref, targets[0], 1 if side == 0 else 0, n * ref.shape[2]))
    return table


def forward_kernel(u, counts, *refs):
    groups = []
    for count in counts[:-1]:
        groups.append(refs[:count])
        refs = refs[count:]
    first_own, first_other, own, other = groups[:4]
    y_hi, y_lo, z_hi, z_lo, ends, powers = refs[:6]
    messages, (spectrum, a_out, b_out, dens) = refs[-4 - counts[-1]:-4], refs[-4:]
    if u == 0:
        own, other = first_own, first_other
    core, g = my_core(), lax.axis_index("grid")
    tiles = first_own[0].shape[2] // LANES
    for side, n, source, target, slot, offset in fields(u, own, other, first_own, first_other):
        half = (core if side == 0 else 1 - core) * (len(first_own) * tiles * SUB)
        for t in range(tiles):
            lanes = pl.ds(t * LANES, LANES)
            value = target[slot, :, pl.ds(offset + t * LANES, LANES)]
            rows = pl.ds(pl.multiple_of(half + (n * tiles + t) * SUB, SUB), SUB)
            for w in range(BLK):
                dens[rows, w * LANES:(w + 1) * LANES] = value * source[1 + w, :, lanes]
    z = (z_hi[...], z_lo[...])
    half = dens.shape[0]
    for q in range(BLK // 2):
        out = dot3(split(dens[:, q * 2 * LANES:(q + 1) * 2 * LANES]), z)
        mirror = turned(out[:, LANES:])
        spectrum[:half, q * LANES:(q + 1) * LANES] = out[:, :LANES] + mirror
        spectrum[half:, q * LANES:(q + 1) * LANES] = out[:, :LANES] - mirror
    for parity in range(2):
        part = pl.ds(parity * half, half)
        spectrum[part, :] = dot3((y_hi[parity], y_lo[parity]), split(spectrum[part, :]))

    def reduce(group, carry):
        lines = pl.ds(pl.multiple_of(group * SUB, SUB), SUB)
        near, far = powers[0, lines, :], powers[1, lines, :]
        for q in range(BLK // 2):
            lanes = slice(q * LANES, (q + 1) * LANES)
            values = []
            for k in range(SUB):
                rows = pl.ds(pl.multiple_of((group * SUB + k) * SUB, SUB), SUB)
                values.append(ends[rows, :] * spectrum[rows, lanes])
            even, odd = sub_sums(values)
            rightward = (even + odd) - near * (even - odd)
            leftward = (even - odd) - far * (even + odd)
            a_out[lines, lanes] = rightward
            b_out[lines, lanes] = leftward
            for k, out in enumerate(messages, 1):
                out[lines, lanes] = jnp.where((g ^ k) > g, rightward, leftward)
        return carry

    lax.fori_loop(0, NY // SUB, reduce, 0)


def backward_kernel(u, counts, flags, *refs):
    groups = []
    for count in counts:
        groups.append(refs[:count])
        refs = refs[count:]
    own, other, received = groups
    (y_hi, y_lo, z_hi, z_lo, inverse, basis, powers, steady, spectrum, a_in, b_in) = refs[:11]
    out, work, pot = refs[-3:]
    core, g = my_core(), lax.axis_index("grid")
    tiles = own[0].shape[2] // LANES
    first, last = basis[0], basis[1]

    def ends(group, carry):
        lines = pl.ds(pl.multiple_of(group * SUB, SUB), SUB)
        scale, r, slab = steady[0, lines, :], steady[1, lines, :], steady[2, lines, :]
        decays = [None, jnp.ones((SUB, LANES), f32), slab]
        while len(decays) <= len(received):
            decays.append(decays[-1] * slab)
        for q in range(BLK // 2):
            lanes = slice(q * LANES, (q + 1) * LANES)
            from_left = from_right = jnp.zeros((SUB, LANES), f32)
            for n, ref in enumerate(received, 1):
                distance = jnp.abs((g ^ n) - g)
                factor = decays[n]
                for d in range(1, n):
                    factor = jnp.where(distance == d, decays[d], factor)
                value = factor * ref[lines, lanes]
                is_left = (g ^ n) < g
                from_left = from_left + jnp.where(is_left, value, 0.0)
                from_right = from_right + jnp.where(is_left, 0.0, value)
            before = scale * (powers[2, lines, :] * from_left
                              + r * powers[3, lines, :] * (b_in[lines, lanes] + slab * from_right))
            after = scale * (powers[4, lines, :] * from_right
                             + r * powers[5, lines, :] * (a_in[lines, lanes] + slab * from_left))
            for k in range(SUB):
                rows = pl.ds(pl.multiple_of((group * SUB + k) * SUB, SUB), SUB)
                edge = first * before[k:k + 1] + last * after[k:k + 1]
                work[rows, lanes] = inverse[rows, :] * (spectrum[rows, lanes] + edge)
        return carry

    lax.fori_loop(0, NY // SUB, ends, 0)
    z = (z_hi[...], z_lo[...])
    half = pot.shape[0]
    for parity in range(2):
        part = pl.ds(parity * half, half)
        work[part, :] = dot3((y_hi[parity], y_lo[parity]), split(work[part, :]))
    for q in range(BLK // 2):
        lanes = slice(q * LANES, (q + 1) * LANES)
        even, odd = work[:half, lanes], work[half:, lanes]
        rows = jnp.concatenate([even + odd, turned(even - odd)], axis=1)
        pot[:, q * 2 * LANES:(q + 1) * 2 * LANES] = dot3(split(rows), z)
    live = [jnp.broadcast_to(flags[u * BLK + w:u * BLK + w + 1, :], (SUB, LANES)) for w in range(BLK)]
    for side, group in ((0, own), (1, other)):
        half = (core if side == 0 else 1 - core) * (len(own) * tiles)
        for n, ref in enumerate(group):
            for t in range(tiles):
                lanes = pl.ds(t * LANES, LANES)
                at = half + n * tiles + t
                rows = pl.ds(pl.multiple_of(at * SUB, SUB), SUB)
                total = None
                for w in range(BLK):
                    term = live[w] * (pot[rows, w * LANES:(w + 1) * LANES] * ref[1 + w, :, lanes])
                    total = term if total is None else total + term
                out[:, pl.ds(pl.multiple_of(at * LANES, LANES), LANES)] = -total


def place_kernel(match, *refs):
    parts, (out, rows, sem) = refs[:-4], refs[-3:]
    pair = BLK // 2
    blocks = out.shape[0] // BLK
    core = my_core()
    values = []
    for part in parts:
        values += [part] if len(part.shape) == 2 else [part.at[n] for n in range(part.shape[0])]
    parts, count = values, len(values) // pair
    near = jnp.max(match[0:1, :]).astype(jnp.int32)
    far = jnp.max(match[1:2, :]).astype(jnp.int32) if count > 6 else None

    def hits(b, side):
        at = 2 * b + side
        bits = [(near & (1 << (at * 3 + n))) for n in range(3)]
        if far is not None:
            bits.append(far & (1 << at))
        return [(bit, side * count // 2 + n) for n, bit in enumerate(bits)]

    def found(b, side):
        at = 2 * b + side
        any_near = near & (7 << (at * 3))
        return any_near != 0 if far is None else (any_near != 0) | ((far & (1 << at)) != 0)

    def move(b, side):
        which = core if side == 0 else 1 - core
        at = b * BLK + which * pair
        return pltpu.make_async_copy(rows.at[b, side], out.at[pl.ds(at, pair)], sem.at[b, side])

    for b in range(blocks):
        for side in range(2):

            @pl.when(found(b, side))
            def _():
                rows[b, side] = jnp.zeros(rows.shape[2:], f32)
                for hit, n in hits(b, side):

                    @pl.when(hit != 0)
                    def _():
                        for u in range(pair):
                            rows[b, side, u] += parts[u * count + n][...]

                move(b, side).start()

    for b in range(blocks):
        for side in range(2):

            @pl.when(found(b, side))
            def _():
                move(b, side).wait()


def tile_device(orbitals, rotation, tile_list, pair_mask):
    shape = per_device, planes, width = orbitals.shape
    n_orb, n_grid = lax.axis_size("orb"), lax.axis_size("grid")
    size_x = planes * n_grid
    half = width // 2
    chips = n_orb // 2
    axes = ("orb", "grid")

    def swap(x, even, odd):
        moves = []
        for a in range(n_orb):
            flip = even if a % 2 == 0 else odd
            moves += [(a * n_grid + b, (a ^ flip) * n_grid + b) for b in range(n_grid)]
        return lax.ppermute(x, axes, moves)

    def cross(x, k):
        moves = [(a * n_grid + b, a * n_grid + (b ^ k)) for a in range(n_orb) for b in range(n_grid)]
        return lax.ppermute(x, axes, moves)

    chunk = half // CHUNKS
    orbitals = pltpu.with_memory_space_constraint(orbitals, pltpu.HBM)

    part = jax.ShapeDtypeStruct((per_device, planes, chunk), f32)
    fetched = pl.pallas_call(
        fetch_kernel, out_shape=[part] * (2 * CHUNKS), in_specs=[HBM], out_specs=[VM] * (2 * CHUNKS),
        scratch_shapes=[pltpu.VMEM(shape, f32), DMA((2 * CHUNKS,))], name="fetch", compiler_params=grant(8),
    )(orbitals)
    theirs, mine = [], fetched[CHUNKS:]
    for taken in fetched[:CHUNKS]:
        theirs.append(swap(taken, 1, 1))

    pair = BLK // 2
    firsts = (BLK + 2) * chips
    rows = (firsts + 2 * (pair - 1) * chips) * SUB
    wide_table = jax.ShapeDtypeStruct((rows, 2 * LANES), bf16)
    blocks = per_device // BLK
    c, r = line_np()
    c, r = line_np()
    host = jnp.asarray(host_np(chips).reshape(-1))
    high, low = pl.pallas_call(
        functools.partial(setup_kernel, per_device), out_shape=[wide_table] * 2,
        in_specs=[SM, SM, VM, ANY], out_specs=[VM] * 2, name="setup", compiler_params=grant(8),
    )(tile_list, host, rotation, taken)

    def rotate(first, count, fields, *after):
        part = jax.ShapeDtypeStruct((count, planes, chunk * (len(fields) // 2)), f32)
        send, keep = pl.pallas_call(
            functools.partial(rotate_kernel, first * SUB), out_shape=(part, part),
            in_specs=[VM] * (2 + len(fields)) + [ANY] * len(after),
            out_specs=(VM, VM), compiler_params=grant(8),
        )(high, low, *fields, *after)
        return send, keep, swap(send, 2, 4)

    sums, last = [], ()
    for n in range(CHUNKS):
        sums.append(rotate(0, firsts // 2, [mine[n], theirs[n]], *last))
        last = (sums[-1][0],)
    both = [x for n in range(CHUNKS) for x in (mine[n], theirs[n])]
    sums.append(rotate(firsts, (pair - 1) * chips, both, *last))
    passing, own, other = [], [], []

    def pass_on(n, *after, spec=ANY):
        _, keep, got = sums[n]
        count = keep.shape[0] // 2
        value = pl.pallas_call(
            pass_kernel, out_shape=jax.ShapeDtypeStruct((count,) + keep.shape[1:], f32),
            in_specs=[VM] * 2 + [spec] * len(after), out_specs=VM, compiler_params=grant(4),
        )(keep, got, *after)
        passing.append((keep, got, swap(value, 4, 2)))
        return value

    def finish(n, *after):
        keep, got, passed = passing[n]
        own.append(pl.pallas_call(
            finish_kernel, out_shape=jax.ShapeDtypeStruct(passed.shape, f32), in_specs=[VM] * 3 + [ANY] * len(after),
            out_specs=VM, compiler_params=grant(4),
        )(keep, got, passed, *after))
        other.append(swap(own[-1], 1, 1))
        return own[-1]

    step = pass_on(0, sums[-1][0])
    empty, powers, flags, match, alone = pl.pallas_call(
        functools.partial(ready_kernel, per_device, n_grid),
        out_shape=(pltpu.HBM(shape, f32), jax.ShapeDtypeStruct((6, NY, LANES), f32),
                   jax.ShapeDtypeStruct((pair * BLK, LANES), f32), jax.ShapeDtypeStruct((SUB, LANES), f32),
                   jax.ShapeDtypeStruct((1,), jnp.int32)),
        in_specs=[SM, SM, VM, VM, ANY], out_specs=(HBM, VM, VM, VM, SM),
        scratch_shapes=[pltpu.VMEM((pair, planes, width), f32), DMA((per_device // pair,))], name="ready",
        compiler_params=grant(4),
    )(tile_list, host, pair_mask, jnp.asarray(np.log(r), f32), step)
    step = pass_on(1, empty, spec=HBM)
    for n in range(2, CHUNKS):
        step = pass_on(n, step)
    for n in range(CHUNKS):
        step = finish(n, step)
    last = (pass_on(CHUNKS, step),)

    sine_x, eigen_x = sine_np(planes), eigen_np(planes)
    ends = jnp.asarray(np.einsum("jp,pkl->kjl", sine_x, r[None] ** np.arange(planes - 1, -1, -1)[:, None, None])
                       .reshape(-1, LANES), f32)
    inverse = jnp.asarray((COUPLING / (eigen_x[None, :, None] + c[:, None, :])).reshape(-1, LANES), f32)
    basis = jnp.asarray(np.broadcast_to(sine_x[:, [0, -1]].T[:, :, None], (2, planes, LANES)), f32)
    steady = jnp.asarray(np.stack([r / ((1 - r**2) * (1 - r ** (2 * size_x + 2))), r, r**planes]), f32)

    y_there, y_back = y_tables()
    y_hi, y_lo = halves_np(y_there)
    yt_hi, yt_lo = halves_np(y_back)
    z_hi, z_lo = halves_np(z_table())
    zt_hi, zt_lo = halves_np(z_table().T)
    solved = []
    lines = jax.ShapeDtypeStruct((NY, 2 * LANES), f32)
    cube = (NY * SUB, 2 * LANES)
    wide = pltpu.VMEM((width // LANES * SUB, BLK * LANES), f32)
    base_own, base_other = own[:CHUNKS], other[:CHUNKS]
    for u in range(pair):
        if u:
            finish(CHUNKS, *last)
        more_own, more_other = own[CHUNKS:][:u], other[CHUNKS:][:u]
        counts = (CHUNKS, CHUNKS, len(more_own), len(more_other))
        inputs = [*base_own, *base_other, *more_own, *more_other, y_hi, y_lo, z_hi, z_lo, ends, powers]
        *messages, spectrum, a, b = pl.pallas_call(
            functools.partial(forward_kernel, u, counts + (n_grid - 1,)),
            out_shape=[lines] * (n_grid - 1) + [jax.ShapeDtypeStruct(cube, f32), lines, lines],
            in_specs=[VM] * len(inputs) + [ANY] * len(last),
            out_specs=[VM] * (n_grid + 2),
            scratch_shapes=[wide],
            compiler_params=grant(16),
        )(*inputs, *last)
        last = (spectrum,)
        received = []
        for k, message in enumerate(messages, 1):
            received.append(cross(message, k))
        solved.append((spectrum, a, b, received))

    terms, last = [], ()
    for u, (spectrum, a, b, received) in enumerate(solved):
        inputs = [*base_own, *base_other, *received, yt_hi, yt_lo, zt_hi, zt_lo, inverse, basis, powers, steady,
                  spectrum, a, b]
        terms.append(pl.pallas_call(
            functools.partial(backward_kernel, u, (CHUNKS, CHUNKS, len(received))),
            out_shape=jax.ShapeDtypeStruct((planes, width), f32),
            in_specs=[VM] * (1 + len(inputs)) + [ANY] * len(last),
            out_specs=VM,
            scratch_shapes=[pltpu.VMEM(cube, f32), wide],
            compiler_params=grant(16),
        )(flags, *inputs, *last))
        last = (terms[-1],)

    near_1 = [swap(term, 2, 4) for term in terms]
    near_2 = [swap(term, 4, 2) for term in terms]
    own_parts = [[term, x, y] for term, x, y in zip(terms, near_1, near_2)]
    sib_parts = []
    for term, x, y in own_parts:
        joined = pl.pallas_call(
            join_kernel, out_shape=jax.ShapeDtypeStruct((2,) + term.shape, f32), in_specs=[VM] * 2, out_specs=VM,
            compiler_params=grant(4),
        )(x, y)
        given = swap(term, 1, 1)
        sib_parts.append([given, swap(joined, 1, 1)])

    def place(target, groups):
        parts = [part for group in groups for part in group]
        return pl.pallas_call(
            place_kernel,
            out_shape=pltpu.HBM(shape, f32),
            in_specs=[VM] * (1 + len(parts)) + [HBM],
            out_specs=HBM,
            input_output_aliases={len(parts) + 1: 0},
            scratch_shapes=[pltpu.VMEM((blocks, 2, pair, planes, width), f32), DMA((blocks, 2))],
            name="place",
            compiler_params=grant(8),
        )(match, *parts, target)

    def place_near(target, mine, sibs):
        return place(target, [a + b for a, b in zip(mine, sibs)])

    def place_far(target, mine, sibs):
        far = [swap(group[1], 4, 2) for group in mine]
        return place(target, [a + [x] + b + [swap(x, 1, 1)] for a, b, x in zip(mine, sibs, far)])

    return lax.cond(alone[0] != 0, place_far, place_near, empty, own_parts, sib_parts)


def sine_table(length):
    wave_index = jnp.arange(length, dtype=f32) + 1.0
    return jnp.sqrt(2.0 / (length + 1.0)) * jnp.sin(
        jnp.pi * wave_index[:, None] * wave_index[None, :] / (length + 1.0)
    )


def eigen_values(length):
    wave_index = jnp.arange(length, dtype=f32) + 1.0
    return 2.0 - 2.0 * jnp.cos(jnp.pi * wave_index / (length + 1.0))


def green_kernel(size_x, size_y, size_z):
    summed = (
        eigen_values(size_x)[:, None, None]
        + eigen_values(size_y)[None, :, None]
        + eigen_values(size_z)[None, None, :]
    )
    return COUPLING / (summed + SCREENING)


def pair_lists(tile_list, pair_mask):
    within = jnp.arange(BLK * BLK, dtype=jnp.int32)
    targets = (BLK * tile_list[:, 0:1] + within[None, :] // BLK).reshape(-1)
    sources = (BLK * tile_list[:, 1:2] + within[None, :] % BLK).reshape(-1)
    return (targets, sources, pair_mask[targets, sources])


def compact(targets, sources, live_flags, number):
    ranking = jnp.cumsum(live_flags) - 1
    places = jnp.where(live_flags == 1, ranking, number)
    picked = (
        jnp.zeros((number,), jnp.int32)
        .at[places]
        .set(jnp.arange(live_flags.shape[0], dtype=jnp.int32), mode="drop")
    )
    return (targets[picked], sources[picked])


def along_z(values, matrix):
    number, planes, width_yz = values.shape
    size_z = matrix.shape[0]
    shaped = values.reshape(number, planes, width_yz // size_z, size_z)
    return jnp.einsum("pxrz,zk->pxrk", shaped, matrix, precision=precise).reshape(number, planes, width_yz)


def along_y(values, matrix):
    number, planes, width_yz = values.shape
    size_y = matrix.shape[0]
    shaped = values.reshape(number, planes, size_y, width_yz // size_y)
    return jnp.einsum("pxyz,yk->pxkz", shaped, matrix, precision=precise).reshape(number, planes, width_yz)


def along_x(values, matrix):
    return jnp.einsum("pxc,xk->pkc", values, matrix, precision=precise)


def any_device(orbitals, rotation, tile_list, pair_mask):
    n_grid = lax.axis_size("grid")
    number_orbitals, size_x = rotation.shape[0], orbitals.shape[1] * n_grid
    rotated = jnp.einsum(
        "ij,ixc->jxc",
        rotation,
        lax.all_to_all(orbitals, "orb", split_axis=2, concat_axis=0, tiled=True),
        precision=precise,
    )
    planes, width_yz = rotated.shape[1:]
    targets, sources, live_flags = pair_lists(tile_list, pair_mask)
    matrix_x, matrix_y, matrix_z = sine_table(size_x), sine_table(NY), sine_table(NZ)
    kernel = green_kernel(size_x, NY, NZ).reshape(size_x, NY * NZ)
    orbital_ids = jnp.arange(number_orbitals, dtype=jnp.int32)
    targets, sources = compact(targets, sources, live_flags, targets.shape[0] // 2)
    density = rotated[targets] * rotated[sources]
    number = density.shape[0]
    spectrum = along_z(density, matrix_z)
    spectrum = lax.all_to_all(spectrum, "orb", split_axis=0, concat_axis=2, tiled=True)
    spectrum = along_y(spectrum, matrix_y)
    spectrum = lax.all_to_all(spectrum, "grid", split_axis=0, concat_axis=1, tiled=True)
    spectrum = along_x(along_x(spectrum, matrix_x) * kernel, matrix_x)
    spectrum = lax.all_to_all(spectrum, "grid", split_axis=1, concat_axis=0, tiled=True)
    spectrum = along_y(spectrum, matrix_y)
    spectrum = lax.all_to_all(spectrum, "orb", split_axis=2, concat_axis=0, tiled=True)
    potential = along_z(spectrum, matrix_z)
    products = potential * rotated[sources]
    selector = (targets[None, :] == orbital_ids[:, None]).astype(f32)
    partial_value = -jnp.dot(selector, products.reshape(number, planes * width_yz), precision=precise)
    partial_value = partial_value.reshape(number_orbitals, planes, width_yz)
    return lax.all_to_all(partial_value, "orb", split_axis=0, concat_axis=2, tiled=True)


def solution(mesh):
    n_orb, n_grid = mesh.shape["orb"], mesh.shape["grid"]

    def on_device(orbitals, rotation, tile_list, pair_mask):
        per_device, planes, width = orbitals.shape
        fits = n_orb == 8 and 2 * tile_list.shape[0] == n_orb and planes == SUB and per_device % BLK == 0
        fits = fits and width == NY * NZ and 2 * NZ == LANES and n_grid in (2, 4, 8)
        fits = fits and per_device * SUB == LANES and rotation.shape == (LANES, LANES)
        if not fits:
            return any_device(orbitals, rotation, tile_list, pair_mask)
        return tile_device(orbitals, rotation, tile_list, pair_mask)

    in_specs = (P("orb", "grid", None), P(), P(), P())
    out_specs = P("orb", "grid", None)
    return jax.shard_map(on_device, mesh=mesh, in_specs=in_specs, out_specs=out_specs, check_vma=False)
```

```python
import functools
import itertools

import jax
import jax.numpy as jnp
import numpy as np
from jax import lax
from jax.experimental import pallas as pl
from jax.experimental.pallas import tpu as pltpu
from jax.sharding import PartitionSpec as P


BLK = 4
NY = 64
NZ = 64
LANES = 128
SUB = 8
CHUNKS = 2
COUPLING = 0.25
SCREENING = 0.1

precise = lax.Precision.HIGHEST
f32 = jnp.float32
bf16 = jnp.bfloat16

VM = pl.BlockSpec(memory_space=pltpu.VMEM)
SM = pl.BlockSpec(memory_space=pltpu.SMEM)
ANY = pl.BlockSpec(memory_space=pl.ANY)
HBM = pl.BlockSpec(memory_space=pltpu.HBM)
DMA = pltpu.SemaphoreType.DMA


def grant(mib):
    return pltpu.CompilerParams(vmem_limit_bytes=mib << 20)


def sine_np(n):
    k = np.arange(1, n + 1, dtype=np.float64)
    return np.sqrt(2.0 / (n + 1)) * np.sin(np.pi * k[:, None] * k[None, :] / (n + 1))


def eigen_np(n):
    k = np.arange(1, n + 1, dtype=np.float64)
    return 2.0 - 2.0 * np.cos(np.pi * k / (n + 1))


def halves_np(table):
    high = np.asarray(table, np.float32).astype(jnp.bfloat16)
    low = (np.asarray(table, np.float64) - high.astype(np.float64)).astype(jnp.bfloat16)
    return jnp.asarray(high), jnp.asarray(low)


def y_order():
    rows = LANES // NZ
    return np.arange(NY).reshape(NY // rows, rows).T.reshape(-1)


def y_tables():
    sine, planes = sine_np(NY), sine_np(SUB)
    even, odd = np.kron(sine[0::2, 0::2], planes), np.kron(sine[1::2, 0::2], planes)
    return np.stack([even, odd]), np.stack([even, odd.T])


def turned(x):
    count = x.shape[0] // SUB
    return jnp.concatenate([x[(count - 1 - t) * SUB:(count - t) * SUB] for t in range(count)])


def z_table():
    half = LANES // NZ
    sine = sine_np(NZ)
    table = np.zeros((2, half, NZ, half, 2, NZ))
    for pair in range(2):
        for h in range(half):
            table[pair, h, :, h, pair, :] = sine
    return table.reshape(2 * half * NZ, half * 2 * NZ)


def line_np():
    c = eigen_np(NY)[y_order()][:, None] + eigen_np(NZ)[None, :] + SCREENING
    c = np.concatenate([c, c], axis=1)
    return c, 2.0 / (2.0 + c + np.sqrt(c * (c + 4.0)))


def host_np(chips):
    table = np.zeros((chips**chips, chips), np.int32)
    for owners in itertools.product(range(chips), repeat=chips):
        best = None
        for tiles in itertools.permutations(range(chips)):
            hops = [bin(chip ^ owners[tile]).count("1") for chip, tile in enumerate(tiles)]
            cost = (max(hops), sum(hops))
            if best is None or cost < best[0]:
                best = (cost, tiles)
        table[sum(own * chips**t for t, own in enumerate(owners))] = best[1]
    return table


def dot(a, b):
    return jnp.dot(a, b, preferred_element_type=f32)


def split(x):
    high = x.astype(bf16)
    return high, (x - high.astype(f32)).astype(bf16)


def dot3(a, b):
    return dot(a[0], b[0]) + dot(a[0], b[1]) + dot(a[1], b[0])


def my_core():
    return lax.rem(lax.axis_index("orb"), 2)


def my_place():
    o = lax.axis_index("orb")
    return o, lax.rem(o, 2), lax.div(o, 2)


def fetch_kernel(source, *rest):
    outs, (whole, sem) = rest[:-2], rest[-2:]
    copies = [pltpu.make_async_copy(source.at[n], whole.at[n], sem.at[n]) for n in range(whole.shape[0])]
    for copy in copies:
        copy.start()
    for copy in copies:
        copy.wait()
    core = my_core()
    copies = []
    for n, out in enumerate(outs):
        side = 1 - core if n < CHUNKS else core
        at = side * (whole.shape[2] // 2) + n % CHUNKS * out.shape[2]
        lanes = pl.ds(pl.multiple_of(at, LANES), out.shape[2])
        copies.append(pltpu.make_async_copy(whole.at[:, :, lanes], out, sem.at[n]))
    for copy in copies:
        copy.start()
    for copy in copies:
        copy.wait()


class Place:
    def __init__(self, per_device, tiles, host):
        self.o, self.core, self.chip = my_place()
        self.tiles, self.host = tiles, host
        self.chips = tiles.shape[0]
        owners = [lax.div(tiles[t, 0] * BLK, 2 * per_device) for t in range(self.chips)]
        key, same = 0, True
        for t in range(self.chips):
            key = key + owners[t] * self.chips**t
            same = same & (owners[t] == owners[0])
        self.key, self.same = key, same
        self.bit_1 = jnp.where(self.core == 0, 1, 2)
        self.bit_2 = 3 - self.bit_1

    def tile(self, chip):
        return self.host[self.key * self.chips + chip]

    def heads(self, chip):
        tile = self.tile(chip)
        return BLK * self.tiles[tile, 0], BLK * self.tiles[tile, 1]


def setup_kernel(per_device, tiles, host, rotation, after, high, low):
    core = my_core()
    at = Place(per_device, tiles, host)
    pair = BLK // 2
    heads = [at.heads(chip) for chip in (at.chip ^ 3, at.chip ^ at.bit_1, at.chip ^ at.bit_2, at.chip)]
    wanted = []
    for a, b in heads:
        wanted += [a + (1 - core) * pair] + [b + w for w in range(BLK)] + [a + core * pair]
    for u in range(1, pair):
        for a, b in heads:
            wanted += [a + (1 - core) * pair + u, a + core * pair + u]
    lane = lax.broadcasted_iota(jnp.int32, (SUB, LANES), 1)
    chosen = jnp.concatenate([jnp.where(lane == n, 1.0, 0.0) for n in wanted]).astype(bf16)
    rows = chosen.shape[0]
    row = lax.broadcasted_iota(jnp.int32, (LANES, LANES), 0)
    column = lax.broadcasted_iota(jnp.int32, (LANES, LANES), 1)
    columns = [
        jnp.where(row - (at.o ^ e) * per_device == jnp.right_shift(column, 3), 1.0, 0.0).astype(bf16)
        for e in range(2)
    ]
    keep = (lax.broadcasted_iota(jnp.int32, (rows, LANES), 0) & (SUB - 1)) == (
        lax.broadcasted_iota(jnp.int32, (rows, LANES), 1) & (SUB - 1)
    )
    for out, values in zip((high, low), split(rotation[...])):
        picked = lax.dot_general(chosen, values, (((1,), (1,)), ((), ())), preferred_element_type=f32).astype(bf16)
        for e in range(2):
            out[:, e * LANES:(e + 1) * LANES] = jnp.where(keep, dot(picked, columns[e]), 0.0).astype(bf16)


def ready_kernel(per_device, n_grid, tiles, host, mask, log_r, *rest):
    out, powers, flags, match, alone, zeros, sem = rest[-7:]
    zeros[...] = jnp.zeros(zeros.shape, f32)
    step = zeros.shape[0]
    copies = [
        pltpu.make_async_copy(zeros, out.at[pl.ds(n * step, step)], sem.at[n]) for n in range(out.shape[0] // step)
    ]
    for copy in copies:
        copy.start()
    begin, size_x = SUB * lax.axis_index("grid"), SUB * n_grid
    exponents = (
        2 * begin + SUB + 1,
        2 * size_x + 1 - SUB - 2 * begin,
        2 * size_x + 2 - 2 * begin,
        2 * begin,
        2 * begin + 2 * SUB + 2,
        2 * size_x - 2 * SUB - 2 * begin,
    )
    for n, exponent in enumerate(exponents):
        power = jnp.exp(exponent.astype(f32) * log_r[...])
        powers[n] = power if n < 2 else 1.0 - power
    at = Place(per_device, tiles, host)
    alone[0] = at.same.astype(jnp.int32)
    a, b = at.heads(at.chip)
    pair = BLK // 2
    live = mask[...].astype(f32)
    row = lax.broadcasted_iota(jnp.int32, live.shape, 0)
    column = lax.broadcasted_iota(jnp.int32, (1, live.shape[1]), 1)
    for u in range(pair):
        line = jnp.sum(jnp.where(row == a + at.core * pair + u, live, 0.0), axis=0, keepdims=True)
        for w in range(BLK):
            flag = jnp.sum(jnp.where(column == b + w, line, 0.0), axis=1, keepdims=True)
            flags[u * BLK + w:u * BLK + w + 1, :] = jnp.broadcast_to(flag, (1, LANES))
    blocks = per_device // BLK
    flips = ((0, at.bit_1, at.bit_2), (0, at.bit_2, at.bit_1))
    near, far = 0, 0
    for side in range(2):
        homes = [tiles[at.tile(at.chip ^ flip), 0] for flip in flips[side] + (3,)]
        for block in range(blocks):
            bits = [(home == at.o * blocks + block).astype(jnp.int32) for home in homes]
            for n in range(3):
                near = near + bits[n] * (1 << ((2 * block + side) * 3 + n))
            far = far + bits[3] * (1 << (2 * block + side))
    match[0:1, :] = jnp.full((1, LANES), near.astype(f32))
    match[1:2, :] = jnp.full((1, LANES), far.astype(f32))
    for copy in copies:
        copy.wait()


def join_kernel(x, y, out):
    out[0] = x[...]
    out[1] = y[...]


def rotate_kernel(first, high, low, *rest):
    send, keep = rest[-2:]
    rows = send.shape[0] * SUB
    part = pl.ds(first, 2 * rows)
    table = (high[part, :], low[part, :])
    at = 0
    step = 2 * LANES
    while at < send.shape[2]:
        width = rest[0].shape[2]
        n, inner = at // width, at % width
        lanes = slice(inner, inner + step)
        mine, theirs = rest[2 * n], rest[2 * n + 1]
        depth = mine.shape[0] * SUB
        cells = jnp.concatenate([mine[:, :, lanes].reshape(depth, step), theirs[:, :, lanes].reshape(depth, step)])
        total = dot3(table, split(cells))
        lanes = slice(at, at + step)
        send[:, :, lanes] = total[:rows].reshape(send.shape[0], SUB, step)
        keep[:, :, lanes] = total[rows:].reshape(keep.shape[0], SUB, step)
        at += step


def pass_kernel(keep, got, *rest):
    out = rest[-1]
    count = out.shape[0]
    out[...] = keep[:count] + got[:count]


def finish_kernel(keep, got, passed, *rest):
    out = rest[-1]
    count = out.shape[0]
    out[...] = keep[count:] + got[count:] + passed[...]


def sub_sums(values):
    row = lax.broadcasted_iota(jnp.int32, values[0].shape, 0)
    for s in (4, 2):
        low = (row & s) == 0
        paired = []
        for n in range(s):
            a, b = values[n], values[n + s]
            paired.append(jnp.where(low, a, pltpu.roll(b, s, 0)) + jnp.where(low, pltpu.roll(a, SUB - s, 0), b))
        values = paired
    even = (row & 1) == 0
    a, b = values
    return jnp.where(even, a, pltpu.roll(b, 1, 0)), jnp.where(even, pltpu.roll(a, SUB - 1, 0), b)


def fields(u, own, other, first_own, first_other):
    table = []
    for side, sources, targets in ((0, first_own, own), (1, first_other, other)):
        for n, ref in enumerate(sources):
            if u == 0:
                table.append((side, n, ref, targets[n], BLK + 1 if side == 0 else 0, 0))
            else:
                table.append((side, n, ref, targets[0], 1 if side == 0 else 0, n * ref.shape[2]))
    return table


def forward_kernel(u, counts, *refs):
    groups = []
    for count in counts[:-1]:
        groups.append(refs[:count])
        refs = refs[count:]
    first_own, first_other, own, other = groups[:4]
    y_hi, y_lo, z_hi, z_lo, ends, powers = refs[:6]
    messages, (spectrum, a_out, b_out, dens) = refs[-4 - counts[-1]:-4], refs[-4:]
    if u == 0:
        own, other = first_own, first_other
    core, g = my_core(), lax.axis_index("grid")
    tiles = first_own[0].shape[2] // LANES
    for side, n, source, target, slot, offset in fields(u, own, other, first_own, first_other):
        half = (core if side == 0 else 1 - core) * (len(first_own) * tiles * SUB)
        for t in range(tiles):
            lanes = pl.ds(t * LANES, LANES)
            value = target[slot, :, pl.ds(offset + t * LANES, LANES)]
            rows = pl.ds(pl.multiple_of(half + (n * tiles + t) * SUB, SUB), SUB)
            for w in range(BLK):
                dens[rows, w * LANES:(w + 1) * LANES] = value * source[1 + w, :, lanes]
    z = (z_hi[...], z_lo[...])
    half = dens.shape[0]
    for q in range(BLK // 2):
        out = dot3(split(dens[:, q * 2 * LANES:(q + 1) * 2 * LANES]), z)
        mirror = turned(out[:, LANES:])
        spectrum[:half, q * LANES:(q + 1) * LANES] = out[:, :LANES] + mirror
        spectrum[half:, q * LANES:(q + 1) * LANES] = out[:, :LANES] - mirror
    for parity in range(2):
        part = pl.ds(parity * half, half)
        spectrum[part, :] = dot3((y_hi[parity], y_lo[parity]), split(spectrum[part, :]))

    def reduce(group, carry):
        lines = pl.ds(pl.multiple_of(group * SUB, SUB), SUB)
        near, far = powers[0, lines, :], powers[1, lines, :]
        for q in range(BLK // 2):
            lanes = slice(q * LANES, (q + 1) * LANES)
            values = []
            for k in range(SUB):
                rows = pl.ds(pl.multiple_of((group * SUB + k) * SUB, SUB), SUB)
                values.append(ends[rows, :] * spectrum[rows, lanes])
            even, odd = sub_sums(values)
            rightward = (even + odd) - near * (even - odd)
            leftward = (even - odd) - far * (even + odd)
            a_out[lines, lanes] = rightward
            b_out[lines, lanes] = leftward
            for k, out in enumerate(messages, 1):
                out[lines, lanes] = jnp.where((g ^ k) > g, rightward, leftward)
        return carry

    lax.fori_loop(0, NY // SUB, reduce, 0)


def backward_kernel(u, counts, flags, *refs):
    groups = []
    for count in counts:
        groups.append(refs[:count])
        refs = refs[count:]
    own, other, received = groups
    (y_hi, y_lo, z_hi, z_lo, inverse, basis, powers, steady, spectrum, a_in, b_in) = refs[:11]
    out, work, pot = refs[-3:]
    core, g = my_core(), lax.axis_index("grid")
    tiles = own[0].shape[2] // LANES
    first, last = basis[0], basis[1]

    def ends(group, carry):
        lines = pl.ds(pl.multiple_of(group * SUB, SUB), SUB)
        scale, r, slab = steady[0, lines, :], steady[1, lines, :], steady[2, lines, :]
        decays = [None, jnp.ones((SUB, LANES), f32), slab]
        while len(decays) <= len(received):
            decays.append(decays[-1] * slab)
        for q in range(BLK // 2):
            lanes = slice(q * LANES, (q + 1) * LANES)
            from_left = from_right = jnp.zeros((SUB, LANES), f32)
            for n, ref in enumerate(received, 1):
                distance = jnp.abs((g ^ n) - g)
                factor = decays[n]
                for d in range(1, n):
                    factor = jnp.where(distance == d, decays[d], factor)
                value = factor * ref[lines, lanes]
                is_left = (g ^ n) < g
                from_left = from_left + jnp.where(is_left, value, 0.0)
                from_right = from_right + jnp.where(is_left, 0.0, value)
            before = scale * (powers[2, lines, :] * from_left
                              + r * powers[3, lines, :] * (b_in[lines, lanes] + slab * from_right))
            after = scale * (powers[4, lines, :] * from_right
                             + r * powers[5, lines, :] * (a_in[lines, lanes] + slab * from_left))
            for k in range(SUB):
                rows = pl.ds(pl.multiple_of((group * SUB + k) * SUB, SUB), SUB)
                edge = first * before[k:k + 1] + last * after[k:k + 1]
                work[rows, lanes] = inverse[rows, :] * (spectrum[rows, lanes] + edge)
        return carry

    lax.fori_loop(0, NY // SUB, ends, 0)
    z = (z_hi[...], z_lo[...])
    half = pot.shape[0]
    for parity in range(2):
        part = pl.ds(parity * half, half)
        work[part, :] = dot3((y_hi[parity], y_lo[parity]), split(work[part, :]))
    for q in range(BLK // 2):
        lanes = slice(q * LANES, (q + 1) * LANES)
        even, odd = work[:half, lanes], work[half:, lanes]
        rows = jnp.concatenate([even + odd, turned(even - odd)], axis=1)
        pot[:, q * 2 * LANES:(q + 1) * 2 * LANES] = dot3(split(rows), z)
    live = [jnp.broadcast_to(flags[u * BLK + w:u * BLK + w + 1, :], (SUB, LANES)) for w in range(BLK)]
    for side, group in ((0, own), (1, other)):
        half = (core if side == 0 else 1 - core) * (len(own) * tiles)
        for n, ref in enumerate(group):
            for t in range(tiles):
                lanes = pl.ds(t * LANES, LANES)
                at = half + n * tiles + t
                rows = pl.ds(pl.multiple_of(at * SUB, SUB), SUB)
                total = None
                for w in range(BLK):
                    term = live[w] * (pot[rows, w * LANES:(w + 1) * LANES] * ref[1 + w, :, lanes])
                    total = term if total is None else total + term
                out[:, pl.ds(pl.multiple_of(at * LANES, LANES), LANES)] = -total


def place_kernel(match, *refs):
    parts, (out, rows, sem) = refs[:-4], refs[-3:]
    pair = BLK // 2
    blocks = out.shape[0] // BLK
    core = my_core()
    values = []
    for part in parts:
        values += [part] if len(part.shape) == 2 else [part.at[n] for n in range(part.shape[0])]
    parts, count = values, len(values) // pair
    near = jnp.max(match[0:1, :]).astype(jnp.int32)
    far = jnp.max(match[1:2, :]).astype(jnp.int32) if count > 6 else None

    def hits(b, side):
        at = 2 * b + side
        bits = [(near & (1 << (at * 3 + n))) for n in range(3)]
        if far is not None:
            bits.append(far & (1 << at))
        return [(bit, side * count // 2 + n) for n, bit in enumerate(bits)]

    def found(b, side):
        at = 2 * b + side
        any_near = near & (7 << (at * 3))
        return any_near != 0 if far is None else (any_near != 0) | ((far & (1 << at)) != 0)

    def move(b, side):
        which = core if side == 0 else 1 - core
        at = b * BLK + which * pair
        return pltpu.make_async_copy(rows.at[b, side], out.at[pl.ds(at, pair)], sem.at[b, side])

    for b in range(blocks):
        for side in range(2):

            @pl.when(found(b, side))
            def _():
                rows[b, side] = jnp.zeros(rows.shape[2:], f32)
                for hit, n in hits(b, side):

                    @pl.when(hit != 0)
                    def _():
                        for u in range(pair):
                            rows[b, side, u] += parts[u * count + n][...]

                move(b, side).start()

    for b in range(blocks):
        for side in range(2):

            @pl.when(found(b, side))
            def _():
                move(b, side).wait()


def tile_device(orbitals, rotation, tile_list, pair_mask):
    shape = per_device, planes, width = orbitals.shape
    n_orb, n_grid = lax.axis_size("orb"), lax.axis_size("grid")
    size_x = planes * n_grid
    half = width // 2
    chips = n_orb // 2
    axes = ("orb", "grid")

    def swap(x, even, odd):
        moves = []
        for a in range(n_orb):
            flip = even if a % 2 == 0 else odd
            moves += [(a * n_grid + b, (a ^ flip) * n_grid + b) for b in range(n_grid)]
        return lax.ppermute(x, axes, moves)

    def cross(x, k):
        moves = [(a * n_grid + b, a * n_grid + (b ^ k)) for a in range(n_orb) for b in range(n_grid)]
        return lax.ppermute(x, axes, moves)

    chunk = half // CHUNKS
    orbitals = pltpu.with_memory_space_constraint(orbitals, pltpu.HBM)

    part = jax.ShapeDtypeStruct((per_device, planes, chunk), f32)
    fetched = pl.pallas_call(
        fetch_kernel, out_shape=[part] * (2 * CHUNKS), in_specs=[HBM], out_specs=[VM] * (2 * CHUNKS),
        scratch_shapes=[pltpu.VMEM(shape, f32), DMA((max(per_device, 2 * CHUNKS),))], name="fetch", compiler_params=grant(8),
    )(orbitals)
    theirs, mine = [], fetched[CHUNKS:]
    for taken in fetched[:CHUNKS]:
        theirs.append(swap(taken, 1, 1))

    pair = BLK // 2
    firsts = (BLK + 2) * chips
    rows = (firsts + 2 * (pair - 1) * chips) * SUB
    wide_table = jax.ShapeDtypeStruct((rows, 2 * LANES), bf16)
    blocks = per_device // BLK
    c, r = line_np()
    c, r = line_np()
    host = jnp.asarray(host_np(chips).reshape(-1))
    high, low = pl.pallas_call(
        functools.partial(setup_kernel, per_device), out_shape=[wide_table] * 2,
        in_specs=[SM, SM, VM, ANY], out_specs=[VM] * 2, name="setup", compiler_params=grant(8),
    )(tile_list, host, rotation, taken)

    def rotate(first, count, fields, *after):
        part = jax.ShapeDtypeStruct((count, planes, chunk * (len(fields) // 2)), f32)
        send, keep = pl.pallas_call(
            functools.partial(rotate_kernel, first * SUB), out_shape=(part, part),
            in_specs=[VM] * (2 + len(fields)) + [ANY] * len(after),
            out_specs=(VM, VM), compiler_params=grant(8),
        )(high, low, *fields, *after)
        return send, keep, swap(send, 2, 4)

    sums, last = [], ()
    for n in range(CHUNKS):
        sums.append(rotate(0, firsts // 2, [mine[n], theirs[n]], *last))
        last = (sums[-1][0],)
    both = [x for n in range(CHUNKS) for x in (mine[n], theirs[n])]
    sums.append(rotate(firsts, (pair - 1) * chips, both, *last))
    passing, own, other = [], [], []

    def pass_on(n, *after, spec=ANY):
        _, keep, got = sums[n]
        count = keep.shape[0] // 2
        value = pl.pallas_call(
            pass_kernel, out_shape=jax.ShapeDtypeStruct((count,) + keep.shape[1:], f32),
            in_specs=[VM] * 2 + [spec] * len(after), out_specs=VM, compiler_params=grant(4),
        )(keep, got, *after)
        passing.append((keep, got, swap(value, 4, 2)))
        return value

    def finish(n, *after):
        keep, got, passed = passing[n]
        own.append(pl.pallas_call(
            finish_kernel, out_shape=jax.ShapeDtypeStruct(passed.shape, f32), in_specs=[VM] * 3 + [ANY] * len(after),
            out_specs=VM, compiler_params=grant(4),
        )(keep, got, passed, *after))
        other.append(swap(own[-1], 1, 1))
        return own[-1]

    step = pass_on(0, sums[-1][0])
    empty, powers, flags, match, alone = pl.pallas_call(
        functools.partial(ready_kernel, per_device, n_grid),
        out_shape=(pltpu.HBM(shape, f32), jax.ShapeDtypeStruct((6, NY, LANES), f32),
                   jax.ShapeDtypeStruct((pair * BLK, LANES), f32), jax.ShapeDtypeStruct((SUB, LANES), f32),
                   jax.ShapeDtypeStruct((1,), jnp.int32)),
        in_specs=[SM, SM, VM, VM, ANY], out_specs=(HBM, VM, VM, VM, SM),
        scratch_shapes=[pltpu.VMEM((pair, planes, width), f32), DMA((per_device // pair,))], name="ready",
        compiler_params=grant(4),
    )(tile_list, host, pair_mask, jnp.asarray(np.log(r), f32), step)
    step = pass_on(1, empty, spec=HBM)
    for n in range(2, CHUNKS):
        step = pass_on(n, step)
    for n in range(CHUNKS):
        step = finish(n, step)
    last = (pass_on(CHUNKS, step),)

    sine_x, eigen_x = sine_np(planes), eigen_np(planes)
    ends = jnp.asarray(np.einsum("jp,pkl->kjl", sine_x, r[None] ** np.arange(planes - 1, -1, -1)[:, None, None])
                       .reshape(-1, LANES), f32)
    inverse = jnp.asarray((COUPLING / (eigen_x[None, :, None] + c[:, None, :])).reshape(-1, LANES), f32)
    basis = jnp.asarray(np.broadcast_to(sine_x[:, [0, -1]].T[:, :, None], (2, planes, LANES)), f32)
    steady = jnp.asarray(np.stack([r / ((1 - r**2) * (1 - r ** (2 * size_x + 2))), r, r**planes]), f32)

    y_there, y_back = y_tables()
    y_hi, y_lo = halves_np(y_there)
    yt_hi, yt_lo = halves_np(y_back)
    z_hi, z_lo = halves_np(z_table())
    zt_hi, zt_lo = halves_np(z_table().T)
    solved = []
    lines = jax.ShapeDtypeStruct((NY, 2 * LANES), f32)
    cube = (NY * SUB, 2 * LANES)
    wide = pltpu.VMEM((width // LANES * SUB, BLK * LANES), f32)
    base_own, base_other = own[:CHUNKS], other[:CHUNKS]
    for u in range(pair):
        if u:
            finish(CHUNKS, *last)
        more_own, more_other = own[CHUNKS:][:u], other[CHUNKS:][:u]
        counts = (CHUNKS, CHUNKS, len(more_own), len(more_other))
        inputs = [*base_own, *base_other, *more_own, *more_other, y_hi, y_lo, z_hi, z_lo, ends, powers]
        *messages, spectrum, a, b = pl.pallas_call(
            functools.partial(forward_kernel, u, counts + (n_grid - 1,)),
            out_shape=[lines] * (n_grid - 1) + [jax.ShapeDtypeStruct(cube, f32), lines, lines],
            in_specs=[VM] * len(inputs) + [ANY] * len(last),
            out_specs=[VM] * (n_grid + 2),
            scratch_shapes=[wide],
            compiler_params=grant(16),
        )(*inputs, *last)
        last = (spectrum,)
        received = []
        for k, message in enumerate(messages, 1):
            received.append(cross(message, k))
        solved.append((spectrum, a, b, received))

    terms, last = [], ()
    for u, (spectrum, a, b, received) in enumerate(solved):
        inputs = [*base_own, *base_other, *received, yt_hi, yt_lo, zt_hi, zt_lo, inverse, basis, powers, steady,
                  spectrum, a, b]
        terms.append(pl.pallas_call(
            functools.partial(backward_kernel, u, (CHUNKS, CHUNKS, len(received))),
            out_shape=jax.ShapeDtypeStruct((planes, width), f32),
            in_specs=[VM] * (1 + len(inputs)) + [ANY] * len(last),
            out_specs=VM,
            scratch_shapes=[pltpu.VMEM(cube, f32), wide],
            compiler_params=grant(16),
        )(flags, *inputs, *last))
        last = (terms[-1],)

    near_1 = [swap(term, 2, 4) for term in terms]
    near_2 = [swap(term, 4, 2) for term in terms]
    own_parts = [[term, x, y] for term, x, y in zip(terms, near_1, near_2)]
    sib_parts = []
    for term, x, y in own_parts:
        joined = pl.pallas_call(
            join_kernel, out_shape=jax.ShapeDtypeStruct((2,) + term.shape, f32), in_specs=[VM] * 2, out_specs=VM,
            compiler_params=grant(4),
        )(x, y)
        given = swap(term, 1, 1)
        sib_parts.append([given, swap(joined, 1, 1)])

    def place(target, groups):
        parts = [part for group in groups for part in group]
        return pl.pallas_call(
            place_kernel,
            out_shape=pltpu.HBM(shape, f32),
            in_specs=[VM] * (1 + len(parts)) + [HBM],
            out_specs=HBM,
            input_output_aliases={len(parts) + 1: 0},
            scratch_shapes=[pltpu.VMEM((blocks, 2, pair, planes, width), f32), DMA((blocks, 2))],
            name="place",
            compiler_params=grant(8),
        )(match, *parts, target)

    def place_near(target, mine, sibs):
        return place(target, [a + b for a, b in zip(mine, sibs)])

    def place_far(target, mine, sibs):
        far = [swap(group[1], 4, 2) for group in mine]
        return place(target, [a + [x] + b + [swap(x, 1, 1)] for a, b, x in zip(mine, sibs, far)])

    return lax.cond(alone[0] != 0, place_far, place_near, empty, own_parts, sib_parts)


def sine_table(length):
    wave_index = jnp.arange(length, dtype=f32) + 1.0
    return jnp.sqrt(2.0 / (length + 1.0)) * jnp.sin(
        jnp.pi * wave_index[:, None] * wave_index[None, :] / (length + 1.0)
    )


def eigen_values(length):
    wave_index = jnp.arange(length, dtype=f32) + 1.0
    return 2.0 - 2.0 * jnp.cos(jnp.pi * wave_index / (length + 1.0))


def green_kernel(size_x, size_y, size_z):
    summed = (
        eigen_values(size_x)[:, None, None]
        + eigen_values(size_y)[None, :, None]
        + eigen_values(size_z)[None, None, :]
    )
    return COUPLING / (summed + SCREENING)


def pair_lists(tile_list, pair_mask):
    within = jnp.arange(BLK * BLK, dtype=jnp.int32)
    targets = (BLK * tile_list[:, 0:1] + within[None, :] // BLK).reshape(-1)
    sources = (BLK * tile_list[:, 1:2] + within[None, :] % BLK).reshape(-1)
    return (targets, sources, pair_mask[targets, sources])


def compact(targets, sources, live_flags, number):
    ranking = jnp.cumsum(live_flags) - 1
    places = jnp.where(live_flags == 1, ranking, number)
    picked = (
        jnp.zeros((number,), jnp.int32)
        .at[places]
        .set(jnp.arange(live_flags.shape[0], dtype=jnp.int32), mode="drop")
    )
    return (targets[picked], sources[picked])


def along_z(values, matrix):
    number, planes, width_yz = values.shape
    size_z = matrix.shape[0]
    shaped = values.reshape(number, planes, width_yz // size_z, size_z)
    return jnp.einsum("pxrz,zk->pxrk", shaped, matrix, precision=precise).reshape(number, planes, width_yz)


def along_y(values, matrix):
    number, planes, width_yz = values.shape
    size_y = matrix.shape[0]
    shaped = values.reshape(number, planes, size_y, width_yz // size_y)
    return jnp.einsum("pxyz,yk->pxkz", shaped, matrix, precision=precise).reshape(number, planes, width_yz)


def along_x(values, matrix):
    return jnp.einsum("pxc,xk->pkc", values, matrix, precision=precise)


def any_device(orbitals, rotation, tile_list, pair_mask):
    n_grid = lax.axis_size("grid")
    number_orbitals, size_x = rotation.shape[0], orbitals.shape[1] * n_grid
    rotated = jnp.einsum(
        "ij,ixc->jxc",
        rotation,
        lax.all_to_all(orbitals, "orb", split_axis=2, concat_axis=0, tiled=True),
        precision=precise,
    )
    planes, width_yz = rotated.shape[1:]
    targets, sources, live_flags = pair_lists(tile_list, pair_mask)
    matrix_x, matrix_y, matrix_z = sine_table(size_x), sine_table(NY), sine_table(NZ)
    kernel = green_kernel(size_x, NY, NZ).reshape(size_x, NY * NZ)
    orbital_ids = jnp.arange(number_orbitals, dtype=jnp.int32)
    targets, sources = compact(targets, sources, live_flags, targets.shape[0] // 2)
    density = rotated[targets] * rotated[sources]
    number = density.shape[0]
    spectrum = along_z(density, matrix_z)
    spectrum = lax.all_to_all(spectrum, "orb", split_axis=0, concat_axis=2, tiled=True)
    spectrum = along_y(spectrum, matrix_y)
    spectrum = lax.all_to_all(spectrum, "grid", split_axis=0, concat_axis=1, tiled=True)
    spectrum = along_x(along_x(spectrum, matrix_x) * kernel, matrix_x)
    spectrum = lax.all_to_all(spectrum, "grid", split_axis=1, concat_axis=0, tiled=True)
    spectrum = along_y(spectrum, matrix_y)
    spectrum = lax.all_to_all(spectrum, "orb", split_axis=2, concat_axis=0, tiled=True)
    potential = along_z(spectrum, matrix_z)
    products = potential * rotated[sources]
    selector = (targets[None, :] == orbital_ids[:, None]).astype(f32)
    partial_value = -jnp.dot(selector, products.reshape(number, planes * width_yz), precision=precise)
    partial_value = partial_value.reshape(number_orbitals, planes, width_yz)
    return lax.all_to_all(partial_value, "orb", split_axis=0, concat_axis=2, tiled=True)


def solution(mesh):
    n_orb, n_grid = mesh.shape["orb"], mesh.shape["grid"]

    def on_device(orbitals, rotation, tile_list, pair_mask):
        per_device, planes, width = orbitals.shape
        fits = n_orb == 8 and 2 * tile_list.shape[0] == n_orb and planes == SUB and per_device % BLK == 0
        fits = fits and width == NY * NZ and 2 * NZ == LANES and n_grid in (2, 4, 8)
        fits = fits and per_device * SUB == LANES and rotation.shape == (LANES, LANES)
        if not fits:
            return any_device(orbitals, rotation, tile_list, pair_mask)
        return tile_device(orbitals, rotation, tile_list, pair_mask)

    in_specs = (P("orb", "grid", None), P(), P(), P())
    out_specs = P("orb", "grid", None)
    return jax.shard_map(on_device, mesh=mesh, in_specs=in_specs, out_specs=out_specs, check_vma=False)
```

```python
import functools
import itertools

import jax
import jax.numpy as jnp
import numpy as np
from jax import lax
from jax.experimental import pallas as pl
from jax.experimental.pallas import tpu as pltpu
from jax.sharding import PartitionSpec as P


BLK = 4
NY = 64
NZ = 64
LANES = 128
SUB = 8
CHUNKS = 2
COUPLING = 0.25
SCREENING = 0.1

precise = lax.Precision.HIGHEST
f32 = jnp.float32
bf16 = jnp.bfloat16

VM = pl.BlockSpec(memory_space=pltpu.VMEM)
SM = pl.BlockSpec(memory_space=pltpu.SMEM)
ANY = pl.BlockSpec(memory_space=pl.ANY)
HBM = pl.BlockSpec(memory_space=pltpu.HBM)
DMA = pltpu.SemaphoreType.DMA


def grant(mib):
    return pltpu.CompilerParams(vmem_limit_bytes=mib << 20)


def sine_np(n):
    k = np.arange(1, n + 1, dtype=np.float64)
    return np.sqrt(2.0 / (n + 1)) * np.sin(np.pi * k[:, None] * k[None, :] / (n + 1))


def eigen_np(n):
    k = np.arange(1, n + 1, dtype=np.float64)
    return 2.0 - 2.0 * np.cos(np.pi * k / (n + 1))


def halves_np(table):
    high = np.asarray(table, np.float32).astype(jnp.bfloat16)
    low = (np.asarray(table, np.float64) - high.astype(np.float64)).astype(jnp.bfloat16)
    return jnp.asarray(high), jnp.asarray(low)


def y_order():
    rows = LANES // NZ
    return np.arange(NY).reshape(NY // rows, rows).T.reshape(-1)


def y_tables():
    sine, planes = sine_np(NY), sine_np(SUB)
    even, odd = np.kron(sine[0::2, 0::2], planes), np.kron(sine[1::2, 0::2], planes)
    return np.stack([even, odd]), np.stack([even, odd.T])


def turned(x):
    count = x.shape[0] // SUB
    return jnp.concatenate([x[(count - 1 - t) * SUB:(count - t) * SUB] for t in range(count)])


def z_table():
    half = LANES // NZ
    sine = sine_np(NZ)
    table = np.zeros((2, half, NZ, half, 2, NZ))
    for pair in range(2):
        for h in range(half):
            table[pair, h, :, h, pair, :] = sine
    return table.reshape(2 * half * NZ, half * 2 * NZ)


def line_np():
    c = eigen_np(NY)[y_order()][:, None] + eigen_np(NZ)[None, :] + SCREENING
    c = np.concatenate([c, c], axis=1)
    return c, 2.0 / (2.0 + c + np.sqrt(c * (c + 4.0)))


def host_np(chips):
    table = np.zeros((chips**chips, chips), np.int32)
    for owners in itertools.product(range(chips), repeat=chips):
        best = None
        for tiles in itertools.permutations(range(chips)):
            hops = [bin(chip ^ owners[tile]).count("1") for chip, tile in enumerate(tiles)]
            cost = (max(hops), sum(hops))
            if best is None or cost < best[0]:
                best = (cost, tiles)
        table[sum(own * chips**t for t, own in enumerate(owners))] = best[1]
    return table


def dot(a, b):
    return jnp.dot(a, b, preferred_element_type=f32)


def split(x):
    high = x.astype(bf16)
    return high, (x - high.astype(f32)).astype(bf16)


def dot3(a, b):
    return dot(a[0], b[0]) + dot(a[0], b[1]) + dot(a[1], b[0])


def my_core():
    return lax.rem(lax.axis_index("orb"), 2)


def my_place():
    o = lax.axis_index("orb")
    return o, lax.rem(o, 2), lax.div(o, 2)


def fetch(source, whole, sem, side):
    number, half = sem.shape[0], whole.shape[2]
    step = whole.shape[0] // number
    lanes = pl.ds(pl.multiple_of(side * half, LANES), half)
    return [
        pltpu.make_async_copy(source.at[pl.ds(n * step, step), :, lanes], whole.at[pl.ds(n * step, step)], sem.at[n])
        for n in range(number)
    ]


def hand_out(whole, outs):
    for n, out in enumerate(outs):
        out[...] = whole[:, :, n * out.shape[2]:(n + 1) * out.shape[2]]


def fetch_kernel(source, *rest):
    outs, (whole, sem) = rest[:-2], rest[-2:]
    copies = fetch(source, whole, sem, 1 - my_core())
    for copy in copies:
        copy.start()
    for copy in copies:
        copy.wait()
    hand_out(whole, outs)


class Place:
    def __init__(self, per_device, tiles, host):
        self.o, self.core, self.chip = my_place()
        self.tiles, self.host = tiles, host
        self.chips = tiles.shape[0]
        owners = [lax.div(tiles[t, 0] * BLK, 2 * per_device) for t in range(self.chips)]
        key, same = 0, True
        for t in range(self.chips):
            key = key + owners[t] * self.chips**t
            same = same & (owners[t] == owners[0])
        self.key, self.same = key, same
        self.bit_1 = jnp.where(self.core == 0, 1, 2)
        self.bit_2 = 3 - self.bit_1

    def tile(self, chip):
        return self.host[self.key * self.chips + chip]

    def heads(self, chip):
        tile = self.tile(chip)
        return BLK * self.tiles[tile, 0], BLK * self.tiles[tile, 1]


def setup_kernel(per_device, tiles, host, rotation, source, after, *rest):
    outs, (high, low, whole, sem) = rest[:-4], rest[-4:]
    core = my_core()
    copies = fetch(source, whole, sem, core)
    for copy in copies:
        copy.start()
    at = Place(per_device, tiles, host)
    pair = BLK // 2
    heads = [at.heads(chip) for chip in (at.chip ^ 3, at.chip ^ at.bit_1, at.chip ^ at.bit_2, at.chip)]
    wanted = []
    for a, b in heads:
        wanted += [a + (1 - core) * pair] + [b + w for w in range(BLK)] + [a + core * pair]
    for u in range(1, pair):
        for a, b in heads:
            wanted += [a + (1 - core) * pair + u, a + core * pair + u]
    lane = lax.broadcasted_iota(jnp.int32, (SUB, LANES), 1)
    chosen = jnp.concatenate([jnp.where(lane == n, 1.0, 0.0) for n in wanted]).astype(bf16)
    rows = chosen.shape[0]
    row = lax.broadcasted_iota(jnp.int32, (LANES, LANES), 0)
    column = lax.broadcasted_iota(jnp.int32, (LANES, LANES), 1)
    columns = [
        jnp.where(row - (at.o ^ e) * per_device == jnp.right_shift(column, 3), 1.0, 0.0).astype(bf16)
        for e in range(2)
    ]
    keep = (lax.broadcasted_iota(jnp.int32, (rows, LANES), 0) & (SUB - 1)) == (
        lax.broadcasted_iota(jnp.int32, (rows, LANES), 1) & (SUB - 1)
    )
    for out, values in zip((high, low), split(rotation[...])):
        picked = lax.dot_general(chosen, values, (((1,), (1,)), ((), ())), preferred_element_type=f32).astype(bf16)
        for e in range(2):
            out[:, e * LANES:(e + 1) * LANES] = jnp.where(keep, dot(picked, columns[e]), 0.0).astype(bf16)
    for copy in copies:
        copy.wait()
    hand_out(whole, outs)


def ready_kernel(per_device, n_grid, tiles, host, mask, log_r, *rest):
    out, powers, flags, match, alone, zeros, sem = rest[-7:]
    zeros[...] = jnp.zeros(zeros.shape, f32)
    step = zeros.shape[0]
    copies = [
        pltpu.make_async_copy(zeros, out.at[pl.ds(n * step, step)], sem.at[n]) for n in range(out.shape[0] // step)
    ]
    for copy in copies:
        copy.start()
    begin, size_x = SUB * lax.axis_index("grid"), SUB * n_grid
    exponents = (
        2 * begin + SUB + 1,
        2 * size_x + 1 - SUB - 2 * begin,
        2 * size_x + 2 - 2 * begin,
        2 * begin,
        2 * begin + 2 * SUB + 2,
        2 * size_x - 2 * SUB - 2 * begin,
    )
    for n, exponent in enumerate(exponents):
        power = jnp.exp(exponent.astype(f32) * log_r[...])
        powers[n] = power if n < 2 else 1.0 - power
    at = Place(per_device, tiles, host)
    alone[0] = at.same.astype(jnp.int32)
    a, b = at.heads(at.chip)
    pair = BLK // 2
    live = mask[...].astype(f32)
    row = lax.broadcasted_iota(jnp.int32, live.shape, 0)
    column = lax.broadcasted_iota(jnp.int32, (1, live.shape[1]), 1)
    for u in range(pair):
        line = jnp.sum(jnp.where(row == a + at.core * pair + u, live, 0.0), axis=0, keepdims=True)
        for w in range(BLK):
            flag = jnp.sum(jnp.where(column == b + w, line, 0.0), axis=1, keepdims=True)
            flags[u * BLK + w:u * BLK + w + 1, :] = jnp.broadcast_to(flag, (1, LANES))
    blocks = per_device // BLK
    flips = ((0, at.bit_1, at.bit_2), (0, at.bit_2, at.bit_1))
    near, far = 0, 0
    for side in range(2):
        homes = [tiles[at.tile(at.chip ^ flip), 0] for flip in flips[side] + (3,)]
        for block in range(blocks):
            bits = [(home == at.o * blocks + block).astype(jnp.int32) for home in homes]
            for n in range(3):
                near = near + bits[n] * (1 << ((2 * block + side) * 3 + n))
            far = far + bits[3] * (1 << (2 * block + side))
    match[0:1, :] = jnp.full((1, LANES), near.astype(f32))
    match[1:2, :] = jnp.full((1, LANES), far.astype(f32))
    for copy in copies:
        copy.wait()


def join_kernel(x, y, out):
    out[0] = x[...]
    out[1] = y[...]


def rotate_kernel(first, high, low, *rest):
    send, keep = rest[-2:]
    rows = send.shape[0] * SUB
    part = pl.ds(first, 2 * rows)
    table = (high[part, :], low[part, :])
    at = 0
    step = 2 * LANES
    while at < send.shape[2]:
        width = rest[0].shape[2]
        n, inner = at // width, at % width
        lanes = slice(inner, inner + step)
        mine, theirs = rest[2 * n], rest[2 * n + 1]
        depth = mine.shape[0] * SUB
        cells = jnp.concatenate([mine[:, :, lanes].reshape(depth, step), theirs[:, :, lanes].reshape(depth, step)])
        total = dot3(table, split(cells))
        lanes = slice(at, at + step)
        send[:, :, lanes] = total[:rows].reshape(send.shape[0], SUB, step)
        keep[:, :, lanes] = total[rows:].reshape(keep.shape[0], SUB, step)
        at += step


def pass_kernel(keep, got, *rest):
    out = rest[-1]
    count = out.shape[0]
    out[...] = keep[:count] + got[:count]


def finish_kernel(keep, got, passed, *rest):
    out = rest[-1]
    count = out.shape[0]
    out[...] = keep[count:] + got[count:] + passed[...]


def sub_sums(values):
    row = lax.broadcasted_iota(jnp.int32, values[0].shape, 0)
    for s in (4, 2):
        low = (row & s) == 0
        paired = []
        for n in range(s):
            a, b = values[n], values[n + s]
            paired.append(jnp.where(low, a, pltpu.roll(b, s, 0)) + jnp.where(low, pltpu.roll(a, SUB - s, 0), b))
        values = paired
    even = (row & 1) == 0
    a, b = values
    return jnp.where(even, a, pltpu.roll(b, 1, 0)), jnp.where(even, pltpu.roll(a, SUB - 1, 0), b)


def fields(u, own, other, first_own, first_other):
    table = []
    for side, sources, targets in ((0, first_own, own), (1, first_other, other)):
        for n, ref in enumerate(sources):
            if u == 0:
                table.append((side, n, ref, targets[n], BLK + 1 if side == 0 else 0, 0))
            else:
                table.append((side, n, ref, targets[0], 1 if side == 0 else 0, n * ref.shape[2]))
    return table


def forward_kernel(u, counts, *refs):
    groups = []
    for count in counts[:-1]:
        groups.append(refs[:count])
        refs = refs[count:]
    first_own, first_other, own, other = groups[:4]
    y_hi, y_lo, z_hi, z_lo, ends, powers = refs[:6]
    messages, (spectrum, a_out, b_out, dens) = refs[-4 - counts[-1]:-4], refs[-4:]
    if u == 0:
        own, other = first_own, first_other
    core, g = my_core(), lax.axis_index("grid")
    tiles = first_own[0].shape[2] // LANES
    for side, n, source, target, slot, offset in fields(u, own, other, first_own, first_other):
        half = (core if side == 0 else 1 - core) * (len(first_own) * tiles * SUB)
        for t in range(tiles):
            lanes = pl.ds(t * LANES, LANES)
            value = target[slot, :, pl.ds(offset + t * LANES, LANES)]
            rows = pl.ds(pl.multiple_of(half + (n * tiles + t) * SUB, SUB), SUB)
            for w in range(BLK):
                dens[rows, w * LANES:(w + 1) * LANES] = value * source[1 + w, :, lanes]
    z = (z_hi[...], z_lo[...])
    half = dens.shape[0]
    for q in range(BLK // 2):
        out = dot3(split(dens[:, q * 2 * LANES:(q + 1) * 2 * LANES]), z)
        mirror = turned(out[:, LANES:])
        spectrum[:half, q * LANES:(q + 1) * LANES] = out[:, :LANES] + mirror
        spectrum[half:, q * LANES:(q + 1) * LANES] = out[:, :LANES] - mirror
    for parity in range(2):
        part = pl.ds(parity * half, half)
        spectrum[part, :] = dot3((y_hi[parity], y_lo[parity]), split(spectrum[part, :]))

    def reduce(group, carry):
        lines = pl.ds(pl.multiple_of(group * SUB, SUB), SUB)
        near, far = powers[0, lines, :], powers[1, lines, :]
        for q in range(BLK // 2):
            lanes = slice(q * LANES, (q + 1) * LANES)
            values = []
            for k in range(SUB):
                rows = pl.ds(pl.multiple_of((group * SUB + k) * SUB, SUB), SUB)
                values.append(ends[rows, :] * spectrum[rows, lanes])
            even, odd = sub_sums(values)
            rightward = (even + odd) - near * (even - odd)
            leftward = (even - odd) - far * (even + odd)
            a_out[lines, lanes] = rightward
            b_out[lines, lanes] = leftward
            for k, out in enumerate(messages, 1):
                out[lines, lanes] = jnp.where((g ^ k) > g, rightward, leftward)
        return carry

    lax.fori_loop(0, NY // SUB, reduce, 0)


def backward_kernel(u, counts, flags, *refs):
    groups = []
    for count in counts:
        groups.append(refs[:count])
        refs = refs[count:]
    own, other, received = groups
    (y_hi, y_lo, z_hi, z_lo, inverse, basis, powers, steady, spectrum, a_in, b_in) = refs[:11]
    out, work, pot = refs[-3:]
    core, g = my_core(), lax.axis_index("grid")
    tiles = own[0].shape[2] // LANES
    first, last = basis[0], basis[1]

    def ends(group, carry):
        lines = pl.ds(pl.multiple_of(group * SUB, SUB), SUB)
        scale, r, slab = steady[0, lines, :], steady[1, lines, :], steady[2, lines, :]
        decays = [None, jnp.ones((SUB, LANES), f32), slab]
        while len(decays) <= len(received):
            decays.append(decays[-1] * slab)
        for q in range(BLK // 2):
            lanes = slice(q * LANES, (q + 1) * LANES)
            from_left = from_right = jnp.zeros((SUB, LANES), f32)
            for n, ref in enumerate(received, 1):
                distance = jnp.abs((g ^ n) - g)
                factor = decays[n]
                for d in range(1, n):
                    factor = jnp.where(distance == d, decays[d], factor)
                value = factor * ref[lines, lanes]
                is_left = (g ^ n) < g
                from_left = from_left + jnp.where(is_left, value, 0.0)
                from_right = from_right + jnp.where(is_left, 0.0, value)
            before = scale * (powers[2, lines, :] * from_left
                              + r * powers[3, lines, :] * (b_in[lines, lanes] + slab * from_right))
            after = scale * (powers[4, lines, :] * from_right
                             + r * powers[5, lines, :] * (a_in[lines, lanes] + slab * from_left))
            for k in range(SUB):
                rows = pl.ds(pl.multiple_of((group * SUB + k) * SUB, SUB), SUB)
                edge = first * before[k:k + 1] + last * after[k:k + 1]
                work[rows, lanes] = inverse[rows, :] * (spectrum[rows, lanes] + edge)
        return carry

    lax.fori_loop(0, NY // SUB, ends, 0)
    z = (z_hi[...], z_lo[...])
    half = pot.shape[0]
    for parity in range(2):
        part = pl.ds(parity * half, half)
        work[part, :] = dot3((y_hi[parity], y_lo[parity]), split(work[part, :]))
    for q in range(BLK // 2):
        lanes = slice(q * LANES, (q + 1) * LANES)
        even, odd = work[:half, lanes], work[half:, lanes]
        rows = jnp.concatenate([even + odd, turned(even - odd)], axis=1)
        pot[:, q * 2 * LANES:(q + 1) * 2 * LANES] = dot3(split(rows), z)
    live = [jnp.broadcast_to(flags[u * BLK + w:u * BLK + w + 1, :], (SUB, LANES)) for w in range(BLK)]
    for side, group in ((0, own), (1, other)):
        half = (core if side == 0 else 1 - core) * (len(own) * tiles)
        for n, ref in enumerate(group):
            for t in range(tiles):
                lanes = pl.ds(t * LANES, LANES)
                at = half + n * tiles + t
                rows = pl.ds(pl.multiple_of(at * SUB, SUB), SUB)
                total = None
                for w in range(BLK):
                    term = live[w] * (pot[rows, w * LANES:(w + 1) * LANES] * ref[1 + w, :, lanes])
                    total = term if total is None else total + term
                out[:, pl.ds(pl.multiple_of(at * LANES, LANES), LANES)] = -total


def place_kernel(match, *refs):
    parts, (out, rows, sem) = refs[:-4], refs[-3:]
    pair = BLK // 2
    blocks = out.shape[0] // BLK
    core = my_core()
    values = []
    for part in parts:
        values += [part] if len(part.shape) == 2 else [part.at[n] for n in range(part.shape[0])]
    parts, count = values, len(values) // pair
    near = jnp.max(match[0:1, :]).astype(jnp.int32)
    far = jnp.max(match[1:2, :]).astype(jnp.int32) if count > 6 else None

    def hits(b, side):
        at = 2 * b + side
        bits = [(near & (1 << (at * 3 + n))) for n in range(3)]
        if far is not None:
            bits.append(far & (1 << at))
        return [(bit, side * count // 2 + n) for n, bit in enumerate(bits)]

    def found(b, side):
        at = 2 * b + side
        any_near = near & (7 << (at * 3))
        return any_near != 0 if far is None else (any_near != 0) | ((far & (1 << at)) != 0)

    def move(b, side):
        which = core if side == 0 else 1 - core
        at = b * BLK + which * pair
        return pltpu.make_async_copy(rows.at[b, side], out.at[pl.ds(at, pair)], sem.at[b, side])

    for b in range(blocks):
        for side in range(2):

            @pl.when(found(b, side))
            def _():
                rows[b, side] = jnp.zeros(rows.shape[2:], f32)
                for hit, n in hits(b, side):

                    @pl.when(hit != 0)
                    def _():
                        for u in range(pair):
                            rows[b, side, u] += parts[u * count + n][...]

                move(b, side).start()

    for b in range(blocks):
        for side in range(2):

            @pl.when(found(b, side))
            def _():
                move(b, side).wait()


def tile_device(orbitals, rotation, tile_list, pair_mask):
    shape = per_device, planes, width = orbitals.shape
    n_orb, n_grid = lax.axis_size("orb"), lax.axis_size("grid")
    size_x = planes * n_grid
    half = width // 2
    chips = n_orb // 2
    axes = ("orb", "grid")

    def swap(x, even, odd):
        moves = []
        for a in range(n_orb):
            flip = even if a % 2 == 0 else odd
            moves += [(a * n_grid + b, (a ^ flip) * n_grid + b) for b in range(n_grid)]
        return lax.ppermute(x, axes, moves)

    def cross(x, k):
        moves = [(a * n_grid + b, a * n_grid + (b ^ k)) for a in range(n_orb) for b in range(n_grid)]
        return lax.ppermute(x, axes, moves)

    chunk = half // CHUNKS
    orbitals = pltpu.with_memory_space_constraint(orbitals, pltpu.HBM)

    part = jax.ShapeDtypeStruct((per_device, planes, chunk), f32)
    scratch = [pltpu.VMEM((per_device, planes, half), f32), DMA((4,))]
    fetched = pl.pallas_call(
        fetch_kernel, out_shape=[part] * CHUNKS, in_specs=[HBM], out_specs=[VM] * CHUNKS,
        scratch_shapes=scratch, name="fetch", compiler_params=grant(8),
    )(orbitals)
    theirs = []
    for taken in fetched:
        theirs.append(swap(taken, 1, 1))

    pair = BLK // 2
    firsts = (BLK + 2) * chips
    rows = (firsts + 2 * (pair - 1) * chips) * SUB
    wide_table = jax.ShapeDtypeStruct((rows, 2 * LANES), bf16)
    blocks = per_device // BLK
    c, r = line_np()
    c, r = line_np()
    host = jnp.asarray(host_np(chips).reshape(-1))
    *mine, high, low = pl.pallas_call(
        functools.partial(setup_kernel, per_device), out_shape=[part] * CHUNKS + [wide_table] * 2,
        in_specs=[SM, SM, VM, HBM, ANY], out_specs=[VM] * (CHUNKS + 2), scratch_shapes=scratch, name="setup",
        compiler_params=grant(8),
    )(tile_list, host, rotation, orbitals, taken)

    def rotate(first, count, fields, *after):
        part = jax.ShapeDtypeStruct((count, planes, chunk * (len(fields) // 2)), f32)
        send, keep = pl.pallas_call(
            functools.partial(rotate_kernel, first * SUB), out_shape=(part, part),
            in_specs=[VM] * (2 + len(fields)) + [ANY] * len(after),
            out_specs=(VM, VM), compiler_params=grant(8),
        )(high, low, *fields, *after)
        return send, keep, swap(send, 2, 4)

    sums, last = [], ()
    for n in range(CHUNKS):
        sums.append(rotate(0, firsts // 2, [mine[n], theirs[n]], *last))
        last = (sums[-1][0],)
    both = [x for n in range(CHUNKS) for x in (mine[n], theirs[n])]
    sums.append(rotate(firsts, (pair - 1) * chips, both, *last))
    passing, own, other = [], [], []

    def pass_on(n, *after, spec=ANY):
        _, keep, got = sums[n]
        count = keep.shape[0] // 2
        value = pl.pallas_call(
            pass_kernel, out_shape=jax.ShapeDtypeStruct((count,) + keep.shape[1:], f32),
            in_specs=[VM] * 2 + [spec] * len(after), out_specs=VM, compiler_params=grant(4),
        )(keep, got, *after)
        passing.append((keep, got, swap(value, 4, 2)))
        return value

    def finish(n, *after):
        keep, got, passed = passing[n]
        own.append(pl.pallas_call(
            finish_kernel, out_shape=jax.ShapeDtypeStruct(passed.shape, f32), in_specs=[VM] * 3 + [ANY] * len(after),
            out_specs=VM, compiler_params=grant(4),
        )(keep, got, passed, *after))
        other.append(swap(own[-1], 1, 1))
        return own[-1]

    step = pass_on(0, sums[-1][0])
    empty, powers, flags, match, alone = pl.pallas_call(
        functools.partial(ready_kernel, per_device, n_grid),
        out_shape=(pltpu.HBM(shape, f32), jax.ShapeDtypeStruct((6, NY, LANES), f32),
                   jax.ShapeDtypeStruct((pair * BLK, LANES), f32), jax.ShapeDtypeStruct((SUB, LANES), f32),
                   jax.ShapeDtypeStruct((1,), jnp.int32)),
        in_specs=[SM, SM, VM, VM, ANY], out_specs=(HBM, VM, VM, VM, SM),
        scratch_shapes=[pltpu.VMEM((pair, planes, width), f32), DMA((per_device // pair,))], name="ready",
        compiler_params=grant(4),
    )(tile_list, host, pair_mask, jnp.asarray(np.log(r), f32), step)
    step = pass_on(1, empty, spec=HBM)
    for n in range(2, CHUNKS):
        step = pass_on(n, step)
    for n in range(CHUNKS):
        step = finish(n, step)
    last = (pass_on(CHUNKS, step),)

    sine_x, eigen_x = sine_np(planes), eigen_np(planes)
    ends = jnp.asarray(np.einsum("jp,pkl->kjl", sine_x, r[None] ** np.arange(planes - 1, -1, -1)[:, None, None])
                       .reshape(-1, LANES), f32)
    inverse = jnp.asarray((COUPLING / (eigen_x[None, :, None] + c[:, None, :])).reshape(-1, LANES), f32)
    basis = jnp.asarray(np.broadcast_to(sine_x[:, [0, -1]].T[:, :, None], (2, planes, LANES)), f32)
    steady = jnp.asarray(np.stack([r / ((1 - r**2) * (1 - r ** (2 * size_x + 2))), r, r**planes]), f32)

    y_there, y_back = y_tables()
    y_hi, y_lo = halves_np(y_there)
    yt_hi, yt_lo = halves_np(y_back)
    z_hi, z_lo = halves_np(z_table())
    zt_hi, zt_lo = halves_np(z_table().T)
    solved = []
    lines = jax.ShapeDtypeStruct((NY, 2 * LANES), f32)
    cube = (NY * SUB, 2 * LANES)
    wide = pltpu.VMEM((width // LANES * SUB, BLK * LANES), f32)
    base_own, base_other = own[:CHUNKS], other[:CHUNKS]
    for u in range(pair):
        if u:
            finish(CHUNKS, *last)
        more_own, more_other = own[CHUNKS:][:u], other[CHUNKS:][:u]
        counts = (CHUNKS, CHUNKS, len(more_own), len(more_other))
        inputs = [*base_own, *base_other, *more_own, *more_other, y_hi, y_lo, z_hi, z_lo, ends, powers]
        *messages, spectrum, a, b = pl.pallas_call(
            functools.partial(forward_kernel, u, counts + (n_grid - 1,)),
            out_shape=[lines] * (n_grid - 1) + [jax.ShapeDtypeStruct(cube, f32), lines, lines],
            in_specs=[VM] * len(inputs) + [ANY] * len(last),
            out_specs=[VM] * (n_grid + 2),
            scratch_shapes=[wide],
            compiler_params=grant(16),
        )(*inputs, *last)
        last = (spectrum,)
        received = []
        for k, message in enumerate(messages, 1):
            received.append(cross(message, k))
        solved.append((spectrum, a, b, received))

    terms, last = [], ()
    for u, (spectrum, a, b, received) in enumerate(solved):
        inputs = [*base_own, *base_other, *received, yt_hi, yt_lo, zt_hi, zt_lo, inverse, basis, powers, steady,
                  spectrum, a, b]
        terms.append(pl.pallas_call(
            functools.partial(backward_kernel, u, (CHUNKS, CHUNKS, len(received))),
            out_shape=jax.ShapeDtypeStruct((planes, width), f32),
            in_specs=[VM] * (1 + len(inputs)) + [ANY] * len(last),
            out_specs=VM,
            scratch_shapes=[pltpu.VMEM(cube, f32), wide],
            compiler_params=grant(16),
        )(flags, *inputs, *last))
        last = (terms[-1],)

    near_1 = [swap(term, 2, 4) for term in terms]
    near_2 = [swap(term, 4, 2) for term in terms]
    own_parts = [[term, x, y] for term, x, y in zip(terms, near_1, near_2)]
    sib_parts = []
    for term, x, y in own_parts:
        joined = pl.pallas_call(
            join_kernel, out_shape=jax.ShapeDtypeStruct((2,) + term.shape, f32), in_specs=[VM] * 2, out_specs=VM,
            compiler_params=grant(4),
        )(x, y)
        given = swap(term, 1, 1)
        sib_parts.append([given, swap(joined, 1, 1)])

    def place(target, groups):
        parts = [part for group in groups for part in group]
        return pl.pallas_call(
            place_kernel,
            out_shape=pltpu.HBM(shape, f32),
            in_specs=[VM] * (1 + len(parts)) + [HBM],
            out_specs=HBM,
            input_output_aliases={len(parts) + 1: 0},
            scratch_shapes=[pltpu.VMEM((blocks, 2, pair, planes, width), f32), DMA((blocks, 2))],
            name="place",
            compiler_params=grant(8),
        )(match, *parts, target)

    def place_near(target, mine, sibs):
        return place(target, [a + b for a, b in zip(mine, sibs)])

    def place_far(target, mine, sibs):
        far = [swap(group[1], 4, 2) for group in mine]
        return place(target, [a + [x] + b + [swap(x, 1, 1)] for a, b, x in zip(mine, sibs, far)])

    return lax.cond(alone[0] != 0, place_far, place_near, empty, own_parts, sib_parts)


def sine_table(length):
    wave_index = jnp.arange(length, dtype=f32) + 1.0
    return jnp.sqrt(2.0 / (length + 1.0)) * jnp.sin(
        jnp.pi * wave_index[:, None] * wave_index[None, :] / (length + 1.0)
    )


def eigen_values(length):
    wave_index = jnp.arange(length, dtype=f32) + 1.0
    return 2.0 - 2.0 * jnp.cos(jnp.pi * wave_index / (length + 1.0))


def green_kernel(size_x, size_y, size_z):
    summed = (
        eigen_values(size_x)[:, None, None]
        + eigen_values(size_y)[None, :, None]
        + eigen_values(size_z)[None, None, :]
    )
    return COUPLING / (summed + SCREENING)


def pair_lists(tile_list, pair_mask):
    within = jnp.arange(BLK * BLK, dtype=jnp.int32)
    targets = (BLK * tile_list[:, 0:1] + within[None, :] // BLK).reshape(-1)
    sources = (BLK * tile_list[:, 1:2] + within[None, :] % BLK).reshape(-1)
    return (targets, sources, pair_mask[targets, sources])


def compact(targets, sources, live_flags, number):
    ranking = jnp.cumsum(live_flags) - 1
    places = jnp.where(live_flags == 1, ranking, number)
    picked = (
        jnp.zeros((number,), jnp.int32)
        .at[places]
        .set(jnp.arange(live_flags.shape[0], dtype=jnp.int32), mode="drop")
    )
    return (targets[picked], sources[picked])


def along_z(values, matrix):
    number, planes, width_yz = values.shape
    size_z = matrix.shape[0]
    shaped = values.reshape(number, planes, width_yz // size_z, size_z)
    return jnp.einsum("pxrz,zk->pxrk", shaped, matrix, precision=precise).reshape(number, planes, width_yz)


def along_y(values, matrix):
    number, planes, width_yz = values.shape
    size_y = matrix.shape[0]
    shaped = values.reshape(number, planes, size_y, width_yz // size_y)
    return jnp.einsum("pxyz,yk->pxkz", shaped, matrix, precision=precise).reshape(number, planes, width_yz)


def along_x(values, matrix):
    return jnp.einsum("pxc,xk->pkc", values, matrix, precision=precise)


def any_device(orbitals, rotation, tile_list, pair_mask):
    n_grid = lax.axis_size("grid")
    number_orbitals, size_x = rotation.shape[0], orbitals.shape[1] * n_grid
    rotated = jnp.einsum(
        "ij,ixc->jxc",
        rotation,
        lax.all_to_all(orbitals, "orb", split_axis=2, concat_axis=0, tiled=True),
        precision=precise,
    )
    planes, width_yz = rotated.shape[1:]
    targets, sources, live_flags = pair_lists(tile_list, pair_mask)
    matrix_x, matrix_y, matrix_z = sine_table(size_x), sine_table(NY), sine_table(NZ)
    kernel = green_kernel(size_x, NY, NZ).reshape(size_x, NY * NZ)
    orbital_ids = jnp.arange(number_orbitals, dtype=jnp.int32)
    targets, sources = compact(targets, sources, live_flags, targets.shape[0] // 2)
    density = rotated[targets] * rotated[sources]
    number = density.shape[0]
    spectrum = along_z(density, matrix_z)
    spectrum = lax.all_to_all(spectrum, "orb", split_axis=0, concat_axis=2, tiled=True)
    spectrum = along_y(spectrum, matrix_y)
    spectrum = lax.all_to_all(spectrum, "grid", split_axis=0, concat_axis=1, tiled=True)
    spectrum = along_x(along_x(spectrum, matrix_x) * kernel, matrix_x)
    spectrum = lax.all_to_all(spectrum, "grid", split_axis=1, concat_axis=0, tiled=True)
    spectrum = along_y(spectrum, matrix_y)
    spectrum = lax.all_to_all(spectrum, "orb", split_axis=2, concat_axis=0, tiled=True)
    potential = along_z(spectrum, matrix_z)
    products = potential * rotated[sources]
    selector = (targets[None, :] == orbital_ids[:, None]).astype(f32)
    partial_value = -jnp.dot(selector, products.reshape(number, planes * width_yz), precision=precise)
    partial_value = partial_value.reshape(number_orbitals, planes, width_yz)
    return lax.all_to_all(partial_value, "orb", split_axis=0, concat_axis=2, tiled=True)


def solution(mesh):
    n_orb, n_grid = mesh.shape["orb"], mesh.shape["grid"]

    def on_device(orbitals, rotation, tile_list, pair_mask):
        per_device, planes, width = orbitals.shape
        fits = n_orb == 8 and 2 * tile_list.shape[0] == n_orb and planes == SUB and per_device % BLK == 0
        fits = fits and width == NY * NZ and 2 * NZ == LANES and n_grid in (2, 4, 8)
        fits = fits and per_device * SUB == LANES and rotation.shape == (LANES, LANES)
        if not fits:
            return any_device(orbitals, rotation, tile_list, pair_mask)
        return tile_device(orbitals, rotation, tile_list, pair_mask)

    in_specs = (P("orb", "grid", None), P(), P(), P())
    out_specs = P("orb", "grid", None)
    return jax.shard_map(on_device, mesh=mesh, in_specs=in_specs, out_specs=out_specs, check_vma=False)
```
